32 devices in a mesh: lon: 8 (over y, x, core), lat: 4 (over z).
Axes of the slice: x: 2, y: 2, z: 4, core: 2. Of those that a mesh axis runs over, the one named last changes fastest.
Arguments:
- checkpoint: float32 [4, 256, 9600], P('lat', 'lon'), may hold values from -6 to 6
- slot_dest: int32 [4, 256], P('lat'), may hold values from -1 to 255, as said below
- kmt: int32 [640, 3840], P('lat', 'lon'), may hold values from 0 to 2, as said below
- kappa: float32 [2, 640, 3840], P(None, 'lat', 'lon'), may hold values from 0.02 to 0.2
Outputs:
- new_tracer: float32 [2, 2, 640, 3840], P(None, None, 'lat', 'lon')
- stream: float32 [640, 3840], P('lat', 'lon')
The draws below stay inside these ranges and needn't reach their ends.
Inputs may be any that keep to these rules, and one draw needn't show every extreme that they name: `slot_dest`: in each band every value e * 32 + p is named by at most one slot; at most 4 slots of one checkpoint owner's 32 slots name one new owner e, and exactly 4 for some pair in every band. Positions that no slot names are land blocks. kmt is 0 on every point of a land block.
All inputs are finite; a program needn't handle non-finite values.
Results may differ from the reference program's by a relative error of at most 0.0001.
Values sent between devices are 32-bit elements; how exact they have to be, the bound alone decides.
No kernel may reach another device: no remote copies, remote signals or barrier semaphores. Data moves between devices by JAX's collectives and lax.ppermute only.
A program may use at most 128 MiB of HBM per device.

```python
import math
import jax
import jax.numpy as jnp

BH = 40
BW = 60
LEV = 2
BX = 8
BY = 4
ITERS = 3
Q = 32
PAYN = 9600
GY = 640
GX = 3840
N_LON = 8
N_LAT = 4


def ocean_layout(key):
    base = jax.random.fold_in(key, 11)
    capacity = Q // N_LON

    def one_band(band_key):
        keys = jax.random.split(band_key, 4)
        spots = jax.vmap(lambda k: jax.random.permutation(k, Q))(jax.random.split(keys[0], N_LON))
        slots = jax.vmap(lambda k: jax.random.permutation(k, Q))(jax.random.split(keys[1], N_LON))
        offset = jax.random.randint(keys[2], (), 1, N_LON)
        shape = (N_LON, N_LON, capacity)
        source = jnp.broadcast_to(jnp.arange(N_LON, dtype=jnp.int32)[:, None, None], shape)
        target = jnp.broadcast_to(jnp.arange(N_LON, dtype=jnp.int32)[None, :, None], shape)
        copy_id = jnp.broadcast_to(jnp.arange(capacity, dtype=jnp.int32)[None, None, :], shape)
        draw_ten = jax.random.randint(keys[3], shape, 0, 10)
        ocean = (draw_ten < 7) | (source == (target + offset) % N_LON)
        position = spots[target, source * capacity + copy_id]
        slot = slots[source, target * capacity + copy_id]
        value = jnp.where(ocean, target * Q + position, -1)
        dest = jnp.zeros((N_LON, Q), jnp.int32).at[source, slot].set(value)
        present = jnp.zeros((N_LON, Q), jnp.int32).at[target, position].set(ocean.astype(jnp.int32))
        return (dest.reshape(N_LON * Q), present)
    return jax.vmap(one_band)(jax.random.split(base, N_LAT))


def draw_slot_dest(key, part):
    dest, present = ocean_layout(key)
    return dest.astype(jnp.int32)


def draw_kmt(key, part):
    dest, present = ocean_layout(key)
    blockmap = present.reshape(N_LAT, N_LON, BY, BX).transpose(0, 2, 1, 3).reshape(N_LAT * BY, N_LON * BX)
    cells = jnp.repeat(jnp.repeat(blockmap, BH, axis=0), BW, axis=1)
    draw_many = jax.random.randint(jax.random.fold_in(key, 23), (GY, GX), 0, 16)
    levels = jnp.where(draw_many < 2, 0, 1 + draw_many % LEV)
    return (cells * levels).astype(jnp.int32)


def steps_of(key, shape, shards, least, top_value):
    factor_of = 1.0
    for dim, blocks in shards:
        heights = jax.random.uniform(jax.random.fold_in(jax.random.fold_in(key, 6), dim), (blocks,), jnp.float32, least / len(shards), top_value / len(shards))
        factor_of = factor_of * jnp.repeat(jnp.exp(heights), shape[dim] // blocks).reshape((-1,) + (1,) * (len(shape) - 1 - dim))
    return factor_of


def scatter_about(key, dims, deviation, limit, cuts=(), kind=jnp.bfloat16):
    array = jax.random.normal(key, dims, jnp.float32) * deviation
    if len(cuts) > 0:
        array = steps_of(key, dims, cuts, -0.22, 0.18) * array
    return jnp.clip(array, min=-limit, max=limit).astype(kind)


def setup_inputs(seed: int = 0) -> dict:
    seeds = jax.random.split(jax.random.key(seed), 5)
    return {
        "checkpoint": scatter_about(seeds[0], (N_LAT, N_LON * Q, PAYN), 1.0, 6.0, ((0, 4), (1, 8)), jnp.float32),
        "slot_dest": draw_slot_dest(jax.random.fold_in(seeds[4], 71), 0),
        "kmt": draw_kmt(jax.random.fold_in(seeds[4], 71), 0),
        "kappa": jnp.clip(jnp.exp(math.log(0.2) - 2.3025851 * jax.random.uniform(seeds[3], (LEV, GY, GX), jnp.float32) ** steps_of(seeds[3], (LEV, GY, GX), ((1, 4), (2, 8)), -0.2, 0.2)), 0.02, 0.2),
    }


thermal = 0.25
haline = 0.75
cabbeling = 0.05


def widen(field):
    beside_all = jnp.concatenate([field[..., -1:], field, field[..., :1]], axis=-1)
    pad_width = [(0, 0)] * (field.ndim - 2) + [(1, 1), (0, 0)]
    return jnp.pad(beside_all, pad_width)


def operate(vector, depth, column):
    wide = widen(vector)
    edges = wide[2:, 1:-1] + wide[:-2, 1:-1] + wide[1:-1, 2:] + wide[1:-1, :-2]
    corners = wide[2:, 2:] + wide[2:, :-2] + wide[:-2, 2:] + wide[:-2, :-2]
    return column * ((6.0 + depth) * vector - edges - 0.5 * corners)


def reference(checkpoint, slot_dest, kmt, kappa):
    total = N_LAT * N_LON * Q
    band = jnp.arange(N_LAT, dtype=jnp.int32)[:, None]
    target = jnp.where(slot_dest >= 0, band * (N_LON * Q) + slot_dest, total).astype(jnp.int32)
    blocks = checkpoint.reshape(total, PAYN)
    placed = jnp.zeros((total + 1, PAYN), jnp.float32).at[target.reshape(-1)].set(blocks)[:total]
    field = placed.reshape(N_LAT, N_LON, BY, BX, 2, LEV, BH, BW)
    field = field.transpose(4, 5, 0, 2, 6, 1, 3, 7).reshape(2, LEV, GY, GX)
    levels = jnp.arange(LEV, dtype=jnp.int32)
    wet = (levels[:, None, None] < kmt[None]).astype(jnp.float32)
    tracer = field * wet
    tracer_w = widen(tracer)
    wet_w = widen(wet)
    kappa_w = widen(kappa)
    tracer_c = tracer_w[..., 1:-1, 1:-1]
    wet_c = wet_w[:, 1:-1, 1:-1]
    kappa_c = kappa_w[:, 1:-1, 1:-1]
    change = jnp.zeros_like(tracer)
    for dy, dx in ((0, 1), (0, -1), (1, 0), (-1, 0)):
        rows = slice(1 + dy, 1 + dy + GY)
        cols = slice(1 + dx, 1 + dx + GX)
        face = 0.5 * (kappa_c + kappa_w[:, rows, cols]) * wet_c * wet_w[:, rows, cols]
        change = change + face * (tracer_w[..., rows, cols] - tracer_c)
    new_tracer = wet * (tracer + change)
    dz = 1.0 + 0.5 * jnp.arange(LEV, dtype=jnp.float32)
    temp = new_tracer[0]
    salt = new_tracer[1]
    density = wet * (haline * salt - thermal * temp - cabbeling * temp * temp)
    forcing = jnp.sum(dz[:, None, None] * density, axis=0)
    depth = jnp.sum(dz[:, None, None] * wet, axis=0)
    column = (kmt > 0).astype(jnp.float32)
    stream = jnp.zeros_like(forcing)
    residual = column * forcing
    direction = residual
    norm_now = jnp.sum(residual * residual)
    for step in range(ITERS):
        image = operate(direction, depth, column)
        alpha = norm_now / jnp.sum(direction * image)
        stream = stream + alpha * direction
        residual = residual - alpha * image
        norm_next = jnp.sum(residual * residual)
        direction = residual + (norm_next / norm_now) * direction
        norm_now = norm_next
    return new_tracer, stream
```

```python
import functools

import jax
import jax.numpy as jnp
from jax import lax
from jax.experimental import pallas as pl
from jax.experimental.pallas import tpu as pltpu
from jax.sharding import PartitionSpec as P


BH = 40
BW = 60
LEV = 2
HALO = 4
LANES = 128
SUB = 8
PAD = 2 * SUB
ROWS = LEV * BH
SHIFT = 8.0
SCALE = 8.0

thermal = 0.25
haline = 0.75
cabbeling = 0.05

VM = pl.BlockSpec(memory_space=pltpu.VMEM)
SM = pl.BlockSpec(memory_space=pltpu.SMEM)
HB = pl.BlockSpec(memory_space=pl.ANY)
F32 = jnp.float32


def params():
    return pltpu.CompilerParams(vmem_limit_bytes=24 << 20)


def cost(flops, moved):
    return pl.CostEstimate(flops=flops, bytes_accessed=moved, transcendentals=0)


def shaped(*dims, dtype=F32):
    return jax.ShapeDtypeStruct(dims, dtype)


def lanes():
    return lax.broadcasted_iota(jnp.int32, (SUB, LANES), 1)


def turn(value, amount):
    if isinstance(amount, int):
        amount %= LANES
        if amount == 0:
            return value
    return pltpu.roll(value, amount, 1)


def strip_lane(side, by, level, tracer, block_rows):
    return HALO * (((side * block_rows + by) * LEV + level) * 2 + tracer)


def pack_kernel(n, cap, bx_n, by_n, *refs):
    dest, me_ref, blocks = refs[:3]
    outs = refs[3 : 3 + n]
    flat, packs, count, sems = refs[3 + n :]
    slots = blocks.shape[0]
    me = me_ref[0]
    lane = lanes()
    zero = jnp.zeros((SUB, LANES), F32)
    length = packs.shape[1]

    def clear(k, carry):
        count[k] = 0
        for row in range(0, length, SUB):
            packs[k, row : row + SUB, :] = zero
        return carry

    lax.fori_loop(0, n, clear, 0)

    def regroup(group, carry):
        first = pl.multiple_of(group * SUB, SUB)

        def load(q):
            return blocks[pl.ds(first, SUB), q * LANES : (q + 1) * LANES]

        def piece(start, target):
            q, o = divmod(start, LANES)
            value = load(q)
            if o + BW > LANES:
                value = jnp.where(lane >= o, value, load(q + 1))
            return turn(value, target - o)

        for row in range(ROWS):
            value = jnp.where(
                lane < BW, piece(row * BW, 0), piece((ROWS + row) * BW, BW)
            )
            flat[pl.ds(first * ROWS + row, SUB, stride=ROWS), :] = value
        return carry

    lax.fori_loop(0, slots // SUB, regroup, 0)

    def strip(i, owner, by, side):
        k = lax.bitwise_xor(owner, me)
        for level in range(LEV):
            for tracer in range(2):
                source = tracer * BW + (BW - HALO if side == 0 else 0)
                target = strip_lane(side, by, level, tracer, by_n)
                amount = lax.rem(target - source + LANES, LANES)
                here = (lane >= target) & (lane < target + HALO)
                for row in range(0, BH, SUB):
                    at = pl.multiple_of(i * ROWS + level * BH + row, SUB)
                    value = pltpu.roll(flat[pl.ds(at, SUB), :], amount, 1)
                    old = packs[k, cap * ROWS + row : cap * ROWS + row + SUB, :]
                    packs[k, cap * ROWS + row : cap * ROWS + row + SUB, :] = jnp.where(
                        here, value, old
                    )

    def place(i, carry):
        d = dest[me * slots + i]

        @pl.when(d >= 0)
        def _():
            owner = lax.div(d, slots)
            spot = lax.rem(d, slots)
            k = lax.bitwise_xor(owner, me)
            c = count[k]
            count[k] = c + 1
            for row in range(0, ROWS, SUB):
                packs[k, pl.ds(pl.multiple_of(c * ROWS + row, SUB), SUB), :] = flat[
                    pl.ds(pl.multiple_of(i * ROWS + row, SUB), SUB), :
                ]
            bx = lax.rem(spot, bx_n)
            by = lax.div(spot, bx_n)

            @pl.when(bx == bx_n - 1)
            def _():
                strip(i, lax.rem(owner + 1, n), by, 0)

            @pl.when(bx == 0)
            def _():
                strip(i, lax.rem(owner + n - 1, n), by, 1)

        return carry

    lax.fori_loop(0, slots, place, 0)
    copies = [
        pltpu.make_async_copy(packs.at[k], outs[k], sems.at[k]) for k in range(n)
    ]
    for copy in copies:
        copy.start()
    for copy in copies:
        copy.wait()


def edge_kernel(n, cap, bx_n, by_n, length, dest, me_ref, kmt, kappa, west, east, table):
    lane = lanes()
    me = me_ref[0]
    slots = bx_n * by_n
    last = kmt.shape[1] - HALO
    zero = jnp.zeros((SUB, LANES), F32)
    for row in range(0, BH, SUB):
        for out, start in ((west, 0), (east, last)):
            tile = start // LANES * LANES
            width = min(LANES, kmt.shape[1] - tile)
            total = zero
            for by in range(by_n):
                for ch in range(1 + LEV):
                    at = slice(by * BH + row, by * BH + row + SUB)
                    if ch == 0:
                        value = kmt[at, tile : tile + width].astype(F32)
                    else:
                        value = kappa[ch - 1, at, tile : tile + width]
                    if width < LANES:
                        value = jnp.concatenate([value, zero[:, width:]], axis=1)
                    target = HALO * (by * (1 + LEV) + ch)
                    value = turn(value, target - (start - tile))
                    total = jnp.where(
                        (lane >= target) & (lane < target + HALO), value, total
                    )
            out[row : row + SUB, :] = total

    for p in range(slots + 2 * by_n):
        table[p] = 0

    def owner_loop(s, carry):
        base = lax.bitwise_xor(s, me) * length

        def slot_loop(i, c):
            d = dest[s * slots + i]
            owner = lax.select(d >= 0, lax.div(d, slots), -2)
            spot = lax.rem(d, slots)
            by = lax.div(spot, bx_n)
            bx = lax.rem(spot, bx_n)
            mine = owner == me

            @pl.when(mine)
            def _():
                table[spot] = base + c * ROWS

            @pl.when((owner == lax.rem(me + n - 1, n)) & (bx == bx_n - 1))
            def _():
                table[slots + by] = base + cap * ROWS

            @pl.when((owner == lax.rem(me + 1, n)) & (bx == 0))
            def _():
                table[slots + by_n + by] = base + cap * ROWS

            return c + mine.astype(jnp.int32)

        lax.fori_loop(0, slots, slot_loop, 0)
        return carry

    lax.fori_loop(0, n, owner_loop, 0)


def grid_kernel(n, bx_n, by_n, *refs):
    packs = refs[:n]
    table, kmt, kappa, from_west, from_east = refs[n : n + 5]
    grid, north, south, store, sems = refs[n + 5 :]
    lane = lanes()
    slots = bx_n * by_n
    length = packs[0].shape[0]
    tiles = grid.shape[1]
    cols = kmt.shape[1]
    own = cols - (tiles - 1) * LANES
    copies = [
        pltpu.make_async_copy(
            packs[k], store.at[pl.ds(k * length, length), :], sems.at[k]
        )
        for k in range(n)
    ]
    for copy in copies:
        copy.start()

    def halo(value, east_value, east_lane, west_value, west_lane):
        value = jnp.where(
            (lane >= own) & (lane < own + HALO),
            turn(east_value, own - east_lane),
            value,
        )
        return jnp.where(
            lane >= LANES - HALO, turn(west_value, LANES - HALO - west_lane), value
        )

    for by in range(by_n):

        def auxiliary(g, carry, by=by):
            at = pl.ds(pl.multiple_of(by * BH + g * SUB, SUB), SUB)
            block = pl.ds(pl.multiple_of(g * SUB, SUB), SUB)
            for ch in range(1 + LEV):
                for j in range(tiles):
                    width = min(LANES, cols - j * LANES)
                    part = slice(j * LANES, j * LANES + width)
                    if ch == 0:
                        value = kmt[at, part].astype(F32)
                    else:
                        value = kappa[ch - 1, at, part]
                    grid[ch, j, at, 0:width] = value
                j = tiles - 1
                at_lane = HALO * (by * (1 + LEV) + ch)
                grid[ch, j, at, :] = halo(
                    grid[ch, j, at, :],
                    from_east[block, :],
                    at_lane,
                    from_west[block, :],
                    at_lane,
                )
            return carry

        lax.fori_loop(0, BH // SUB, auxiliary, 0)

    for copy in copies:
        copy.wait()

    for by in range(by_n):
        base = [table[by * bx_n + bx] for bx in range(bx_n)]
        west = table[slots + by]
        east = table[slots + by_n + by]

        def lay(g, carry, by=by, base=base, west=west, east=east):
            at = pl.ds(pl.multiple_of(by * BH + g * SUB, SUB), SUB)
            levels = [grid[0, j, at, :] for j in range(tiles)]

            def rows(start):
                return store[pl.ds(pl.multiple_of(start + g * SUB, SUB), SUB), :]

            west_value = rows(west)
            east_value = rows(east)
            for level in range(LEV):
                blocks = [rows(base[bx] + level * BH) for bx in range(bx_n)]
                for tracer in range(2):
                    turned = [
                        turn(blocks[bx], BW * (bx - tracer)) for bx in range(bx_n)
                    ]
                    for j in range(tiles):
                        value = None
                        for bx in range(bx_n):
                            start = bx * BW - j * LANES
                            if start >= LANES or start + BW <= 0:
                                continue
                            if value is None:
                                value = turned[bx]
                            else:
                                value = jnp.where(lane >= start, turned[bx], value)
                        if j == tiles - 1:
                            value = halo(
                                value,
                                east_value,
                                strip_lane(1, by, level, tracer, by_n),
                                west_value,
                                strip_lane(0, by, level, tracer, by_n),
                            )
                        grid[1 + LEV + tracer * LEV + level, j, at, :] = jnp.where(
                            levels[j] > level, value, 0.0
                        )
            return carry

        lax.fori_loop(0, BH // SUB, lay, 0)

    height = grid.shape[2]
    for ch in range(1 + 3 * LEV):
        for j in range(tiles):
            at = slice(ch * HALO, (ch + 1) * HALO)
            north[j, at, :] = grid[ch, j, 0:HALO, :]
            south[j, at, :] = grid[ch, j, height - HALO : height, :]


def sideways(values):
    lane = lanes()
    count = len(values)
    left = [turn(v, 1) for v in values]
    right = [turn(v, -1) for v in values]
    west = [
        jnp.where(lane == 0, left[(j - 1) % count], left[j]) for j in range(count)
    ]
    east = [
        jnp.where(lane == LANES - 1, right[(j + 1) % count], right[j])
        for j in range(count)
    ]
    return east, west


def solve_kernel(
    cols, grid, north, south, tracer_out, powers, sums, field, sem
):
    lane = lanes()
    tiles = grid.shape[1]
    height = grid.shape[2]
    own = cols - (tiles - 1) * LANES
    copy = pltpu.make_async_copy(
        grid, field.at[:, :, pl.ds(PAD, height), :], sem
    )
    copy.start()
    for ch in range(1 + 3 * LEV):
        for j in range(tiles):
            at = slice(ch * HALO, (ch + 1) * HALO)
            field[ch, j, PAD - HALO : PAD, :] = north[j, at, :]
            field[ch, j, PAD + height : PAD + height + HALO, :] = south[j, at, :]
    copy.wait()
    first, end = PAD // SUB, (PAD + height) // SUB

    def three(ref, lead, g):
        start = pl.multiple_of(g * SUB, SUB)
        here = [ref[lead, j, pl.ds(start, SUB), :] for j in range(tiles)]
        above = [ref[lead, j, pl.ds(start - 1, SUB), :] for j in range(tiles)]
        below = [ref[lead, j, pl.ds(start + 1, SUB), :] for j in range(tiles)]
        return here, above, below

    def diffuse(g, mine):
        at = pl.ds(pl.multiple_of(g * SUB, SUB), SUB)
        level_c, level_a, level_b = three(field, 0, g)
        forcing = [jnp.zeros((SUB, LANES), F32)] * tiles
        for level in range(LEV):
            kappa_c, kappa_a, kappa_b = three(field, 1 + level, g)
            wet_c = [(v > level).astype(F32) for v in level_c]
            wet_a = [(v > level).astype(F32) for v in level_a]
            wet_b = [(v > level).astype(F32) for v in level_b]
            wet_e, _ = sideways(wet_c)
            kappa_e, _ = sideways(kappa_c)
            face_e = [
                0.5 * (kappa_c[j] + kappa_e[j]) * (wet_c[j] * wet_e[j])
                for j in range(tiles)
            ]
            face_a = [
                0.5 * (kappa_c[j] + kappa_a[j]) * (wet_c[j] * wet_a[j])
                for j in range(tiles)
            ]
            face_b = [
                0.5 * (kappa_c[j] + kappa_b[j]) * (wet_c[j] * wet_b[j])
                for j in range(tiles)
            ]
            fresh = []
            for tracer in range(2):
                ch = 1 + LEV + tracer * LEV + level
                here, above, below = three(field, ch, g)
                to_east, _ = sideways(here)
                flux = [face_e[j] * (to_east[j] - here[j]) for j in range(tiles)]
                _, flux_w = sideways(flux)
                new = []
                for j in range(tiles):
                    change = (
                        flux[j]
                        - flux_w[j]
                        + face_a[j] * (above[j] - here[j])
                        + face_b[j] * (below[j] - here[j])
                    )
                    new.append(wet_c[j] * (here[j] + change))
                if mine:
                    out = pl.ds(pl.multiple_of(g * SUB - PAD, SUB), SUB)
                    for j in range(tiles):
                        width = min(LANES, cols - j * LANES)
                        tracer_out[
                            tracer, level, out, j * LANES : j * LANES + width
                        ] = new[j][:, :width]
                fresh.append(new)
            thickness = 1.0 + 0.5 * level
            for j in range(tiles):
                temp, salt = fresh[0][j], fresh[1][j]
                density = wet_c[j] * (
                    haline * salt - thermal * temp - cabbeling * temp * temp
                )
                forcing[j] = forcing[j] + thickness * density
        for j in range(tiles):
            powers[0, j, at, :] = jnp.where(level_c[j] > 0, forcing[j], 0.0)

    def over(body, carry):
        return lax.fori_loop(first, end, body, carry)

    diffuse(first - 1, False)
    over(lambda g, c: (diffuse(g, True), c)[1], 0)
    diffuse(end, False)

    def apply(source, g):
        here, above, below = three(powers, source, g)
        at = pl.ds(pl.multiple_of(g * SUB, SUB), SUB)
        pair = [above[j] + below[j] for j in range(tiles)]
        mixed = [here[j] + 0.5 * pair[j] for j in range(tiles)]
        east, west = sideways(mixed)
        result = []
        for j in range(tiles):
            level = field[0, j, at, :]
            depth = (level > 0).astype(F32)
            for k in range(1, LEV):
                depth = depth + (1.0 + 0.5 * k) * (level > k).astype(F32)
            total = (
                (6.0 - SHIFT + depth) * here[j] - pair[j] - (east[j] + west[j])
            ) * (1.0 / SCALE)
            result.append(jnp.where(level > 0, total, 0.0))
        return here, result

    def inside(value, j):
        return value if j < tiles - 1 else jnp.where(lane < own, value, 0.0)

    def power(target, g, put=True):
        here, result = apply(target - 1, g)
        if put:
            at = pl.ds(pl.multiple_of(g * SUB, SUB), SUB)
            for j in range(tiles):
                powers[target, j, at, :] = result[j]
        return here, result

    zero = jnp.zeros((SUB, LANES), F32)

    def first_power(g, carry):
        here, result = power(1, g)
        a, b = carry
        for j in range(tiles):
            v = inside(here[j], j)
            a = a + v * v
            b = b + v * inside(result[j], j)
        return a, b

    power(1, first - 1)
    a, b = over(first_power, (zero, zero))
    power(1, end)
    a = jnp.sum(a, axis=(0, 1), keepdims=True)
    b = jnp.sum(b, axis=(0, 1), keepdims=True)
    centre = jnp.where(a > 0, b / jnp.where(a > 0, a, 1.0), 0.0)
    power(2, first - 1)
    over(lambda g, c: (power(2, g), c)[1], 0)
    power(2, end)
    wide = jnp.broadcast_to(centre, (SUB, LANES))

    def last_power(g, carry):
        carry = list(carry)
        here, result = power(3, g, False)
        at = pl.ds(pl.multiple_of(g * SUB, SUB), SUB)
        for j in range(tiles):
            q0 = inside(powers[0, j, at, :], j)
            q1 = inside(powers[1, j, at, :], j)
            q2 = inside(here[j], j)
            q3 = inside(result[j], j)
            b1 = q1 - wide * q0
            c2 = q2 - wide * q1
            c3 = q3 - wide * q2
            b2 = c2 - wide * b1
            b3 = (c3 - wide * c2) - wide * b2
            terms = (q0, b1, b2, b3)
            for at_pair, (x, y) in enumerate(PAIRS):
                carry[at_pair] = carry[at_pair] + terms[x] * terms[y]
        return tuple(carry)

    totals = over(last_power, (zero,) * len(PAIRS))
    row = jnp.where(lane[:1] == 0, wide[:1], 0.0)
    for at_pair, total in enumerate(totals):
        total = jnp.sum(total, axis=(0, 1), keepdims=True)
        row = jnp.where(lane[:1] == at_pair + 1, total, row)
    sums[...] = jnp.broadcast_to(row, sums.shape)


PAIRS = ((0, 0), (0, 1), (0, 2), (0, 3), (1, 1), (1, 2), (1, 3), (2, 2), (2, 3))


def combine_kernel(cols, sums, powers, stream):
    values = sums[...]
    lane = lax.broadcasted_iota(jnp.int32, values.shape, 1)

    def column(k):
        return jnp.sum(jnp.where(lane == k, values, 0.0), axis=1, keepdims=True)

    centre = column(0)
    gram = {pair: column(at + 1) for at, pair in enumerate(PAIRS)}

    def local(c):
        c = list(c) + [None] * (4 - len(c))
        c0, c1, c2, c3 = c
        result = [c0 + jnp.zeros_like(centre)]
        if c1 is not None:
            inner = c1
            slope = c1 + jnp.zeros_like(centre)
            if c2 is not None:
                inner = c1 + centre * (c2 if c3 is None else c2 + centre * c3)
                slope = c1 + centre * (
                    2.0 * c2 if c3 is None else 2.0 * c2 + 3.0 * (centre * c3)
                )
            result = [c0 + centre * inner, slope]
        if c2 is not None:
            result.append(c2 + jnp.zeros_like(centre) if c3 is None else c2 + 3.0 * (centre * c3))
        if c3 is not None:
            result.append(c3 + jnp.zeros_like(centre))
        return result

    def inner(x, y):
        u, v = local(x), local(y)
        total = jnp.zeros_like(centre)
        for i in range(len(u)):
            for j in range(len(v)):
                total = total + (u[i] * v[j]) * gram[(min(i, j), max(i, j))]
        return jnp.sum(total, axis=0, keepdims=True)

    def operate(c):
        result = [SHIFT * x for x in c] + [None]
        for i, x in enumerate(c):
            term = SCALE * x
            result[i + 1] = term if result[i + 1] is None else result[i + 1] + term
        return result

    one = jnp.ones((1, 1), F32)
    stream_c = [None] * 3
    residual, direction = [one], [one]
    norm = inner(residual, residual)
    for step in range(3):
        image = operate(direction)
        alpha = norm / inner(direction, image)
        for i, x in enumerate(direction):
            stream_c[i] = alpha * x if stream_c[i] is None else stream_c[i] + alpha * x
        if step == 2:
            break
        residual = [
            (residual[i] - alpha * image[i]) if i < len(residual) else -alpha * image[i]
            for i in range(len(image))
        ]
        fresh = inner(residual, residual)
        ratio = fresh / norm
        direction = [
            (residual[i] + ratio * direction[i]) if i < len(direction) else residual[i]
            for i in range(len(residual))
        ]
        norm = fresh

    tiles = powers.shape[1]
    height = stream.shape[0]
    weights = [jnp.broadcast_to(c, (SUB, LANES)) for c in stream_c]

    def write(g, carry):
        at = pl.ds(pl.multiple_of(g * SUB + PAD, SUB), SUB)
        out = pl.ds(pl.multiple_of(g * SUB, SUB), SUB)
        for j in range(tiles):
            width = min(LANES, cols - j * LANES)
            value = (
                weights[0] * powers[0, j, at, :]
                + weights[1] * powers[1, j, at, :]
                + weights[2] * powers[2, j, at, :]
            )
            stream[out, j * LANES : j * LANES + width] = value[:, :width]
        return carry

    lax.fori_loop(0, height // SUB, write, 0)


def body(checkpoint, slot_dest, kmt, kappa):
    n = lax.axis_size("lon")
    lats = lax.axis_size("lat")
    me = lax.axis_index("lon").astype(jnp.int32).reshape(1)
    blocks = checkpoint[0]
    dest = slot_dest[0]
    slots, values = blocks.shape
    rows, cols = kmt.shape
    by_n, bx_n = rows // BH, cols // BW
    cap = slots // n
    length = cap * ROWS + BH
    tiles = -(-(cols + 2 * HALO) // LANES)

    packs = pl.pallas_call(
        functools.partial(pack_kernel, n, cap, bx_n, by_n),
        out_shape=[shaped(length, LANES)] * n,
        in_specs=[SM, SM, VM],
        out_specs=[HB] * n,
        scratch_shapes=[
            pltpu.VMEM((slots * ROWS, LANES), F32),
            pltpu.VMEM((n, length, LANES), F32),
            pltpu.SMEM((n,), jnp.int32),
            pltpu.SemaphoreType.DMA((n,)),
        ],
        compiler_params=params(),
        cost_estimate=cost(4 << 20, 4 << 20),
        name="pack",
    )(dest, me, blocks)

    order = sorted(range(1, n), key=lambda k: (-bin(k >> 1).count("1"), k & 1, k))
    received = {0: packs[0]}
    for k in order:
        received[k] = lax.ppermute(packs[k], "lon", [(i, i ^ k) for i in range(n)])

    west, east, table = pl.pallas_call(
        functools.partial(edge_kernel, n, cap, bx_n, by_n, length),
        out_shape=[
            shaped(BH, LANES),
            shaped(BH, LANES),
            shaped(slots + 2 * by_n, dtype=jnp.int32),
        ],
        in_specs=[SM, SM, VM, VM],
        out_specs=[VM, VM, SM],
        compiler_params=params(),
        cost_estimate=cost(1 << 20, 1 << 20),
        name="edge",
    )(dest, me, kmt, kappa)
    from_west = lax.ppermute(east, "lon", [(i, (i + 1) % n) for i in range(n)])
    from_east = lax.ppermute(west, "lon", [(i, (i - 1) % n) for i in range(n)])

    channels = 1 + 3 * LEV
    rim = -(-channels * HALO // SUB) * SUB
    grid, north, south = pl.pallas_call(
        functools.partial(grid_kernel, n, bx_n, by_n),
        out_shape=[
            shaped(channels, tiles, rows, LANES),
            shaped(tiles, rim, LANES),
            shaped(tiles, rim, LANES),
        ],
        in_specs=[HB] * n + [SM, VM, VM, VM, VM],
        out_specs=[VM, VM, VM],
        scratch_shapes=[
            pltpu.VMEM((n * length, LANES), F32),
            pltpu.SemaphoreType.DMA((n,)),
        ],
        compiler_params=params(),
        cost_estimate=cost(4 << 20, 4 << 20),
        name="grid",
    )(*[received[k] for k in range(n)], table, kmt, kappa, from_west, from_east)

    up = [(i, i + 1) for i in range(lats - 1)]
    above = lax.ppermute(south, "lat", up)
    below = lax.ppermute(north, "lat", [(j, i) for i, j in up])

    deep = rows + 2 * PAD
    devices = n * lats
    tracer, powers, sums = pl.pallas_call(
        functools.partial(solve_kernel, cols),
        out_shape=[
            shaped(2, LEV, rows, cols),
            shaped(3, tiles, deep, LANES),
            shaped(devices, LANES),
        ],
        in_specs=[HB, VM, VM],
        out_specs=[VM, VM, VM],
        scratch_shapes=[
            pltpu.VMEM((channels, tiles, deep, LANES), F32),
            pltpu.SemaphoreType.DMA,
        ],
        compiler_params=params(),
        cost_estimate=cost(16 << 20, 6 << 20),
        name="solve",
    )(grid, above, below)

    everyone = lax.all_to_all(sums, ("lon", "lat"), 0, 0, tiled=True)
    stream = pl.pallas_call(
        functools.partial(combine_kernel, cols),
        out_shape=shaped(rows, cols),
        in_specs=[VM, VM],
        out_specs=VM,
        compiler_params=params(),
        cost_estimate=cost(1 << 20, 2 << 20),
        name="combine",
    )(everyone, powers)
    return tracer, stream


def solution(mesh):
    placed = (P("lat", "lon", None), P("lat", None), P("lat", "lon"), P(None, "lat", "lon"))
    return jax.shard_map(
        body,
        mesh=mesh,
        in_specs=placed,
        out_specs=(P(None, None, "lat", "lon"), P("lat", "lon")),
        check_vma=False,
    )
```

```python
import functools

import jax
import jax.numpy as jnp
from jax import lax
from jax.experimental import pallas as pl
from jax.experimental.pallas import tpu as pltpu
from jax.sharding import PartitionSpec as P


BH = 40
BW = 60
LEV = 2
HALO = 4
LANES = 128
SUB = 8
PAD = SUB
EDGE = 4 * SUB
ROWS = LEV * BH
SHIFT = 8.0
SCALE = 8.0

thermal = 0.25
haline = 0.75
cabbeling = 0.05

VM = pl.BlockSpec(memory_space=pltpu.VMEM)
SM = pl.BlockSpec(memory_space=pltpu.SMEM)
HB = pl.BlockSpec(memory_space=pltpu.HBM)
F32 = jnp.float32


def params():
    return pltpu.CompilerParams(vmem_limit_bytes=24 << 20)


def cost(flops, moved):
    return pl.CostEstimate(flops=flops, bytes_accessed=moved, transcendentals=0)


def shaped(*dims, dtype=F32):
    return jax.ShapeDtypeStruct(dims, dtype)


def lanes():
    return lax.broadcasted_iota(jnp.int32, (SUB, LANES), 1)


def turn(value, amount):
    if isinstance(amount, int):
        amount %= LANES
        if amount == 0:
            return value
    return pltpu.roll(value, amount, 1)


def strip_lane(side, by, level, tracer, block_rows):
    return HALO * (((side * block_rows + by) * LEV + level) * 2 + tracer)


def edge_spot(cap, piece):
    if piece < 4 * cap:
        return piece // 2 * BH, LANES - 2 * HALO + piece % 2 * HALO
    return cap * ROWS + BH, HALO * (piece - 4 * cap)


def package_rows(cap, by_n):
    return cap * ROWS + (2 * BH if by_n * (1 + LEV) > 4 * cap else BH)


def pack_kernel(n, cap, bx_n, by_n, *refs):
    me_ref, dest_hbm, blocks_hbm, kmt_hbm, kappa_hbm = refs[:5]
    outs = refs[5 : 5 + n]
    dest, blocks, kmt, kappa, flat, strips, edges, source, count, sems = refs[5 + n :]
    groups = blocks.shape[0]
    slots = groups * SUB
    me = me_ref[0]
    lane = lanes()
    length = outs[0].shape[0]
    cols = kmt.shape[1]
    first = pltpu.make_async_copy(dest_hbm, dest, sems.at[groups])
    first.start()
    copies = [
        pltpu.make_async_copy(
            blocks_hbm.at[0, pl.ds(g * SUB, SUB), :], blocks.at[g], sems.at[g]
        )
        for g in range(groups)
    ]
    for copy in copies:
        copy.start()
    others = [
        pltpu.make_async_copy(kmt_hbm, kmt, sems.at[groups + 1]),
        pltpu.make_async_copy(kappa_hbm, kappa, sems.at[groups + 2]),
    ]
    for copy in others:
        copy.start()
    for k in range(n):
        count[k] = 0
    for at in range(n * cap):
        source[at] = 0
    first.wait()

    def assign(i, carry):
        d = dest[0, me * slots + i]

        @pl.when(d >= 0)
        def _():
            k = lax.bitwise_xor(lax.div(d, slots), me)
            c = count[k]
            count[k] = c + 1
            source[k * cap + c] = lax.div(i, SUB) * (ROWS * SUB) + lax.rem(i, SUB)

        return carry

    lax.fori_loop(0, slots, assign, 0)

    for g in range(groups):
        copies[g].wait()

    def regroup(group, carry):
        def load(q):
            return blocks[group, :, q * LANES : (q + 1) * LANES]

        def piece(start, target):
            q, o = divmod(start, LANES)
            value = load(q)
            if o + BW > LANES:
                value = jnp.where(lane >= o, value, load(q + 1))
            return turn(value, target - o)

        for row in range(ROWS):
            value = jnp.where(
                lane < BW, piece(row * BW, 0), piece((ROWS + row) * BW, BW)
            )
            at = pl.multiple_of(group * (ROWS * SUB) + row * SUB, SUB)
            flat[pl.ds(at, SUB), :] = value
        return carry

    lax.fori_loop(0, groups, regroup, 0)

    def rows_of(start, row):
        return flat[pl.ds(start + row * SUB, SUB, stride=SUB), :]

    def strip(i, owner, by, side):
        k = lax.bitwise_xor(owner, me)
        start = lax.div(i, SUB) * (ROWS * SUB) + lax.rem(i, SUB)
        for level in range(LEV):
            for row in range(0, BH, SUB):
                value = rows_of(start, level * BH + row)
                old = strips[k, row : row + SUB, :]
                for tracer in range(2):
                    origin = tracer * BW + (BW - HALO if side == 0 else 0)
                    target = strip_lane(side, by, level, tracer, by_n)
                    amount = lax.rem(target - origin + LANES, LANES)
                    here = (lane >= target) & (lane < target + HALO)
                    old = jnp.where(here, pltpu.roll(value, amount, 1), old)
                strips[k, row : row + SUB, :] = old

    def edge(i, carry):
        d = dest[0, me * slots + i]
        owner = lax.div(d, slots)
        spot = lax.rem(d, slots)
        bx = lax.rem(spot, bx_n)
        by = lax.div(spot, bx_n)

        @pl.when((d >= 0) & (bx == bx_n - 1))
        def _():
            strip(i, lax.rem(owner + 1, n), by, 0)

        @pl.when((d >= 0) & (bx == 0))
        def _():
            strip(i, lax.rem(owner + n - 1, n), by, 1)

        return carry

    lax.fori_loop(0, slots, edge, 0)

    for copy in others:
        copy.wait()
    zero = jnp.zeros((SUB, LANES), F32)
    for at in range(0, edges.shape[1], SUB):
        for side in range(2):
            edges[side, at : at + SUB, :] = zero
    for side, start in ((0, cols - HALO), (1, 0)):
        tile = start // LANES * LANES
        width = min(LANES, cols - tile)
        for piece in range(by_n * (1 + LEV)):
            by, ch = divmod(piece, 1 + LEV)
            base, target = edge_spot(cap, piece)
            if piece >= 4 * cap:
                base -= cap * ROWS + BH - 2 * cap * BH
            for row in range(0, BH, SUB):
                at = slice(by * BH + row, by * BH + row + SUB)
                if ch == 0:
                    value = kmt[at, tile : tile + width].astype(F32)
                else:
                    value = kappa[ch - 1, at, tile : tile + width]
                if width < LANES:
                    value = jnp.concatenate([value, zero[:, width:]], axis=1)
                value = turn(value, target - (start - tile))
                here = (lane >= target) & (lane < target + HALO)
                old = edges[side, base + row : base + row + SUB, :]
                edges[side, base + row : base + row + SUB, :] = jnp.where(
                    here, value, old
                )

    eastern = lax.bitwise_xor(lax.rem(me + 1, n), me)
    in_blocks = min(edges.shape[1], 2 * cap * BH)
    for k in range(n):
        which = jnp.where(eastern == k, 0, 1)
        for c in range(cap):
            start = source[k * cap + c]
            for row in range(0, ROWS, SUB):
                value = rows_of(start, row)
                at = c * ROWS + row
                if at < in_blocks:
                    value = jnp.where(
                        lane >= LANES - 2 * HALO, edges[which, at : at + SUB, :], value
                    )
                outs[k][at : at + SUB, :] = value
        for row in range(0, BH, SUB):
            at = cap * ROWS + row
            outs[k][at : at + SUB, :] = strips[k, row : row + SUB, :]
            if length > cap * ROWS + BH:
                outs[k][at + BH : at + BH + SUB, :] = edges[
                    which, in_blocks + row : in_blocks + row + SUB, :
                ]


def base_kernel(n, cap, bx_n, by_n, me_ref, dest, kmt, kappa, table, grid):
    me = me_ref[0]
    slots = bx_n * by_n
    channels, tiles, deep, _ = grid.shape
    cols = kmt.shape[1]
    zero = jnp.zeros((SUB, LANES), F32)
    for at in range(n * cap):
        table[at] = -1
    for at in range(2 * by_n):
        table[n * cap + at] = -1

    def clear(g, carry):
        at = pl.ds(pl.multiple_of(g * SUB, SUB), SUB)
        for ch in range(channels):
            for j in range(tiles):
                grid[ch, j, at, :] = zero
        return carry

    lax.fori_loop(0, deep // SUB, clear, 0)

    def lay(g, carry):
        at = pl.ds(pl.multiple_of(g * SUB, SUB), SUB)
        out = pl.ds(pl.multiple_of(g * SUB + PAD, SUB), SUB)
        for ch in range(1 + LEV):
            for j in range(tiles):
                width = min(LANES, cols - j * LANES)
                part = slice(j * LANES, j * LANES + width)
                if ch == 0:
                    value = kmt[at, part].astype(F32)
                else:
                    value = kappa[ch - 1, at, part]
                grid[ch, j, out, 0:width] = value
        return carry

    lax.fori_loop(0, kmt.shape[0] // SUB, lay, 0)
    west = lax.rem(me + n - 1, n)
    east = lax.rem(me + 1, n)

    def owner_loop(s, carry):
        k = lax.bitwise_xor(s, me)

        def slot_loop(i, c):
            d = dest[0, s * slots + i]
            spot = d - me * slots
            mine = (spot >= 0) & (spot < slots)
            from_west = d - west * slots
            from_east = d - east * slots

            @pl.when(mine)
            def _():
                table[k * cap + c] = spot

            @pl.when(
                (from_west >= 0)
                & (from_west < slots)
                & (lax.rem(from_west, bx_n) == bx_n - 1)
            )
            def _():
                table[n * cap + lax.div(from_west, bx_n)] = k

            @pl.when(
                (from_east >= 0) & (from_east < slots) & (lax.rem(from_east, bx_n) == 0)
            )
            def _():
                table[n * cap + by_n + lax.div(from_east, bx_n)] = k

            return c + mine.astype(jnp.int32)

        lax.fori_loop(0, slots, slot_loop, 0, unroll=8)
        return carry

    lax.fori_loop(0, n, owner_loop, 0)


def place_kernel(n, cap, bx_n, by_n, cols, which, *refs):
    count = len(which)
    me_ref, table, before = refs[:3]
    packs = refs[3 : 3 + count]
    grid, *rims = refs[3 + count :]
    me = me_ref[0]
    lane = lanes()
    channels, tiles, deep, _ = grid.shape
    last = tiles - 1
    own = cols - last * LANES
    halo_lane = (own, LANES - HALO)

    def copy(g, carry):
        at = pl.ds(pl.multiple_of(g * SUB, SUB), SUB)
        for ch in range(channels):
            for j in range(tiles):
                grid[ch, j, at, :] = before[ch, j, at, :]
        return carry

    lax.fori_loop(0, deep // SUB, copy, 0)

    def mark(ch, at, value, start):
        here = (lane >= start) & (lane < start + HALO)
        grid[ch, last, at, :] = jnp.where(here, value, grid[ch, last, at, :])

    for k, pack in zip(which, packs):

        def block(c, carry, k=k, pack=pack):
            spot = table[k * cap + c]

            @pl.when(spot >= 0)
            def _():
                by = lax.div(spot, bx_n)
                offset = lax.rem(spot, bx_n) * BW
                tile = lax.div(offset, LANES)
                start = lax.rem(offset, LANES)
                amounts = [
                    lax.rem(start - tracer * BW + LANES, LANES) for tracer in range(2)
                ]
                here = (lane >= start) & (lane < start + BW)
                spill = lane < start + BW - LANES

                def lay(target, mask):
                    for level in range(LEV):
                        for row in range(0, BH, SUB):
                            at = pl.ds(
                                pl.multiple_of(by * BH + row + PAD, SUB), SUB
                            )
                            place = pl.multiple_of(c * ROWS + level * BH + row, SUB)
                            value = pack[pl.ds(place, SUB), :]
                            wet = mask & (grid[0, target, at, :] > level)
                            for tracer in range(2):
                                ch = 1 + LEV + tracer * LEV + level
                                grid[ch, target, at, :] = jnp.where(
                                    wet,
                                    pltpu.roll(value, amounts[tracer], 1),
                                    grid[ch, target, at, :],
                                )

                lay(tile, here)

                @pl.when(start + BW > LANES)
                def _():
                    lay(tile + 1, spill)

            return carry

        lax.fori_loop(0, cap, block, 0)

        def strip(index, carry, k=k, pack=pack):
            @pl.when(table[n * cap + index] == k)
            def _():
                by = lax.rem(index, by_n)
                start = jnp.where(index < by_n, halo_lane[1], halo_lane[0])
                for level in range(LEV):
                    for tracer in range(2):
                        origin = strip_lane(0, index, level, tracer, by_n)
                        amount = lax.rem(start - origin + LANES, LANES)
                        for row in range(0, BH, SUB):
                            at = pl.ds(
                                pl.multiple_of(by * BH + row + PAD, SUB), SUB
                            )
                            place = cap * ROWS + row
                            value = pltpu.roll(pack[place : place + SUB, :], amount, 1)
                            mark(1 + LEV + tracer * LEV + level, at, value, start)

            return carry

        lax.fori_loop(0, 2 * by_n, strip, 0)

        for neighbour, start in ((me + n - 1, halo_lane[1]), (me + 1, halo_lane[0])):

            @pl.when(lax.bitwise_xor(lax.rem(neighbour, n), me) == k)
            def _(start=start, pack=pack):
                for piece in range(by_n * (1 + LEV)):
                    by, ch = divmod(piece, 1 + LEV)
                    base, origin = edge_spot(cap, piece)
                    for row in range(0, BH, SUB):
                        at = by * BH + row + PAD
                        mark(
                            ch,
                            slice(at, at + SUB),
                            turn(pack[base + row : base + row + SUB, :], start - origin),
                            start,
                        )

    if not rims:
        return
    north, south = rims
    rim = (lane >= own) & (lane < own + HALO) | (lane >= LANES - HALO)

    def mask(g, carry):
        at = pl.ds(pl.multiple_of(g * SUB + PAD, SUB), SUB)
        wet = grid[0, last, at, :]
        for ch in range(1 + LEV, channels):
            level = (ch - 1 - LEV) % LEV
            grid[ch, last, at, :] = jnp.where(
                rim & (wet <= level), 0.0, grid[ch, last, at, :]
            )
        return carry

    lax.fori_loop(0, deep // SUB - 2, mask, 0)
    for ch in range(channels):
        for j in range(tiles):
            at = slice(ch * HALO, (ch + 1) * HALO)
            north[j, at, :] = grid[ch, j, PAD : PAD + HALO, :]
            south[j, at, :] = grid[ch, j, deep - PAD - HALO : deep - PAD, :]


def sideways(values):
    lane = lanes()
    count = len(values)
    left = [turn(v, 1) for v in values]
    right = [turn(v, -1) for v in values]
    west = [
        jnp.where(lane == 0, left[(j - 1) % count], left[j]) for j in range(count)
    ]
    east = [
        jnp.where(lane == LANES - 1, right[(j + 1) % count], right[j])
        for j in range(count)
    ]
    return east, west


def three(load, start):
    return load(start), load(start - 1), load(start + 1)


def diffuse(load, start):
    tiles = len(load(0, start))
    span = range(tiles)
    level_c, level_a, level_b = three(functools.partial(load, 0), start)
    level_e, _ = sideways(level_c)
    both_e = [jnp.minimum(level_c[j], level_e[j]) for j in span]
    both_a = [jnp.minimum(level_c[j], level_a[j]) for j in span]
    both_b = [jnp.minimum(level_c[j], level_b[j]) for j in span]
    forcing = [None] * tiles
    fresh = [[None] * LEV for _ in range(2)]
    for level in range(LEV):
        kappa_c, kappa_a, kappa_b = three(functools.partial(load, 1 + level), start)
        kappa_e, _ = sideways(kappa_c)
        face_e, face_a, face_b = (
            [jnp.where(both[j] > level, kappa_c[j] + other[j], 0.0) for j in span]
            for both, other in (
                (both_e, kappa_e),
                (both_a, kappa_a),
                (both_b, kappa_b),
            )
        )
        for tracer in range(2):
            ch = 1 + LEV + tracer * LEV + level
            here, above, below = three(functools.partial(load, ch), start)
            to_east, _ = sideways(here)
            flux = [face_e[j] * (to_east[j] - here[j]) for j in span]
            _, flux_w = sideways(flux)
            fresh[tracer][level] = [
                jnp.where(
                    level_c[j] > level,
                    here[j]
                    + 0.5
                    * (
                        (flux[j] - flux_w[j])
                        + face_a[j] * (above[j] - here[j])
                        + face_b[j] * (below[j] - here[j])
                    ),
                    0.0,
                )
                for j in span
            ]
        thickness = 1.0 + 0.5 * level
        for j in span:
            temp, salt = fresh[0][level][j], fresh[1][level][j]
            density = haline * salt - temp * (thermal + cabbeling * temp)
            if level:
                density = forcing[j] + thickness * density
            forcing[j] = density
    return fresh, forcing


def apply(here, above, below, levels):
    span = range(len(here))
    pair = [above[j] + below[j] for j in span]
    mixed = [here[j] + 0.5 * pair[j] for j in span]
    east, west = sideways(mixed)
    result = []
    for j in span:
        diagonal = 6.0 - SHIFT + 1.0
        total = jnp.full((SUB, LANES), diagonal / SCALE, F32)
        for k in range(1, LEV):
            diagonal += 1.0 + 0.5 * k
            total = jnp.where(levels[j] > k, diagonal / SCALE, total)
        total = total * here[j] - (pair[j] + (east[j] + west[j])) * (1.0 / SCALE)
        result.append(jnp.where(levels[j] > 0, total, 0.0))
    return result


def gather_products(carry, powers, centre, keep):
    carry = list(carry)
    span = range(len(powers[0]))
    for j in span:
        q0, q1, q2, q3 = (keep(q[j], j) for q in powers)
        b1 = q1 - centre * q0
        c2 = q2 - centre * q1
        c3 = q3 - centre * q2
        b2 = c2 - centre * b1
        b3 = (c3 - centre * c2) - centre * b2
        terms = (q0, b1, b2, b3)
        for at, (x, y) in enumerate(PAIRS):
            carry[at] = carry[at] + terms[x] * terms[y]
    return tuple(carry)


def total_row(totals):
    lane = lanes()[:1]
    row = jnp.zeros((1, LANES), F32)
    for at, total in enumerate(totals):
        total = jnp.sum(total, axis=(0, 1), keepdims=True)
        row = jnp.where(lane == at + 1, total, row)
    return row


def put_tracer(target, fresh, cols, at):
    for tracer in range(2):
        for level in range(LEV):
            for j, value in enumerate(fresh[tracer][level]):
                width = min(LANES, cols - j * LANES)
                target[tracer, level, at, j * LANES : j * LANES + width] = value[
                    :, :width
                ]


def inner_kernel(cols, grid, tracer_out, powers, sums):
    lane = lanes()
    line = lax.broadcasted_iota(jnp.int32, (SUB, LANES), 0)
    _, tiles, deep, _ = grid.shape
    own = cols - (tiles - 1) * LANES
    first, end = PAD // SUB, (deep - PAD) // SUB
    zero = jnp.zeros((SUB, LANES), F32)

    def rows(ref, lead, start):
        return [ref[lead, j, pl.ds(start, SUB), :] for j in range(tiles)]

    def top(g):
        return pl.multiple_of(g * SUB, SUB)

    def step(g, carry):
        fresh, forcing = diffuse(functools.partial(rows, grid), top(g))
        put_tracer(
            tracer_out, fresh, cols, pl.ds(pl.multiple_of(g * SUB - PAD, SUB), SUB)
        )
        for j in range(tiles):
            powers[0, j, pl.ds(top(g), SUB), :] = forcing[j]
        return carry

    lax.fori_loop(first, end, step, 0)

    def inside(value, j):
        return value if j < tiles - 1 else jnp.where(lane < own, value, 0.0)

    def upper(value, j):
        return jnp.where(line >= HALO, inside(value, j), 0.0)

    def lower(value, j):
        return jnp.where(line < SUB - HALO, inside(value, j), 0.0)

    def power(g, source):
        here, above, below = three(functools.partial(rows, powers, source), top(g))
        return here, apply(here, above, below, rows(grid, 0, top(g)))

    def put(g, target):
        here, result = power(g, target - 1)
        for j in range(tiles):
            powers[target, j, pl.ds(top(g), SUB), :] = result[j]
        return here, result

    def first_power(g, carry, keep=inside):
        here, result = put(g, 1)
        a, b = carry
        for j in range(tiles):
            v = keep(here[j], j)
            a = a + v * v
            b = b + v * keep(result[j], j)
        return a, b

    def everywhere(body, carry):
        carry = body(first, carry, upper)
        carry = lax.fori_loop(first + 1, end - 1, body, carry)
        return body(end - 1, carry, lower)

    a, b = everywhere(first_power, (zero, zero))
    a = jnp.sum(a, axis=(0, 1), keepdims=True)
    b = jnp.sum(b, axis=(0, 1), keepdims=True)
    centre = jnp.where(a > 0, b / jnp.where(a > 0, a, 1.0), 0.0)
    centre = jnp.broadcast_to(centre, (SUB, LANES))
    lax.fori_loop(first, end, lambda g, c: (put(g, 2), c)[1], 0)

    def products(g, carry, keep=inside):
        here, result = power(g, 2)
        lower_powers = [rows(powers, k, top(g)) for k in range(2)]
        return gather_products(carry, (*lower_powers, here, result), centre, keep)

    totals = everywhere(products, (zero,) * len(PAIRS))
    row = jnp.where(lane[:1] == 0, centre[:1], total_row(totals))
    sums[...] = jnp.broadcast_to(row, sums.shape)


def border_kernel(
    cols, grid, north, south, powers, part, tracer_in, tracer_out, border, sums,
    field, local, fresh_rows, sems,
):
    lane = lanes()
    line = lax.broadcasted_iota(jnp.int32, (SUB, LANES), 0)
    channels, tiles, deep, _ = grid.shape
    own = cols - (tiles - 1) * LANES
    half = EDGE // 2
    for ch in range(channels):
        for j in range(tiles):
            at = slice(ch * HALO, (ch + 1) * HALO)
            for row in range(0, half, SUB):
                field[0, ch, j, half + row : half + row + SUB, :] = grid[
                    ch, j, PAD + row : PAD + row + SUB, :
                ]
                low = deep - PAD - half + row
                field[1, ch, j, row : row + SUB, :] = grid[ch, j, low : low + SUB, :]
            field[0, ch, j, half - HALO : half, :] = north[j, at, :]
            field[1, ch, j, half : half + HALO, :] = south[j, at, :]
    for k in range(2):
        for j in range(tiles):
            local[0, k, j, EDGE - SUB : EDGE, :] = powers[
                k, j, PAD + SUB : PAD + 2 * SUB, :
            ]
            local[1, k, j, 0:SUB, :] = powers[
                k, j, deep - PAD - 2 * SUB : deep - PAD - SUB, :
            ]
    centre = jnp.broadcast_to(part[0:1, 0:1], (SUB, LANES))

    def border_side(side, totals):
        def rows(ref, lead, start):
            return [ref[side, lead, j, pl.ds(start, SUB), :] for j in range(tiles)]

        mine = pl.multiple_of(half - side * SUB, SUB)

        def step(g, carry):
            start = pl.multiple_of(g * SUB, SUB)
            fresh, forcing = diffuse(functools.partial(rows, field), start)
            for j in range(tiles):
                local[side, 0, j, pl.ds(start, SUB), :] = forcing[j]

            @pl.when(start == mine)
            def _():
                put_tracer(fresh_rows.at[side], fresh, cols, slice(0, SUB))

            return carry

        lax.fori_loop(1, 3, step, 0)

        def power(start, source):
            here, above, below = three(functools.partial(rows, local, source), start)
            return here, apply(here, above, below, rows(field, 0, start))

        for target in range(1, 3):
            for start in range(SUB, 3 * SUB, SUB):
                result = power(start, target - 1)[1]
                for j in range(tiles):
                    local[side, target, j, start : start + SUB, :] = result[j]
        here, result = power(mine, 2)
        lower_powers = [rows(local, k, mine) for k in range(2)]
        for k, values in enumerate((*lower_powers, here)):
            for j in range(tiles):
                border[side, k, j] = values[j]
        bound = side * (SUB - HALO)
        rim = (line >= bound) & (line < bound + HALO)

        def keep(value, j):
            inside = rim if j < tiles - 1 else rim & (lane < own)
            return jnp.where(inside, value, 0.0)

        return gather_products(totals, (*lower_powers, here, result), centre, keep)

    zero = jnp.zeros((SUB, LANES), F32)
    totals = lax.fori_loop(0, 2, border_side, (zero,) * len(PAIRS))
    height = tracer_out.shape[2]
    copies = [
        pltpu.make_async_copy(
            fresh_rows.at[side],
            tracer_out.at[:, :, pl.ds(side * (height - SUB), SUB), :],
            sems.at[side],
        )
        for side in range(2)
    ]
    for copy in copies:
        copy.start()
    sums[...] = jnp.broadcast_to(part[0:1, :] + total_row(totals), sums.shape)
    for copy in copies:
        copy.wait()


PAIRS = ((0, 0), (0, 1), (0, 2), (0, 3), (1, 1), (1, 2), (1, 3), (2, 2), (2, 3))


def combine_kernel(cols, sums, powers, border, stream):
    values = sums[...]
    lane = lax.broadcasted_iota(jnp.int32, values.shape, 1)

    def column(k):
        return jnp.sum(jnp.where(lane == k, values, 0.0), axis=1, keepdims=True)

    centre = column(0)
    gram = {pair: column(at + 1) for at, pair in enumerate(PAIRS)}

    def local(c):
        c = list(c) + [None] * (4 - len(c))
        c0, c1, c2, c3 = c
        result = [c0 + jnp.zeros_like(centre)]
        if c1 is not None:
            inner = c1
            slope = c1 + jnp.zeros_like(centre)
            if c2 is not None:
                inner = c1 + centre * (c2 if c3 is None else c2 + centre * c3)
                slope = c1 + centre * (
                    2.0 * c2 if c3 is None else 2.0 * c2 + 3.0 * (centre * c3)
                )
            result = [c0 + centre * inner, slope]
        if c2 is not None:
            result.append(c2 + jnp.zeros_like(centre) if c3 is None else c2 + 3.0 * (centre * c3))
        if c3 is not None:
            result.append(c3 + jnp.zeros_like(centre))
        return result

    def inner(x, y):
        u, v = local(x), local(y)
        total = jnp.zeros_like(centre)
        for i in range(len(u)):
            for j in range(len(v)):
                total = total + (u[i] * v[j]) * gram[(min(i, j), max(i, j))]
        return jnp.sum(total, axis=0, keepdims=True)

    def operate(c):
        result = [SHIFT * x for x in c] + [None]
        for i, x in enumerate(c):
            term = SCALE * x
            result[i + 1] = term if result[i + 1] is None else result[i + 1] + term
        return result

    one = jnp.ones((1, 1), F32)
    stream_c = [None] * 3
    residual, direction = [one], [one]
    norm = inner(residual, residual)
    for step in range(3):
        image = operate(direction)
        alpha = norm / inner(direction, image)
        for i, x in enumerate(direction):
            stream_c[i] = alpha * x if stream_c[i] is None else stream_c[i] + alpha * x
        if step == 2:
            break
        residual = [
            (residual[i] - alpha * image[i]) if i < len(residual) else -alpha * image[i]
            for i in range(len(image))
        ]
        fresh = inner(residual, residual)
        ratio = fresh / norm
        direction = [
            (residual[i] + ratio * direction[i]) if i < len(direction) else residual[i]
            for i in range(len(residual))
        ]
        norm = fresh

    tiles = powers.shape[1]
    height = stream.shape[0]
    weights = [jnp.broadcast_to(c, (SUB, LANES)) for c in stream_c]

    def put(out, load):
        for j in range(tiles):
            width = min(LANES, cols - j * LANES)
            value = sum(weights[k] * load(k, j) for k in range(3))
            stream[out, j * LANES : j * LANES + width] = value[:, :width]

    def write(g, carry):
        at = pl.ds(pl.multiple_of(g * SUB + PAD, SUB), SUB)
        out = pl.ds(pl.multiple_of(g * SUB, SUB), SUB)
        put(out, lambda k, j: powers[k, j, at, :])
        return carry

    put(slice(0, SUB), lambda k, j: border[0, k, j])
    lax.fori_loop(1, height // SUB - 1, write, 0, unroll=3)
    put(slice(height - SUB, height), lambda k, j: border[1, k, j])


def body(checkpoint, slot_dest, kmt, kappa):
    n = lax.axis_size("lon")
    lats = lax.axis_size("lat")
    me = lax.axis_index("lon").astype(jnp.int32).reshape(1)
    _, slots, values = checkpoint.shape
    rows, cols = kmt.shape
    by_n, bx_n = rows // BH, cols // BW
    cap = slots // n
    length = package_rows(cap, by_n)
    tiles = -(-(cols + 2 * HALO) // LANES)
    groups = slots // SUB
    edge_rows = -(-by_n * (1 + LEV) // 2) * BH
    if by_n * (1 + LEV) > 4 * cap:
        edge_rows = 2 * cap * BH + BH

    packs = pl.pallas_call(
        functools.partial(pack_kernel, n, cap, bx_n, by_n),
        out_shape=[shaped(length, LANES)] * n,
        in_specs=[SM, HB, HB, HB, HB],
        out_specs=[VM] * n,
        scratch_shapes=[
            pltpu.SMEM((1, n * slots), jnp.int32),
            pltpu.VMEM((groups, SUB, values), F32),
            pltpu.VMEM((rows, cols), jnp.int32),
            pltpu.VMEM((LEV, rows, cols), F32),
            pltpu.VMEM((slots * ROWS, LANES), F32),
            pltpu.VMEM((n, BH, LANES), F32),
            pltpu.VMEM((2, edge_rows, LANES), F32),
            pltpu.SMEM((n * cap,), jnp.int32),
            pltpu.SMEM((n,), jnp.int32),
            pltpu.SemaphoreType.DMA((groups + 3,)),
        ],
        compiler_params=params(),
        cost_estimate=cost(4 << 20, 4 << 20),
        name="pack",
    )(me, slot_dest, checkpoint, kmt, kappa)

    order = sorted(range(1, n), key=lambda k: (-bin(k >> 1).count("1"), k & 1, k))
    received = {0: packs[0]}
    for k in order:
        received[k] = lax.ppermute(packs[k], "lon", [(i, i ^ k) for i in range(n)])

    channels = 1 + 3 * LEV
    deep = rows + 2 * PAD
    table, grid = pl.pallas_call(
        functools.partial(base_kernel, n, cap, bx_n, by_n),
        out_shape=[
            shaped(n * cap + 2 * by_n, dtype=jnp.int32),
            shaped(channels, tiles, deep, LANES),
        ],
        in_specs=[SM, SM, VM, VM],
        out_specs=[SM, VM],
        compiler_params=params(),
        cost_estimate=cost(1 << 20, 2 << 20),
        name="base",
    )(me, slot_dest, kmt, kappa)

    rim = -(-channels * HALO // SUB) * SUB
    early = [0, 1] + order[: n // 2 - 1]
    late = [k for k in order if k not in early]
    for which in (early, late):
        shapes = [shaped(channels, tiles, deep, LANES)]
        if which is late:
            shapes += [shaped(tiles, rim, LANES)] * 2
        grid, *rims = pl.pallas_call(
            functools.partial(place_kernel, n, cap, bx_n, by_n, cols, which),
            out_shape=shapes,
            in_specs=[SM, SM] + [VM] * (1 + len(which)),
            out_specs=[VM] * len(shapes),
            compiler_params=params(),
            cost_estimate=cost(2 << 20, 2 << 20),
            name="early" if which is early else "late",
        )(me, table, grid, *[received[k] for k in which])
    north, south = rims

    up = [(i, i + 1) for i in range(lats - 1)]
    above = lax.ppermute(south, "lat", up)
    below = lax.ppermute(north, "lat", [(j, i) for i, j in up])

    devices = n * lats
    tracer_shape = shaped(2, LEV, rows, cols)
    tracer, powers, part = pl.pallas_call(
        functools.partial(inner_kernel, cols),
        out_shape=[
            tracer_shape,
            shaped(3, tiles, deep, LANES),
            shaped(SUB, LANES),
        ],
        in_specs=[VM],
        out_specs=[VM, VM, VM],
        compiler_params=params(),
        cost_estimate=cost(16 << 20, 6 << 20),
        name="inner",
    )(grid)
    tracer, border, sums = pl.pallas_call(
        functools.partial(border_kernel, cols),
        out_shape=[
            tracer_shape,
            shaped(2, 3, tiles, SUB, LANES),
            shaped(devices, LANES),
        ],
        in_specs=[VM, VM, VM, VM, VM, HB],
        out_specs=[HB, VM, VM],
        scratch_shapes=[
            pltpu.VMEM((2, channels, tiles, EDGE, LANES), F32),
            pltpu.VMEM((2, 3, tiles, EDGE, LANES), F32),
            pltpu.VMEM((2, 2, LEV, SUB, cols), F32),
            pltpu.SemaphoreType.DMA((2,)),
        ],
        input_output_aliases={5: 0},
        compiler_params=params(),
        cost_estimate=cost(2 << 20, 1 << 20),
        name="border",
    )(grid, above, below, powers, part, tracer)

    everyone = lax.all_to_all(sums, ("lon", "lat"), 0, 0, tiled=True)
    stream = pl.pallas_call(
        functools.partial(combine_kernel, cols),
        out_shape=shaped(rows, cols),
        in_specs=[VM, VM, VM],
        out_specs=VM,
        compiler_params=params(),
        cost_estimate=cost(1 << 20, 2 << 20),
        name="combine",
    )(everyone, powers, border)
    return tracer, stream


def solution(mesh):
    placed = (P("lat", "lon", None), P("lat", None), P("lat", "lon"), P(None, "lat", "lon"))
    return jax.shard_map(
        body,
        mesh=mesh,
        in_specs=placed,
        out_specs=(P(None, None, "lat", "lon"), P("lat", "lon")),
        check_vma=False,
    )
```

```python
import functools

import jax
import jax.numpy as jnp
from jax import lax
from jax.experimental import pallas as pl
from jax.experimental.pallas import tpu as pltpu
from jax.sharding import PartitionSpec as P


BH = 40
BW = 60
LEV = 2
HALO = 4
LANES = 128
SUB = 8
PAD = SUB
EDGE = 4 * SUB
ROWS = LEV * BH
HALF = LANES // 2
SHIFT = 8.0
SCALE = 8.0

thermal = 0.25
haline = 0.75
cabbeling = 0.05

VM = pl.BlockSpec(memory_space=pltpu.VMEM)
SM = pl.BlockSpec(memory_space=pltpu.SMEM)
HB = pl.BlockSpec(memory_space=pltpu.HBM)
F32 = jnp.float32


def params():
    return pltpu.CompilerParams(vmem_limit_bytes=24 << 20)


def cost(flops, moved):
    return pl.CostEstimate(flops=flops, bytes_accessed=moved, transcendentals=0)


def shaped(*dims, dtype=F32):
    return jax.ShapeDtypeStruct(dims, dtype)


def lanes():
    return lax.broadcasted_iota(jnp.int32, (SUB, LANES), 1)


def turn(value, amount):
    if isinstance(amount, int):
        amount %= LANES
        if amount == 0:
            return value
    return pltpu.roll(value, amount, 1)


def strip_lane(side, by, level, tracer, block_rows):
    return HALO * (((side * block_rows + by) * LEV + level) * 2 + tracer)


def edge_spot(cap, piece):
    if piece < 4 * cap:
        return piece // 2 * BH, HALF * (1 + piece % 2) - HALO
    return cap * ROWS + BH, HALO * (piece - 4 * cap)


def package_rows(cap, by_n):
    return cap * ROWS + (2 * BH if by_n * (1 + LEV) > 4 * cap else BH)


def pack_kernel(n, cap, bx_n, by_n, *refs):
    me_ref, dest_hbm, blocks_hbm, kmt_hbm, kappa_hbm = refs[:5]
    outs = refs[5 : 5 + n]
    dest, blocks, kmt, kappa, flat, strips, edges, source, count, sems = refs[5 + n :]
    groups = blocks.shape[0]
    slots = groups * SUB
    me = me_ref[0]
    lane = lanes()
    length = outs[0].shape[0]
    cols = kmt.shape[1]
    first = pltpu.make_async_copy(dest_hbm, dest, sems.at[groups])
    first.start()
    copies = [
        pltpu.make_async_copy(
            blocks_hbm.at[0, pl.ds(g * SUB, SUB), :], blocks.at[g], sems.at[g]
        )
        for g in range(groups)
    ]
    for copy in copies:
        copy.start()
    others = [
        pltpu.make_async_copy(kmt_hbm, kmt, sems.at[groups + 1]),
        pltpu.make_async_copy(kappa_hbm, kappa, sems.at[groups + 2]),
    ]
    for copy in others:
        copy.start()
    for k in range(n):
        count[k] = 0
    for at in range(n * cap):
        source[at] = 0
    first.wait()

    def assign(i, carry):
        d = dest[0, me * slots + i]

        @pl.when(d >= 0)
        def _():
            k = lax.bitwise_xor(lax.div(d, slots), me)
            c = count[k]
            count[k] = c + 1
            source[k * cap + c] = lax.div(i, SUB) * (ROWS * SUB) + lax.rem(i, SUB)

        return carry

    lax.fori_loop(0, slots, assign, 0)

    for g in range(groups):
        copies[g].wait()

    def regroup(group, carry):
        def load(q):
            return blocks[group, :, q * LANES : (q + 1) * LANES]

        limit = blocks.shape[2] // LANES - 1
        for row in range(ROWS):
            q, o = divmod(row * BW, LANES)
            p = (ROWS + row) * BW // LANES
            if o == 0:
                value = jnp.where(lane >= HALF, load(p), load(q))
            elif o <= HALF:
                low = load(p if o == HALF else min(p + 1, limit))
                value = jnp.where(lane >= o, load(q), low)
                if o < HALF:
                    value = jnp.where(lane >= o + HALF, load(p), value)
            else:
                value = jnp.where(lane >= o - HALF, load(p), load(q + 1))
                value = jnp.where(lane >= o, load(q), value)
            value = turn(value, -o)
            at = pl.multiple_of(group * (ROWS * SUB) + row * SUB, SUB)
            flat[pl.ds(at, SUB), :] = value
        return carry

    lax.fori_loop(0, groups, regroup, 0)

    def rows_of(start, row):
        return flat[pl.ds(start + row * SUB, SUB, stride=SUB), :]

    def strip(i, owner, by, side):
        k = lax.bitwise_xor(owner, me)
        start = lax.div(i, SUB) * (ROWS * SUB) + lax.rem(i, SUB)
        for level in range(LEV):
            for row in range(0, BH, SUB):
                value = rows_of(start, level * BH + row)
                old = strips[k, row : row + SUB, :]
                for tracer in range(2):
                    origin = tracer * HALF + (BW - HALO if side == 0 else 0)
                    target = strip_lane(side, by, level, tracer, by_n)
                    amount = lax.rem(target - origin + LANES, LANES)
                    here = (lane >= target) & (lane < target + HALO)
                    old = jnp.where(here, pltpu.roll(value, amount, 1), old)
                strips[k, row : row + SUB, :] = old

    def edge(i, carry):
        d = dest[0, me * slots + i]
        owner = lax.div(d, slots)
        spot = lax.rem(d, slots)
        bx = lax.rem(spot, bx_n)
        by = lax.div(spot, bx_n)

        @pl.when((d >= 0) & (bx == bx_n - 1))
        def _():
            strip(i, lax.rem(owner + 1, n), by, 0)

        @pl.when((d >= 0) & (bx == 0))
        def _():
            strip(i, lax.rem(owner + n - 1, n), by, 1)

        return carry

    lax.fori_loop(0, slots, edge, 0)

    for copy in others:
        copy.wait()
    zero = jnp.zeros((SUB, LANES), F32)
    for at in range(0, edges.shape[1], SUB):
        for side in range(2):
            edges[side, at : at + SUB, :] = zero
    for side, start in ((0, cols - HALO), (1, 0)):
        tile = start // LANES * LANES
        width = min(LANES, cols - tile)
        for piece in range(by_n * (1 + LEV)):
            by, ch = divmod(piece, 1 + LEV)
            base, target = edge_spot(cap, piece)
            if piece >= 4 * cap:
                base -= cap * ROWS + BH - 2 * cap * BH
            for row in range(0, BH, SUB):
                at = slice(by * BH + row, by * BH + row + SUB)
                if ch == 0:
                    value = kmt[at, tile : tile + width].astype(F32)
                else:
                    value = kappa[ch - 1, at, tile : tile + width]
                if width < LANES:
                    value = jnp.concatenate([value, zero[:, width:]], axis=1)
                value = turn(value, target - (start - tile))
                here = (lane >= target) & (lane < target + HALO)
                old = edges[side, base + row : base + row + SUB, :]
                edges[side, base + row : base + row + SUB, :] = jnp.where(
                    here, value, old
                )

    eastern = lax.bitwise_xor(lax.rem(me + 1, n), me)
    spare = (lane & (HALF - 1)) >= HALF - HALO
    in_blocks = min(edges.shape[1], 2 * cap * BH)
    for k in range(n):
        which = jnp.where(eastern == k, 0, 1)
        for c in range(cap):
            start = source[k * cap + c]
            for row in range(0, ROWS, SUB):
                value = rows_of(start, row)
                at = c * ROWS + row
                if at < in_blocks:
                    value = jnp.where(spare, edges[which, at : at + SUB, :], value)
                outs[k][at : at + SUB, :] = value
        for row in range(0, BH, SUB):
            at = cap * ROWS + row
            outs[k][at : at + SUB, :] = strips[k, row : row + SUB, :]
            if length > cap * ROWS + BH:
                outs[k][at + BH : at + BH + SUB, :] = edges[
                    which, in_blocks + row : in_blocks + row + SUB, :
                ]


def base_kernel(n, cap, bx_n, by_n, me_ref, dest, kmt, kappa, table, grid):
    me = me_ref[0]
    slots = bx_n * by_n
    channels, tiles, deep, _ = grid.shape
    cols = kmt.shape[1]
    zero = jnp.zeros((SUB, LANES), F32)
    for at in range(n * cap):
        table[at] = -1
    for at in range(2 * by_n):
        table[n * cap + at] = -1

    def clear(g, carry):
        at = pl.ds(pl.multiple_of(g * SUB, SUB), SUB)
        for ch in range(channels):
            for j in range(tiles):
                grid[ch, j, at, :] = zero
        return carry

    lax.fori_loop(0, deep // SUB, clear, 0)

    def lay(g, carry):
        at = pl.ds(pl.multiple_of(g * SUB, SUB), SUB)
        out = pl.ds(pl.multiple_of(g * SUB + PAD, SUB), SUB)
        for ch in range(1 + LEV):
            for j in range(tiles):
                width = min(LANES, cols - j * LANES)
                part = slice(j * LANES, j * LANES + width)
                if ch == 0:
                    value = kmt[at, part].astype(F32)
                else:
                    value = kappa[ch - 1, at, part]
                grid[ch, j, out, 0:width] = value
        return carry

    lax.fori_loop(0, kmt.shape[0] // SUB, lay, 0)
    west = lax.rem(me + n - 1, n)
    east = lax.rem(me + 1, n)

    def owner_loop(s, carry):
        k = lax.bitwise_xor(s, me)

        def slot_loop(i, c):
            d = dest[0, s * slots + i]
            spot = d - me * slots
            mine = (spot >= 0) & (spot < slots)
            from_west = d - west * slots
            from_east = d - east * slots

            @pl.when(mine)
            def _():
                table[k * cap + c] = spot

            @pl.when(
                (from_west >= 0)
                & (from_west < slots)
                & (lax.rem(from_west, bx_n) == bx_n - 1)
            )
            def _():
                table[n * cap + lax.div(from_west, bx_n)] = k

            @pl.when(
                (from_east >= 0) & (from_east < slots) & (lax.rem(from_east, bx_n) == 0)
            )
            def _():
                table[n * cap + by_n + lax.div(from_east, bx_n)] = k

            return c + mine.astype(jnp.int32)

        lax.fori_loop(0, slots, slot_loop, 0, unroll=8)
        return carry

    lax.fori_loop(0, n, owner_loop, 0)


def place_kernel(n, cap, bx_n, by_n, cols, which, *refs):
    count = len(which)
    me_ref, table, before = refs[:3]
    odd = me_ref[1]
    packs = refs[3 : 3 + count]
    grid, *rims = refs[3 + count :]
    me = me_ref[0]
    lane = lanes()
    channels, tiles, deep, _ = grid.shape
    last = tiles - 1
    own = cols - last * LANES
    halo_lane = (own, LANES - HALO)

    def copy(g, carry):
        at = pl.ds(pl.multiple_of(g * SUB, SUB), SUB)
        for ch in range(channels):
            for j in range(tiles):
                grid[ch, j, at, :] = before[ch, j, at, :]
        return carry

    lax.fori_loop(0, deep // SUB, copy, 0, unroll=2)

    def mark(ch, at, value, start):
        here = (lane >= start) & (lane < start + HALO)
        pltpu.store(grid.at[ch, last, at, :], value, mask=here)

    for k, pack in zip(which, packs):

        for c in range(cap):
            spot = table[k * cap + c]
            valid = spot >= 0
            spot = jnp.maximum(spot, 0)
            by = lax.div(spot, bx_n)
            offset = lax.rem(spot, bx_n) * BW
            tile = lax.div(offset, LANES)
            following = jnp.minimum(tile + 1, last)
            start = lax.rem(offset, LANES)
            begin = jnp.where(valid, start, LANES)
            here = (lane >= begin) & (lane < begin + BW)
            spill = lane < jnp.where(valid, start + BW - LANES, 0)
            for row in range(0, BH, SUB):
                at = pl.ds(pl.multiple_of(by * BH + row + PAD, SUB), SUB)
                depth = grid[0, tile, at, :], grid[0, following, at, :]
                for level in range(LEV):
                    place = c * ROWS + level * BH + row
                    value = pack[place : place + SUB, :]
                    masks = here & (depth[0] > level), spill & (depth[1] > level)
                    for tracer in range(2):
                        ch = 1 + LEV + tracer * LEV + level
                        turned = pltpu.roll(
                            value, lax.rem(start + tracer * HALF, LANES), 1
                        )
                        for target, mask in zip((tile, following), masks):
                            pltpu.store(grid.at[ch, target, at, :], turned, mask=mask)

        def strip(index, carry, k=k, pack=pack):
            @pl.when(table[n * cap + index] == k)
            def _():
                by = lax.rem(index, by_n)
                start = jnp.where(index < by_n, halo_lane[1], halo_lane[0])
                for level in range(LEV):
                    for tracer in range(2):
                        origin = strip_lane(0, index, level, tracer, by_n)
                        amount = lax.rem(start - origin + LANES, LANES)
                        for row in range(0, BH, SUB):
                            at = pl.ds(
                                pl.multiple_of(by * BH + row + PAD, SUB), SUB
                            )
                            place = cap * ROWS + row
                            value = pltpu.roll(pack[place : place + SUB, :], amount, 1)
                            mark(1 + LEV + tracer * LEV + level, at, value, start)

            return carry

        lax.fori_loop(0, 2 * by_n, strip, 0)

        for neighbour, start in ((me + n - 1, halo_lane[1]), (me + 1, halo_lane[0])):

            @pl.when(lax.bitwise_xor(lax.rem(neighbour, n), me) == k)
            def _(start=start, pack=pack):
                for piece in range(by_n * (1 + LEV)):
                    by, ch = divmod(piece, 1 + LEV)
                    base, origin = edge_spot(cap, piece)
                    for row in range(0, BH, SUB):
                        at = by * BH + row + PAD
                        mark(
                            ch,
                            slice(at, at + SUB),
                            turn(pack[base + row : base + row + SUB, :], start - origin),
                            start,
                        )

    if not rims:
        return
    rim = (lane >= own) & (lane < own + HALO) | (lane >= LANES - HALO)

    def mask(g, carry):
        at = pl.ds(pl.multiple_of(g * SUB + PAD, SUB), SUB)
        wet = grid[0, last, at, :]
        for ch in range(1 + LEV, channels):
            level = (ch - 1 - LEV) % LEV
            grid[ch, last, at, :] = jnp.where(
                rim & (wet <= level), 0.0, grid[ch, last, at, :]
            )
        return carry

    lax.fori_loop(0, deep // SUB - 2, mask, 0, unroll=4)
    low = deep - PAD - HALO
    for rows, first in zip(rims, (odd, 1 - odd)):
        at = jnp.where(first == 1, PAD, low)
        for ch in range(channels):
            for j in range(tiles):
                rows[j, ch * HALO : (ch + 1) * HALO, :] = grid[
                    ch, j, pl.ds(at, HALO), :
                ]


def sideways(values):
    lane = lanes()
    count = len(values)
    left = [turn(v, 1) for v in values]
    right = [turn(v, -1) for v in values]
    west = [
        jnp.where(lane == 0, left[(j - 1) % count], left[j]) for j in range(count)
    ]
    east = [
        jnp.where(lane == LANES - 1, right[(j + 1) % count], right[j])
        for j in range(count)
    ]
    return east, west


def three(load, start):
    return load(start), load(start - 1), load(start + 1)


def diffuse(load, start):
    tiles = len(load(0, start))
    span = range(tiles)
    level_c, level_a, level_b = three(functools.partial(load, 0), start)
    level_e, _ = sideways(level_c)
    both_e = [jnp.minimum(level_c[j], level_e[j]) for j in span]
    both_a = [jnp.minimum(level_c[j], level_a[j]) for j in span]
    both_b = [jnp.minimum(level_c[j], level_b[j]) for j in span]
    forcing = [None] * tiles
    fresh = [[None] * LEV for _ in range(2)]
    for level in range(LEV):
        kappa_c, kappa_a, kappa_b = three(functools.partial(load, 1 + level), start)
        kappa_e, _ = sideways(kappa_c)
        face_e, face_a, face_b = (
            [jnp.where(both[j] > level, kappa_c[j] + other[j], 0.0) for j in span]
            for both, other in (
                (both_e, kappa_e),
                (both_a, kappa_a),
                (both_b, kappa_b),
            )
        )
        for tracer in range(2):
            ch = 1 + LEV + tracer * LEV + level
            here, above, below = three(functools.partial(load, ch), start)
            to_east, _ = sideways(here)
            flux = [face_e[j] * (to_east[j] - here[j]) for j in span]
            _, flux_w = sideways(flux)
            fresh[tracer][level] = [
                jnp.where(
                    level_c[j] > level,
                    here[j]
                    + 0.5
                    * (
                        (flux[j] - flux_w[j])
                        + face_a[j] * (above[j] - here[j])
                        + face_b[j] * (below[j] - here[j])
                    ),
                    0.0,
                )
                for j in span
            ]
        thickness = 1.0 + 0.5 * level
        for j in span:
            temp, salt = fresh[0][level][j], fresh[1][level][j]
            density = haline * salt - temp * (thermal + cabbeling * temp)
            if level:
                density = forcing[j] + thickness * density
            forcing[j] = density
    return fresh, forcing


def apply(here, above, below, levels):
    span = range(len(here))
    pair = [above[j] + below[j] for j in span]
    mixed = [here[j] + 0.5 * pair[j] for j in span]
    east, west = sideways(mixed)
    result = []
    for j in span:
        diagonal = 6.0 - SHIFT + 1.0
        total = jnp.full((SUB, LANES), diagonal / SCALE, F32)
        for k in range(1, LEV):
            diagonal += 1.0 + 0.5 * k
            total = jnp.where(levels[j] > k, diagonal / SCALE, total)
        total = total * here[j] - (pair[j] + (east[j] + west[j])) * (1.0 / SCALE)
        result.append(jnp.where(levels[j] > 0, total, 0.0))
    return result


def gather_products(carry, powers, centre, keep):
    carry = list(carry)
    span = range(len(powers[0]))
    for j in span:
        q0, q1, q2, q3 = (keep(q[j], j) for q in powers)
        b1 = q1 - centre * q0
        c2 = q2 - centre * q1
        c3 = q3 - centre * q2
        b2 = c2 - centre * b1
        b3 = (c3 - centre * c2) - centre * b2
        terms = (q0, b1, b2, b3)
        for at, (x, y) in enumerate(PAIRS):
            carry[at] = carry[at] + terms[x] * terms[y]
    return tuple(carry)


def total_row(totals):
    lane = lanes()[:1]
    row = jnp.zeros((1, LANES), F32)
    for at, total in enumerate(totals):
        total = jnp.sum(total, axis=(0, 1), keepdims=True)
        row = jnp.where(lane == at + 1, total, row)
    return row


def put_tracer(target, fresh, cols, at):
    for tracer in range(2):
        for level in range(LEV):
            for j, value in enumerate(fresh[tracer][level]):
                width = min(LANES, cols - j * LANES)
                target[tracer, level, at, j * LANES : j * LANES + width] = value[
                    :, :width
                ]


def inner_kernel(cols, grid, tracer_out, powers, sums):
    lane = lanes()
    line = lax.broadcasted_iota(jnp.int32, (SUB, LANES), 0)
    _, tiles, deep, _ = grid.shape
    own = cols - (tiles - 1) * LANES
    first, end = PAD // SUB, (deep - PAD) // SUB
    zero = jnp.zeros((SUB, LANES), F32)

    def rows(ref, lead, start):
        return [ref[lead, j, pl.ds(start, SUB), :] for j in range(tiles)]

    def top(g):
        return pl.multiple_of(g * SUB, SUB)

    def step(g, carry):
        fresh, forcing = diffuse(functools.partial(rows, grid), top(g))
        put_tracer(
            tracer_out, fresh, cols, pl.ds(pl.multiple_of(g * SUB - PAD, SUB), SUB)
        )
        for j in range(tiles):
            powers[0, j, pl.ds(top(g), SUB), :] = forcing[j]
        return carry

    lax.fori_loop(first, end, step, 0, unroll=2)

    def inside(value, j):
        return value if j < tiles - 1 else jnp.where(lane < own, value, 0.0)

    def upper(value, j):
        return jnp.where(line >= HALO, inside(value, j), 0.0)

    def lower(value, j):
        return jnp.where(line < SUB - HALO, inside(value, j), 0.0)

    def power(g, source):
        here, above, below = three(functools.partial(rows, powers, source), top(g))
        return here, apply(here, above, below, rows(grid, 0, top(g)))

    def put(g, target):
        here, result = power(g, target - 1)
        for j in range(tiles):
            powers[target, j, pl.ds(top(g), SUB), :] = result[j]
        return here, result

    def first_power(g, carry, keep=inside):
        here, result = put(g, 1)
        a, b = carry
        for j in range(tiles):
            v = keep(here[j], j)
            a = a + v * v
            b = b + v * keep(result[j], j)
        return a, b

    def everywhere(body, carry):
        carry = body(first, carry, upper)
        carry = lax.fori_loop(first + 1, end - 1, body, carry, unroll=end - first - 2)
        return body(end - 1, carry, lower)

    a, b = everywhere(first_power, (zero, zero))
    a = jnp.sum(a, axis=(0, 1), keepdims=True)
    b = jnp.sum(b, axis=(0, 1), keepdims=True)
    centre = jnp.where(a > 0, b / jnp.where(a > 0, a, 1.0), 0.0)
    centre = jnp.broadcast_to(centre, (SUB, LANES))
    lax.fori_loop(
        first, end, lambda g, c: (put(g, 2), c)[1], 0, unroll=end - first
    )

    def products(g, carry, keep=inside):
        here, result = power(g, 2)
        lower_powers = [rows(powers, k, top(g)) for k in range(2)]
        return gather_products(carry, (*lower_powers, here, result), centre, keep)

    totals = everywhere(products, (zero,) * len(PAIRS))
    row = jnp.where(lane[:1] == 0, centre[:1], total_row(totals))
    sums[...] = jnp.broadcast_to(row, sums.shape)


def border_kernel(
    cols, me_ref, grid, pair_rows, other_rows, powers, part, tracer_in, tracer_out,
    border, sums,
    field, local, fresh_rows, sems,
):
    lane = lanes()
    line = lax.broadcasted_iota(jnp.int32, (SUB, LANES), 0)
    channels, tiles, deep, _ = grid.shape
    own = cols - (tiles - 1) * LANES
    half = EDGE // 2
    even = me_ref[1] == 0
    for ch in range(channels):
        for j in range(tiles):
            at = slice(ch * HALO, (ch + 1) * HALO)
            for row in range(0, half, SUB):
                field[0, ch, j, half + row : half + row + SUB, :] = grid[
                    ch, j, PAD + row : PAD + row + SUB, :
                ]
                low = deep - PAD - half + row
                field[1, ch, j, row : row + SUB, :] = grid[ch, j, low : low + SUB, :]
            pair, other = pair_rows[j, at, :], other_rows[j, at, :]
            field[0, ch, j, half - HALO : half, :] = jnp.where(even, other, pair)
            field[1, ch, j, half : half + HALO, :] = jnp.where(even, pair, other)
    for k in range(2):
        for j in range(tiles):
            local[0, k, j, EDGE - SUB : EDGE, :] = powers[
                k, j, PAD + SUB : PAD + 2 * SUB, :
            ]
            local[1, k, j, 0:SUB, :] = powers[
                k, j, deep - PAD - 2 * SUB : deep - PAD - SUB, :
            ]
    centre = jnp.broadcast_to(part[0:1, 0:1], (SUB, LANES))

    def rows_of(side):
        def rows(ref, lead, start):
            return [ref[side, lead, j, pl.ds(start, SUB), :] for j in range(tiles)]

        return rows

    height = tracer_out.shape[2]
    copies = []
    for side in range(2):
        rows = rows_of(side)
        mine = half - side * SUB
        for start in range(SUB, 3 * SUB, SUB):
            fresh, forcing = diffuse(functools.partial(rows, field), start)
            for j in range(tiles):
                local[side, 0, j, start : start + SUB, :] = forcing[j]
            if start == mine:
                put_tracer(fresh_rows.at[side], fresh, cols, slice(0, SUB))
        copies.append(
            pltpu.make_async_copy(
                fresh_rows.at[side],
                tracer_out.at[:, :, pl.ds(side * (height - SUB), SUB), :],
                sems.at[side],
            )
        )
        copies[-1].start()

    def power(side, start, source):
        rows = rows_of(side)
        here, above, below = three(functools.partial(rows, local, source), start)
        return here, apply(here, above, below, rows(field, 0, start))

    for target in range(1, 3):
        for side in range(2):
            for start in range(SUB, 3 * SUB, SUB):
                result = power(side, start, target - 1)[1]
                for j in range(tiles):
                    local[side, target, j, start : start + SUB, :] = result[j]
    totals = (jnp.zeros((SUB, LANES), F32),) * len(PAIRS)
    for side in range(2):
        mine = half - side * SUB
        here, result = power(side, mine, 2)
        lower_powers = [rows_of(side)(local, k, mine) for k in range(2)]
        for k, values in enumerate((*lower_powers, here)):
            for j in range(tiles):
                border[side, k, j] = values[j]
        bound = side * (SUB - HALO)
        rim = (line >= bound) & (line < bound + HALO)

        def keep(value, j, rim=rim):
            inside = rim if j < tiles - 1 else rim & (lane < own)
            return jnp.where(inside, value, 0.0)

        totals = gather_products(
            totals, (*lower_powers, here, result), centre, keep
        )
    sums[...] = jnp.broadcast_to(part[0:1, :] + total_row(totals), sums.shape)
    for copy in copies:
        copy.wait()


PAIRS = ((0, 0), (0, 1), (0, 2), (0, 3), (1, 1), (1, 2), (1, 3), (2, 2), (2, 3))


def combine_kernel(cols, sums, powers, border, stream):
    values = sums[...]
    lane = lax.broadcasted_iota(jnp.int32, values.shape, 1)

    def column(k):
        return jnp.sum(jnp.where(lane == k, values, 0.0), axis=1, keepdims=True)

    centre = column(0)
    gram = {pair: column(at + 1) for at, pair in enumerate(PAIRS)}

    def local(c):
        c = list(c) + [None] * (4 - len(c))
        c0, c1, c2, c3 = c
        result = [c0 + jnp.zeros_like(centre)]
        if c1 is not None:
            inner = c1
            slope = c1 + jnp.zeros_like(centre)
            if c2 is not None:
                inner = c1 + centre * (c2 if c3 is None else c2 + centre * c3)
                slope = c1 + centre * (
                    2.0 * c2 if c3 is None else 2.0 * c2 + 3.0 * (centre * c3)
                )
            result = [c0 + centre * inner, slope]
        if c2 is not None:
            result.append(c2 + jnp.zeros_like(centre) if c3 is None else c2 + 3.0 * (centre * c3))
        if c3 is not None:
            result.append(c3 + jnp.zeros_like(centre))
        return result

    def inner(x, y):
        u, v = local(x), local(y)
        total = jnp.zeros_like(centre)
        for i in range(len(u)):
            for j in range(len(v)):
                total = total + (u[i] * v[j]) * gram[(min(i, j), max(i, j))]
        return jnp.sum(total, axis=0, keepdims=True)

    def operate(c):
        result = [SHIFT * x for x in c] + [None]
        for i, x in enumerate(c):
            term = SCALE * x
            result[i + 1] = term if result[i + 1] is None else result[i + 1] + term
        return result

    one = jnp.ones((1, 1), F32)
    stream_c = [None] * 3
    residual, direction = [one], [one]
    norm = inner(residual, residual)
    for step in range(3):
        image = operate(direction)
        alpha = norm / inner(direction, image)
        for i, x in enumerate(direction):
            stream_c[i] = alpha * x if stream_c[i] is None else stream_c[i] + alpha * x
        if step == 2:
            break
        residual = [
            (residual[i] - alpha * image[i]) if i < len(residual) else -alpha * image[i]
            for i in range(len(image))
        ]
        fresh = inner(residual, residual)
        ratio = fresh / norm
        direction = [
            (residual[i] + ratio * direction[i]) if i < len(direction) else residual[i]
            for i in range(len(residual))
        ]
        norm = fresh

    tiles = powers.shape[1]
    height = stream.shape[0]
    weights = [jnp.broadcast_to(c, (SUB, LANES)) for c in stream_c]

    def put(out, load):
        for j in range(tiles):
            width = min(LANES, cols - j * LANES)
            value = sum(weights[k] * load(k, j) for k in range(3))
            stream[out, j * LANES : j * LANES + width] = value[:, :width]

    def write(g, carry):
        at = pl.ds(pl.multiple_of(g * SUB + PAD, SUB), SUB)
        out = pl.ds(pl.multiple_of(g * SUB, SUB), SUB)
        put(out, lambda k, j: powers[k, j, at, :])
        return carry

    put(slice(0, SUB), lambda k, j: border[0, k, j])
    lax.fori_loop(1, height // SUB - 1, write, 0, unroll=3)
    put(slice(height - SUB, height), lambda k, j: border[1, k, j])


def body(checkpoint, slot_dest, kmt, kappa):
    n = lax.axis_size("lon")
    lats = lax.axis_size("lat")
    lat = lax.axis_index("lat")
    me = jnp.stack([lax.axis_index("lon"), lax.rem(lat, 2)]).astype(jnp.int32)
    _, slots, values = checkpoint.shape
    rows, cols = kmt.shape
    by_n, bx_n = rows // BH, cols // BW
    cap = slots // n
    length = package_rows(cap, by_n)
    tiles = -(-(cols + 2 * HALO) // LANES)
    groups = slots // SUB
    edge_rows = -(-by_n * (1 + LEV) // 2) * BH
    if by_n * (1 + LEV) > 4 * cap:
        edge_rows = 2 * cap * BH + BH

    packs = pl.pallas_call(
        functools.partial(pack_kernel, n, cap, bx_n, by_n),
        out_shape=[shaped(length, LANES)] * n,
        in_specs=[SM, HB, HB, HB, HB],
        out_specs=[VM] * n,
        scratch_shapes=[
            pltpu.SMEM((1, n * slots), jnp.int32),
            pltpu.VMEM((groups, SUB, values), F32),
            pltpu.VMEM((rows, cols), jnp.int32),
            pltpu.VMEM((LEV, rows, cols), F32),
            pltpu.VMEM((slots * ROWS, LANES), F32),
            pltpu.VMEM((n, BH, LANES), F32),
            pltpu.VMEM((2, edge_rows, LANES), F32),
            pltpu.SMEM((n * cap,), jnp.int32),
            pltpu.SMEM((n,), jnp.int32),
            pltpu.SemaphoreType.DMA((groups + 3,)),
        ],
        compiler_params=params(),
        cost_estimate=cost(4 << 20, 4 << 20),
        name="pack",
    )(
        me,
        *[
            pltpu.with_memory_space_constraint(x, pltpu.HBM)
            for x in (slot_dest, checkpoint, kmt, kappa)
        ],
    )

    order = sorted(range(1, n), key=lambda k: (-bin(k >> 1).count("1"), k & 1, k))
    received = {0: packs[0]}
    for k in order:
        received[k] = lax.ppermute(packs[k], "lon", [(i, i ^ k) for i in range(n)])

    channels = 1 + 3 * LEV
    deep = rows + 2 * PAD
    table, grid = pl.pallas_call(
        functools.partial(base_kernel, n, cap, bx_n, by_n),
        out_shape=[
            shaped(n * cap + 2 * by_n, dtype=jnp.int32),
            shaped(channels, tiles, deep, LANES),
        ],
        in_specs=[SM, SM, VM, VM],
        out_specs=[SM, VM],
        compiler_params=params(),
        cost_estimate=cost(1 << 20, 2 << 20),
        name="base",
    )(me, slot_dest, kmt, kappa)

    rim = -(-channels * HALO // SUB) * SUB
    quarter = n // 4
    parts = [
        [0, 1] + order[:quarter],
        order[quarter : 2 * quarter],
        order[2 * quarter : -1],
    ]
    for stage, which in enumerate(parts):
        shapes = [shaped(channels, tiles, deep, LANES)]
        if stage == len(parts) - 1:
            shapes += [shaped(tiles, rim, LANES)] * 2
        grid, *rims = pl.pallas_call(
            functools.partial(place_kernel, n, cap, bx_n, by_n, cols, which),
            out_shape=shapes,
            in_specs=[SM, SM] + [VM] * (1 + len(which)),
            out_specs=[VM] * len(shapes),
            compiler_params=params(),
            cost_estimate=cost(2 << 20, 2 << 20),
            name=f"place{stage}",
        )(me, table, grid, *[received[k] for k in which])

    swaps = [
        [(i, i ^ 1) for i in range(lats) if i ^ 1 < lats],
        [(i, j) for i in range(lats) for j in [(i - 1 ^ 1) + 1] if 0 <= j < lats],
    ]
    pair_rows, other_rows = (
        lax.ppermute(value, "lat", swap) for value, swap in zip(rims, swaps)
    )

    devices = n * lats
    tracer_shape = shaped(2, LEV, rows, cols)
    tracer, powers, part = pl.pallas_call(
        functools.partial(inner_kernel, cols),
        out_shape=[
            tracer_shape,
            shaped(3, tiles, deep, LANES),
            shaped(SUB, LANES),
        ],
        in_specs=[VM],
        out_specs=[VM, VM, VM],
        compiler_params=params(),
        cost_estimate=cost(16 << 20, 6 << 20),
        name="inner",
    )(grid)
    tracer, border, sums = pl.pallas_call(
        functools.partial(border_kernel, cols),
        out_shape=[
            tracer_shape,
            shaped(2, 3, tiles, SUB, LANES),
            shaped(devices, LANES),
        ],
        in_specs=[SM, VM, VM, VM, VM, VM, HB],
        out_specs=[HB, VM, VM],
        scratch_shapes=[
            pltpu.VMEM((2, channels, tiles, EDGE, LANES), F32),
            pltpu.VMEM((2, 3, tiles, EDGE, LANES), F32),
            pltpu.VMEM((2, 2, LEV, SUB, cols), F32),
            pltpu.SemaphoreType.DMA((2,)),
        ],
        input_output_aliases={6: 0},
        compiler_params=params(),
        cost_estimate=cost(2 << 20, 1 << 20),
        name="border",
    )(me, grid, pair_rows, other_rows, powers, part, tracer)

    everyone = lax.all_to_all(sums, ("lon", "lat"), 0, 0, tiled=True)
    stream = pl.pallas_call(
        functools.partial(combine_kernel, cols),
        out_shape=shaped(rows, cols),
        in_specs=[VM, VM, VM],
        out_specs=VM,
        compiler_params=params(),
        cost_estimate=cost(1 << 20, 2 << 20),
        name="combine",
    )(everyone, powers, border)
    return tracer, stream


def solution(mesh):
    placed = (P("lat", "lon", None), P("lat", None), P("lat", "lon"), P(None, "lat", "lon"))
    return jax.shard_map(
        body,
        mesh=mesh,
        in_specs=placed,
        out_specs=(P(None, None, "lat", "lon"), P("lat", "lon")),
        check_vma=False,
    )
```

```python
import functools

import jax
import jax.numpy as jnp
from jax import lax
from jax.experimental import pallas as pl
from jax.experimental.pallas import tpu as pltpu
from jax.sharding import PartitionSpec as P


BH = 40
BW = 60
LEV = 2
HALO = 4
LANES = 128
SUB = 8
PAD = SUB
EDGE = 4 * SUB
ROWS = LEV * BH
HALF = LANES // 2
SHIFT = 8.0
SCALE = 8.0

thermal = 0.25
haline = 0.75
cabbeling = 0.05

VM = pl.BlockSpec(memory_space=pltpu.VMEM)
SM = pl.BlockSpec(memory_space=pltpu.SMEM)
HB = pl.BlockSpec(memory_space=pltpu.HBM)
F32 = jnp.float32


def params():
    return pltpu.CompilerParams(vmem_limit_bytes=24 << 20)


def cost(flops, moved):
    return pl.CostEstimate(flops=flops, bytes_accessed=moved, transcendentals=0)


def shaped(*dims, dtype=F32):
    return jax.ShapeDtypeStruct(dims, dtype)


def lanes():
    return lax.broadcasted_iota(jnp.int32, (SUB, LANES), 1)


def turn(value, amount):
    if isinstance(amount, int):
        amount %= LANES
        if amount == 0:
            return value
    return pltpu.roll(value, amount, 1)


def strip_lane(side, by, level, tracer, block_rows):
    return HALO * ((side * block_rows + by) * LEV + level) + HALF * tracer


def edge_spot(cap, piece):
    if piece < 4 * cap:
        return piece // 2 * BH, HALF * (1 + piece % 2) - HALO
    return cap * ROWS + BH, HALO * (piece - 4 * cap)


def package_rows(cap, by_n):
    return cap * ROWS + (2 * BH if by_n * (1 + LEV) > 4 * cap else BH)


def block_rows(flat, start, row):
    return flat[pl.ds(start + row * SUB, SUB, stride=SUB), :]


def block_start(i):
    return lax.div(i, SUB) * (ROWS * SUB) + lax.rem(i, SUB)


def fill_strips(n, bx_n, by_n, me, dest, flat, strips, wanted):
    slots = bx_n * by_n
    lane = lanes()

    def strip(i, k, by, side):
        start = block_start(i)
        for level in range(LEV):
            target = strip_lane(side, by, level, 0, by_n)
            amount = lax.rem(target - (BW - HALO if side == 0 else 0) + LANES, LANES)
            spot = lane & (HALF - 1)
            here = (spot >= target) & (spot < target + HALO)
            for row in range(0, BH, SUB):
                value = block_rows(flat, start, level * BH + row)
                pltpu.store(
                    strips.at[k, row : row + SUB, :],
                    pltpu.roll(value, amount, 1),
                    mask=here,
                )

    def edge(i, carry):
        d = dest[0, me * slots + i]
        owner = lax.div(d, slots)
        spot = lax.rem(d, slots)
        bx = lax.rem(spot, bx_n)
        by = lax.div(spot, bx_n)
        for side, column, other in ((0, bx_n - 1, 1), (1, 0, n - 1)):
            k = lax.bitwise_xor(lax.rem(owner + other, n), me)

            @pl.when((d >= 0) & (bx == column) & wanted(k))
            def _(k=k, side=side):
                strip(i, k, by, side)

        return carry

    lax.fori_loop(0, slots, edge, 0)


def assemble(out, k, cap, source, flat, strips, edges=None, which=None, in_blocks=0):
    spare = (lanes() & (HALF - 1)) >= HALF - HALO
    for c in range(cap):
        start = source[k * cap + c]
        for row in range(0, ROWS, SUB):
            value = block_rows(flat, start, row)
            at = c * ROWS + row
            if at < in_blocks:
                value = jnp.where(spare, edges[which, at : at + SUB, :], value)
            out[at : at + SUB, :] = value
    for row in range(0, BH, SUB):
        at = cap * ROWS + row
        out[at : at + SUB, :] = strips[k, row : row + SUB, :]


def first_kernel(n, cap, bx_n, by_n, *refs):
    me_ref, dest_hbm, blocks_hbm = refs[:3]
    outs = refs[3 : n // 2 + 2]
    dest, source, flat, blocks, strips, count, sems = refs[n // 2 + 2 :]
    groups = blocks.shape[0]
    slots = groups * SUB
    me = me_ref[0]
    lane = lanes()
    first = pltpu.make_async_copy(dest_hbm, dest, sems.at[groups])
    first.start()

    def loading(g):
        rows = pl.ds(pl.multiple_of(g * SUB, SUB), SUB)
        return pltpu.make_async_copy(
            blocks_hbm.at[0, rows, :], blocks.at[g], sems.at[g]
        )

    for g in range(groups):
        loading(g).start()
    for k in range(n):
        count[k] = 0
    for at in range(n * cap):
        source[at] = 0
    first.wait()

    def assign(i, carry):
        d = dest[0, me * slots + i]

        @pl.when(d >= 0)
        def _():
            k = lax.bitwise_xor(lax.div(d, slots), me)
            c = count[k]
            count[k] = c + 1
            source[k * cap + c] = block_start(i)

        return carry

    lax.fori_loop(0, slots, assign, 0)

    def regroup(group, carry):
        loading(group).wait()

        def load(q):
            return blocks[group, :, q * LANES : (q + 1) * LANES]

        limit = blocks.shape[2] // LANES - 1
        for row in range(ROWS):
            q, o = divmod(row * BW, LANES)
            p = (ROWS + row) * BW // LANES
            if o == 0:
                value = jnp.where(lane >= HALF, load(p), load(q))
            elif o <= HALF:
                low = load(p if o == HALF else min(p + 1, limit))
                value = jnp.where(lane >= o, load(q), low)
                if o < HALF:
                    value = jnp.where(lane >= o + HALF, load(p), value)
            else:
                value = jnp.where(lane >= o - HALF, load(p), load(q + 1))
                value = jnp.where(lane >= o, load(q), value)
            at = pl.multiple_of(group * (ROWS * SUB) + row * SUB, SUB)
            flat[pl.ds(at, SUB), :] = turn(value, -o)
        return carry

    lax.fori_loop(0, groups, regroup, 0)
    fill_strips(
        n, bx_n, by_n, me, dest, flat, strips, lambda k: (k > 0) & (k & 1 == 0)
    )
    for k in range(2, n, 2):
        assemble(outs[k // 2 - 1], k, cap, source, flat, strips)


def second_kernel(n, cap, bx_n, by_n, *refs):
    me_ref, dest, source, flat, kmt_hbm, kappa_hbm = refs[:6]
    outs = refs[6 : n // 2 + 7]
    kmt, kappa, strips, edges, sems = refs[n // 2 + 7 :]
    me = me_ref[0]
    lane = lanes()
    length = outs[0].shape[0]
    cols = kmt.shape[1]
    copies = [
        pltpu.make_async_copy(kmt_hbm, kmt, sems.at[0]),
        pltpu.make_async_copy(kappa_hbm, kappa, sems.at[1]),
    ]
    for copy in copies:
        copy.start()
    fill_strips(
        n, bx_n, by_n, me, dest, flat, strips, lambda k: (k == 0) | (k & 1 == 1)
    )
    for copy in copies:
        copy.wait()
    zero = jnp.zeros((SUB, LANES), F32)
    for at in range(0, edges.shape[1], SUB):
        for side in range(2):
            edges[side, at : at + SUB, :] = zero
    for side, start in ((0, cols - HALO), (1, 0)):
        tile = start // LANES * LANES
        width = min(LANES, cols - tile)
        for piece in range(by_n * (1 + LEV)):
            by, ch = divmod(piece, 1 + LEV)
            base, target = edge_spot(cap, piece)
            if piece >= 4 * cap:
                base -= cap * ROWS + BH - 2 * cap * BH
            here = (lane >= target) & (lane < target + HALO)
            for row in range(0, BH, SUB):
                at = slice(by * BH + row, by * BH + row + SUB)
                if ch == 0:
                    value = kmt[at, tile : tile + width].astype(F32)
                else:
                    value = kappa[ch - 1, at, tile : tile + width]
                if width < LANES:
                    value = jnp.concatenate([value, zero[:, width:]], axis=1)
                pltpu.store(
                    edges.at[side, base + row : base + row + SUB, :],
                    turn(value, target - (start - tile)),
                    mask=here,
                )
    eastern = lax.bitwise_xor(lax.rem(me + 1, n), me)
    in_blocks = min(edges.shape[1], 2 * cap * BH)
    for out, k in zip(outs, [0, *range(1, n, 2)]):
        which = jnp.where(eastern == k, 0, 1)
        assemble(out, k, cap, source, flat, strips, edges, which, in_blocks)
        if length > cap * ROWS + BH:
            for row in range(0, BH, SUB):
                at = cap * ROWS + BH + row
                out[at : at + SUB, :] = edges[
                    which, in_blocks + row : in_blocks + row + SUB, :
                ]


def base_kernel(n, cap, bx_n, by_n, me_ref, dest, kmt, kappa, table, grid, bringer):
    me = me_ref[0]
    slots = bx_n * by_n
    channels, tiles, deep, _ = grid.shape
    cols = kmt.shape[1]
    zero = jnp.zeros((SUB, LANES), F32)
    west = lax.rem(me + n - 1, n)
    east = lax.rem(me + 1, n)
    for at in range(n * (cap + 1)):
        table[at] = -1
    sides = [(west, by * bx_n + bx_n - 1) for by in range(by_n)]
    sides += [(east, by * bx_n) for by in range(by_n)]
    for owner, spot in sides:
        bringer[owner * slots + spot + 1] = -1

    def owner_loop(s, carry):
        k = lax.bitwise_xor(s, me)

        def slot_loop(i, c):
            d = dest[0, s * slots + i]
            bringer[d + 1] = k
            spot = d - me * slots
            mine = (spot >= 0) & (spot < slots)
            table[k * (cap + 1) + c] = jnp.where(mine, spot, -1)
            return c + mine.astype(jnp.int32)

        lax.fori_loop(0, slots, slot_loop, 0, unroll=8)
        return carry

    lax.fori_loop(0, n, owner_loop, 0)
    for at, (owner, spot) in enumerate(sides):
        table[n * (cap + 1) + at] = bringer[owner * slots + spot + 1]

    def clear(g, carry):
        at = pl.ds(pl.multiple_of(g * SUB, SUB), SUB)
        for ch in range(channels):
            for j in range(tiles):
                grid[ch, j, at, :] = zero
        return carry

    lax.fori_loop(0, deep // SUB, clear, 0)

    def lay(g, carry):
        at = pl.ds(pl.multiple_of(g * SUB, SUB), SUB)
        out = pl.ds(pl.multiple_of(g * SUB + PAD, SUB), SUB)
        for ch in range(1 + LEV):
            for j in range(tiles):
                width = min(LANES, cols - j * LANES)
                part = slice(j * LANES, j * LANES + width)
                if ch == 0:
                    value = kmt[at, part].astype(F32)
                else:
                    value = kappa[ch - 1, at, part]
                grid[ch, j, out, 0:width] = value
        return carry

    lax.fori_loop(0, kmt.shape[0] // SUB, lay, 0)


def place_kernel(n, cap, bx_n, by_n, cols, which, *refs):
    count = len(which)
    me_ref, table, _ = refs[:3]
    odd = me_ref[1]
    packs = refs[3 : 3 + count]
    grid, *rims = refs[3 + count :]
    me = me_ref[0]
    lane = lanes()
    channels, tiles, deep, _ = grid.shape
    last = tiles - 1
    own = cols - last * LANES
    halo_lane = (own, LANES - HALO)

    def mark(ch, at, value, start):
        here = (lane >= start) & (lane < start + HALO)
        pltpu.store(grid.at[ch, last, at, :], value, mask=here)

    for k, pack in zip(which, packs):

        for c in range(cap):
            spot = table[k * (cap + 1) + c]
            valid = spot >= 0
            spot = jnp.maximum(spot, 0)
            by = lax.div(spot, bx_n)
            offset = lax.rem(spot, bx_n) * BW
            tile = lax.div(offset, LANES)
            following = jnp.minimum(tile + 1, last)
            start = lax.rem(offset, LANES)
            begin = jnp.where(valid, start, LANES)
            here = (lane >= begin) & (lane < begin + BW)
            spill = lane < jnp.where(valid, start + BW - LANES, 0)
            for row in range(0, BH, SUB):
                at = pl.ds(pl.multiple_of(by * BH + row + PAD, SUB), SUB)
                depth = grid[0, tile, at, :], grid[0, following, at, :]
                for level in range(LEV):
                    place = c * ROWS + level * BH + row
                    value = pack[place : place + SUB, :]
                    masks = here & (depth[0] > level), spill & (depth[1] > level)
                    for tracer in range(2):
                        ch = 1 + LEV + tracer * LEV + level
                        turned = pltpu.roll(
                            value, lax.rem(start + tracer * HALF, LANES), 1
                        )
                        for target, mask in zip((tile, following), masks):
                            pltpu.store(grid.at[ch, target, at, :], turned, mask=mask)

        def strip(index, carry, k=k, pack=pack):
            @pl.when(table[n * (cap + 1) + index] == k)
            def _():
                by = lax.rem(index, by_n)
                start = jnp.where(index < by_n, halo_lane[1], halo_lane[0])
                for level in range(LEV):
                    for tracer in range(2):
                        origin = strip_lane(0, index, level, tracer, by_n)
                        amount = lax.rem(start - origin + LANES, LANES)
                        for row in range(0, BH, SUB):
                            at = pl.ds(
                                pl.multiple_of(by * BH + row + PAD, SUB), SUB
                            )
                            place = cap * ROWS + row
                            value = pltpu.roll(pack[place : place + SUB, :], amount, 1)
                            mark(1 + LEV + tracer * LEV + level, at, value, start)

            return carry

        lax.fori_loop(0, 2 * by_n, strip, 0)

        for neighbour, start in ((me + n - 1, halo_lane[1]), (me + 1, halo_lane[0])):
            if k % 2 == 0:
                continue

            @pl.when(lax.bitwise_xor(lax.rem(neighbour, n), me) == k)
            def _(start=start, pack=pack):
                for piece in range(by_n * (1 + LEV)):
                    by, ch = divmod(piece, 1 + LEV)
                    base, origin = edge_spot(cap, piece)
                    for row in range(0, BH, SUB):
                        at = by * BH + row + PAD
                        mark(
                            ch,
                            slice(at, at + SUB),
                            turn(pack[base + row : base + row + SUB, :], start - origin),
                            start,
                        )

    if not rims:
        return
    rim = (lane >= own) & (lane < own + HALO) | (lane >= LANES - HALO)

    def mask(g, carry):
        at = pl.ds(pl.multiple_of(g * SUB + PAD, SUB), SUB)
        wet = grid[0, last, at, :]
        for ch in range(1 + LEV, channels):
            level = (ch - 1 - LEV) % LEV
            grid[ch, last, at, :] = jnp.where(
                rim & (wet <= level), 0.0, grid[ch, last, at, :]
            )
        return carry

    lax.fori_loop(0, deep // SUB - 2, mask, 0, unroll=4)
    low = deep - PAD - HALO
    for rows, first in zip(rims, (odd, 1 - odd)):
        at = jnp.where(first == 1, PAD, low)
        for ch in range(channels):
            for j in range(tiles):
                rows[j, ch * HALO : (ch + 1) * HALO, :] = grid[
                    ch, j, pl.ds(at, HALO), :
                ]


def sideways(values):
    lane = lanes()
    count = len(values)
    left = [turn(v, 1) for v in values]
    right = [turn(v, -1) for v in values]
    west = [
        jnp.where(lane == 0, left[(j - 1) % count], left[j]) for j in range(count)
    ]
    east = [
        jnp.where(lane == LANES - 1, right[(j + 1) % count], right[j])
        for j in range(count)
    ]
    return east, west


def three(load, start):
    return load(start), load(start - 1), load(start + 1)


def diffuse(load, start):
    tiles = len(load(0, start))
    span = range(tiles)
    level_c, level_a, level_b = three(functools.partial(load, 0), start)
    level_e, _ = sideways(level_c)
    both_e = [jnp.minimum(level_c[j], level_e[j]) for j in span]
    both_a = [jnp.minimum(level_c[j], level_a[j]) for j in span]
    both_b = [jnp.minimum(level_c[j], level_b[j]) for j in span]
    forcing = [None] * tiles
    fresh = [[None] * LEV for _ in range(2)]
    for level in range(LEV):
        kappa_c, kappa_a, kappa_b = three(functools.partial(load, 1 + level), start)
        kappa_e, _ = sideways(kappa_c)
        face_e, face_a, face_b = (
            [jnp.where(both[j] > level, kappa_c[j] + other[j], 0.0) for j in span]
            for both, other in (
                (both_e, kappa_e),
                (both_a, kappa_a),
                (both_b, kappa_b),
            )
        )
        for tracer in range(2):
            ch = 1 + LEV + tracer * LEV + level
            here, above, below = three(functools.partial(load, ch), start)
            to_east, _ = sideways(here)
            flux = [face_e[j] * (to_east[j] - here[j]) for j in span]
            _, flux_w = sideways(flux)
            fresh[tracer][level] = [
                jnp.where(
                    level_c[j] > level,
                    here[j]
                    + 0.5
                    * (
                        (flux[j] - flux_w[j])
                        + face_a[j] * (above[j] - here[j])
                        + face_b[j] * (below[j] - here[j])
                    ),
                    0.0,
                )
                for j in span
            ]
        thickness = 1.0 + 0.5 * level
        for j in span:
            temp, salt = fresh[0][level][j], fresh[1][level][j]
            density = haline * salt - temp * (thermal + cabbeling * temp)
            if level:
                density = forcing[j] + thickness * density
            forcing[j] = density
    return fresh, forcing


def apply(here, above, below, levels):
    span = range(len(here))
    pair = [above[j] + below[j] for j in span]
    mixed = [here[j] + 0.5 * pair[j] for j in span]
    east, west = sideways(mixed)
    result = []
    for j in span:
        diagonal = 6.0 - SHIFT + 1.0
        total = jnp.full((SUB, LANES), diagonal / SCALE, F32)
        for k in range(1, LEV):
            diagonal += 1.0 + 0.5 * k
            total = jnp.where(levels[j] > k, diagonal / SCALE, total)
        total = total * here[j] - (pair[j] + (east[j] + west[j])) * (1.0 / SCALE)
        result.append(jnp.where(levels[j] > 0, total, 0.0))
    return result


def gather_products(carry, powers, centre, keep):
    carry = list(carry)
    span = range(len(powers[0]))
    for j in span:
        q0, q1, q2, q3 = (keep(q[j], j) for q in powers)
        b1 = q1 - centre * q0
        c2 = q2 - centre * q1
        c3 = q3 - centre * q2
        b2 = c2 - centre * b1
        b3 = (c3 - centre * c2) - centre * b2
        terms = (q0, b1, b2, b3)
        for at, (x, y) in enumerate(PAIRS):
            carry[at] = carry[at] + terms[x] * terms[y]
    return tuple(carry)


def total_row(totals):
    lane = lanes()[:1]
    row = jnp.zeros((1, LANES), F32)
    for at, total in enumerate(totals):
        total = jnp.sum(total, axis=(0, 1), keepdims=True)
        row = jnp.where(lane == at + 1, total, row)
    return row


def put_tracer(target, fresh, cols, at):
    for tracer in range(2):
        for level in range(LEV):
            for j, value in enumerate(fresh[tracer][level]):
                width = min(LANES, cols - j * LANES)
                target[tracer, level, at, j * LANES : j * LANES + width] = value[
                    :, :width
                ]


def inner_kernel(cols, grid, tracer_out, powers, sums):
    lane = lanes()
    line = lax.broadcasted_iota(jnp.int32, (SUB, LANES), 0)
    _, tiles, deep, _ = grid.shape
    own = cols - (tiles - 1) * LANES
    first, end = PAD // SUB, (deep - PAD) // SUB
    zero = jnp.zeros((SUB, LANES), F32)

    def rows(ref, lead, start):
        return [ref[lead, j, pl.ds(start, SUB), :] for j in range(tiles)]

    def top(g):
        return pl.multiple_of(g * SUB, SUB)

    def step(g, carry):
        fresh, forcing = diffuse(functools.partial(rows, grid), top(g))
        put_tracer(
            tracer_out, fresh, cols, pl.ds(pl.multiple_of(g * SUB - PAD, SUB), SUB)
        )
        for j in range(tiles):
            powers[0, j, pl.ds(top(g), SUB), :] = forcing[j]
        return carry

    lax.fori_loop(first, end, step, 0, unroll=2)

    def inside(value, j):
        return value if j < tiles - 1 else jnp.where(lane < own, value, 0.0)

    def upper(value, j):
        return jnp.where(line >= HALO, inside(value, j), 0.0)

    def lower(value, j):
        return jnp.where(line < SUB - HALO, inside(value, j), 0.0)

    def power(g, source):
        here, above, below = three(functools.partial(rows, powers, source), top(g))
        return here, apply(here, above, below, rows(grid, 0, top(g)))

    def put(g, target):
        here, result = power(g, target - 1)
        for j in range(tiles):
            powers[target, j, pl.ds(top(g), SUB), :] = result[j]
        return here, result

    def first_power(g, carry, keep=inside):
        here, result = put(g, 1)
        a, b = carry
        for j in range(tiles):
            v = keep(here[j], j)
            a = a + v * v
            b = b + v * keep(result[j], j)
        return a, b

    def everywhere(body, carry):
        carry = body(first, carry, upper)
        carry = lax.fori_loop(first + 1, end - 1, body, carry, unroll=end - first - 2)
        return body(end - 1, carry, lower)

    a, b = everywhere(first_power, (zero, zero))
    a = jnp.sum(a, axis=(0, 1), keepdims=True)
    b = jnp.sum(b, axis=(0, 1), keepdims=True)
    centre = jnp.where(a > 0, b / jnp.where(a > 0, a, 1.0), 0.0)
    centre = jnp.broadcast_to(centre, (SUB, LANES))
    lax.fori_loop(
        first, end, lambda g, c: (put(g, 2), c)[1], 0, unroll=end - first
    )

    def products(g, carry, keep=inside):
        here, result = power(g, 2)
        lower_powers = [rows(powers, k, top(g)) for k in range(2)]
        return gather_products(carry, (*lower_powers, here, result), centre, keep)

    totals = everywhere(products, (zero,) * len(PAIRS))
    row = jnp.where(lane[:1] == 0, centre[:1], total_row(totals))
    sums[...] = jnp.broadcast_to(row, sums.shape)


def border_kernel(
    cols, me_ref, grid, pair_rows, other_rows, powers, part, tracer_in, tracer_out,
    border, sums,
    field, local, fresh_rows, sems,
):
    lane = lanes()
    line = lax.broadcasted_iota(jnp.int32, (SUB, LANES), 0)
    channels, tiles, deep, _ = grid.shape
    own = cols - (tiles - 1) * LANES
    half = EDGE // 2
    even = me_ref[1] == 0
    for ch in range(channels):
        for j in range(tiles):
            at = slice(ch * HALO, (ch + 1) * HALO)
            for row in range(0, half, SUB):
                field[0, ch, j, half + row : half + row + SUB, :] = grid[
                    ch, j, PAD + row : PAD + row + SUB, :
                ]
                low = deep - PAD - half + row
                field[1, ch, j, row : row + SUB, :] = grid[ch, j, low : low + SUB, :]
            pair, other = pair_rows[j, at, :], other_rows[j, at, :]
            field[0, ch, j, half - HALO : half, :] = jnp.where(even, other, pair)
            field[1, ch, j, half : half + HALO, :] = jnp.where(even, pair, other)
    for k in range(2):
        for j in range(tiles):
            local[0, k, j, EDGE - SUB : EDGE, :] = powers[
                k, j, PAD + SUB : PAD + 2 * SUB, :
            ]
            local[1, k, j, 0:SUB, :] = powers[
                k, j, deep - PAD - 2 * SUB : deep - PAD - SUB, :
            ]
    centre = jnp.broadcast_to(part[0:1, 0:1], (SUB, LANES))

    def rows_of(side):
        def rows(ref, lead, start):
            return [ref[side, lead, j, pl.ds(start, SUB), :] for j in range(tiles)]

        return rows

    height = tracer_out.shape[2]
    copies = []
    for side in range(2):
        rows = rows_of(side)
        mine = half - side * SUB
        for start in range(SUB, 3 * SUB, SUB):
            fresh, forcing = diffuse(functools.partial(rows, field), start)
            for j in range(tiles):
                local[side, 0, j, start : start + SUB, :] = forcing[j]
            if start == mine:
                put_tracer(fresh_rows.at[side], fresh, cols, slice(0, SUB))
        copies.append(
            pltpu.make_async_copy(
                fresh_rows.at[side],
                tracer_out.at[:, :, pl.ds(side * (height - SUB), SUB), :],
                sems.at[side],
            )
        )
        copies[-1].start()

    def power(side, start, source):
        rows = rows_of(side)
        here, above, below = three(functools.partial(rows, local, source), start)
        return here, apply(here, above, below, rows(field, 0, start))

    for target in range(1, 3):
        for side in range(2):
            for start in range(SUB, 3 * SUB, SUB):
                result = power(side, start, target - 1)[1]
                for j in range(tiles):
                    local[side, target, j, start : start + SUB, :] = result[j]
    totals = (jnp.zeros((SUB, LANES), F32),) * len(PAIRS)
    for side in range(2):
        mine = half - side * SUB
        here, result = power(side, mine, 2)
        lower_powers = [rows_of(side)(local, k, mine) for k in range(2)]
        for k, values in enumerate((*lower_powers, here)):
            for j in range(tiles):
                border[side, k, j] = values[j]
        bound = side * (SUB - HALO)
        rim = (line >= bound) & (line < bound + HALO)

        def keep(value, j, rim=rim):
            inside = rim if j < tiles - 1 else rim & (lane < own)
            return jnp.where(inside, value, 0.0)

        totals = gather_products(
            totals, (*lower_powers, here, result), centre, keep
        )
    sums[...] = jnp.broadcast_to(part[0:1, :] + total_row(totals), sums.shape)
    for copy in copies:
        copy.wait()


PAIRS = ((0, 0), (0, 1), (0, 2), (0, 3), (1, 1), (1, 2), (1, 3), (2, 2), (2, 3))


def combine_kernel(cols, sums, powers, border, stream):
    values = sums[...]
    lane = lax.broadcasted_iota(jnp.int32, values.shape, 1)

    def column(k):
        return jnp.sum(jnp.where(lane == k, values, 0.0), axis=1, keepdims=True)

    centre = column(0)
    gram = {pair: column(at + 1) for at, pair in enumerate(PAIRS)}

    def local(c):
        c = list(c) + [None] * (4 - len(c))
        c0, c1, c2, c3 = c
        result = [c0 + jnp.zeros_like(centre)]
        if c1 is not None:
            inner = c1
            slope = c1 + jnp.zeros_like(centre)
            if c2 is not None:
                inner = c1 + centre * (c2 if c3 is None else c2 + centre * c3)
                slope = c1 + centre * (
                    2.0 * c2 if c3 is None else 2.0 * c2 + 3.0 * (centre * c3)
                )
            result = [c0 + centre * inner, slope]
        if c2 is not None:
            result.append(c2 + jnp.zeros_like(centre) if c3 is None else c2 + 3.0 * (centre * c3))
        if c3 is not None:
            result.append(c3 + jnp.zeros_like(centre))
        return result

    def inner(x, y):
        u, v = local(x), local(y)
        total = jnp.zeros_like(centre)
        for i in range(len(u)):
            for j in range(len(v)):
                total = total + (u[i] * v[j]) * gram[(min(i, j), max(i, j))]
        return jnp.sum(total, axis=0, keepdims=True)

    def operate(c):
        result = [SHIFT * x for x in c] + [None]
        for i, x in enumerate(c):
            term = SCALE * x
            result[i + 1] = term if result[i + 1] is None else result[i + 1] + term
        return result

    one = jnp.ones((1, 1), F32)
    stream_c = [None] * 3
    residual, direction = [one], [one]
    norm = inner(residual, residual)
    for step in range(3):
        image = operate(direction)
        alpha = norm / inner(direction, image)
        for i, x in enumerate(direction):
            stream_c[i] = alpha * x if stream_c[i] is None else stream_c[i] + alpha * x
        if step == 2:
            break
        residual = [
            (residual[i] - alpha * image[i]) if i < len(residual) else -alpha * image[i]
            for i in range(len(image))
        ]
        fresh = inner(residual, residual)
        ratio = fresh / norm
        direction = [
            (residual[i] + ratio * direction[i]) if i < len(direction) else residual[i]
            for i in range(len(residual))
        ]
        norm = fresh

    tiles = powers.shape[1]
    height = stream.shape[0]
    weights = [jnp.broadcast_to(c, (SUB, LANES)) for c in stream_c]

    def put(out, load):
        for j in range(tiles):
            width = min(LANES, cols - j * LANES)
            value = sum(weights[k] * load(k, j) for k in range(3))
            stream[out, j * LANES : j * LANES + width] = value[:, :width]

    def write(g, carry):
        at = pl.ds(pl.multiple_of(g * SUB + PAD, SUB), SUB)
        out = pl.ds(pl.multiple_of(g * SUB, SUB), SUB)
        put(out, lambda k, j: powers[k, j, at, :])
        return carry

    put(slice(0, SUB), lambda k, j: border[0, k, j])
    lax.fori_loop(1, height // SUB - 1, write, 0, unroll=3)
    put(slice(height - SUB, height), lambda k, j: border[1, k, j])


def body(checkpoint, slot_dest, kmt, kappa):
    n = lax.axis_size("lon")
    lats = lax.axis_size("lat")
    lat = lax.axis_index("lat")
    me = jnp.stack([lax.axis_index("lon"), lax.rem(lat, 2)]).astype(jnp.int32)
    _, slots, values = checkpoint.shape
    rows, cols = kmt.shape
    by_n, bx_n = rows // BH, cols // BW
    cap = slots // n
    length = package_rows(cap, by_n)
    tiles = -(-(cols + 2 * HALO) // LANES)
    groups = slots // SUB
    edge_rows = -(-by_n * (1 + LEV) // 2) * BH
    if by_n * (1 + LEV) > 4 * cap:
        edge_rows = 2 * cap * BH + BH

    def fixed(value):
        return pltpu.with_memory_space_constraint(value, pltpu.HBM)

    kernels = (n, cap, bx_n, by_n)
    *packs, dest, source, flat = pl.pallas_call(
        functools.partial(first_kernel, *kernels),
        out_shape=[shaped(length, LANES)] * (n // 2 - 1)
        + [
            shaped(1, n * slots, dtype=jnp.int32),
            shaped(n * cap, dtype=jnp.int32),
            shaped(slots * ROWS, LANES),
        ],
        in_specs=[SM, HB, HB],
        out_specs=[VM] * (n // 2 - 1) + [SM, SM, VM],
        scratch_shapes=[
            pltpu.VMEM((groups, SUB, values), F32),
            pltpu.VMEM((n, BH, LANES), F32),
            pltpu.SMEM((n,), jnp.int32),
            pltpu.SemaphoreType.DMA((groups + 1,)),
        ],
        compiler_params=params(),
        cost_estimate=cost(2 << 20, 4 << 20),
        name="first",
    )(me, fixed(slot_dest), fixed(checkpoint))

    def send(value, k):
        return lax.ppermute(value, "lon", [(i, i ^ k) for i in range(n)])

    order = sorted(range(1, n), key=lambda k: (k & 1, k < 2, -bin(k >> 1).count("1"), k))
    received = {k: send(packs[k // 2 - 1], k) for k in order if k % 2 == 0}
    own, *packs = pl.pallas_call(
        functools.partial(second_kernel, *kernels),
        out_shape=[shaped(length, LANES)] * (n // 2 + 1),
        in_specs=[SM, SM, SM, VM, HB, HB],
        out_specs=[VM] * (n // 2 + 1),
        scratch_shapes=[
            pltpu.VMEM((rows, cols), jnp.int32),
            pltpu.VMEM((LEV, rows, cols), F32),
            pltpu.VMEM((n, BH, LANES), F32),
            pltpu.VMEM((2, edge_rows, LANES), F32),
            pltpu.SemaphoreType.DMA((2,)),
        ],
        compiler_params=params(),
        cost_estimate=cost(2 << 20, 4 << 20),
        name="second",
    )(me, dest, source, flat, fixed(kmt), fixed(kappa))
    received |= {k: send(packs[k // 2], k) for k in order if k % 2}
    received[0] = own

    channels = 1 + 3 * LEV
    deep = rows + 2 * PAD
    table, grid = pl.pallas_call(
        functools.partial(base_kernel, n, cap, bx_n, by_n),
        out_shape=[
            shaped(n * (cap + 1) + 2 * by_n, dtype=jnp.int32),
            shaped(channels, tiles, deep, LANES),
        ],
        in_specs=[SM, SM, VM, VM],
        out_specs=[SM, VM],
        scratch_shapes=[pltpu.SMEM((n * slots + 1,), jnp.int32)],
        compiler_params=params(),
        cost_estimate=cost(1 << 20, 2 << 20),
        name="base",
    )(me, dest, kmt, kappa)

    def held(value):
        return pltpu.with_memory_space_constraint(value, pltpu.VMEM)

    rim = -(-channels * HALO // SUB) * SUB
    half, quarter = n // 2 - 1, n // 4
    odd = order[half:]
    parts = [
        [0] + order[:half],
        odd[-1:] + odd[: quarter - 1],
        odd[quarter - 1 : -1],
    ]
    for stage, which in enumerate(parts):
        shapes = [shaped(channels, tiles, deep, LANES)]
        if stage == len(parts) - 1:
            shapes += [shaped(tiles, rim, LANES)] * 2
        grid, *rims = pl.pallas_call(
            functools.partial(place_kernel, n, cap, bx_n, by_n, cols, which),
            out_shape=shapes,
            in_specs=[SM, SM] + [VM] * (1 + len(which)),
            out_specs=[VM] * len(shapes),
            input_output_aliases={2: 0},
            compiler_params=params(),
            cost_estimate=cost(2 << 20, 2 << 20),
            name=f"place{stage}",
        )(me, table, held(grid), *[received[k] for k in which])

    swaps = [
        [(i, i ^ 1) for i in range(lats) if i ^ 1 < lats],
        [(i, j) for i in range(lats) for j in [(i - 1 ^ 1) + 1] if 0 <= j < lats],
    ]
    pair_rows, other_rows = (
        lax.ppermute(value, "lat", swap) for value, swap in zip(rims, swaps)
    )

    devices = n * lats
    tracer_shape = shaped(2, LEV, rows, cols)
    tracer, powers, part = pl.pallas_call(
        functools.partial(inner_kernel, cols),
        out_shape=[
            tracer_shape,
            shaped(3, tiles, deep, LANES),
            shaped(SUB, LANES),
        ],
        in_specs=[VM],
        out_specs=[VM, VM, VM],
        compiler_params=params(),
        cost_estimate=cost(16 << 20, 6 << 20),
        name="inner",
    )(grid)
    tracer, border, sums = pl.pallas_call(
        functools.partial(border_kernel, cols),
        out_shape=[
            tracer_shape,
            shaped(2, 3, tiles, SUB, LANES),
            shaped(devices, LANES),
        ],
        in_specs=[SM, VM, VM, VM, VM, VM, HB],
        out_specs=[HB, VM, VM],
        scratch_shapes=[
            pltpu.VMEM((2, channels, tiles, EDGE, LANES), F32),
            pltpu.VMEM((2, 3, tiles, EDGE, LANES), F32),
            pltpu.VMEM((2, 2, LEV, SUB, cols), F32),
            pltpu.SemaphoreType.DMA((2,)),
        ],
        input_output_aliases={6: 0},
        compiler_params=params(),
        cost_estimate=cost(2 << 20, 1 << 20),
        name="border",
    )(me, grid, pair_rows, other_rows, powers, part, tracer)

    everyone = lax.all_to_all(sums, ("lon", "lat"), 0, 0, tiled=True)
    stream = pl.pallas_call(
        functools.partial(combine_kernel, cols),
        out_shape=shaped(rows, cols),
        in_specs=[VM, VM, VM],
        out_specs=VM,
        compiler_params=params(),
        cost_estimate=cost(1 << 20, 2 << 20),
        name="combine",
    )(everyone, powers, border)
    return tracer, stream


def solution(mesh):
    placed = (P("lat", "lon", None), P("lat", None), P("lat", "lon"), P(None, "lat", "lon"))
    return jax.shard_map(
        body,
        mesh=mesh,
        in_specs=placed,
        out_specs=(P(None, None, "lat", "lon"), P("lat", "lon")),
        check_vma=False,
    )
```

```python
import functools

import jax
import jax.numpy as jnp
from jax import lax
from jax.experimental import pallas as pl
from jax.experimental.pallas import tpu as pltpu
from jax.sharding import PartitionSpec as P


BH = 40
BW = 60
LEV = 2
HALO = 4
LANES = 128
SUB = 8
PAD = SUB
EDGE = 4 * SUB
ROWS = LEV * BH
HALF = LANES // 2
SHIFT = 8.0
SCALE = 8.0

thermal = 0.25
haline = 0.75
cabbeling = 0.05

VM = pl.BlockSpec(memory_space=pltpu.VMEM)
SM = pl.BlockSpec(memory_space=pltpu.SMEM)
HB = pl.BlockSpec(memory_space=pltpu.HBM)
F32 = jnp.float32


def params():
    return pltpu.CompilerParams(vmem_limit_bytes=24 << 20)


def cost(flops, moved):
    return pl.CostEstimate(flops=flops, bytes_accessed=moved, transcendentals=0)


def shaped(*dims, dtype=F32):
    return jax.ShapeDtypeStruct(dims, dtype)


def lanes():
    return lax.broadcasted_iota(jnp.int32, (SUB, LANES), 1)


def turn(value, amount):
    if isinstance(amount, int):
        amount %= LANES
        if amount == 0:
            return value
    return pltpu.roll(value, amount, 1)


def strip_lane(side, by, level, tracer, block_rows):
    return HALO * ((side * block_rows + by) * LEV + level) + HALF * tracer


def edge_spot(cap, piece):
    if piece < 4 * cap:
        return piece // 2 * BH, HALF * (1 + piece % 2) - HALO
    return cap * ROWS + BH, HALO * (piece - 4 * cap)


def package_rows(cap, by_n):
    return cap * ROWS + (2 * BH if by_n * (1 + LEV) > 4 * cap else BH)


def block_rows(flat, start, row):
    return flat[pl.ds(start + row * SUB, SUB, stride=SUB), :]


def block_start(i):
    return lax.div(i, SUB) * (ROWS * SUB) + lax.rem(i, SUB)


def plan(n, cap, bx_n, me, dest, source, count, todo, wanted):
    slots = todo.shape[0] - 1
    for k in range(n + 1):
        count[k] = 0
    for at in range(n * cap + 1):
        source[at] = 0

    def assign(i, found):
        d = dest[0, me * slots + i]
        used = d >= 0
        place = jnp.maximum(d, 0)
        owner = lax.div(place, slots)
        k = jnp.where(used, lax.bitwise_xor(owner, me), n)
        c = count[k]
        count[k] = c + 1
        source[jnp.where(used, k * cap + c, n * cap)] = block_start(i)
        bx = lax.rem(place, bx_n)
        partner = lax.bitwise_xor(
            lax.rem(owner + jnp.where(bx == 0, n - 1, 1), n), me
        )
        todo[found] = i
        holds = used & ((bx == 0) | (bx == bx_n - 1)) & wanted(partner)
        return found + holds.astype(jnp.int32)

    return lax.fori_loop(0, slots, assign, 0, unroll=4)


def fill_strips(n, bx_n, by_n, me, dest, flat, strips, todo, found):
    slots = bx_n * by_n
    spot_lane = lanes() & (HALF - 1)

    def strip(at, carry):
        i = todo[at]
        place = dest[0, me * slots + i]
        spot = lax.rem(place, slots)
        by = lax.div(spot, bx_n)
        side = (lax.rem(spot, bx_n) == 0).astype(jnp.int32)
        owner = lax.div(place, slots)
        k = lax.bitwise_xor(lax.rem(owner + jnp.where(side == 0, 1, n - 1), n), me)
        start = block_start(i)
        origin = jnp.where(side == 0, BW - HALO, 0)
        for level in range(LEV):
            target = strip_lane(side, by, level, 0, by_n)
            amount = lax.rem(target - origin + LANES, LANES)
            here = (spot_lane >= target) & (spot_lane < target + HALO)
            for row in range(0, BH, SUB):
                value = block_rows(flat, start, level * BH + row)
                pltpu.store(
                    strips.at[k, row : row + SUB, :],
                    pltpu.roll(value, amount, 1),
                    mask=here,
                )
        return carry

    lax.fori_loop(0, found, strip, 0)


def assemble(out, k, cap, source, flat, strips, edges=None, which=None, in_blocks=0):
    spare = (lanes() & (HALF - 1)) >= HALF - HALO
    for c in range(cap):
        start = source[k * cap + c]
        for row in range(0, ROWS, SUB):
            value = block_rows(flat, start, row)
            at = c * ROWS + row
            if at < in_blocks:
                value = jnp.where(spare, edges[which, at : at + SUB, :], value)
            out[at : at + SUB, :] = value
    for row in range(0, BH, SUB):
        at = cap * ROWS + row
        out[at : at + SUB, :] = strips[k, row : row + SUB, :]


def first_kernel(n, cap, bx_n, by_n, *refs):
    me_ref, dest_hbm, blocks_hbm = refs[:3]
    outs = refs[3 : n // 2 + 2]
    flat, dest, source, todo, blocks, strips, count, sems = refs[n // 2 + 2 :]
    groups = blocks.shape[0]
    slots = groups * SUB
    me = me_ref[0]
    lane = lanes()
    first = pltpu.make_async_copy(dest_hbm, dest, sems.at[groups])
    first.start()

    def loading(g):
        rows = pl.ds(pl.multiple_of(g * SUB, SUB), SUB)
        return pltpu.make_async_copy(
            blocks_hbm.at[0, rows, :], blocks.at[g], sems.at[g]
        )

    for g in range(groups):
        loading(g).start()
    first.wait()
    found = plan(
        n, cap, bx_n, me, dest, source, count, todo, lambda k: (k > 0) & (k & 1 == 0)
    )

    def regroup(group, carry):
        loading(group).wait()

        def load(q):
            return blocks[group, :, q * LANES : (q + 1) * LANES]

        limit = blocks.shape[2] // LANES - 1
        for row in range(ROWS):
            q, o = divmod(row * BW, LANES)
            p = (ROWS + row) * BW // LANES
            if o == 0:
                value = jnp.where(lane >= HALF, load(p), load(q))
            elif o <= HALF:
                low = load(p if o == HALF else min(p + 1, limit))
                value = jnp.where(lane >= o, load(q), low)
                if o < HALF:
                    value = jnp.where(lane >= o + HALF, load(p), value)
            else:
                value = jnp.where(lane >= o - HALF, load(p), load(q + 1))
                value = jnp.where(lane >= o, load(q), value)
            at = pl.multiple_of(group * (ROWS * SUB) + row * SUB, SUB)
            flat[pl.ds(at, SUB), :] = turn(value, -o)
        return carry

    lax.fori_loop(0, groups, regroup, 0)
    fill_strips(n, bx_n, by_n, me, dest, flat, strips, todo, found)
    for k in range(2, n, 2):
        assemble(outs[k // 2 - 1], k, cap, source, flat, strips)


def second_kernel(n, cap, bx_n, by_n, *refs):
    me_ref, dest_hbm, flat, kmt_hbm, kappa_hbm = refs[:5]
    outs = refs[5 : n // 2 + 6]
    dest, source, todo, kmt, kappa, strips, edges, count, sems = refs[n // 2 + 6 :]
    me = me_ref[0]
    lane = lanes()
    length = outs[0].shape[0]
    cols = kmt.shape[1]
    first, *copies = [
        pltpu.make_async_copy(dest_hbm, dest, sems.at[0]),
        pltpu.make_async_copy(kmt_hbm, kmt, sems.at[1]),
        pltpu.make_async_copy(kappa_hbm, kappa, sems.at[2]),
    ]
    for copy in (first, *copies):
        copy.start()
    first.wait()
    found = plan(
        n, cap, bx_n, me, dest, source, count, todo, lambda k: (k == 0) | (k & 1 == 1)
    )
    fill_strips(n, bx_n, by_n, me, dest, flat, strips, todo, found)
    for copy in copies:
        copy.wait()
    zero = jnp.zeros((SUB, LANES), F32)
    for at in range(0, edges.shape[1], SUB):
        for side in range(2):
            edges[side, at : at + SUB, :] = zero
    for side, start in ((0, cols - HALO), (1, 0)):
        tile = start // LANES * LANES
        width = min(LANES, cols - tile)
        for piece in range(by_n * (1 + LEV)):
            by, ch = divmod(piece, 1 + LEV)
            base, target = edge_spot(cap, piece)
            if piece >= 4 * cap:
                base -= cap * ROWS + BH - 2 * cap * BH
            here = (lane >= target) & (lane < target + HALO)
            for row in range(0, BH, SUB):
                at = slice(by * BH + row, by * BH + row + SUB)
                if ch == 0:
                    value = kmt[at, tile : tile + width].astype(F32)
                else:
                    value = kappa[ch - 1, at, tile : tile + width]
                if width < LANES:
                    value = jnp.concatenate([value, zero[:, width:]], axis=1)
                pltpu.store(
                    edges.at[side, base + row : base + row + SUB, :],
                    turn(value, target - (start - tile)),
                    mask=here,
                )
    eastern = lax.bitwise_xor(lax.rem(me + 1, n), me)
    in_blocks = min(edges.shape[1], 2 * cap * BH)
    for out, k in zip(outs, [0, *range(1, n, 2)]):
        which = jnp.where(eastern == k, 0, 1)
        assemble(out, k, cap, source, flat, strips, edges, which, in_blocks)
        if length > cap * ROWS + BH:
            for row in range(0, BH, SUB):
                at = cap * ROWS + BH + row
                out[at : at + SUB, :] = edges[
                    which, in_blocks + row : in_blocks + row + SUB, :
                ]


def base_kernel(n, cap, bx_n, by_n, me_ref, dest, kmt, kappa, table, grid, bringer):
    me = me_ref[0]
    slots = bx_n * by_n
    channels, tiles, deep, _ = grid.shape
    cols = kmt.shape[1]
    zero = jnp.zeros((SUB, LANES), F32)
    west = lax.rem(me + n - 1, n)
    east = lax.rem(me + 1, n)
    for at in range(n * (cap + 1)):
        table[at] = -1
    sides = [(west, by * bx_n + bx_n - 1) for by in range(by_n)]
    sides += [(east, by * bx_n) for by in range(by_n)]
    for owner, spot in sides:
        bringer[owner * slots + spot + 1] = -1

    def owner_loop(s, carry):
        k = lax.bitwise_xor(s, me)

        def slot_loop(i, c):
            d = dest[0, s * slots + i]
            bringer[d + 1] = k
            spot = d - me * slots
            mine = (spot >= 0) & (spot < slots)
            table[k * (cap + 1) + c] = jnp.where(mine, spot, -1)
            return c + mine.astype(jnp.int32)

        lax.fori_loop(0, slots, slot_loop, 0, unroll=8)
        return carry

    lax.fori_loop(0, n, owner_loop, 0)
    counts = n * (cap + 1)
    lists = counts + n + 1
    for k in range(n + 1):
        table[counts + k] = 0
    for at, (owner, spot) in enumerate(sides):
        k = bringer[owner * slots + spot + 1]
        k = jnp.where(k < 0, n, k)
        c = table[counts + k]
        table[counts + k] = c + 1
        table[lists + k * len(sides) + c] = at

    def clear(g, carry):
        at = pl.ds(pl.multiple_of(g * SUB, SUB), SUB)
        for ch in range(channels):
            for j in range(tiles):
                grid[ch, j, at, :] = zero
        return carry

    lax.fori_loop(0, deep // SUB, clear, 0)

    def lay(g, carry):
        at = pl.ds(pl.multiple_of(g * SUB, SUB), SUB)
        out = pl.ds(pl.multiple_of(g * SUB + PAD, SUB), SUB)
        for ch in range(1 + LEV):
            for j in range(tiles):
                width = min(LANES, cols - j * LANES)
                part = slice(j * LANES, j * LANES + width)
                if ch == 0:
                    value = kmt[at, part].astype(F32)
                else:
                    value = kappa[ch - 1, at, part]
                grid[ch, j, out, 0:width] = value
        return carry

    lax.fori_loop(0, kmt.shape[0] // SUB, lay, 0)


def place_kernel(n, cap, bx_n, by_n, cols, which, *refs):
    count = len(which)
    me_ref, table, _ = refs[:3]
    odd = me_ref[1]
    packs = refs[3 : 3 + count]
    grid, *rims = refs[3 + count :]
    me = me_ref[0]
    lane = lanes()
    channels, tiles, deep, _ = grid.shape
    last = tiles - 1
    own = cols - last * LANES
    halo_lane = (own, LANES - HALO)

    def mark(ch, at, value, start):
        here = (lane >= start) & (lane < start + HALO)
        pltpu.store(grid.at[ch, last, at, :], value, mask=here)

    for k, pack in zip(which, packs):

        for c in range(cap):
            spot = table[k * (cap + 1) + c]
            valid = spot >= 0
            spot = jnp.maximum(spot, 0)
            by = lax.div(spot, bx_n)
            offset = lax.rem(spot, bx_n) * BW
            tile = lax.div(offset, LANES)
            following = jnp.minimum(tile + 1, last)
            start = lax.rem(offset, LANES)
            begin = jnp.where(valid, start, LANES)
            here = (lane >= begin) & (lane < begin + BW)
            spill = lane < jnp.where(valid, start + BW - LANES, 0)
            for row in range(0, BH, SUB):
                at = pl.ds(pl.multiple_of(by * BH + row + PAD, SUB), SUB)
                depth = grid[0, tile, at, :], grid[0, following, at, :]
                for level in range(LEV):
                    place = c * ROWS + level * BH + row
                    value = pack[place : place + SUB, :]
                    masks = here & (depth[0] > level), spill & (depth[1] > level)
                    for tracer in range(2):
                        ch = 1 + LEV + tracer * LEV + level
                        turned = pltpu.roll(
                            value, lax.rem(start + tracer * HALF, LANES), 1
                        )
                        for target, mask in zip((tile, following), masks):
                            pltpu.store(grid.at[ch, target, at, :], turned, mask=mask)

        counts = n * (cap + 1)
        lists = counts + n + 1 + k * 2 * by_n

        def strip(at, carry, pack=pack, lists=lists):
            index = table[lists + at]
            by = lax.rem(index, by_n)
            start = jnp.where(index < by_n, halo_lane[1], halo_lane[0])
            for row in range(0, BH, SUB):
                rows = pl.ds(pl.multiple_of(by * BH + row + PAD, SUB), SUB)
                value = pack[cap * ROWS + row : cap * ROWS + row + SUB, :]
                for level in range(LEV):
                    for tracer in range(2):
                        origin = strip_lane(0, index, level, tracer, by_n)
                        amount = lax.rem(start - origin + LANES, LANES)
                        mark(
                            1 + LEV + tracer * LEV + level,
                            rows,
                            pltpu.roll(value, amount, 1),
                            start,
                        )
            return carry

        lax.fori_loop(0, table[counts + k], strip, 0)

        for neighbour, start in ((me + n - 1, halo_lane[1]), (me + 1, halo_lane[0])):
            if k % 2 == 0:
                continue

            @pl.when(lax.bitwise_xor(lax.rem(neighbour, n), me) == k)
            def _(start=start, pack=pack):
                for piece in range(by_n * (1 + LEV)):
                    by, ch = divmod(piece, 1 + LEV)
                    base, origin = edge_spot(cap, piece)
                    for row in range(0, BH, SUB):
                        at = by * BH + row + PAD
                        mark(
                            ch,
                            slice(at, at + SUB),
                            turn(pack[base + row : base + row + SUB, :], start - origin),
                            start,
                        )

    if not rims:
        return
    rim = (lane >= own) & (lane < own + HALO) | (lane >= LANES - HALO)

    def mask(g, carry):
        at = pl.ds(pl.multiple_of(g * SUB + PAD, SUB), SUB)
        wet = grid[0, last, at, :]
        for ch in range(1 + LEV, channels):
            level = (ch - 1 - LEV) % LEV
            grid[ch, last, at, :] = jnp.where(
                rim & (wet <= level), 0.0, grid[ch, last, at, :]
            )
        return carry

    lax.fori_loop(0, deep // SUB - 2, mask, 0, unroll=4)
    low = deep - PAD - HALO
    for rows, first in zip(rims, (1 - odd, odd)):
        at = jnp.where(first == 1, PAD, low)
        for ch in range(channels):
            for j in range(tiles):
                rows[j, ch * HALO : (ch + 1) * HALO, :] = grid[
                    ch, j, pl.ds(at, HALO), :
                ]


def sideways(values):
    lane = lanes()
    count = len(values)
    left = [turn(v, 1) for v in values]
    right = [turn(v, -1) for v in values]
    west = [
        jnp.where(lane == 0, left[(j - 1) % count], left[j]) for j in range(count)
    ]
    east = [
        jnp.where(lane == LANES - 1, right[(j + 1) % count], right[j])
        for j in range(count)
    ]
    return east, west


def three(load, start):
    return load(start), load(start - 1), load(start + 1)


def diffuse(load, start):
    tiles = len(load(0, start))
    span = range(tiles)
    level_c, level_a, level_b = three(functools.partial(load, 0), start)
    level_e, _ = sideways(level_c)
    both_e = [jnp.minimum(level_c[j], level_e[j]) for j in span]
    both_a = [jnp.minimum(level_c[j], level_a[j]) for j in span]
    both_b = [jnp.minimum(level_c[j], level_b[j]) for j in span]
    forcing = [None] * tiles
    fresh = [[None] * LEV for _ in range(2)]
    for level in range(LEV):
        kappa_c, kappa_a, kappa_b = three(functools.partial(load, 1 + level), start)
        kappa_e, _ = sideways(kappa_c)
        face_e, face_a, face_b = (
            [jnp.where(both[j] > level, kappa_c[j] + other[j], 0.0) for j in span]
            for both, other in (
                (both_e, kappa_e),
                (both_a, kappa_a),
                (both_b, kappa_b),
            )
        )
        for tracer in range(2):
            ch = 1 + LEV + tracer * LEV + level
            here, above, below = three(functools.partial(load, ch), start)
            to_east, _ = sideways(here)
            flux = [face_e[j] * (to_east[j] - here[j]) for j in span]
            _, flux_w = sideways(flux)
            fresh[tracer][level] = [
                jnp.where(
                    level_c[j] > level,
                    here[j]
                    + 0.5
                    * (
                        (flux[j] - flux_w[j])
                        + face_a[j] * (above[j] - here[j])
                        + face_b[j] * (below[j] - here[j])
                    ),
                    0.0,
                )
                for j in span
            ]
        thickness = 1.0 + 0.5 * level
        for j in span:
            temp, salt = fresh[0][level][j], fresh[1][level][j]
            density = haline * salt - temp * (thermal + cabbeling * temp)
            if level:
                density = forcing[j] + thickness * density
            forcing[j] = density
    return fresh, forcing


def apply(here, above, below, levels):
    span = range(len(here))
    pair = [above[j] + below[j] for j in span]
    mixed = [here[j] + 0.5 * pair[j] for j in span]
    east, west = sideways(mixed)
    result = []
    for j in span:
        diagonal = 6.0 - SHIFT + 1.0
        total = jnp.full((SUB, LANES), diagonal / SCALE, F32)
        for k in range(1, LEV):
            diagonal += 1.0 + 0.5 * k
            total = jnp.where(levels[j] > k, diagonal / SCALE, total)
        total = total * here[j] - (pair[j] + (east[j] + west[j])) * (1.0 / SCALE)
        result.append(jnp.where(levels[j] > 0, total, 0.0))
    return result


def gather_products(carry, powers, centre, keep):
    carry = list(carry)
    span = range(len(powers[0]))
    for j in span:
        q0, q1, q2, q3 = (keep(q[j], j) for q in powers)
        b1 = q1 - centre * q0
        c2 = q2 - centre * q1
        c3 = q3 - centre * q2
        b2 = c2 - centre * b1
        b3 = (c3 - centre * c2) - centre * b2
        terms = (q0, b1, b2, b3)
        for at, (x, y) in enumerate(PAIRS):
            carry[at] = carry[at] + terms[x] * terms[y]
    return tuple(carry)


def total_row(totals):
    lane = lanes()[:1]
    row = jnp.zeros((1, LANES), F32)
    for at, total in enumerate(totals):
        total = jnp.sum(total, axis=(0, 1), keepdims=True)
        row = jnp.where(lane == at + 1, total, row)
    return row


def put_tracer(target, fresh, cols, at):
    for tracer in range(2):
        for level in range(LEV):
            for j, value in enumerate(fresh[tracer][level]):
                width = min(LANES, cols - j * LANES)
                target[tracer, level, at, j * LANES : j * LANES + width] = value[
                    :, :width
                ]


def inner_kernel(cols, grid, tracer_out, powers, sums):
    lane = lanes()
    line = lax.broadcasted_iota(jnp.int32, (SUB, LANES), 0)
    _, tiles, deep, _ = grid.shape
    own = cols - (tiles - 1) * LANES
    first, end = PAD // SUB, (deep - PAD) // SUB
    zero = jnp.zeros((SUB, LANES), F32)

    def rows(ref, lead, start):
        return [ref[lead, j, pl.ds(start, SUB), :] for j in range(tiles)]

    def top(g):
        return pl.multiple_of(g * SUB, SUB)

    def step(g, carry):
        fresh, forcing = diffuse(functools.partial(rows, grid), top(g))
        put_tracer(
            tracer_out, fresh, cols, pl.ds(pl.multiple_of(g * SUB - PAD, SUB), SUB)
        )
        for j in range(tiles):
            powers[0, j, pl.ds(top(g), SUB), :] = forcing[j]
        return carry

    lax.fori_loop(first, end, step, 0, unroll=2)

    def inside(value, j):
        return value if j < tiles - 1 else jnp.where(lane < own, value, 0.0)

    def upper(value, j):
        return jnp.where(line >= HALO, inside(value, j), 0.0)

    def lower(value, j):
        return jnp.where(line < SUB - HALO, inside(value, j), 0.0)

    def power(g, source):
        here, above, below = three(functools.partial(rows, powers, source), top(g))
        return here, apply(here, above, below, rows(grid, 0, top(g)))

    def put(g, target):
        here, result = power(g, target - 1)
        for j in range(tiles):
            powers[target, j, pl.ds(top(g), SUB), :] = result[j]
        return here, result

    def first_power(g, carry, keep=inside):
        here, result = put(g, 1)
        a, b = carry
        for j in range(tiles):
            v = keep(here[j], j)
            a = a + v * v
            b = b + v * keep(result[j], j)
        return a, b

    def everywhere(body, carry):
        carry = body(first, carry, upper)
        carry = lax.fori_loop(first + 1, end - 1, body, carry, unroll=end - first - 2)
        return body(end - 1, carry, lower)

    a, b = everywhere(first_power, (zero, zero))
    a = jnp.sum(a, axis=(0, 1), keepdims=True)
    b = jnp.sum(b, axis=(0, 1), keepdims=True)
    centre = jnp.where(a > 0, b / jnp.where(a > 0, a, 1.0), 0.0)
    centre = jnp.broadcast_to(centre, (SUB, LANES))
    lax.fori_loop(
        first, end, lambda g, c: (put(g, 2), c)[1], 0, unroll=end - first
    )

    def products(g, carry, keep=inside):
        here, result = power(g, 2)
        lower_powers = [rows(powers, k, top(g)) for k in range(2)]
        return gather_products(carry, (*lower_powers, here, result), centre, keep)

    totals = everywhere(products, (zero,) * len(PAIRS))
    row = jnp.where(lane[:1] == 0, centre[:1], total_row(totals))
    sums[...] = jnp.broadcast_to(row, sums.shape)


def border_kernel(
    cols, me_ref, grid, other_rows, pair_rows, powers, part, tracer_in, tracer_out,
    border, sums,
    field, local, fresh_rows, sems,
):
    lane = lanes()
    line = lax.broadcasted_iota(jnp.int32, (SUB, LANES), 0)
    channels, tiles, deep, _ = grid.shape
    own = cols - (tiles - 1) * LANES
    half = EDGE // 2
    even = me_ref[1] == 0
    for ch in range(channels):
        for j in range(tiles):
            at = slice(ch * HALO, (ch + 1) * HALO)
            for row in range(0, half, SUB):
                field[0, ch, j, half + row : half + row + SUB, :] = grid[
                    ch, j, PAD + row : PAD + row + SUB, :
                ]
                low = deep - PAD - half + row
                field[1, ch, j, row : row + SUB, :] = grid[ch, j, low : low + SUB, :]
            pair, other = pair_rows[j, at, :], other_rows[j, at, :]
            field[0, ch, j, half - HALO : half, :] = jnp.where(even, other, pair)
            field[1, ch, j, half : half + HALO, :] = jnp.where(even, pair, other)
    for k in range(2):
        for j in range(tiles):
            local[0, k, j, EDGE - SUB : EDGE, :] = powers[
                k, j, PAD + SUB : PAD + 2 * SUB, :
            ]
            local[1, k, j, 0:SUB, :] = powers[
                k, j, deep - PAD - 2 * SUB : deep - PAD - SUB, :
            ]
    centre = jnp.broadcast_to(part[0:1, 0:1], (SUB, LANES))

    def rows_of(side):
        def rows(ref, lead, start):
            return [ref[side, lead, j, pl.ds(start, SUB), :] for j in range(tiles)]

        return rows

    height = tracer_out.shape[2]
    copies = []
    for side in range(2):
        rows = rows_of(side)
        mine = half - side * SUB
        for start in range(SUB, 3 * SUB, SUB):
            fresh, forcing = diffuse(functools.partial(rows, field), start)
            for j in range(tiles):
                local[side, 0, j, start : start + SUB, :] = forcing[j]
            if start == mine:
                put_tracer(fresh_rows.at[side], fresh, cols, slice(0, SUB))
        copies.append(
            pltpu.make_async_copy(
                fresh_rows.at[side],
                tracer_out.at[:, :, pl.ds(side * (height - SUB), SUB), :],
                sems.at[side],
            )
        )
        copies[-1].start()

    def power(side, start, source):
        rows = rows_of(side)
        here, above, below = three(functools.partial(rows, local, source), start)
        return here, apply(here, above, below, rows(field, 0, start))

    for target in range(1, 3):
        for side in range(2):
            for start in range(SUB, 3 * SUB, SUB):
                result = power(side, start, target - 1)[1]
                for j in range(tiles):
                    local[side, target, j, start : start + SUB, :] = result[j]
    totals = (jnp.zeros((SUB, LANES), F32),) * len(PAIRS)
    for side in range(2):
        mine = half - side * SUB
        here, result = power(side, mine, 2)
        lower_powers = [rows_of(side)(local, k, mine) for k in range(2)]
        for k, values in enumerate((*lower_powers, here)):
            for j in range(tiles):
                border[side, k, j] = values[j]
        bound = side * (SUB - HALO)
        rim = (line >= bound) & (line < bound + HALO)

        def keep(value, j, rim=rim):
            inside = rim if j < tiles - 1 else rim & (lane < own)
            return jnp.where(inside, value, 0.0)

        totals = gather_products(
            totals, (*lower_powers, here, result), centre, keep
        )
    sums[...] = jnp.broadcast_to(part[0:1, :] + total_row(totals), sums.shape)
    for copy in copies:
        copy.wait()


PAIRS = ((0, 0), (0, 1), (0, 2), (0, 3), (1, 1), (1, 2), (1, 3), (2, 2), (2, 3))


def combine_kernel(cols, sums, powers, border, stream):
    values = sums[...]
    lane = lax.broadcasted_iota(jnp.int32, values.shape, 1)

    def column(k):
        return jnp.sum(jnp.where(lane == k, values, 0.0), axis=1, keepdims=True)

    centre = column(0)
    gram = {pair: column(at + 1) for at, pair in enumerate(PAIRS)}

    def local(c):
        c = list(c) + [None] * (4 - len(c))
        c0, c1, c2, c3 = c
        result = [c0 + jnp.zeros_like(centre)]
        if c1 is not None:
            inner = c1
            slope = c1 + jnp.zeros_like(centre)
            if c2 is not None:
                inner = c1 + centre * (c2 if c3 is None else c2 + centre * c3)
                slope = c1 + centre * (
                    2.0 * c2 if c3 is None else 2.0 * c2 + 3.0 * (centre * c3)
                )
            result = [c0 + centre * inner, slope]
        if c2 is not None:
            result.append(c2 + jnp.zeros_like(centre) if c3 is None else c2 + 3.0 * (centre * c3))
        if c3 is not None:
            result.append(c3 + jnp.zeros_like(centre))
        return result

    def inner(x, y):
        u, v = local(x), local(y)
        total = jnp.zeros_like(centre)
        for i in range(len(u)):
            for j in range(len(v)):
                total = total + (u[i] * v[j]) * gram[(min(i, j), max(i, j))]
        return jnp.sum(total, axis=0, keepdims=True)

    def operate(c):
        result = [SHIFT * x for x in c] + [None]
        for i, x in enumerate(c):
            term = SCALE * x
            result[i + 1] = term if result[i + 1] is None else result[i + 1] + term
        return result

    one = jnp.ones((1, 1), F32)
    stream_c = [None] * 3
    residual, direction = [one], [one]
    norm = inner(residual, residual)
    for step in range(3):
        image = operate(direction)
        alpha = norm / inner(direction, image)
        for i, x in enumerate(direction):
            stream_c[i] = alpha * x if stream_c[i] is None else stream_c[i] + alpha * x
        if step == 2:
            break
        residual = [
            (residual[i] - alpha * image[i]) if i < len(residual) else -alpha * image[i]
            for i in range(len(image))
        ]
        fresh = inner(residual, residual)
        ratio = fresh / norm
        direction = [
            (residual[i] + ratio * direction[i]) if i < len(direction) else residual[i]
            for i in range(len(residual))
        ]
        norm = fresh

    tiles = powers.shape[1]
    height = stream.shape[0]
    weights = [jnp.broadcast_to(c, (SUB, LANES)) for c in stream_c]

    def put(out, load):
        for j in range(tiles):
            width = min(LANES, cols - j * LANES)
            value = sum(weights[k] * load(k, j) for k in range(3))
            stream[out, j * LANES : j * LANES + width] = value[:, :width]

    def write(g, carry):
        at = pl.ds(pl.multiple_of(g * SUB + PAD, SUB), SUB)
        out = pl.ds(pl.multiple_of(g * SUB, SUB), SUB)
        put(out, lambda k, j: powers[k, j, at, :])
        return carry

    put(slice(0, SUB), lambda k, j: border[0, k, j])
    lax.fori_loop(1, height // SUB - 1, write, 0, unroll=3)
    put(slice(height - SUB, height), lambda k, j: border[1, k, j])


def body(checkpoint, slot_dest, kmt, kappa):
    n = lax.axis_size("lon")
    lats = lax.axis_size("lat")
    lat = lax.axis_index("lat")
    me = jnp.stack([lax.axis_index("lon"), lax.rem(lat, 2)]).astype(jnp.int32)
    _, slots, values = checkpoint.shape
    rows, cols = kmt.shape
    by_n, bx_n = rows // BH, cols // BW
    cap = slots // n
    length = package_rows(cap, by_n)
    tiles = -(-(cols + 2 * HALO) // LANES)
    groups = slots // SUB
    edge_rows = -(-by_n * (1 + LEV) // 2) * BH
    if by_n * (1 + LEV) > 4 * cap:
        edge_rows = 2 * cap * BH + BH

    def fixed(value):
        return pltpu.with_memory_space_constraint(value, pltpu.HBM)

    kernels = (n, cap, bx_n, by_n)
    lists = [
        pltpu.SMEM((1, n * slots), jnp.int32),
        pltpu.SMEM((n * cap + 1,), jnp.int32),
        pltpu.SMEM((slots + 1,), jnp.int32),
    ]
    *packs, flat = pl.pallas_call(
        functools.partial(first_kernel, *kernels),
        out_shape=[shaped(length, LANES)] * (n // 2 - 1)
        + [shaped(slots * ROWS, LANES)],
        in_specs=[SM, HB, HB],
        out_specs=[VM] * (n // 2),
        scratch_shapes=lists
        + [
            pltpu.VMEM((groups, SUB, values), F32),
            pltpu.VMEM((n, BH, LANES), F32),
            pltpu.SMEM((n + 1,), jnp.int32),
            pltpu.SemaphoreType.DMA((groups + 1,)),
        ],
        compiler_params=params(),
        cost_estimate=cost(2 << 20, 4 << 20),
        name="first",
    )(me, fixed(slot_dest), fixed(checkpoint))

    def send(value, k):
        return lax.ppermute(value, "lon", [(i, i ^ k) for i in range(n)])

    order = sorted(range(1, n), key=lambda k: (k & 1, k < 2, -bin(k >> 1).count("1"), k))
    received = {k: send(packs[k // 2 - 1], k) for k in order if k % 2 == 0}
    own, *packs = pl.pallas_call(
        functools.partial(second_kernel, *kernels),
        out_shape=[shaped(length, LANES)] * (n // 2 + 1),
        in_specs=[SM, HB, VM, HB, HB],
        out_specs=[VM] * (n // 2 + 1),
        scratch_shapes=lists
        + [
            pltpu.VMEM((rows, cols), jnp.int32),
            pltpu.VMEM((LEV, rows, cols), F32),
            pltpu.VMEM((n, BH, LANES), F32),
            pltpu.VMEM((2, edge_rows, LANES), F32),
            pltpu.SMEM((n + 1,), jnp.int32),
            pltpu.SemaphoreType.DMA((3,)),
        ],
        compiler_params=params(),
        cost_estimate=cost(2 << 20, 4 << 20),
        name="second",
    )(me, fixed(slot_dest), flat, fixed(kmt), fixed(kappa))
    received |= {k: send(packs[k // 2], k) for k in order if k % 2}
    received[0] = own

    channels = 1 + 3 * LEV
    deep = rows + 2 * PAD
    table, grid = pl.pallas_call(
        functools.partial(base_kernel, n, cap, bx_n, by_n),
        out_shape=[
            shaped(n * (cap + 1) + (n + 1) * (1 + 2 * by_n), dtype=jnp.int32),
            shaped(channels, tiles, deep, LANES),
        ],
        in_specs=[SM, SM, VM, VM],
        out_specs=[SM, VM],
        scratch_shapes=[pltpu.SMEM((n * slots + 1,), jnp.int32)],
        compiler_params=params(),
        cost_estimate=cost(1 << 20, 2 << 20),
        name="base",
    )(me, slot_dest, kmt, kappa)

    def held(value):
        return pltpu.with_memory_space_constraint(value, pltpu.VMEM)

    rim = -(-channels * HALO // SUB) * SUB
    half, quarter = n // 2 - 1, n // 4
    odd = order[half:]
    parts = [
        [0] + order[:half],
        odd[-1:] + odd[: quarter - 1],
        odd[quarter - 1 : -1],
    ]
    for stage, which in enumerate(parts):
        shapes = [shaped(channels, tiles, deep, LANES)]
        if stage == len(parts) - 1:
            shapes += [shaped(tiles, rim, LANES)] * 2
        grid, *rims = pl.pallas_call(
            functools.partial(place_kernel, n, cap, bx_n, by_n, cols, which),
            out_shape=shapes,
            in_specs=[SM, SM] + [VM] * (1 + len(which)),
            out_specs=[VM] * len(shapes),
            input_output_aliases={2: 0},
            compiler_params=params(),
            cost_estimate=cost(2 << 20, 2 << 20),
            name=f"place{stage}",
        )(me, table, held(grid), *[received[k] for k in which])

    swaps = [
        [(i, i ^ 1) for i in range(lats) if i ^ 1 < lats],
        [(i, j) for i in range(lats) for j in [(i - 1 ^ 1) + 1] if 0 <= j < lats],
    ]
    other_rows, pair_rows = (
        lax.ppermute(value, "lat", swap) for value, swap in zip(rims, swaps[::-1])
    )

    devices = n * lats
    tracer_shape = shaped(2, LEV, rows, cols)
    tracer, powers, part = pl.pallas_call(
        functools.partial(inner_kernel, cols),
        out_shape=[
            tracer_shape,
            shaped(3, tiles, deep, LANES),
            shaped(SUB, LANES),
        ],
        in_specs=[VM],
        out_specs=[VM, VM, VM],
        compiler_params=params(),
        cost_estimate=cost(16 << 20, 6 << 20),
        name="inner",
    )(grid)
    tracer, border, sums = pl.pallas_call(
        functools.partial(border_kernel, cols),
        out_shape=[
            tracer_shape,
            shaped(2, 3, tiles, SUB, LANES),
            shaped(devices, LANES),
        ],
        in_specs=[SM, VM, VM, VM, VM, VM, HB],
        out_specs=[HB, VM, VM],
        scratch_shapes=[
            pltpu.VMEM((2, channels, tiles, EDGE, LANES), F32),
            pltpu.VMEM((2, 3, tiles, EDGE, LANES), F32),
            pltpu.VMEM((2, 2, LEV, SUB, cols), F32),
            pltpu.SemaphoreType.DMA((2,)),
        ],
        input_output_aliases={6: 0},
        compiler_params=params(),
        cost_estimate=cost(2 << 20, 1 << 20),
        name="border",
    )(me, grid, other_rows, pair_rows, powers, part, tracer)

    everyone = lax.all_to_all(sums, ("lon", "lat"), 0, 0, tiled=True)
    stream = pl.pallas_call(
        functools.partial(combine_kernel, cols),
        out_shape=shaped(rows, cols),
        in_specs=[VM, VM, VM],
        out_specs=VM,
        compiler_params=params(),
        cost_estimate=cost(1 << 20, 2 << 20),
        name="combine",
    )(everyone, powers, border)
    return tracer, stream


def solution(mesh):
    placed = (P("lat", "lon", None), P("lat", None), P("lat", "lon"), P(None, "lat", "lon"))
    return jax.shard_map(
        body,
        mesh=mesh,
        in_specs=placed,
        out_specs=(P(None, None, "lat", "lon"), P("lat", "lon")),
        check_vma=False,
    )
```

```python
import functools

import jax
import jax.numpy as jnp
from jax import lax
from jax.experimental import pallas as pl
from jax.experimental.pallas import tpu as pltpu
from jax.sharding import PartitionSpec as P


BH = 40
BW = 60
LEV = 2
HALO = 4
LANES = 128
SUB = 8
PAD = SUB
EDGE = 4 * SUB
ROWS = LEV * BH
HALF = LANES // 2
SHIFT = 8.0
SCALE = 8.0

thermal = 0.25
haline = 0.75
cabbeling = 0.05

VM = pl.BlockSpec(memory_space=pltpu.VMEM)
SM = pl.BlockSpec(memory_space=pltpu.SMEM)
HB = pl.BlockSpec(memory_space=pltpu.HBM)
F32 = jnp.float32


def params():
    return pltpu.CompilerParams(vmem_limit_bytes=24 << 20)


def cost(flops, moved):
    return pl.CostEstimate(flops=flops, bytes_accessed=moved, transcendentals=0)


def shaped(*dims, dtype=F32):
    return jax.ShapeDtypeStruct(dims, dtype)


def lanes():
    return lax.broadcasted_iota(jnp.int32, (SUB, LANES), 1)


def turn(value, amount):
    if isinstance(amount, int):
        amount %= LANES
        if amount == 0:
            return value
    return pltpu.roll(value, amount, 1)


def strip_lane(side, by, level, tracer, block_rows):
    return HALO * ((side * block_rows + by) * LEV + level) + HALF * tracer


def edge_spot(cap, piece):
    if piece < 4 * cap:
        return piece // 2 * BH, HALF * (1 + piece % 2) - HALO
    return cap * ROWS + BH, HALO * (piece - 4 * cap)


def package_rows(cap, by_n):
    return cap * ROWS + (2 * BH if by_n * (1 + LEV) > 4 * cap else BH)


def block_rows(flat, start, row):
    return flat[pl.ds(start + row * SUB, SUB, stride=SUB), :]


def block_start(i):
    return lax.div(i, SUB) * (ROWS * SUB) + lax.rem(i, SUB)


def plan(n, cap, bx_n, me, dest, source, count, todo, wanted):
    slots = todo.shape[0] - 1
    for k in range(n + 1):
        count[k] = 0
    for at in range(n * cap + 1):
        source[at] = 0

    def assign(i, found):
        d = dest[0, me * slots + i]
        used = d >= 0
        place = jnp.maximum(d, 0)
        owner = lax.div(place, slots)
        k = jnp.where(used, lax.bitwise_xor(owner, me), n)
        c = count[k]
        count[k] = c + 1
        source[jnp.where(used, k * cap + c, n * cap)] = block_start(i)
        bx = lax.rem(place, bx_n)
        partner = lax.bitwise_xor(
            lax.rem(owner + jnp.where(bx == 0, n - 1, 1), n), me
        )
        todo[found] = i
        holds = used & ((bx == 0) | (bx == bx_n - 1)) & wanted(partner)
        return found + holds.astype(jnp.int32)

    return lax.fori_loop(0, slots, assign, 0, unroll=4)


def fill_strips(n, bx_n, by_n, me, dest, flat, strips, todo, found):
    slots = bx_n * by_n
    spot_lane = lanes() & (HALF - 1)

    def strip(at, carry):
        i = todo[at]
        place = dest[0, me * slots + i]
        spot = lax.rem(place, slots)
        by = lax.div(spot, bx_n)
        side = (lax.rem(spot, bx_n) == 0).astype(jnp.int32)
        owner = lax.div(place, slots)
        k = lax.bitwise_xor(lax.rem(owner + jnp.where(side == 0, 1, n - 1), n), me)
        start = block_start(i)
        origin = jnp.where(side == 0, BW - HALO, 0)
        for level in range(LEV):
            target = strip_lane(side, by, level, 0, by_n)
            amount = lax.rem(target - origin + LANES, LANES)
            here = (spot_lane >= target) & (spot_lane < target + HALO)
            for row in range(0, BH, SUB):
                value = block_rows(flat, start, level * BH + row)
                pltpu.store(
                    strips.at[k, row : row + SUB, :],
                    pltpu.roll(value, amount, 1),
                    mask=here,
                )
        return carry

    lax.fori_loop(0, found, strip, 0)


def assemble(out, k, cap, source, flat, strips, edges=None, which=None, in_blocks=0):
    spare = (lanes() & (HALF - 1)) >= HALF - HALO
    for c in range(cap):
        start = source[k * cap + c]
        for row in range(0, ROWS, SUB):
            value = block_rows(flat, start, row)
            at = c * ROWS + row
            if at < in_blocks:
                value = jnp.where(spare, edges[which, at : at + SUB, :], value)
            out[at : at + SUB, :] = value
    for row in range(0, BH, SUB):
        at = cap * ROWS + row
        out[at : at + SUB, :] = strips[k, row : row + SUB, :]


def first_kernel(n, cap, bx_n, by_n, *refs):
    me_ref, dest_hbm, blocks_hbm = refs[:3]
    outs = refs[3 : n // 2 + 2]
    flat, dest, source, todo, blocks, strips, count, sems = refs[n // 2 + 2 :]
    groups = blocks.shape[0]
    slots = groups * SUB
    me = me_ref[0]
    lane = lanes()
    first = pltpu.make_async_copy(dest_hbm, dest, sems.at[groups])
    first.start()

    def loading(g):
        rows = pl.ds(pl.multiple_of(g * SUB, SUB), SUB)
        return pltpu.make_async_copy(
            blocks_hbm.at[0, rows, :], blocks.at[g], sems.at[g]
        )

    for g in range(groups):
        loading(g).start()
    first.wait()
    found = plan(
        n, cap, bx_n, me, dest, source, count, todo, lambda k: (k > 0) & (k & 1 == 0)
    )

    def regroup(group, carry):
        loading(group).wait()

        def load(q):
            return blocks[group, :, q * LANES : (q + 1) * LANES]

        limit = blocks.shape[2] // LANES - 1
        for row in range(ROWS):
            q, o = divmod(row * BW, LANES)
            p = (ROWS + row) * BW // LANES
            if o == 0:
                value = jnp.where(lane >= HALF, load(p), load(q))
            elif o <= HALF:
                low = load(p if o == HALF else min(p + 1, limit))
                value = jnp.where(lane >= o, load(q), low)
                if o < HALF:
                    value = jnp.where(lane >= o + HALF, load(p), value)
            else:
                value = jnp.where(lane >= o - HALF, load(p), load(q + 1))
                value = jnp.where(lane >= o, load(q), value)
            at = pl.multiple_of(group * (ROWS * SUB) + row * SUB, SUB)
            flat[pl.ds(at, SUB), :] = turn(value, -o)
        return carry

    lax.fori_loop(0, groups, regroup, 0)
    fill_strips(n, bx_n, by_n, me, dest, flat, strips, todo, found)
    for k in range(2, n, 2):
        assemble(outs[k // 2 - 1], k, cap, source, flat, strips)


def second_kernel(n, cap, bx_n, by_n, *refs):
    me_ref, dest_hbm, flat, kmt_hbm, kappa_hbm = refs[:5]
    outs = refs[5 : n // 2 + 6]
    dest, source, todo, kmt, kappa, strips, edges, count, sems = refs[n // 2 + 6 :]
    me = me_ref[0]
    lane = lanes()
    length = outs[0].shape[0]
    cols = kmt.shape[1]
    first, *copies = [
        pltpu.make_async_copy(dest_hbm, dest, sems.at[0]),
        pltpu.make_async_copy(kmt_hbm, kmt, sems.at[1]),
        pltpu.make_async_copy(kappa_hbm, kappa, sems.at[2]),
    ]
    for copy in (first, *copies):
        copy.start()
    first.wait()
    found = plan(
        n, cap, bx_n, me, dest, source, count, todo, lambda k: (k == 0) | (k & 1 == 1)
    )
    fill_strips(n, bx_n, by_n, me, dest, flat, strips, todo, found)
    for copy in copies:
        copy.wait()
    zero = jnp.zeros((SUB, LANES), F32)
    for at in range(0, edges.shape[1], SUB):
        for side in range(2):
            edges[side, at : at + SUB, :] = zero
    for side, start in ((0, cols - HALO), (1, 0)):
        tile = start // LANES * LANES
        width = min(LANES, cols - tile)
        for piece in range(by_n * (1 + LEV)):
            by, ch = divmod(piece, 1 + LEV)
            base, target = edge_spot(cap, piece)
            if piece >= 4 * cap:
                base -= cap * ROWS + BH - 2 * cap * BH
            here = (lane >= target) & (lane < target + HALO)
            for row in range(0, BH, SUB):
                at = slice(by * BH + row, by * BH + row + SUB)
                if ch == 0:
                    value = kmt[at, tile : tile + width].astype(F32)
                else:
                    value = kappa[ch - 1, at, tile : tile + width]
                if width < LANES:
                    value = jnp.concatenate([value, zero[:, width:]], axis=1)
                pltpu.store(
                    edges.at[side, base + row : base + row + SUB, :],
                    turn(value, target - (start - tile)),
                    mask=here,
                )
    eastern = lax.bitwise_xor(lax.rem(me + 1, n), me)
    in_blocks = min(edges.shape[1], 2 * cap * BH)
    for out, k in zip(outs, [0, *range(1, n, 2)]):
        which = jnp.where(eastern == k, 0, 1)
        assemble(out, k, cap, source, flat, strips, edges, which, in_blocks)
        if length > cap * ROWS + BH:
            for row in range(0, BH, SUB):
                at = cap * ROWS + BH + row
                out[at : at + SUB, :] = edges[
                    which, in_blocks + row : in_blocks + row + SUB, :
                ]


def base_kernel(n, cap, bx_n, by_n, me_ref, dest, kmt, kappa, table, grid, bringer):
    me = me_ref[0]
    slots = bx_n * by_n
    channels, tiles, deep, _ = grid.shape
    cols = kmt.shape[1]
    zero = jnp.zeros((SUB, LANES), F32)
    west = lax.rem(me + n - 1, n)
    east = lax.rem(me + 1, n)
    for at in range(n * (cap + 1)):
        table[at] = -1
    sides = [(west, by * bx_n + bx_n - 1) for by in range(by_n)]
    sides += [(east, by * bx_n) for by in range(by_n)]
    for owner, spot in sides:
        bringer[owner * slots + spot + 1] = -1

    def owner_loop(s, carry):
        k = lax.bitwise_xor(s, me)

        def slot_loop(i, c):
            d = dest[0, s * slots + i]
            bringer[d + 1] = k
            spot = d - me * slots
            mine = (spot >= 0) & (spot < slots)
            table[k * (cap + 1) + c] = jnp.where(mine, spot, -1)
            return c + mine.astype(jnp.int32)

        lax.fori_loop(0, slots, slot_loop, 0, unroll=8)
        return carry

    lax.fori_loop(0, n, owner_loop, 0)
    counts = n * (cap + 1)
    lists = counts + n + 1
    for k in range(n + 1):
        table[counts + k] = 0
    for at, (owner, spot) in enumerate(sides):
        k = bringer[owner * slots + spot + 1]
        k = jnp.where(k < 0, n, k)
        c = table[counts + k]
        table[counts + k] = c + 1
        table[lists + k * len(sides) + c] = at

    def clear(g, carry):
        at = pl.ds(pl.multiple_of(g * SUB, SUB), SUB)
        for ch in range(channels):
            for j in range(tiles):
                grid[ch, j, at, :] = zero
        return carry

    lax.fori_loop(0, deep // SUB, clear, 0)

    def lay(g, carry):
        at = pl.ds(pl.multiple_of(g * SUB, SUB), SUB)
        out = pl.ds(pl.multiple_of(g * SUB + PAD, SUB), SUB)
        for ch in range(1 + LEV):
            for j in range(tiles):
                width = min(LANES, cols - j * LANES)
                part = slice(j * LANES, j * LANES + width)
                if ch == 0:
                    value = kmt[at, part].astype(F32)
                else:
                    value = kappa[ch - 1, at, part]
                grid[ch, j, out, 0:width] = value
        return carry

    lax.fori_loop(0, kmt.shape[0] // SUB, lay, 0)


def place_kernel(n, cap, bx_n, by_n, cols, which, *refs):
    count = len(which)
    me_ref, table, _ = refs[:3]
    odd = me_ref[1]
    packs = refs[3 : 3 + count]
    grid, *rims = refs[3 + count :]
    me = me_ref[0]
    lane = lanes()
    channels, tiles, deep, _ = grid.shape
    last = tiles - 1
    own = cols - last * LANES
    halo_lane = (own, LANES - HALO)

    def mark(ch, at, value, start):
        here = (lane >= start) & (lane < start + HALO)
        pltpu.store(grid.at[ch, last, at, :], value, mask=here)

    for k, pack in zip(which, packs):

        for c in range(cap):
            spot = table[k * (cap + 1) + c]
            valid = spot >= 0
            spot = jnp.maximum(spot, 0)
            by = lax.div(spot, bx_n)
            offset = lax.rem(spot, bx_n) * BW
            tile = lax.div(offset, LANES)
            following = jnp.minimum(tile + 1, last)
            start = lax.rem(offset, LANES)
            begin = jnp.where(valid, start, LANES)
            here = (lane >= begin) & (lane < begin + BW)
            spill = lane < jnp.where(valid, start + BW - LANES, 0)
            for row in range(0, BH, SUB):
                at = pl.ds(pl.multiple_of(by * BH + row + PAD, SUB), SUB)
                depth = grid[0, tile, at, :], grid[0, following, at, :]
                for level in range(LEV):
                    place = c * ROWS + level * BH + row
                    value = pack[place : place + SUB, :]
                    masks = here & (depth[0] > level), spill & (depth[1] > level)
                    for tracer in range(2):
                        ch = 1 + LEV + tracer * LEV + level
                        turned = pltpu.roll(
                            value, lax.rem(start + tracer * HALF, LANES), 1
                        )
                        for target, mask in zip((tile, following), masks):
                            pltpu.store(grid.at[ch, target, at, :], turned, mask=mask)

        counts = n * (cap + 1)
        lists = counts + n + 1 + k * 2 * by_n

        def strip(at, carry, pack=pack, lists=lists):
            index = table[lists + at]
            by = lax.rem(index, by_n)
            start = jnp.where(index < by_n, halo_lane[1], halo_lane[0])
            for row in range(0, BH, SUB):
                rows = pl.ds(pl.multiple_of(by * BH + row + PAD, SUB), SUB)
                value = pack[cap * ROWS + row : cap * ROWS + row + SUB, :]
                for level in range(LEV):
                    for tracer in range(2):
                        origin = strip_lane(0, index, level, tracer, by_n)
                        amount = lax.rem(start - origin + LANES, LANES)
                        mark(
                            1 + LEV + tracer * LEV + level,
                            rows,
                            pltpu.roll(value, amount, 1),
                            start,
                        )
            return carry

        lax.fori_loop(0, table[counts + k], strip, 0)

        for neighbour, start in ((me + n - 1, halo_lane[1]), (me + 1, halo_lane[0])):
            if k % 2 == 0:
                continue

            @pl.when(lax.bitwise_xor(lax.rem(neighbour, n), me) == k)
            def _(start=start, pack=pack):
                for piece in range(by_n * (1 + LEV)):
                    by, ch = divmod(piece, 1 + LEV)
                    base, origin = edge_spot(cap, piece)
                    for row in range(0, BH, SUB):
                        at = by * BH + row + PAD
                        mark(
                            ch,
                            slice(at, at + SUB),
                            turn(pack[base + row : base + row + SUB, :], start - origin),
                            start,
                        )

    if not rims:
        return
    rim = (lane >= own) & (lane < own + HALO) | (lane >= LANES - HALO)

    def mask(g, carry):
        at = pl.ds(pl.multiple_of(g * SUB + PAD, SUB), SUB)
        wet = grid[0, last, at, :]
        for ch in range(1 + LEV, channels):
            level = (ch - 1 - LEV) % LEV
            grid[ch, last, at, :] = jnp.where(
                rim & (wet <= level), 0.0, grid[ch, last, at, :]
            )
        return carry

    lax.fori_loop(0, deep // SUB - 2, mask, 0, unroll=4)
    low = deep - PAD - HALO
    for rows, first in zip(rims, (1 - odd, odd)):
        at = jnp.where(first == 1, PAD, low)
        for ch in range(channels):
            for j in range(tiles):
                rows[j, ch * HALO : (ch + 1) * HALO, :] = grid[
                    ch, j, pl.ds(at, HALO), :
                ]


def sideways(values):
    lane = lanes()
    count = len(values)
    left = [turn(v, 1) for v in values]
    right = [turn(v, -1) for v in values]
    west = [
        jnp.where(lane == 0, left[(j - 1) % count], left[j]) for j in range(count)
    ]
    east = [
        jnp.where(lane == LANES - 1, right[(j + 1) % count], right[j])
        for j in range(count)
    ]
    return east, west


def three(load, start):
    return load(start), load(start - 1), load(start + 1)


def diffuse(load, start):
    tiles = len(load(0, start))
    span = range(tiles)
    level_c, level_a, level_b = three(functools.partial(load, 0), start)
    level_e, _ = sideways(level_c)
    both_e = [jnp.minimum(level_c[j], level_e[j]) for j in span]
    both_a = [jnp.minimum(level_c[j], level_a[j]) for j in span]
    both_b = [jnp.minimum(level_c[j], level_b[j]) for j in span]
    forcing = [None] * tiles
    fresh = [[None] * LEV for _ in range(2)]
    for level in range(LEV):
        kappa_c, kappa_a, kappa_b = three(functools.partial(load, 1 + level), start)
        kappa_e, _ = sideways(kappa_c)
        face_e, face_a, face_b = (
            [jnp.where(both[j] > level, kappa_c[j] + other[j], 0.0) for j in span]
            for both, other in (
                (both_e, kappa_e),
                (both_a, kappa_a),
                (both_b, kappa_b),
            )
        )
        for tracer in range(2):
            ch = 1 + LEV + tracer * LEV + level
            here, above, below = three(functools.partial(load, ch), start)
            to_east, _ = sideways(here)
            flux = [face_e[j] * (to_east[j] - here[j]) for j in span]
            _, flux_w = sideways(flux)
            fresh[tracer][level] = [
                jnp.where(
                    level_c[j] > level,
                    here[j]
                    + 0.5
                    * (
                        (flux[j] - flux_w[j])
                        + face_a[j] * (above[j] - here[j])
                        + face_b[j] * (below[j] - here[j])
                    ),
                    0.0,
                )
                for j in span
            ]
        thickness = 1.0 + 0.5 * level
        for j in span:
            temp, salt = fresh[0][level][j], fresh[1][level][j]
            density = haline * salt - temp * (thermal + cabbeling * temp)
            if level:
                density = forcing[j] + thickness * density
            forcing[j] = density
    return fresh, forcing


def apply(here, above, below, levels):
    span = range(len(here))
    pair = [above[j] + below[j] for j in span]
    mixed = [here[j] + 0.5 * pair[j] for j in span]
    east, west = sideways(mixed)
    result = []
    for j in span:
        diagonal = 6.0 - SHIFT + 1.0
        total = jnp.full((SUB, LANES), diagonal / SCALE, F32)
        for k in range(1, LEV):
            diagonal += 1.0 + 0.5 * k
            total = jnp.where(levels[j] > k, diagonal / SCALE, total)
        total = total * here[j] - (pair[j] + (east[j] + west[j])) * (1.0 / SCALE)
        result.append(jnp.where(levels[j] > 0, total, 0.0))
    return result


def gather_products(carry, powers, centre, keep):
    carry = list(carry)
    span = range(len(powers[0]))
    for j in span:
        q0, q1, q2, q3 = (keep(q[j], j) for q in powers)
        b1 = q1 - centre * q0
        c2 = q2 - centre * q1
        c3 = q3 - centre * q2
        b2 = c2 - centre * b1
        b3 = (c3 - centre * c2) - centre * b2
        terms = (q0, b1, b2, b3)
        for at, (x, y) in enumerate(PAIRS):
            carry[at] = carry[at] + terms[x] * terms[y]
    return tuple(carry)


def total_row(totals):
    lane = lanes()[:1]
    row = jnp.zeros((1, LANES), F32)
    for at, total in enumerate(totals):
        total = jnp.sum(total, axis=(0, 1), keepdims=True)
        row = jnp.where(lane == at + 1, total, row)
    return row


def put_tracer(target, fresh, cols, at):
    for tracer in range(2):
        for level in range(LEV):
            for j, value in enumerate(fresh[tracer][level]):
                width = min(LANES, cols - j * LANES)
                target[tracer, level, at, j * LANES : j * LANES + width] = value[
                    :, :width
                ]


def inner_kernel(cols, grid, tracer_out, powers, sums, edges, fresh_rows, sem):
    lane = lanes()
    line = lax.broadcasted_iota(jnp.int32, (SUB, LANES), 0)
    _, tiles, deep, _ = grid.shape
    own = cols - (tiles - 1) * LANES
    first, end = PAD // SUB, (deep - PAD) // SUB
    zero = jnp.zeros((SUB, LANES), F32)

    def rows(ref, lead, start):
        return [ref[lead, j, pl.ds(start, SUB), :] for j in range(tiles)]

    def top(g):
        return pl.multiple_of(g * SUB, SUB)

    def step(g, carry):
        fresh, forcing = diffuse(functools.partial(rows, grid), top(g))
        put_tracer(
            fresh_rows, fresh, cols, pl.ds(pl.multiple_of(g * SUB - PAD, SUB), SUB)
        )
        for j in range(tiles):
            powers[0, j, pl.ds(top(g), SUB), :] = forcing[j]
        return carry

    lax.fori_loop(first, end, step, 0, unroll=2)
    copy = pltpu.make_async_copy(fresh_rows, tracer_out, sem)
    copy.start()
    height = fresh_rows.shape[2]
    for tracer in range(2):
        for level in range(LEV):
            for side, row in ((0, 0), (1, height - SUB)):
                edges[side, tracer, level] = fresh_rows[
                    tracer, level, row : row + SUB, :
                ]

    def inside(value, j):
        return value if j < tiles - 1 else jnp.where(lane < own, value, 0.0)

    def upper(value, j):
        return jnp.where(line >= HALO, inside(value, j), 0.0)

    def lower(value, j):
        return jnp.where(line < SUB - HALO, inside(value, j), 0.0)

    def power(g, source):
        here, above, below = three(functools.partial(rows, powers, source), top(g))
        return here, apply(here, above, below, rows(grid, 0, top(g)))

    def put(g, target):
        here, result = power(g, target - 1)
        for j in range(tiles):
            powers[target, j, pl.ds(top(g), SUB), :] = result[j]
        return here, result

    def first_power(g, carry, keep=inside):
        here, result = put(g, 1)
        a, b = carry
        for j in range(tiles):
            v = keep(here[j], j)
            a = a + v * v
            b = b + v * keep(result[j], j)
        return a, b

    def everywhere(body, carry):
        carry = body(first, carry, upper)
        carry = lax.fori_loop(first + 1, end - 1, body, carry, unroll=end - first - 2)
        return body(end - 1, carry, lower)

    a, b = everywhere(first_power, (zero, zero))
    a = jnp.sum(a, axis=(0, 1), keepdims=True)
    b = jnp.sum(b, axis=(0, 1), keepdims=True)
    centre = jnp.where(a > 0, b / jnp.where(a > 0, a, 1.0), 0.0)
    centre = jnp.broadcast_to(centre, (SUB, LANES))
    lax.fori_loop(
        first, end, lambda g, c: (put(g, 2), c)[1], 0, unroll=end - first
    )

    def products(g, carry, keep=inside):
        here, result = power(g, 2)
        lower_powers = [rows(powers, k, top(g)) for k in range(2)]
        return gather_products(carry, (*lower_powers, here, result), centre, keep)

    totals = everywhere(products, (zero,) * len(PAIRS))
    row = jnp.where(lane[:1] == 0, centre[:1], total_row(totals))
    sums[...] = jnp.broadcast_to(row, sums.shape)
    copy.wait()


def border_kernel(
    cols, me_ref, grid, other_rows, pair_rows, powers, part, edges, tracer_in,
    tracer_out, border, sums, field, local, fresh_rows, sems,
):
    lane = lanes()
    line = lax.broadcasted_iota(jnp.int32, (SUB, LANES), 0)
    channels, tiles, deep, _ = grid.shape
    own = cols - (tiles - 1) * LANES
    half = EDGE // 2
    even = me_ref[1] == 0
    for ch in range(channels):
        for j in range(tiles):
            at = slice(ch * HALO, (ch + 1) * HALO)
            field[0, ch, j, half : half + SUB, :] = grid[ch, j, PAD : PAD + SUB, :]
            field[1, ch, j, half - SUB : half, :] = grid[
                ch, j, deep - PAD - SUB : deep - PAD, :
            ]
            pair, other = pair_rows[j, at, :], other_rows[j, at, :]
            field[0, ch, j, half - HALO : half, :] = jnp.where(even, other, pair)
            field[1, ch, j, half : half + HALO, :] = jnp.where(even, pair, other)
    for k in range(3):
        for j in range(tiles):
            local[0, k, j, half : half + SUB, :] = powers[k, j, PAD : PAD + SUB, :]
            local[1, k, j, half - SUB : half, :] = powers[
                k, j, deep - PAD - SUB : deep - PAD, :
            ]
    centre = jnp.broadcast_to(part[0:1, 0:1], (SUB, LANES))

    def rows_of(side):
        def rows(ref, lead, start):
            return [ref[side, lead, j, pl.ds(start, SUB), :] for j in range(tiles)]

        return rows

    height = tracer_out.shape[2]
    start = half - HALO
    copies = []
    for side in range(2):
        fresh, forcing = diffuse(functools.partial(rows_of(side), field), start)
        for j in range(tiles):
            local[side, 0, j, start : start + SUB, :] = forcing[j]
        mine = line == (0 if side == 0 else SUB - 1)
        for tracer in range(2):
            for level in range(LEV):
                for j in range(tiles):
                    width = min(LANES, cols - j * LANES)
                    part_lanes = slice(j * LANES, j * LANES + width)
                    moved = pltpu.roll(fresh[tracer][level][j], HALO, 0)
                    fresh_rows[side, tracer, level, :, part_lanes] = jnp.where(
                        mine[:, :width],
                        moved[:, :width],
                        edges[side, tracer, level, :, part_lanes],
                    )
        copies.append(
            pltpu.make_async_copy(
                fresh_rows.at[side],
                tracer_out.at[:, :, pl.ds(side * (height - SUB), SUB), :],
                sems.at[side],
            )
        )
        copies[-1].start()

    def power(side, source):
        rows = rows_of(side)
        here, above, below = three(functools.partial(rows, local, source), start)
        return here, apply(here, above, below, rows(field, 0, start))

    for target in range(1, 3):
        for side in range(2):
            result = power(side, target - 1)[1]
            for j in range(tiles):
                local[side, target, j, start : start + SUB, :] = result[j]
    totals = (jnp.zeros((SUB, LANES), F32),) * len(PAIRS)
    for side in range(2):
        here, result = power(side, 2)
        lower_powers = [rows_of(side)(local, k, start) for k in range(2)]
        own_rows = half - side * SUB
        for k in range(3):
            for j in range(tiles):
                border[side, k, j] = local[side, k, j, own_rows : own_rows + SUB, :]
        bound = (1 - side) * HALO
        rim = (line >= bound) & (line < bound + HALO)

        def keep(value, j, rim=rim):
            inside = rim if j < tiles - 1 else rim & (lane < own)
            return jnp.where(inside, value, 0.0)

        totals = gather_products(
            totals, (*lower_powers, here, result), centre, keep
        )
    sums[...] = jnp.broadcast_to(part[0:1, :] + total_row(totals), sums.shape)
    for copy in copies:
        copy.wait()


PAIRS = ((0, 0), (0, 1), (0, 2), (0, 3), (1, 1), (1, 2), (1, 3), (2, 2), (2, 3))


def combine_kernel(cols, sums, powers, border, stream_out, stream, sems):
    values = sums[...]
    lane = lax.broadcasted_iota(jnp.int32, values.shape, 1)

    def column(k):
        return jnp.sum(jnp.where(lane == k, values, 0.0), axis=1, keepdims=True)

    centre = column(0)
    gram = {pair: column(at + 1) for at, pair in enumerate(PAIRS)}

    def local(c):
        c = list(c) + [None] * (4 - len(c))
        c0, c1, c2, c3 = c
        result = [c0 + jnp.zeros_like(centre)]
        if c1 is not None:
            inner = c1
            slope = c1 + jnp.zeros_like(centre)
            if c2 is not None:
                inner = c1 + centre * (c2 if c3 is None else c2 + centre * c3)
                slope = c1 + centre * (
                    2.0 * c2 if c3 is None else 2.0 * c2 + 3.0 * (centre * c3)
                )
            result = [c0 + centre * inner, slope]
        if c2 is not None:
            result.append(c2 + jnp.zeros_like(centre) if c3 is None else c2 + 3.0 * (centre * c3))
        if c3 is not None:
            result.append(c3 + jnp.zeros_like(centre))
        return result

    def inner(x, y):
        u, v = local(x), local(y)
        total = jnp.zeros_like(centre)
        for i in range(len(u)):
            for j in range(len(v)):
                total = total + (u[i] * v[j]) * gram[(min(i, j), max(i, j))]
        return jnp.sum(total, axis=0, keepdims=True)

    def operate(c):
        result = [SHIFT * x for x in c] + [None]
        for i, x in enumerate(c):
            term = SCALE * x
            result[i + 1] = term if result[i + 1] is None else result[i + 1] + term
        return result

    one = jnp.ones((1, 1), F32)
    stream_c = [None] * 3
    residual, direction = [one], [one]
    norm = inner(residual, residual)
    for step in range(3):
        image = operate(direction)
        alpha = norm / inner(direction, image)
        for i, x in enumerate(direction):
            stream_c[i] = alpha * x if stream_c[i] is None else stream_c[i] + alpha * x
        if step == 2:
            break
        residual = [
            (residual[i] - alpha * image[i]) if i < len(residual) else -alpha * image[i]
            for i in range(len(image))
        ]
        fresh = inner(residual, residual)
        ratio = fresh / norm
        direction = [
            (residual[i] + ratio * direction[i]) if i < len(direction) else residual[i]
            for i in range(len(residual))
        ]
        norm = fresh

    tiles = powers.shape[1]
    height = stream.shape[0]
    weights = [jnp.broadcast_to(c, (SUB, LANES)) for c in stream_c]

    def put(out, load):
        for j in range(tiles):
            width = min(LANES, cols - j * LANES)
            value = sum(weights[k] * load(k, j) for k in range(3))
            stream[out, j * LANES : j * LANES + width] = value[:, :width]

    def write(g, carry):
        at = pl.ds(pl.multiple_of(g * SUB + PAD, SUB), SUB)
        out = pl.ds(pl.multiple_of(g * SUB, SUB), SUB)
        put(out, lambda k, j: powers[k, j, at, :])
        return carry

    middle = height // SUB // 2 * SUB
    copies = [
        pltpu.make_async_copy(stream.at[part, :], stream_out.at[part, :], sems.at[at])
        for at, part in enumerate((pl.ds(0, middle), pl.ds(middle, height - middle)))
    ]
    put(slice(0, SUB), lambda k, j: border[0, k, j])
    lax.fori_loop(1, middle // SUB, write, 0, unroll=3)
    copies[0].start()
    lax.fori_loop(middle // SUB, height // SUB - 1, write, 0, unroll=3)
    put(slice(height - SUB, height), lambda k, j: border[1, k, j])
    copies[1].start()
    for copy in copies:
        copy.wait()


def body(checkpoint, slot_dest, kmt, kappa):
    n = lax.axis_size("lon")
    lats = lax.axis_size("lat")
    lat = lax.axis_index("lat")
    me = jnp.stack([lax.axis_index("lon"), lax.rem(lat, 2)]).astype(jnp.int32)
    _, slots, values = checkpoint.shape
    rows, cols = kmt.shape
    by_n, bx_n = rows // BH, cols // BW
    cap = slots // n
    length = package_rows(cap, by_n)
    tiles = -(-(cols + 2 * HALO) // LANES)
    groups = slots // SUB
    edge_rows = -(-by_n * (1 + LEV) // 2) * BH
    if by_n * (1 + LEV) > 4 * cap:
        edge_rows = 2 * cap * BH + BH

    def fixed(value):
        return pltpu.with_memory_space_constraint(value, pltpu.HBM)

    kernels = (n, cap, bx_n, by_n)
    lists = [
        pltpu.SMEM((1, n * slots), jnp.int32),
        pltpu.SMEM((n * cap + 1,), jnp.int32),
        pltpu.SMEM((slots + 1,), jnp.int32),
    ]
    *packs, flat = pl.pallas_call(
        functools.partial(first_kernel, *kernels),
        out_shape=[shaped(length, LANES)] * (n // 2 - 1)
        + [shaped(slots * ROWS, LANES)],
        in_specs=[SM, HB, HB],
        out_specs=[VM] * (n // 2),
        scratch_shapes=lists
        + [
            pltpu.VMEM((groups, SUB, values), F32),
            pltpu.VMEM((n, BH, LANES), F32),
            pltpu.SMEM((n + 1,), jnp.int32),
            pltpu.SemaphoreType.DMA((groups + 1,)),
        ],
        compiler_params=params(),
        cost_estimate=cost(2 << 20, 4 << 20),
        name="first",
    )(me, fixed(slot_dest), fixed(checkpoint))

    def send(value, k):
        return lax.ppermute(value, "lon", [(i, i ^ k) for i in range(n)])

    order = sorted(range(1, n), key=lambda k: (k & 1, k < 2, -bin(k >> 1).count("1"), k))
    received = {k: send(packs[k // 2 - 1], k) for k in order if k % 2 == 0}
    own, *packs = pl.pallas_call(
        functools.partial(second_kernel, *kernels),
        out_shape=[shaped(length, LANES)] * (n // 2 + 1),
        in_specs=[SM, HB, VM, HB, HB],
        out_specs=[VM] * (n // 2 + 1),
        scratch_shapes=lists
        + [
            pltpu.VMEM((rows, cols), jnp.int32),
            pltpu.VMEM((LEV, rows, cols), F32),
            pltpu.VMEM((n, BH, LANES), F32),
            pltpu.VMEM((2, edge_rows, LANES), F32),
            pltpu.SMEM((n + 1,), jnp.int32),
            pltpu.SemaphoreType.DMA((3,)),
        ],
        compiler_params=params(),
        cost_estimate=cost(2 << 20, 4 << 20),
        name="second",
    )(me, fixed(slot_dest), flat, fixed(kmt), fixed(kappa))
    received |= {k: send(packs[k // 2], k) for k in order if k % 2}
    received[0] = own

    channels = 1 + 3 * LEV
    deep = rows + 2 * PAD
    table, grid = pl.pallas_call(
        functools.partial(base_kernel, n, cap, bx_n, by_n),
        out_shape=[
            shaped(n * (cap + 1) + (n + 1) * (1 + 2 * by_n), dtype=jnp.int32),
            shaped(channels, tiles, deep, LANES),
        ],
        in_specs=[SM, SM, VM, VM],
        out_specs=[SM, VM],
        scratch_shapes=[pltpu.SMEM((n * slots + 1,), jnp.int32)],
        compiler_params=params(),
        cost_estimate=cost(1 << 20, 2 << 20),
        name="base",
    )(me, slot_dest, kmt, kappa)

    def held(value):
        return pltpu.with_memory_space_constraint(value, pltpu.VMEM)

    rim = -(-channels * HALO // SUB) * SUB
    half, quarter = n // 2 - 1, n // 4
    odd = order[half:]
    parts = [
        [0] + order[:half],
        odd[-1:] + odd[: quarter - 1],
        odd[quarter - 1 : -1],
    ]
    for stage, which in enumerate(parts):
        shapes = [shaped(channels, tiles, deep, LANES)]
        if stage == len(parts) - 1:
            shapes += [shaped(tiles, rim, LANES)] * 2
        grid, *rims = pl.pallas_call(
            functools.partial(place_kernel, n, cap, bx_n, by_n, cols, which),
            out_shape=shapes,
            in_specs=[SM, SM] + [VM] * (1 + len(which)),
            out_specs=[VM] * len(shapes),
            input_output_aliases={2: 0},
            compiler_params=params(),
            cost_estimate=cost(2 << 20, 2 << 20),
            name=f"place{stage}",
        )(me, table, held(grid), *[received[k] for k in which])

    swaps = [
        [(i, i ^ 1) for i in range(lats) if i ^ 1 < lats],
        [(i, j) for i in range(lats) for j in [(i - 1 ^ 1) + 1] if 0 <= j < lats],
    ]
    other_rows, pair_rows = (
        lax.ppermute(value, "lat", swap) for value, swap in zip(rims, swaps[::-1])
    )

    devices = n * lats
    tracer_shape = shaped(2, LEV, rows, cols)
    tracer, powers, part, edges = pl.pallas_call(
        functools.partial(inner_kernel, cols),
        out_shape=[
            tracer_shape,
            shaped(3, tiles, deep, LANES),
            shaped(SUB, LANES),
            shaped(2, 2, LEV, SUB, cols),
        ],
        in_specs=[VM],
        out_specs=[HB, VM, VM, VM],
        scratch_shapes=[
            pltpu.VMEM((2, LEV, rows, cols), F32),
            pltpu.SemaphoreType.DMA,
        ],
        compiler_params=params(),
        cost_estimate=cost(16 << 20, 6 << 20),
        name="inner",
    )(grid)
    tracer, border, sums = pl.pallas_call(
        functools.partial(border_kernel, cols),
        out_shape=[
            tracer_shape,
            shaped(2, 3, tiles, SUB, LANES),
            shaped(devices, LANES),
        ],
        in_specs=[SM, VM, VM, VM, VM, VM, VM, HB],
        out_specs=[HB, VM, VM],
        scratch_shapes=[
            pltpu.VMEM((2, channels, tiles, EDGE, LANES), F32),
            pltpu.VMEM((2, 3, tiles, EDGE, LANES), F32),
            pltpu.VMEM((2, 2, LEV, SUB, cols), F32),
            pltpu.SemaphoreType.DMA((2,)),
        ],
        input_output_aliases={7: 0},
        compiler_params=params(),
        cost_estimate=cost(2 << 20, 1 << 20),
        name="border",
    )(me, grid, other_rows, pair_rows, powers, part, edges, fixed(tracer))

    everyone = lax.all_to_all(sums, ("lon", "lat"), 0, 0, tiled=True)
    stream = pl.pallas_call(
        functools.partial(combine_kernel, cols),
        out_shape=shaped(rows, cols),
        in_specs=[VM, VM, VM],
        out_specs=HB,
        scratch_shapes=[
            pltpu.VMEM((rows, cols), F32),
            pltpu.SemaphoreType.DMA((2,)),
        ],
        compiler_params=params(),
        cost_estimate=cost(1 << 20, 2 << 20),
        name="combine",
    )(everyone, powers, border)
    return tracer, stream


def solution(mesh):
    placed = (P("lat", "lon", None), P("lat", None), P("lat", "lon"), P(None, "lat", "lon"))
    return jax.shard_map(
        body,
        mesh=mesh,
        in_specs=placed,
        out_specs=(P(None, None, "lat", "lon"), P("lat", "lon")),
        check_vma=False,
    )
```

```python
import functools

import jax
import jax.numpy as jnp
from jax import lax
from jax.experimental import pallas as pl
from jax.experimental.pallas import tpu as pltpu
from jax.sharding import PartitionSpec as P


BH = 40
BW = 60
LEV = 2
HALO = 4
LANES = 128
SUB = 8
PAD = SUB
EDGE = 4 * SUB
ROWS = LEV * BH
HALF = LANES // 2
SHIFT = 8.0
SCALE = 8.0

thermal = 0.25
haline = 0.75
cabbeling = 0.05

VM = pl.BlockSpec(memory_space=pltpu.VMEM)
SM = pl.BlockSpec(memory_space=pltpu.SMEM)
HB = pl.BlockSpec(memory_space=pltpu.HBM)
F32 = jnp.float32


def params():
    return pltpu.CompilerParams(vmem_limit_bytes=24 << 20)


def cost(flops, moved):
    return pl.CostEstimate(flops=flops, bytes_accessed=moved, transcendentals=0)


def shaped(*dims, dtype=F32):
    return jax.ShapeDtypeStruct(dims, dtype)


def lanes():
    return lax.broadcasted_iota(jnp.int32, (SUB, LANES), 1)


def turn(value, amount):
    if isinstance(amount, int):
        amount %= LANES
        if amount == 0:
            return value
    return pltpu.roll(value, amount, 1)


def strip_lane(side, by, level, tracer, block_rows):
    return HALO * ((side * block_rows + by) * LEV + level) + HALF * tracer


def edge_spot(cap, piece):
    if piece < 4 * cap:
        return piece // 2 * BH, HALF * (1 + piece % 2) - HALO
    return cap * ROWS + BH, HALO * (piece - 4 * cap)


def package_rows(cap, by_n):
    return cap * ROWS + (2 * BH if by_n * (1 + LEV) > 4 * cap else BH)


def block_rows(flat, start, row):
    return flat[pl.ds(start + row * SUB, SUB, stride=SUB), :]


def block_start(i):
    return lax.div(i, SUB) * (ROWS * SUB) + lax.rem(i, SUB)


def plan(n, cap, bx_n, me, dest, source, count, todo, wanted):
    slots = todo.shape[0] - 1
    for k in range(n + 1):
        count[k] = 0
    for at in range(n * cap + 1):
        source[at] = 0

    def assign(i, found):
        d = dest[0, me * slots + i]
        used = d >= 0
        place = jnp.maximum(d, 0)
        owner = lax.div(place, slots)
        k = jnp.where(used, lax.bitwise_xor(owner, me), n)
        c = count[k]
        count[k] = c + 1
        source[jnp.where(used, k * cap + c, n * cap)] = block_start(i)
        bx = lax.rem(place, bx_n)
        partner = lax.bitwise_xor(
            lax.rem(owner + jnp.where(bx == 0, n - 1, 1), n), me
        )
        todo[found] = i
        holds = used & ((bx == 0) | (bx == bx_n - 1)) & wanted(partner)
        return found + holds.astype(jnp.int32)

    return lax.fori_loop(0, slots, assign, 0, unroll=4)


def fill_strips(n, bx_n, by_n, me, dest, flat, strips, todo, found):
    slots = bx_n * by_n
    spot_lane = lanes() & (HALF - 1)

    def strip(at, carry):
        i = todo[at]
        place = dest[0, me * slots + i]
        spot = lax.rem(place, slots)
        by = lax.div(spot, bx_n)
        side = (lax.rem(spot, bx_n) == 0).astype(jnp.int32)
        owner = lax.div(place, slots)
        k = lax.bitwise_xor(lax.rem(owner + jnp.where(side == 0, 1, n - 1), n), me)
        start = block_start(i)
        origin = jnp.where(side == 0, BW - HALO, 0)
        for level in range(LEV):
            target = strip_lane(side, by, level, 0, by_n)
            amount = lax.rem(target - origin + LANES, LANES)
            here = (spot_lane >= target) & (spot_lane < target + HALO)
            for row in range(0, BH, SUB):
                value = block_rows(flat, start, level * BH + row)
                pltpu.store(
                    strips.at[k, row : row + SUB, :],
                    pltpu.roll(value, amount, 1),
                    mask=here,
                )
        return carry

    lax.fori_loop(0, found, strip, 0)


def assemble(out, k, cap, source, flat, strips, edges=None, which=None, in_blocks=0):
    spare = (lanes() & (HALF - 1)) >= HALF - HALO
    for c in range(cap):
        start = source[k * cap + c]
        for row in range(0, ROWS, SUB):
            value = block_rows(flat, start, row)
            at = c * ROWS + row
            if at < in_blocks:
                value = jnp.where(spare, edges[which, at : at + SUB, :], value)
            out[at : at + SUB, :] = value
    for row in range(0, BH, SUB):
        at = cap * ROWS + row
        out[at : at + SUB, :] = strips[k, row : row + SUB, :]


def first_kernel(n, cap, bx_n, by_n, *refs):
    me_ref, dest_hbm, blocks_hbm = refs[:3]
    outs = refs[3 : n // 2 + 2]
    flat, dest, source, todo, blocks, strips, count, sems = refs[n // 2 + 2 :]
    groups = blocks.shape[0]
    slots = groups * SUB
    me = me_ref[0]
    lane = lanes()
    first = pltpu.make_async_copy(dest_hbm, dest, sems.at[groups])
    first.start()

    def loading(g):
        rows = pl.ds(pl.multiple_of(g * SUB, SUB), SUB)
        return pltpu.make_async_copy(
            blocks_hbm.at[0, rows, :], blocks.at[g], sems.at[g]
        )

    for g in range(groups):
        loading(g).start()
    first.wait()
    found = plan(
        n, cap, bx_n, me, dest, source, count, todo, lambda k: (k > 0) & (k & 1 == 0)
    )

    def regroup(group, carry):
        loading(group).wait()

        def load(q):
            return blocks[group, :, q * LANES : (q + 1) * LANES]

        limit = blocks.shape[2] // LANES - 1
        for row in range(ROWS):
            q, o = divmod(row * BW, LANES)
            p = (ROWS + row) * BW // LANES
            if o == 0:
                value = jnp.where(lane >= HALF, load(p), load(q))
            elif o <= HALF:
                low = load(p if o == HALF else min(p + 1, limit))
                value = jnp.where(lane >= o, load(q), low)
                if o < HALF:
                    value = jnp.where(lane >= o + HALF, load(p), value)
            else:
                value = jnp.where(lane >= o - HALF, load(p), load(q + 1))
                value = jnp.where(lane >= o, load(q), value)
            at = pl.multiple_of(group * (ROWS * SUB) + row * SUB, SUB)
            flat[pl.ds(at, SUB), :] = turn(value, -o)
        return carry

    lax.fori_loop(0, groups, regroup, 0)
    fill_strips(n, bx_n, by_n, me, dest, flat, strips, todo, found)
    for k in range(2, n, 2):
        assemble(outs[k // 2 - 1], k, cap, source, flat, strips)


def second_kernel(n, cap, bx_n, by_n, *refs):
    me_ref, dest_hbm, flat, kmt_hbm, kappa_hbm = refs[:5]
    outs = refs[5 : n // 2 + 6]
    dest, source, todo, kmt, kappa, strips, edges, count, sems = refs[n // 2 + 6 :]
    me = me_ref[0]
    lane = lanes()
    length = outs[0].shape[0]
    cols = kmt.shape[1]
    first, *copies = [
        pltpu.make_async_copy(dest_hbm, dest, sems.at[0]),
        pltpu.make_async_copy(kmt_hbm, kmt, sems.at[1]),
        pltpu.make_async_copy(kappa_hbm, kappa, sems.at[2]),
    ]
    for copy in (first, *copies):
        copy.start()
    first.wait()
    found = plan(
        n, cap, bx_n, me, dest, source, count, todo, lambda k: (k == 0) | (k & 1 == 1)
    )
    fill_strips(n, bx_n, by_n, me, dest, flat, strips, todo, found)
    for copy in copies:
        copy.wait()
    zero = jnp.zeros((SUB, LANES), F32)
    for at in range(0, edges.shape[1], SUB):
        for side in range(2):
            edges[side, at : at + SUB, :] = zero
    for side, start in ((0, cols - HALO), (1, 0)):
        tile = start // LANES * LANES
        width = min(LANES, cols - tile)
        for piece in range(by_n * (1 + LEV)):
            by, ch = divmod(piece, 1 + LEV)
            base, target = edge_spot(cap, piece)
            if piece >= 4 * cap:
                base -= cap * ROWS + BH - 2 * cap * BH
            here = (lane >= target) & (lane < target + HALO)
            for row in range(0, BH, SUB):
                at = slice(by * BH + row, by * BH + row + SUB)
                if ch == 0:
                    value = kmt[at, tile : tile + width].astype(F32)
                else:
                    value = kappa[ch - 1, at, tile : tile + width]
                if width < LANES:
                    value = jnp.concatenate([value, zero[:, width:]], axis=1)
                pltpu.store(
                    edges.at[side, base + row : base + row + SUB, :],
                    turn(value, target - (start - tile)),
                    mask=here,
                )
    eastern = lax.bitwise_xor(lax.rem(me + 1, n), me)
    in_blocks = min(edges.shape[1], 2 * cap * BH)
    for out, k in zip(outs, [0, *range(1, n, 2)]):
        which = jnp.where(eastern == k, 0, 1)
        assemble(out, k, cap, source, flat, strips, edges, which, in_blocks)
        if length > cap * ROWS + BH:
            for row in range(0, BH, SUB):
                at = cap * ROWS + BH + row
                out[at : at + SUB, :] = edges[
                    which, in_blocks + row : in_blocks + row + SUB, :
                ]


def base_kernel(n, cap, bx_n, by_n, me_ref, dest, kmt, kappa, table, grid, bringer):
    me = me_ref[0]
    slots = bx_n * by_n
    channels, tiles, deep, _ = grid.shape
    cols = kmt.shape[1]
    zero = jnp.zeros((SUB, LANES), F32)
    west = lax.rem(me + n - 1, n)
    east = lax.rem(me + 1, n)
    for at in range(n * (cap + 1)):
        table[at] = -1
    sides = [(west, by * bx_n + bx_n - 1) for by in range(by_n)]
    sides += [(east, by * bx_n) for by in range(by_n)]
    for owner, spot in sides:
        bringer[owner * slots + spot + 1] = -1

    def owner_loop(s, carry):
        k = lax.bitwise_xor(s, me)

        def slot_loop(i, c):
            d = dest[0, s * slots + i]
            bringer[d + 1] = k
            spot = d - me * slots
            mine = (spot >= 0) & (spot < slots)
            table[k * (cap + 1) + c] = jnp.where(mine, spot, -1)
            return c + mine.astype(jnp.int32)

        lax.fori_loop(0, slots, slot_loop, 0, unroll=8)
        return carry

    lax.fori_loop(0, n, owner_loop, 0)
    counts = n * (cap + 1)
    lists = counts + n + 1
    for k in range(n + 1):
        table[counts + k] = 0
    for at, (owner, spot) in enumerate(sides):
        k = bringer[owner * slots + spot + 1]
        k = jnp.where(k < 0, n, k)
        c = table[counts + k]
        table[counts + k] = c + 1
        table[lists + k * len(sides) + c] = at

    def clear(g, carry):
        at = pl.ds(pl.multiple_of(g * SUB, SUB), SUB)
        for ch in range(channels):
            for j in range(tiles):
                grid[ch, j, at, :] = zero
        return carry

    lax.fori_loop(0, deep // SUB, clear, 0)

    def lay(g, carry):
        at = pl.ds(pl.multiple_of(g * SUB, SUB), SUB)
        out = pl.ds(pl.multiple_of(g * SUB + PAD, SUB), SUB)
        for ch in range(1 + LEV):
            for j in range(tiles):
                width = min(LANES, cols - j * LANES)
                part = slice(j * LANES, j * LANES + width)
                if ch == 0:
                    value = kmt[at, part].astype(F32)
                else:
                    value = kappa[ch - 1, at, part]
                grid[ch, j, out, 0:width] = value
        return carry

    lax.fori_loop(0, kmt.shape[0] // SUB, lay, 0)


def place_kernel(n, cap, bx_n, by_n, cols, which, *refs):
    count = len(which)
    me_ref, table, _ = refs[:3]
    odd = me_ref[1]
    packs = refs[3 : 3 + count]
    grid, *rims = refs[3 + count :]
    me = me_ref[0]
    lane = lanes()
    channels, tiles, deep, _ = grid.shape
    last = tiles - 1
    own = cols - last * LANES
    halo_lane = (own, LANES - HALO)

    def mark(ch, at, value, start):
        here = (lane >= start) & (lane < start + HALO)
        pltpu.store(grid.at[ch, last, at, :], value, mask=here)

    for k, pack in zip(which, packs):

        for c in range(cap):
            spot = table[k * (cap + 1) + c]
            valid = spot >= 0
            spot = jnp.maximum(spot, 0)
            by = lax.div(spot, bx_n)
            offset = lax.rem(spot, bx_n) * BW
            tile = lax.div(offset, LANES)
            following = jnp.minimum(tile + 1, last)
            start = lax.rem(offset, LANES)
            begin = jnp.where(valid, start, LANES)
            here = (lane >= begin) & (lane < begin + BW)
            spill = lane < jnp.where(valid, start + BW - LANES, 0)
            for row in range(0, BH, SUB):
                at = pl.ds(pl.multiple_of(by * BH + row + PAD, SUB), SUB)
                depth = grid[0, tile, at, :], grid[0, following, at, :]
                for level in range(LEV):
                    place = c * ROWS + level * BH + row
                    value = pack[place : place + SUB, :]
                    masks = here & (depth[0] > level), spill & (depth[1] > level)
                    for tracer in range(2):
                        ch = 1 + LEV + tracer * LEV + level
                        turned = pltpu.roll(
                            value, lax.rem(start + tracer * HALF, LANES), 1
                        )
                        for target, mask in zip((tile, following), masks):
                            pltpu.store(grid.at[ch, target, at, :], turned, mask=mask)

        counts = n * (cap + 1)
        lists = counts + n + 1 + k * 2 * by_n

        def strip(at, carry, pack=pack, lists=lists):
            index = table[lists + at]
            by = lax.rem(index, by_n)
            start = jnp.where(index < by_n, halo_lane[1], halo_lane[0])
            for row in range(0, BH, SUB):
                rows = pl.ds(pl.multiple_of(by * BH + row + PAD, SUB), SUB)
                value = pack[cap * ROWS + row : cap * ROWS + row + SUB, :]
                for level in range(LEV):
                    for tracer in range(2):
                        origin = strip_lane(0, index, level, tracer, by_n)
                        amount = lax.rem(start - origin + LANES, LANES)
                        mark(
                            1 + LEV + tracer * LEV + level,
                            rows,
                            pltpu.roll(value, amount, 1),
                            start,
                        )
            return carry

        lax.fori_loop(0, table[counts + k], strip, 0)

        for neighbour, start in ((me + n - 1, halo_lane[1]), (me + 1, halo_lane[0])):
            if k % 2 == 0:
                continue

            @pl.when(lax.bitwise_xor(lax.rem(neighbour, n), me) == k)
            def _(start=start, pack=pack):
                for piece in range(by_n * (1 + LEV)):
                    by, ch = divmod(piece, 1 + LEV)
                    base, origin = edge_spot(cap, piece)
                    for row in range(0, BH, SUB):
                        at = by * BH + row + PAD
                        mark(
                            ch,
                            slice(at, at + SUB),
                            turn(pack[base + row : base + row + SUB, :], start - origin),
                            start,
                        )

    if not rims:
        return
    rim = (lane >= own) & (lane < own + HALO) | (lane >= LANES - HALO)

    def mask(g, carry):
        at = pl.ds(pl.multiple_of(g * SUB + PAD, SUB), SUB)
        wet = grid[0, last, at, :]
        for ch in range(1 + LEV, channels):
            level = (ch - 1 - LEV) % LEV
            grid[ch, last, at, :] = jnp.where(
                rim & (wet <= level), 0.0, grid[ch, last, at, :]
            )
        return carry

    lax.fori_loop(0, deep // SUB - 2, mask, 0, unroll=4)
    low = deep - PAD - HALO
    for rows, first in zip(rims, (1 - odd, odd)):
        at = jnp.where(first == 1, PAD, low)
        for ch in range(channels):
            for j in range(tiles):
                rows[j, ch * HALO : (ch + 1) * HALO, :] = grid[
                    ch, j, pl.ds(at, HALO), :
                ]


def sideways(values):
    lane = lanes()
    count = len(values)
    left = [turn(v, 1) for v in values]
    right = [turn(v, -1) for v in values]
    west = [
        jnp.where(lane == 0, left[(j - 1) % count], left[j]) for j in range(count)
    ]
    east = [
        jnp.where(lane == LANES - 1, right[(j + 1) % count], right[j])
        for j in range(count)
    ]
    return east, west


def three(load, start):
    return load(start), load(start - 1), load(start + 1)


def diffuse(load, start):
    tiles = len(load(0, start))
    span = range(tiles)
    level_c, level_a, level_b = three(functools.partial(load, 0), start)
    level_e, _ = sideways(level_c)
    both_e = [jnp.minimum(level_c[j], level_e[j]) for j in span]
    both_a = [jnp.minimum(level_c[j], level_a[j]) for j in span]
    both_b = [jnp.minimum(level_c[j], level_b[j]) for j in span]
    forcing = [None] * tiles
    fresh = [[None] * LEV for _ in range(2)]
    for level in range(LEV):
        kappa_c, kappa_a, kappa_b = three(functools.partial(load, 1 + level), start)
        kappa_e, _ = sideways(kappa_c)
        face_e, face_a, face_b = (
            [jnp.where(both[j] > level, kappa_c[j] + other[j], 0.0) for j in span]
            for both, other in (
                (both_e, kappa_e),
                (both_a, kappa_a),
                (both_b, kappa_b),
            )
        )
        for tracer in range(2):
            ch = 1 + LEV + tracer * LEV + level
            here, above, below = three(functools.partial(load, ch), start)
            to_east, _ = sideways(here)
            flux = [face_e[j] * (to_east[j] - here[j]) for j in span]
            _, flux_w = sideways(flux)
            fresh[tracer][level] = [
                jnp.where(
                    level_c[j] > level,
                    here[j]
                    + 0.5
                    * (
                        (flux[j] - flux_w[j])
                        + face_a[j] * (above[j] - here[j])
                        + face_b[j] * (below[j] - here[j])
                    ),
                    0.0,
                )
                for j in span
            ]
        thickness = 1.0 + 0.5 * level
        for j in span:
            temp, salt = fresh[0][level][j], fresh[1][level][j]
            density = haline * salt - temp * (thermal + cabbeling * temp)
            if level:
                density = forcing[j] + thickness * density
            forcing[j] = density
    return fresh, forcing


def apply(here, above, below, levels):
    span = range(len(here))
    pair = [above[j] + below[j] for j in span]
    mixed = [here[j] + 0.5 * pair[j] for j in span]
    east, west = sideways(mixed)
    result = []
    for j in span:
        diagonal = 6.0 - SHIFT + 1.0
        total = jnp.full((SUB, LANES), diagonal / SCALE, F32)
        for k in range(1, LEV):
            diagonal += 1.0 + 0.5 * k
            total = jnp.where(levels[j] > k, diagonal / SCALE, total)
        total = total * here[j] - (pair[j] + (east[j] + west[j])) * (1.0 / SCALE)
        result.append(jnp.where(levels[j] > 0, total, 0.0))
    return result


def gather_products(carry, powers, centre, keep):
    carry = list(carry)
    span = range(len(powers[0]))
    for j in span:
        q0, q1, q2, q3 = (keep(q[j], j) for q in powers)
        b1 = q1 - centre * q0
        c2 = q2 - centre * q1
        c3 = q3 - centre * q2
        b2 = c2 - centre * b1
        b3 = (c3 - centre * c2) - centre * b2
        terms = (q0, b1, b2, b3)
        for at, (x, y) in enumerate(PAIRS):
            carry[at] = carry[at] + terms[x] * terms[y]
    return tuple(carry)


def total_row(totals):
    lane = lanes()[:1]
    row = jnp.zeros((1, LANES), F32)
    for at, total in enumerate(totals):
        total = jnp.sum(total, axis=(0, 1), keepdims=True)
        row = jnp.where(lane == at + 1, total, row)
    return row


def put_tracer(target, fresh, cols, at):
    for tracer in range(2):
        for level in range(LEV):
            for j, value in enumerate(fresh[tracer][level]):
                width = min(LANES, cols - j * LANES)
                target[tracer, level, at, j * LANES : j * LANES + width] = value[
                    :, :width
                ]


def inner_kernel(cols, grid, tracer_out, powers, sums, edges, fresh_rows, sems):
    lane = lanes()
    line = lax.broadcasted_iota(jnp.int32, (SUB, LANES), 0)
    _, tiles, deep, _ = grid.shape
    own = cols - (tiles - 1) * LANES
    first, end = PAD // SUB, (deep - PAD) // SUB
    zero = jnp.zeros((SUB, LANES), F32)

    def rows(ref, lead, start):
        return [ref[lead, j, pl.ds(start, SUB), :] for j in range(tiles)]

    def top(g):
        return pl.multiple_of(g * SUB, SUB)

    def step(g, carry):
        fresh, forcing = diffuse(functools.partial(rows, grid), top(g))
        put_tracer(
            fresh_rows, fresh, cols, pl.ds(pl.multiple_of(g * SUB - PAD, SUB), SUB)
        )
        for j in range(tiles):
            powers[0, j, pl.ds(top(g), SUB), :] = forcing[j]
        return carry

    chunks = sems.shape[0]
    size = (end - first) // chunks
    copies = []
    for chunk in range(chunks):
        begin = first + chunk * size
        stop = end if chunk == chunks - 1 else begin + size
        lax.fori_loop(begin, stop, step, 0, unroll=2)
        at = pl.ds(begin * SUB - PAD, (stop - begin) * SUB)
        copies.append(
            pltpu.make_async_copy(
                fresh_rows.at[:, :, at, :], tracer_out.at[:, :, at, :], sems.at[chunk]
            )
        )
        copies[-1].start()
    height = fresh_rows.shape[2]
    for tracer in range(2):
        for level in range(LEV):
            for side, row in ((0, 0), (1, height - SUB)):
                edges[side, tracer, level] = fresh_rows[
                    tracer, level, row : row + SUB, :
                ]

    def inside(value, j):
        return value if j < tiles - 1 else jnp.where(lane < own, value, 0.0)

    def upper(value, j):
        return jnp.where(line >= HALO, inside(value, j), 0.0)

    def lower(value, j):
        return jnp.where(line < SUB - HALO, inside(value, j), 0.0)

    def power(g, source):
        here, above, below = three(functools.partial(rows, powers, source), top(g))
        return here, apply(here, above, below, rows(grid, 0, top(g)))

    def put(g, target):
        here, result = power(g, target - 1)
        for j in range(tiles):
            powers[target, j, pl.ds(top(g), SUB), :] = result[j]
        return here, result

    def first_power(g, carry, keep=inside):
        here, result = put(g, 1)
        a, b = carry
        for j in range(tiles):
            v = keep(here[j], j)
            a = a + v * v
            b = b + v * keep(result[j], j)
        return a, b

    def everywhere(body, carry):
        carry = body(first, carry, upper)
        carry = lax.fori_loop(first + 1, end - 1, body, carry, unroll=end - first - 2)
        return body(end - 1, carry, lower)

    a, b = everywhere(first_power, (zero, zero))
    a = jnp.sum(a, axis=(0, 1), keepdims=True)
    b = jnp.sum(b, axis=(0, 1), keepdims=True)
    centre = jnp.where(a > 0, b / jnp.where(a > 0, a, 1.0), 0.0)
    centre = jnp.broadcast_to(centre, (SUB, LANES))
    lax.fori_loop(
        first, end, lambda g, c: (put(g, 2), c)[1], 0, unroll=end - first
    )

    def products(g, carry, keep=inside):
        here, result = power(g, 2)
        lower_powers = [rows(powers, k, top(g)) for k in range(2)]
        return gather_products(carry, (*lower_powers, here, result), centre, keep)

    totals = everywhere(products, (zero,) * len(PAIRS))
    for at, total in enumerate((*totals, centre)):
        sums[at] = total
    for copy in copies:
        copy.wait()


def border_kernel(
    cols, me_ref, grid, other_rows, pair_rows, powers, part, edges, border, sums,
    fresh_rows, field, local,
):
    lane = lanes()
    line = lax.broadcasted_iota(jnp.int32, (SUB, LANES), 0)
    channels, tiles, deep, _ = grid.shape
    own = cols - (tiles - 1) * LANES
    half = EDGE // 2
    even = me_ref[1] == 0
    for ch in range(channels):
        for j in range(tiles):
            at = slice(ch * HALO, (ch + 1) * HALO)
            field[0, ch, j, half : half + SUB, :] = grid[ch, j, PAD : PAD + SUB, :]
            field[1, ch, j, half - SUB : half, :] = grid[
                ch, j, deep - PAD - SUB : deep - PAD, :
            ]
            pair, other = pair_rows[j, at, :], other_rows[j, at, :]
            field[0, ch, j, half - HALO : half, :] = jnp.where(even, other, pair)
            field[1, ch, j, half : half + HALO, :] = jnp.where(even, pair, other)
    for k in range(3):
        for j in range(tiles):
            local[0, k, j, half : half + SUB, :] = powers[k, j, PAD : PAD + SUB, :]
            local[1, k, j, half - SUB : half, :] = powers[
                k, j, deep - PAD - SUB : deep - PAD, :
            ]
    centre = part[len(PAIRS)]

    def rows_of(side):
        def rows(ref, lead, start):
            return [ref[side, lead, j, pl.ds(start, SUB), :] for j in range(tiles)]

        return rows

    start = half - HALO
    for side in range(2):
        fresh, forcing = diffuse(functools.partial(rows_of(side), field), start)
        for j in range(tiles):
            local[side, 0, j, start : start + SUB, :] = forcing[j]
        mine = line == (0 if side == 0 else SUB - 1)
        for tracer in range(2):
            for level in range(LEV):
                for j in range(tiles):
                    width = min(LANES, cols - j * LANES)
                    part_lanes = slice(j * LANES, j * LANES + width)
                    moved = pltpu.roll(fresh[tracer][level][j], HALO, 0)
                    fresh_rows[side, tracer, level, :, part_lanes] = jnp.where(
                        mine[:, :width],
                        moved[:, :width],
                        edges[side, tracer, level, :, part_lanes],
                    )

    def power(side, source):
        rows = rows_of(side)
        here, above, below = three(functools.partial(rows, local, source), start)
        return here, apply(here, above, below, rows(field, 0, start))

    for target in range(1, 3):
        for side in range(2):
            result = power(side, target - 1)[1]
            for j in range(tiles):
                local[side, target, j, start : start + SUB, :] = result[j]
    totals = tuple(part[at] for at in range(len(PAIRS)))
    for side in range(2):
        here, result = power(side, 2)
        lower_powers = [rows_of(side)(local, k, start) for k in range(2)]
        own_rows = half - side * SUB
        for k in range(3):
            for j in range(tiles):
                border[side, k, j] = local[side, k, j, own_rows : own_rows + SUB, :]
        bound = (1 - side) * HALO
        rim = (line >= bound) & (line < bound + HALO)

        def keep(value, j, rim=rim):
            inside = rim if j < tiles - 1 else rim & (lane < own)
            return jnp.where(inside, value, 0.0)

        totals = gather_products(
            totals, (*lower_powers, here, result), centre, keep
        )
    row = jnp.where(lane[:1] == 0, centre[:1], total_row(totals))
    sums[...] = jnp.broadcast_to(row, sums.shape)


PAIRS = ((0, 0), (0, 1), (0, 2), (0, 3), (1, 1), (1, 2), (1, 3), (2, 2), (2, 3))


def combine_kernel(
    cols, sums, powers, border, fresh_rows, tracer_in, tracer_out, stream_out, stream, sems
):
    rows = tracer_out.shape[2]
    patches = [
        pltpu.make_async_copy(
            fresh_rows.at[side],
            tracer_out.at[:, :, pl.ds(side * (rows - SUB), SUB), :],
            sems.at[2 + side],
        )
        for side in range(2)
    ]
    for copy in patches:
        copy.start()
    values = sums[...]
    lane = lax.broadcasted_iota(jnp.int32, values.shape, 1)

    def column(k):
        return jnp.sum(jnp.where(lane == k, values, 0.0), axis=1, keepdims=True)

    centre = column(0)
    gram = {pair: column(at + 1) for at, pair in enumerate(PAIRS)}

    def local(c):
        c = list(c) + [None] * (4 - len(c))
        c0, c1, c2, c3 = c
        result = [c0 + jnp.zeros_like(centre)]
        if c1 is not None:
            inner = c1
            slope = c1 + jnp.zeros_like(centre)
            if c2 is not None:
                inner = c1 + centre * (c2 if c3 is None else c2 + centre * c3)
                slope = c1 + centre * (
                    2.0 * c2 if c3 is None else 2.0 * c2 + 3.0 * (centre * c3)
                )
            result = [c0 + centre * inner, slope]
        if c2 is not None:
            result.append(c2 + jnp.zeros_like(centre) if c3 is None else c2 + 3.0 * (centre * c3))
        if c3 is not None:
            result.append(c3 + jnp.zeros_like(centre))
        return result

    def inner(x, y):
        u, v = local(x), local(y)
        total = jnp.zeros_like(centre)
        for i in range(len(u)):
            for j in range(len(v)):
                total = total + (u[i] * v[j]) * gram[(min(i, j), max(i, j))]
        return jnp.sum(total, axis=0, keepdims=True)

    def operate(c):
        result = [SHIFT * x for x in c] + [None]
        for i, x in enumerate(c):
            term = SCALE * x
            result[i + 1] = term if result[i + 1] is None else result[i + 1] + term
        return result

    one = jnp.ones((1, 1), F32)
    stream_c = [None] * 3
    residual, direction = [one], [one]
    norm = inner(residual, residual)
    for step in range(3):
        image = operate(direction)
        alpha = norm / inner(direction, image)
        for i, x in enumerate(direction):
            stream_c[i] = alpha * x if stream_c[i] is None else stream_c[i] + alpha * x
        if step == 2:
            break
        residual = [
            (residual[i] - alpha * image[i]) if i < len(residual) else -alpha * image[i]
            for i in range(len(image))
        ]
        fresh = inner(residual, residual)
        ratio = fresh / norm
        direction = [
            (residual[i] + ratio * direction[i]) if i < len(direction) else residual[i]
            for i in range(len(residual))
        ]
        norm = fresh

    tiles = powers.shape[1]
    height = stream.shape[0]
    weights = [jnp.broadcast_to(c, (SUB, LANES)) for c in stream_c]

    def put(out, load):
        for j in range(tiles):
            width = min(LANES, cols - j * LANES)
            value = sum(weights[k] * load(k, j) for k in range(3))
            stream[out, j * LANES : j * LANES + width] = value[:, :width]

    def write(g, carry):
        at = pl.ds(pl.multiple_of(g * SUB + PAD, SUB), SUB)
        out = pl.ds(pl.multiple_of(g * SUB, SUB), SUB)
        put(out, lambda k, j: powers[k, j, at, :])
        return carry

    middle = height // SUB // 2 * SUB
    copies = [
        pltpu.make_async_copy(stream.at[part, :], stream_out.at[part, :], sems.at[at])
        for at, part in enumerate((pl.ds(0, middle), pl.ds(middle, height - middle)))
    ]
    put(slice(0, SUB), lambda k, j: border[0, k, j])
    lax.fori_loop(1, middle // SUB, write, 0, unroll=3)
    copies[0].start()
    lax.fori_loop(middle // SUB, height // SUB - 1, write, 0, unroll=3)
    put(slice(height - SUB, height), lambda k, j: border[1, k, j])
    copies[1].start()
    for copy in (*patches, *copies):
        copy.wait()


def body(checkpoint, slot_dest, kmt, kappa):
    n = lax.axis_size("lon")
    lats = lax.axis_size("lat")
    lat = lax.axis_index("lat")
    me = jnp.stack([lax.axis_index("lon"), lax.rem(lat, 2)]).astype(jnp.int32)
    _, slots, values = checkpoint.shape
    rows, cols = kmt.shape
    by_n, bx_n = rows // BH, cols // BW
    cap = slots // n
    length = package_rows(cap, by_n)
    tiles = -(-(cols + 2 * HALO) // LANES)
    groups = slots // SUB
    edge_rows = -(-by_n * (1 + LEV) // 2) * BH
    if by_n * (1 + LEV) > 4 * cap:
        edge_rows = 2 * cap * BH + BH

    def fixed(value):
        return pltpu.with_memory_space_constraint(value, pltpu.HBM)

    kernels = (n, cap, bx_n, by_n)
    lists = [
        pltpu.SMEM((1, n * slots), jnp.int32),
        pltpu.SMEM((n * cap + 1,), jnp.int32),
        pltpu.SMEM((slots + 1,), jnp.int32),
    ]
    *packs, flat = pl.pallas_call(
        functools.partial(first_kernel, *kernels),
        out_shape=[shaped(length, LANES)] * (n // 2 - 1)
        + [shaped(slots * ROWS, LANES)],
        in_specs=[SM, HB, HB],
        out_specs=[VM] * (n // 2),
        scratch_shapes=lists
        + [
            pltpu.VMEM((groups, SUB, values), F32),
            pltpu.VMEM((n, BH, LANES), F32),
            pltpu.SMEM((n + 1,), jnp.int32),
            pltpu.SemaphoreType.DMA((groups + 1,)),
        ],
        compiler_params=params(),
        cost_estimate=cost(2 << 20, 4 << 20),
        name="first",
    )(me, fixed(slot_dest), fixed(checkpoint))

    def send(value, k):
        return lax.ppermute(value, "lon", [(i, i ^ k) for i in range(n)])

    order = sorted(range(1, n), key=lambda k: (k & 1, k < 2, -bin(k >> 1).count("1"), k))
    received = {k: send(packs[k // 2 - 1], k) for k in order if k % 2 == 0}
    own, *packs = pl.pallas_call(
        functools.partial(second_kernel, *kernels),
        out_shape=[shaped(length, LANES)] * (n // 2 + 1),
        in_specs=[SM, HB, VM, HB, HB],
        out_specs=[VM] * (n // 2 + 1),
        scratch_shapes=lists
        + [
            pltpu.VMEM((rows, cols), jnp.int32),
            pltpu.VMEM((LEV, rows, cols), F32),
            pltpu.VMEM((n, BH, LANES), F32),
            pltpu.VMEM((2, edge_rows, LANES), F32),
            pltpu.SMEM((n + 1,), jnp.int32),
            pltpu.SemaphoreType.DMA((3,)),
        ],
        compiler_params=params(),
        cost_estimate=cost(2 << 20, 4 << 20),
        name="second",
    )(me, fixed(slot_dest), flat, fixed(kmt), fixed(kappa))
    received |= {k: send(packs[k // 2], k) for k in order if k % 2}
    received[0] = own

    channels = 1 + 3 * LEV
    deep = rows + 2 * PAD
    table, grid = pl.pallas_call(
        functools.partial(base_kernel, n, cap, bx_n, by_n),
        out_shape=[
            shaped(n * (cap + 1) + (n + 1) * (1 + 2 * by_n), dtype=jnp.int32),
            shaped(channels, tiles, deep, LANES),
        ],
        in_specs=[SM, SM, VM, VM],
        out_specs=[SM, VM],
        scratch_shapes=[pltpu.SMEM((n * slots + 1,), jnp.int32)],
        compiler_params=params(),
        cost_estimate=cost(1 << 20, 2 << 20),
        name="base",
    )(me, slot_dest, kmt, kappa)

    def held(value):
        return pltpu.with_memory_space_constraint(value, pltpu.VMEM)

    rim = -(-channels * HALO // SUB) * SUB
    half, quarter = n // 2 - 1, n // 4
    odd = order[half:]
    parts = [
        [0] + order[:half],
        odd[-1:] + odd[: quarter - 1],
        odd[quarter - 1 : -1],
    ]
    for stage, which in enumerate(parts):
        shapes = [shaped(channels, tiles, deep, LANES)]
        if stage == len(parts) - 1:
            shapes += [shaped(tiles, rim, LANES)] * 2
        grid, *rims = pl.pallas_call(
            functools.partial(place_kernel, n, cap, bx_n, by_n, cols, which),
            out_shape=shapes,
            in_specs=[SM, SM] + [VM] * (1 + len(which)),
            out_specs=[VM] * len(shapes),
            input_output_aliases={2: 0},
            compiler_params=params(),
            cost_estimate=cost(2 << 20, 2 << 20),
            name=f"place{stage}",
        )(me, table, held(grid), *[received[k] for k in which])

    swaps = [
        [(i, i ^ 1) for i in range(lats) if i ^ 1 < lats],
        [(i, j) for i in range(lats) for j in [(i - 1 ^ 1) + 1] if 0 <= j < lats],
    ]
    other_rows, pair_rows = (
        lax.ppermute(value, "lat", swap) for value, swap in zip(rims, swaps[::-1])
    )

    devices = n * lats
    tracer_shape = shaped(2, LEV, rows, cols)
    tracer, powers, part, edges = pl.pallas_call(
        functools.partial(inner_kernel, cols),
        out_shape=[
            tracer_shape,
            shaped(3, tiles, deep, LANES),
            shaped(len(PAIRS) + 1, SUB, LANES),
            shaped(2, 2, LEV, SUB, cols),
        ],
        in_specs=[VM],
        out_specs=[HB, VM, VM, VM],
        scratch_shapes=[
            pltpu.VMEM((2, LEV, rows, cols), F32),
            pltpu.SemaphoreType.DMA((5,)),
        ],
        compiler_params=params(),
        cost_estimate=cost(16 << 20, 6 << 20),
        name="inner",
    )(grid)
    border, sums, fresh_rows = pl.pallas_call(
        functools.partial(border_kernel, cols),
        out_shape=[
            shaped(2, 3, tiles, SUB, LANES),
            shaped(devices, LANES),
            shaped(2, 2, LEV, SUB, cols),
        ],
        in_specs=[SM, VM, VM, VM, VM, VM, VM],
        out_specs=[VM, VM, VM],
        scratch_shapes=[
            pltpu.VMEM((2, channels, tiles, EDGE, LANES), F32),
            pltpu.VMEM((2, 3, tiles, EDGE, LANES), F32),
        ],
        compiler_params=params(),
        cost_estimate=cost(2 << 20, 1 << 20),
        name="border",
    )(me, grid, other_rows, pair_rows, powers, part, edges)

    everyone = lax.all_to_all(sums, ("lon", "lat"), 0, 0, tiled=True)
    tracer, stream = pl.pallas_call(
        functools.partial(combine_kernel, cols),
        out_shape=[tracer_shape, shaped(rows, cols)],
        in_specs=[VM, VM, VM, VM, HB],
        out_specs=[HB, HB],
        scratch_shapes=[
            pltpu.VMEM((rows, cols), F32),
            pltpu.SemaphoreType.DMA((4,)),
        ],
        input_output_aliases={4: 0},
        compiler_params=params(),
        cost_estimate=cost(1 << 20, 2 << 20),
        name="combine",
    )(everyone, powers, border, fresh_rows, fixed(tracer))
    return tracer, stream


def solution(mesh):
    placed = (P("lat", "lon", None), P("lat", None), P("lat", "lon"), P(None, "lat", "lon"))
    return jax.shard_map(
        body,
        mesh=mesh,
        in_specs=placed,
        out_specs=(P(None, None, "lat", "lon"), P("lat", "lon")),
        check_vma=False,
    )
```

```python
import functools

import jax
import jax.numpy as jnp
from jax import lax
from jax.experimental import pallas as pl
from jax.experimental.pallas import tpu as pltpu
from jax.sharding import PartitionSpec as P


BH = 40
BW = 60
LEV = 2
HALO = 4
LANES = 128
SUB = 8
PAD = SUB
EDGE = 4 * SUB
ROWS = LEV * BH
HALF = LANES // 2
SHIFT = 8.0
SCALE = 8.0

thermal = 0.25
haline = 0.75
cabbeling = 0.05

VM = pl.BlockSpec(memory_space=pltpu.VMEM)
SM = pl.BlockSpec(memory_space=pltpu.SMEM)
HB = pl.BlockSpec(memory_space=pltpu.HBM)
F32 = jnp.float32


def params():
    return pltpu.CompilerParams(vmem_limit_bytes=24 << 20)


def cost(flops, moved):
    return pl.CostEstimate(flops=flops, bytes_accessed=moved, transcendentals=0)


def shaped(*dims, dtype=F32):
    return jax.ShapeDtypeStruct(dims, dtype)


def lanes():
    return lax.broadcasted_iota(jnp.int32, (SUB, LANES), 1)


def turn(value, amount):
    if isinstance(amount, int):
        amount %= LANES
        if amount == 0:
            return value
    return pltpu.roll(value, amount, 1)


def strip_lane(side, by, level, tracer, block_rows):
    return HALO * ((side * block_rows + by) * LEV + level) + HALF * tracer


def edge_spot(cap, piece):
    if piece < 4 * cap:
        return piece // 2 * BH, HALF * (1 + piece % 2) - HALO
    return cap * ROWS + BH, HALO * (piece - 4 * cap)


def package_rows(cap, by_n):
    return cap * ROWS + (2 * BH if by_n * (1 + LEV) > 4 * cap else BH)


def block_rows(flat, start, row):
    return flat[pl.ds(start + row * SUB, SUB, stride=SUB), :]


def block_start(i):
    return lax.div(i, SUB) * (ROWS * SUB) + lax.rem(i, SUB)


def plan(n, cap, bx_n, me, dest, source, count, todo, wanted):
    slots = todo.shape[0] - 1
    for k in range(n + 1):
        count[k] = 0
    for at in range(n * cap + 1):
        source[at] = 0

    def assign(i, found):
        d = dest[0, me * slots + i]
        used = d >= 0
        place = jnp.maximum(d, 0)
        owner = lax.div(place, slots)
        k = jnp.where(used, lax.bitwise_xor(owner, me), n)
        c = count[k]
        count[k] = c + 1
        source[jnp.where(used, k * cap + c, n * cap)] = block_start(i)
        bx = lax.rem(place, bx_n)
        partner = lax.bitwise_xor(
            lax.rem(owner + jnp.where(bx == 0, n - 1, 1), n), me
        )
        todo[found] = i
        holds = used & ((bx == 0) | (bx == bx_n - 1)) & wanted(partner)
        return found + holds.astype(jnp.int32)

    return lax.fori_loop(0, slots, assign, 0, unroll=4)


def fill_strips(n, bx_n, by_n, me, dest, flat, strips, todo, found):
    slots = bx_n * by_n
    spot_lane = lanes() & (HALF - 1)

    def strip(at, carry):
        i = todo[at]
        place = dest[0, me * slots + i]
        spot = lax.rem(place, slots)
        by = lax.div(spot, bx_n)
        side = (lax.rem(spot, bx_n) == 0).astype(jnp.int32)
        owner = lax.div(place, slots)
        k = lax.bitwise_xor(lax.rem(owner + jnp.where(side == 0, 1, n - 1), n), me)
        start = block_start(i)
        origin = jnp.where(side == 0, BW - HALO, 0)
        for level in range(LEV):
            target = strip_lane(side, by, level, 0, by_n)
            amount = lax.rem(target - origin + LANES, LANES)
            here = (spot_lane >= target) & (spot_lane < target + HALO)
            for row in range(0, BH, SUB):
                value = block_rows(flat, start, level * BH + row)
                pltpu.store(
                    strips.at[k, row : row + SUB, :],
                    pltpu.roll(value, amount, 1),
                    mask=here,
                )
        return carry

    lax.fori_loop(0, found, strip, 0)


def assemble(out, k, cap, source, flat, strips, edges=None, which=None, in_blocks=0):
    spare = (lanes() & (HALF - 1)) >= HALF - HALO
    for c in range(cap):
        start = source[k * cap + c]
        for row in range(0, ROWS, SUB):
            value = block_rows(flat, start, row)
            at = c * ROWS + row
            if at < in_blocks:
                value = jnp.where(spare, edges[which, at : at + SUB, :], value)
            out[at : at + SUB, :] = value
    for row in range(0, BH, SUB):
        at = cap * ROWS + row
        out[at : at + SUB, :] = strips[k, row : row + SUB, :]


def first_kernel(n, cap, bx_n, by_n, *refs):
    me_ref, dest_hbm, blocks_hbm = refs[:3]
    outs = refs[3 : n // 2 + 2]
    flat, dest, source, todo, blocks, strips, count, sems = refs[n // 2 + 2 :]
    groups = blocks.shape[0]
    slots = groups * SUB
    me = me_ref[0]
    lane = lanes()
    first = pltpu.make_async_copy(dest_hbm, dest, sems.at[groups])
    first.start()

    def loading(g):
        rows = pl.ds(pl.multiple_of(g * SUB, SUB), SUB)
        return pltpu.make_async_copy(
            blocks_hbm.at[0, rows, :], blocks.at[g], sems.at[g]
        )

    for g in range(groups):
        loading(g).start()
    first.wait()
    found = plan(
        n, cap, bx_n, me, dest, source, count, todo, lambda k: (k > 0) & (k & 1 == 0)
    )

    def regroup(group, carry):
        loading(group).wait()

        def load(q):
            return blocks[group, :, q * LANES : (q + 1) * LANES]

        limit = blocks.shape[2] // LANES - 1
        for row in range(ROWS):
            q, o = divmod(row * BW, LANES)
            p = (ROWS + row) * BW // LANES
            if o == 0:
                value = jnp.where(lane >= HALF, load(p), load(q))
            elif o <= HALF:
                low = load(p if o == HALF else min(p + 1, limit))
                value = jnp.where(lane >= o, load(q), low)
                if o < HALF:
                    value = jnp.where(lane >= o + HALF, load(p), value)
            else:
                value = jnp.where(lane >= o - HALF, load(p), load(q + 1))
                value = jnp.where(lane >= o, load(q), value)
            at = pl.multiple_of(group * (ROWS * SUB) + row * SUB, SUB)
            flat[pl.ds(at, SUB), :] = turn(value, -o)
        return carry

    lax.fori_loop(0, groups, regroup, 0)
    fill_strips(n, bx_n, by_n, me, dest, flat, strips, todo, found)
    for k in range(2, n, 2):
        assemble(outs[k // 2 - 1], k, cap, source, flat, strips)


def second_kernel(n, cap, bx_n, by_n, *refs):
    me_ref, dest_hbm, flat, kmt_hbm, kappa_hbm = refs[:5]
    outs = refs[5 : n // 2 + 6]
    dest, source, todo, kmt, kappa, strips, edges, count, sems = refs[n // 2 + 6 :]
    me = me_ref[0]
    lane = lanes()
    length = outs[0].shape[0]
    cols = kmt.shape[1]
    first, *copies = [
        pltpu.make_async_copy(dest_hbm, dest, sems.at[0]),
        pltpu.make_async_copy(kmt_hbm, kmt, sems.at[1]),
        pltpu.make_async_copy(kappa_hbm, kappa, sems.at[2]),
    ]
    for copy in (first, *copies):
        copy.start()
    first.wait()
    found = plan(
        n, cap, bx_n, me, dest, source, count, todo, lambda k: (k == 0) | (k & 1 == 1)
    )
    fill_strips(n, bx_n, by_n, me, dest, flat, strips, todo, found)
    for copy in copies:
        copy.wait()
    zero = jnp.zeros((SUB, LANES), F32)
    for at in range(0, edges.shape[1], SUB):
        for side in range(2):
            edges[side, at : at + SUB, :] = zero
    for side, start in ((0, cols - HALO), (1, 0)):
        tile = start // LANES * LANES
        width = min(LANES, cols - tile)
        for piece in range(by_n * (1 + LEV)):
            by, ch = divmod(piece, 1 + LEV)
            base, target = edge_spot(cap, piece)
            if piece >= 4 * cap:
                base -= cap * ROWS + BH - 2 * cap * BH
            here = (lane >= target) & (lane < target + HALO)
            for row in range(0, BH, SUB):
                at = slice(by * BH + row, by * BH + row + SUB)
                if ch == 0:
                    value = kmt[at, tile : tile + width].astype(F32)
                else:
                    value = kappa[ch - 1, at, tile : tile + width]
                if width < LANES:
                    value = jnp.concatenate([value, zero[:, width:]], axis=1)
                pltpu.store(
                    edges.at[side, base + row : base + row + SUB, :],
                    turn(value, target - (start - tile)),
                    mask=here,
                )
    eastern = lax.bitwise_xor(lax.rem(me + 1, n), me)
    in_blocks = min(edges.shape[1], 2 * cap * BH)
    for out, k in zip(outs, [0, *range(1, n, 2)]):
        which = jnp.where(eastern == k, 0, 1)
        assemble(out, k, cap, source, flat, strips, edges, which, in_blocks)
        if length > cap * ROWS + BH:
            for row in range(0, BH, SUB):
                at = cap * ROWS + BH + row
                out[at : at + SUB, :] = edges[
                    which, in_blocks + row : in_blocks + row + SUB, :
                ]


def base_kernel(n, cap, bx_n, by_n, me_ref, dest, kmt, kappa, table, grid, bringer):
    me = me_ref[0]
    slots = bx_n * by_n
    channels, tiles, deep, _ = grid.shape
    cols = kmt.shape[1]
    zero = jnp.zeros((SUB, LANES), F32)
    west = lax.rem(me + n - 1, n)
    east = lax.rem(me + 1, n)
    for at in range(n * (cap + 1)):
        table[at] = -1
    sides = [(west, by * bx_n + bx_n - 1) for by in range(by_n)]
    sides += [(east, by * bx_n) for by in range(by_n)]
    for owner, spot in sides:
        bringer[owner * slots + spot + 1] = -1

    def owner_loop(s, carry):
        k = lax.bitwise_xor(s, me)

        def slot_loop(i, c):
            d = dest[0, s * slots + i]
            bringer[d + 1] = k
            spot = d - me * slots
            mine = (spot >= 0) & (spot < slots)
            table[k * (cap + 1) + c] = jnp.where(mine, spot, -1)
            return c + mine.astype(jnp.int32)

        lax.fori_loop(0, slots, slot_loop, 0, unroll=8)
        return carry

    lax.fori_loop(0, n, owner_loop, 0)
    counts = n * (cap + 1)
    lists = counts + n + 1
    for k in range(n + 1):
        table[counts + k] = 0
    for at, (owner, spot) in enumerate(sides):
        k = bringer[owner * slots + spot + 1]
        k = jnp.where(k < 0, n, k)
        c = table[counts + k]
        table[counts + k] = c + 1
        table[lists + k * len(sides) + c] = at

    def clear(g, carry):
        at = pl.ds(pl.multiple_of(g * SUB, SUB), SUB)
        for ch in range(channels):
            for j in range(tiles):
                grid[ch, j, at, :] = zero
        return carry

    lax.fori_loop(0, deep // SUB, clear, 0)

    def lay(g, carry):
        at = pl.ds(pl.multiple_of(g * SUB, SUB), SUB)
        out = pl.ds(pl.multiple_of(g * SUB + PAD, SUB), SUB)
        for ch in range(1 + LEV):
            for j in range(tiles):
                width = min(LANES, cols - j * LANES)
                part = slice(j * LANES, j * LANES + width)
                if ch == 0:
                    value = kmt[at, part].astype(F32)
                else:
                    value = kappa[ch - 1, at, part]
                grid[ch, j, out, 0:width] = value
        return carry

    lax.fori_loop(0, kmt.shape[0] // SUB, lay, 0)


def place_kernel(n, cap, bx_n, by_n, cols, which, *refs):
    count = len(which)
    me_ref, table, _ = refs[:3]
    odd = me_ref[1]
    packs = refs[3 : 3 + count]
    grid, *rims = refs[3 + count :]
    me = me_ref[0]
    lane = lanes()
    channels, tiles, deep, _ = grid.shape
    last = tiles - 1
    own = cols - last * LANES
    halo_lane = (own, LANES - HALO)

    def mark(ch, at, value, start):
        here = (lane >= start) & (lane < start + HALO)
        pltpu.store(grid.at[ch, last, at, :], value, mask=here)

    for k, pack in zip(which, packs):

        for c in range(cap):
            spot = table[k * (cap + 1) + c]
            valid = spot >= 0
            spot = jnp.maximum(spot, 0)
            by = lax.div(spot, bx_n)
            offset = lax.rem(spot, bx_n) * BW
            tile = lax.div(offset, LANES)
            following = jnp.minimum(tile + 1, last)
            start = lax.rem(offset, LANES)
            begin = jnp.where(valid, start, LANES)
            here = (lane >= begin) & (lane < begin + BW)
            spill = lane < jnp.where(valid, start + BW - LANES, 0)
            for row in range(0, BH, SUB):
                at = pl.ds(pl.multiple_of(by * BH + row + PAD, SUB), SUB)
                depth = grid[0, tile, at, :], grid[0, following, at, :]
                for level in range(LEV):
                    place = c * ROWS + level * BH + row
                    value = pack[place : place + SUB, :]
                    masks = here & (depth[0] > level), spill & (depth[1] > level)
                    for tracer in range(2):
                        ch = 1 + LEV + tracer * LEV + level
                        turned = pltpu.roll(
                            value, lax.rem(start + tracer * HALF, LANES), 1
                        )
                        for target, mask in zip((tile, following), masks):
                            pltpu.store(grid.at[ch, target, at, :], turned, mask=mask)

        counts = n * (cap + 1)
        lists = counts + n + 1 + k * 2 * by_n

        def strip(at, carry, pack=pack, lists=lists):
            index = table[lists + at]
            by = lax.rem(index, by_n)
            start = jnp.where(index < by_n, halo_lane[1], halo_lane[0])
            for row in range(0, BH, SUB):
                rows = pl.ds(pl.multiple_of(by * BH + row + PAD, SUB), SUB)
                value = pack[cap * ROWS + row : cap * ROWS + row + SUB, :]
                for level in range(LEV):
                    for tracer in range(2):
                        origin = strip_lane(0, index, level, tracer, by_n)
                        amount = lax.rem(start - origin + LANES, LANES)
                        mark(
                            1 + LEV + tracer * LEV + level,
                            rows,
                            pltpu.roll(value, amount, 1),
                            start,
                        )
            return carry

        lax.fori_loop(0, table[counts + k], strip, 0)

        for neighbour, start in ((me + n - 1, halo_lane[1]), (me + 1, halo_lane[0])):
            if k % 2 == 0:
                continue

            @pl.when(lax.bitwise_xor(lax.rem(neighbour, n), me) == k)
            def _(start=start, pack=pack):
                for piece in range(by_n * (1 + LEV)):
                    by, ch = divmod(piece, 1 + LEV)
                    base, origin = edge_spot(cap, piece)
                    for row in range(0, BH, SUB):
                        at = by * BH + row + PAD
                        mark(
                            ch,
                            slice(at, at + SUB),
                            turn(pack[base + row : base + row + SUB, :], start - origin),
                            start,
                        )

    if not rims:
        return
    rim = (lane >= own) & (lane < own + HALO) | (lane >= LANES - HALO)

    def mask(g, carry):
        at = pl.ds(pl.multiple_of(g * SUB + PAD, SUB), SUB)
        wet = grid[0, last, at, :]
        for ch in range(1 + LEV, channels):
            level = (ch - 1 - LEV) % LEV
            grid[ch, last, at, :] = jnp.where(
                rim & (wet <= level), 0.0, grid[ch, last, at, :]
            )
        return carry

    lax.fori_loop(0, deep // SUB - 2, mask, 0, unroll=4)
    low = deep - PAD - HALO
    for rows, first in zip(rims, (1 - odd, odd)):
        at = jnp.where(first == 1, PAD, low)
        for ch in range(channels):
            for j in range(tiles):
                spot = (ch * tiles + j) * HALO
                rows[spot : spot + HALO, :] = grid[ch, j, pl.ds(at, HALO), :]


def sideways(values):
    lane = lanes()
    count = len(values)
    left = [turn(v, 1) for v in values]
    right = [turn(v, -1) for v in values]
    west = [
        jnp.where(lane == 0, left[(j - 1) % count], left[j]) for j in range(count)
    ]
    east = [
        jnp.where(lane == LANES - 1, right[(j + 1) % count], right[j])
        for j in range(count)
    ]
    return east, west


def three(load, start):
    return load(start), load(start - 1), load(start + 1)


def diffuse(load, start):
    tiles = len(load(0, start))
    span = range(tiles)
    level_c, level_a, level_b = three(functools.partial(load, 0), start)
    level_e, _ = sideways(level_c)
    both_e = [jnp.minimum(level_c[j], level_e[j]) for j in span]
    both_a = [jnp.minimum(level_c[j], level_a[j]) for j in span]
    both_b = [jnp.minimum(level_c[j], level_b[j]) for j in span]
    forcing = [None] * tiles
    fresh = [[None] * LEV for _ in range(2)]
    for level in range(LEV):
        kappa_c, kappa_a, kappa_b = three(functools.partial(load, 1 + level), start)
        kappa_e, _ = sideways(kappa_c)
        face_e, face_a, face_b = (
            [jnp.where(both[j] > level, kappa_c[j] + other[j], 0.0) for j in span]
            for both, other in (
                (both_e, kappa_e),
                (both_a, kappa_a),
                (both_b, kappa_b),
            )
        )
        for tracer in range(2):
            ch = 1 + LEV + tracer * LEV + level
            here, above, below = three(functools.partial(load, ch), start)
            to_east, _ = sideways(here)
            flux = [face_e[j] * (to_east[j] - here[j]) for j in span]
            _, flux_w = sideways(flux)
            fresh[tracer][level] = [
                jnp.where(
                    level_c[j] > level,
                    here[j]
                    + 0.5
                    * (
                        (flux[j] - flux_w[j])
                        + face_a[j] * (above[j] - here[j])
                        + face_b[j] * (below[j] - here[j])
                    ),
                    0.0,
                )
                for j in span
            ]
        thickness = 1.0 + 0.5 * level
        for j in span:
            temp, salt = fresh[0][level][j], fresh[1][level][j]
            density = haline * salt - temp * (thermal + cabbeling * temp)
            if level:
                density = forcing[j] + thickness * density
            forcing[j] = density
    return fresh, forcing


def apply(here, above, below, levels):
    span = range(len(here))
    pair = [above[j] + below[j] for j in span]
    mixed = [here[j] + 0.5 * pair[j] for j in span]
    east, west = sideways(mixed)
    result = []
    for j in span:
        diagonal = 6.0 - SHIFT + 1.0
        total = jnp.full((SUB, LANES), diagonal / SCALE, F32)
        for k in range(1, LEV):
            diagonal += 1.0 + 0.5 * k
            total = jnp.where(levels[j] > k, diagonal / SCALE, total)
        total = total * here[j] - (pair[j] + (east[j] + west[j])) * (1.0 / SCALE)
        result.append(jnp.where(levels[j] > 0, total, 0.0))
    return result


def gather_products(carry, powers, centre, keep):
    carry = list(carry)
    span = range(len(powers[0]))
    for j in span:
        q0, q1, q2, q3 = (keep(q[j], j) for q in powers)
        b1 = q1 - centre * q0
        c2 = q2 - centre * q1
        c3 = q3 - centre * q2
        b2 = c2 - centre * b1
        b3 = (c3 - centre * c2) - centre * b2
        terms = (q0, b1, b2, b3)
        for at, (x, y) in enumerate(PAIRS):
            carry[at] = carry[at] + terms[x] * terms[y]
    return tuple(carry)


def total_row(totals):
    lane = lanes()[:1]
    row = jnp.zeros((1, LANES), F32)
    for at, total in enumerate(totals):
        total = jnp.sum(total, axis=(0, 1), keepdims=True)
        row = jnp.where(lane == at + 1, total, row)
    return row


def put_tracer(target, fresh, cols, at):
    for tracer in range(2):
        for level in range(LEV):
            for j, value in enumerate(fresh[tracer][level]):
                width = min(LANES, cols - j * LANES)
                target[tracer, level, at, j * LANES : j * LANES + width] = value[
                    :, :width
                ]


def inner_kernel(cols, grid, tracer_out, powers, sums, edges, fresh_rows, sems):
    lane = lanes()
    line = lax.broadcasted_iota(jnp.int32, (SUB, LANES), 0)
    _, tiles, deep, _ = grid.shape
    own = cols - (tiles - 1) * LANES
    first, end = PAD // SUB, (deep - PAD) // SUB
    zero = jnp.zeros((SUB, LANES), F32)

    def rows(ref, lead, start):
        return [ref[lead, j, pl.ds(start, SUB), :] for j in range(tiles)]

    def top(g):
        return pl.multiple_of(g * SUB, SUB)

    def step(g, carry):
        fresh, forcing = diffuse(functools.partial(rows, grid), top(g))
        put_tracer(
            fresh_rows, fresh, cols, pl.ds(pl.multiple_of(g * SUB - PAD, SUB), SUB)
        )
        for j in range(tiles):
            powers[0, j, pl.ds(top(g), SUB), :] = forcing[j]
        return carry

    chunks = sems.shape[0]
    size = (end - first) // chunks
    copies = []
    for chunk in range(chunks):
        begin = first + chunk * size
        stop = end if chunk == chunks - 1 else begin + size
        lax.fori_loop(begin, stop, step, 0, unroll=2)
        at = pl.ds(begin * SUB - PAD, (stop - begin) * SUB)
        copies.append(
            pltpu.make_async_copy(
                fresh_rows.at[:, :, at, :], tracer_out.at[:, :, at, :], sems.at[chunk]
            )
        )
        copies[-1].start()
    height = fresh_rows.shape[2]
    for tracer in range(2):
        for level in range(LEV):
            for side, row in ((0, 0), (1, height - SUB)):
                edges[side, tracer, level] = fresh_rows[
                    tracer, level, row : row + SUB, :
                ]

    def inside(value, j):
        return value if j < tiles - 1 else jnp.where(lane < own, value, 0.0)

    def upper(value, j):
        return jnp.where(line >= HALO, inside(value, j), 0.0)

    def lower(value, j):
        return jnp.where(line < SUB - HALO, inside(value, j), 0.0)

    def power(g, source):
        here, above, below = three(functools.partial(rows, powers, source), top(g))
        return here, apply(here, above, below, rows(grid, 0, top(g)))

    def put(g, target):
        here, result = power(g, target - 1)
        for j in range(tiles):
            powers[target, j, pl.ds(top(g), SUB), :] = result[j]
        return here, result

    def first_power(g, carry, keep=inside):
        here, result = put(g, 1)
        a, b = carry
        for j in range(tiles):
            v = keep(here[j], j)
            a = a + v * v
            b = b + v * keep(result[j], j)
        return a, b

    def everywhere(body, carry):
        carry = body(first, carry, upper)
        carry = lax.fori_loop(first + 1, end - 1, body, carry, unroll=end - first - 2)
        return body(end - 1, carry, lower)

    a, b = everywhere(first_power, (zero, zero))
    a = jnp.sum(a, axis=(0, 1), keepdims=True)
    b = jnp.sum(b, axis=(0, 1), keepdims=True)
    centre = jnp.where(a > 0, b / jnp.where(a > 0, a, 1.0), 0.0)
    centre = jnp.broadcast_to(centre, (SUB, LANES))
    lax.fori_loop(
        first, end, lambda g, c: (put(g, 2), c)[1], 0, unroll=end - first
    )

    def products(g, carry, keep=inside):
        here, result = power(g, 2)
        lower_powers = [rows(powers, k, top(g)) for k in range(2)]
        return gather_products(carry, (*lower_powers, here, result), centre, keep)

    totals = everywhere(products, (zero,) * len(PAIRS))
    for at, total in enumerate((*totals, centre)):
        sums[at] = total
    for copy in copies:
        copy.wait()


def border_kernel(
    cols, me_ref, grid, other_rows, pair_rows, powers, part, edges, border, sums,
    fresh_rows, field, local,
):
    lane = lanes()
    line = lax.broadcasted_iota(jnp.int32, (SUB, LANES), 0)
    channels, tiles, deep, _ = grid.shape
    own = cols - (tiles - 1) * LANES
    half = EDGE // 2
    even = me_ref[1] == 0
    for ch in range(channels):
        for j in range(tiles):
            at = slice((ch * tiles + j) * HALO, (ch * tiles + j + 1) * HALO)
            field[0, ch, j, half : half + SUB, :] = grid[ch, j, PAD : PAD + SUB, :]
            field[1, ch, j, half - SUB : half, :] = grid[
                ch, j, deep - PAD - SUB : deep - PAD, :
            ]
            pair, other = pair_rows[at, :], other_rows[at, :]
            field[0, ch, j, half - HALO : half, :] = jnp.where(even, other, pair)
            field[1, ch, j, half : half + HALO, :] = jnp.where(even, pair, other)
    for k in range(3):
        for j in range(tiles):
            local[0, k, j, half : half + SUB, :] = powers[k, j, PAD : PAD + SUB, :]
            local[1, k, j, half - SUB : half, :] = powers[
                k, j, deep - PAD - SUB : deep - PAD, :
            ]
    centre = part[len(PAIRS)]

    def rows_of(side):
        def rows(ref, lead, start):
            return [ref[side, lead, j, pl.ds(start, SUB), :] for j in range(tiles)]

        return rows

    start = half - HALO
    for side in range(2):
        fresh, forcing = diffuse(functools.partial(rows_of(side), field), start)
        for j in range(tiles):
            local[side, 0, j, start : start + SUB, :] = forcing[j]
        mine = line == (0 if side == 0 else SUB - 1)
        for tracer in range(2):
            for level in range(LEV):
                for j in range(tiles):
                    width = min(LANES, cols - j * LANES)
                    part_lanes = slice(j * LANES, j * LANES + width)
                    moved = pltpu.roll(fresh[tracer][level][j], HALO, 0)
                    fresh_rows[side, tracer, level, :, part_lanes] = jnp.where(
                        mine[:, :width],
                        moved[:, :width],
                        edges[side, tracer, level, :, part_lanes],
                    )

    def power(side, source):
        rows = rows_of(side)
        here, above, below = three(functools.partial(rows, local, source), start)
        return here, apply(here, above, below, rows(field, 0, start))

    for target in range(1, 3):
        for side in range(2):
            result = power(side, target - 1)[1]
            for j in range(tiles):
                local[side, target, j, start : start + SUB, :] = result[j]
    totals = tuple(part[at] for at in range(len(PAIRS)))
    for side in range(2):
        here, result = power(side, 2)
        lower_powers = [rows_of(side)(local, k, start) for k in range(2)]
        own_rows = half - side * SUB
        for k in range(3):
            for j in range(tiles):
                border[side, k, j] = local[side, k, j, own_rows : own_rows + SUB, :]
        bound = (1 - side) * HALO
        rim = (line >= bound) & (line < bound + HALO)

        def keep(value, j, rim=rim):
            inside = rim if j < tiles - 1 else rim & (lane < own)
            return jnp.where(inside, value, 0.0)

        totals = gather_products(
            totals, (*lower_powers, here, result), centre, keep
        )
    row = jnp.where(lane[:1] == 0, centre[:1], total_row(totals))
    sums[...] = jnp.broadcast_to(row, sums.shape)


PAIRS = ((0, 0), (0, 1), (0, 2), (0, 3), (1, 1), (1, 2), (1, 3), (2, 2), (2, 3))


def combine_kernel(
    cols, sums, powers, border, fresh_rows, tracer_in, tracer_out, stream_out, stream, sems
):
    rows = tracer_out.shape[2]
    patches = [
        pltpu.make_async_copy(
            fresh_rows.at[side],
            tracer_out.at[:, :, pl.ds(side * (rows - SUB), SUB), :],
            sems.at[2 + side],
        )
        for side in range(2)
    ]
    for copy in patches:
        copy.start()
    values = sums[...]
    lane = lax.broadcasted_iota(jnp.int32, values.shape, 1)

    def column(k):
        return jnp.sum(jnp.where(lane == k, values, 0.0), axis=1, keepdims=True)

    centre = column(0)
    gram = {pair: column(at + 1) for at, pair in enumerate(PAIRS)}

    def local(c):
        c = list(c) + [None] * (4 - len(c))
        c0, c1, c2, c3 = c
        result = [c0 + jnp.zeros_like(centre)]
        if c1 is not None:
            inner = c1
            slope = c1 + jnp.zeros_like(centre)
            if c2 is not None:
                inner = c1 + centre * (c2 if c3 is None else c2 + centre * c3)
                slope = c1 + centre * (
                    2.0 * c2 if c3 is None else 2.0 * c2 + 3.0 * (centre * c3)
                )
            result = [c0 + centre * inner, slope]
        if c2 is not None:
            result.append(c2 + jnp.zeros_like(centre) if c3 is None else c2 + 3.0 * (centre * c3))
        if c3 is not None:
            result.append(c3 + jnp.zeros_like(centre))
        return result

    def inner(x, y):
        u, v = local(x), local(y)
        total = jnp.zeros_like(centre)
        for i in range(len(u)):
            for j in range(len(v)):
                total = total + (u[i] * v[j]) * gram[(min(i, j), max(i, j))]
        return jnp.sum(total, axis=0, keepdims=True)

    def operate(c):
        result = [SHIFT * x for x in c] + [None]
        for i, x in enumerate(c):
            term = SCALE * x
            result[i + 1] = term if result[i + 1] is None else result[i + 1] + term
        return result

    one = jnp.ones((1, 1), F32)
    stream_c = [None] * 3
    residual, direction = [one], [one]
    norm = inner(residual, residual)
    for step in range(3):
        image = operate(direction)
        alpha = norm / inner(direction, image)
        for i, x in enumerate(direction):
            stream_c[i] = alpha * x if stream_c[i] is None else stream_c[i] + alpha * x
        if step == 2:
            break
        residual = [
            (residual[i] - alpha * image[i]) if i < len(residual) else -alpha * image[i]
            for i in range(len(image))
        ]
        fresh = inner(residual, residual)
        ratio = fresh / norm
        direction = [
            (residual[i] + ratio * direction[i]) if i < len(direction) else residual[i]
            for i in range(len(residual))
        ]
        norm = fresh

    tiles = powers.shape[1]
    height = stream.shape[0]
    weights = [jnp.broadcast_to(c, (SUB, LANES)) for c in stream_c]

    def put(out, load):
        for j in range(tiles):
            width = min(LANES, cols - j * LANES)
            value = sum(weights[k] * load(k, j) for k in range(3))
            stream[out, j * LANES : j * LANES + width] = value[:, :width]

    def write(g, carry):
        at = pl.ds(pl.multiple_of(g * SUB + PAD, SUB), SUB)
        out = pl.ds(pl.multiple_of(g * SUB, SUB), SUB)
        put(out, lambda k, j: powers[k, j, at, :])
        return carry

    middle = height // SUB // 2 * SUB
    copies = [
        pltpu.make_async_copy(stream.at[part, :], stream_out.at[part, :], sems.at[at])
        for at, part in enumerate((pl.ds(0, middle), pl.ds(middle, height - middle)))
    ]
    put(slice(0, SUB), lambda k, j: border[0, k, j])
    lax.fori_loop(1, middle // SUB, write, 0, unroll=3)
    copies[0].start()
    lax.fori_loop(middle // SUB, height // SUB - 1, write, 0, unroll=3)
    put(slice(height - SUB, height), lambda k, j: border[1, k, j])
    copies[1].start()
    for copy in (*patches, *copies):
        copy.wait()


def body(checkpoint, slot_dest, kmt, kappa):
    n = lax.axis_size("lon")
    lats = lax.axis_size("lat")
    lat = lax.axis_index("lat")
    me = jnp.stack([lax.axis_index("lon"), lax.rem(lat, 2)]).astype(jnp.int32)
    _, slots, values = checkpoint.shape
    rows, cols = kmt.shape
    by_n, bx_n = rows // BH, cols // BW
    cap = slots // n
    length = package_rows(cap, by_n)
    tiles = -(-(cols + 2 * HALO) // LANES)
    groups = slots // SUB
    edge_rows = -(-by_n * (1 + LEV) // 2) * BH
    if by_n * (1 + LEV) > 4 * cap:
        edge_rows = 2 * cap * BH + BH

    def fixed(value):
        return pltpu.with_memory_space_constraint(value, pltpu.HBM)

    kernels = (n, cap, bx_n, by_n)
    lists = [
        pltpu.SMEM((1, n * slots), jnp.int32),
        pltpu.SMEM((n * cap + 1,), jnp.int32),
        pltpu.SMEM((slots + 1,), jnp.int32),
    ]
    *packs, flat = pl.pallas_call(
        functools.partial(first_kernel, *kernels),
        out_shape=[shaped(length, LANES)] * (n // 2 - 1)
        + [shaped(slots * ROWS, LANES)],
        in_specs=[SM, HB, HB],
        out_specs=[VM] * (n // 2),
        scratch_shapes=lists
        + [
            pltpu.VMEM((groups, SUB, values), F32),
            pltpu.VMEM((n, BH, LANES), F32),
            pltpu.SMEM((n + 1,), jnp.int32),
            pltpu.SemaphoreType.DMA((groups + 1,)),
        ],
        compiler_params=params(),
        cost_estimate=cost(2 << 20, 4 << 20),
        name="first",
    )(me, fixed(slot_dest), fixed(checkpoint))

    def send(value, k):
        return lax.ppermute(value, "lon", [(i, i ^ k) for i in range(n)])

    order = sorted(range(1, n), key=lambda k: (k & 1, k < 2, -bin(k >> 1).count("1"), k))
    received = {k: send(packs[k // 2 - 1], k) for k in order if k % 2 == 0}
    own, *packs = pl.pallas_call(
        functools.partial(second_kernel, *kernels),
        out_shape=[shaped(length, LANES)] * (n // 2 + 1),
        in_specs=[SM, HB, VM, HB, HB],
        out_specs=[VM] * (n // 2 + 1),
        scratch_shapes=lists
        + [
            pltpu.VMEM((rows, cols), jnp.int32),
            pltpu.VMEM((LEV, rows, cols), F32),
            pltpu.VMEM((n, BH, LANES), F32),
            pltpu.VMEM((2, edge_rows, LANES), F32),
            pltpu.SMEM((n + 1,), jnp.int32),
            pltpu.SemaphoreType.DMA((3,)),
        ],
        compiler_params=params(),
        cost_estimate=cost(2 << 20, 4 << 20),
        name="second",
    )(me, fixed(slot_dest), flat, fixed(kmt), fixed(kappa))
    received |= {k: send(packs[k // 2], k) for k in order if k % 2}
    received[0] = own

    channels = 1 + 3 * LEV
    deep = rows + 2 * PAD
    table, grid = pl.pallas_call(
        functools.partial(base_kernel, n, cap, bx_n, by_n),
        out_shape=[
            shaped(n * (cap + 1) + (n + 1) * (1 + 2 * by_n), dtype=jnp.int32),
            shaped(channels, tiles, deep, LANES),
        ],
        in_specs=[SM, SM, VM, VM],
        out_specs=[SM, VM],
        scratch_shapes=[pltpu.SMEM((n * slots + 1,), jnp.int32)],
        compiler_params=params(),
        cost_estimate=cost(1 << 20, 2 << 20),
        name="base",
    )(me, slot_dest, kmt, kappa)

    def held(value):
        return pltpu.with_memory_space_constraint(value, pltpu.VMEM)

    rim = channels * tiles * HALO
    half, quarter = n // 2 - 1, n // 4
    odd = order[half:]
    parts = [
        [0] + order[:half],
        odd[-1:] + odd[: quarter - 1],
        odd[quarter - 1 : -2],
        odd[-2:-1],
    ]
    parts = [part for part in parts if part]
    for stage, which in enumerate(parts):
        shapes = [shaped(channels, tiles, deep, LANES)]
        if stage == len(parts) - 1:
            shapes += [shaped(rim, LANES)] * 2
        grid, *rims = pl.pallas_call(
            functools.partial(place_kernel, n, cap, bx_n, by_n, cols, which),
            out_shape=shapes,
            in_specs=[SM, SM] + [VM] * (1 + len(which)),
            out_specs=[VM] * len(shapes),
            input_output_aliases={2: 0},
            compiler_params=params(),
            cost_estimate=cost(2 << 20, 2 << 20),
            name=f"place{stage}",
        )(me, table, held(grid), *[received[k] for k in which])

    swaps = [
        [(i, i ^ 1) for i in range(lats) if i ^ 1 < lats],
        [(i, j) for i in range(lats) for j in [(i - 1 ^ 1) + 1] if 0 <= j < lats],
    ]
    other_rows, pair_rows = (
        lax.ppermute(value, "lat", swap) for value, swap in zip(rims, swaps[::-1])
    )

    devices = n * lats
    tracer_shape = shaped(2, LEV, rows, cols)
    tracer, powers, part, edges = pl.pallas_call(
        functools.partial(inner_kernel, cols),
        out_shape=[
            tracer_shape,
            shaped(3, tiles, deep, LANES),
            shaped(len(PAIRS) + 1, SUB, LANES),
            shaped(2, 2, LEV, SUB, cols),
        ],
        in_specs=[VM],
        out_specs=[HB, VM, VM, VM],
        scratch_shapes=[
            pltpu.VMEM((2, LEV, rows, cols), F32),
            pltpu.SemaphoreType.DMA((5,)),
        ],
        compiler_params=params(),
        cost_estimate=cost(16 << 20, 6 << 20),
        name="inner",
    )(grid)
    border, sums, fresh_rows = pl.pallas_call(
        functools.partial(border_kernel, cols),
        out_shape=[
            shaped(2, 3, tiles, SUB, LANES),
            shaped(devices, LANES),
            shaped(2, 2, LEV, SUB, cols),
        ],
        in_specs=[SM, VM, VM, VM, VM, VM, VM],
        out_specs=[VM, VM, VM],
        scratch_shapes=[
            pltpu.VMEM((2, channels, tiles, EDGE, LANES), F32),
            pltpu.VMEM((2, 3, tiles, EDGE, LANES), F32),
        ],
        compiler_params=params(),
        cost_estimate=cost(2 << 20, 1 << 20),
        name="border",
    )(me, grid, other_rows, pair_rows, powers, part, edges)

    everyone = lax.all_to_all(sums, ("lon", "lat"), 0, 0, tiled=True)
    tracer, stream = pl.pallas_call(
        functools.partial(combine_kernel, cols),
        out_shape=[tracer_shape, shaped(rows, cols)],
        in_specs=[VM, VM, VM, VM, HB],
        out_specs=[HB, HB],
        scratch_shapes=[
            pltpu.VMEM((rows, cols), F32),
            pltpu.SemaphoreType.DMA((4,)),
        ],
        input_output_aliases={4: 0},
        compiler_params=params(),
        cost_estimate=cost(1 << 20, 2 << 20),
        name="combine",
    )(everyone, powers, border, fresh_rows, fixed(tracer))
    return tracer, stream


def solution(mesh):
    placed = (P("lat", "lon", None), P("lat", None), P("lat", "lon"), P(None, "lat", "lon"))
    return jax.shard_map(
        body,
        mesh=mesh,
        in_specs=placed,
        out_specs=(P(None, None, "lat", "lon"), P("lat", "lon")),
        check_vma=False,
    )
```

```python
import functools

import jax
import jax.numpy as jnp
from jax import lax
from jax.experimental import pallas as pl
from jax.experimental.pallas import tpu as pltpu
from jax.sharding import PartitionSpec as P


BH = 40
BW = 60
LEV = 2
HALO = 4
LANES = 128
SUB = 8
PAD = SUB
EDGE = 4 * SUB
ROWS = LEV * BH
HALF = LANES // 2
SHIFT = 8.0
SCALE = 8.0

thermal = 0.25
haline = 0.75
cabbeling = 0.05

VM = pl.BlockSpec(memory_space=pltpu.VMEM)
SM = pl.BlockSpec(memory_space=pltpu.SMEM)
HB = pl.BlockSpec(memory_space=pltpu.HBM)
F32 = jnp.float32


def params():
    return pltpu.CompilerParams(vmem_limit_bytes=24 << 20)


def cost(flops, moved):
    return pl.CostEstimate(flops=flops, bytes_accessed=moved, transcendentals=0)


def shaped(*dims, dtype=F32):
    return jax.ShapeDtypeStruct(dims, dtype)


def lanes():
    return lax.broadcasted_iota(jnp.int32, (SUB, LANES), 1)


def turn(value, amount):
    if isinstance(amount, int):
        amount %= LANES
        if amount == 0:
            return value
    return pltpu.roll(value, amount, 1)


def strip_lane(side, by, level, tracer, block_rows):
    return HALO * ((side * block_rows + by) * LEV + level) + HALF * tracer


def edge_spot(cap, piece):
    if piece < 4 * cap:
        return piece // 2 * BH, HALF * (1 + piece % 2) - HALO
    return cap * ROWS + BH, HALO * (piece - 4 * cap)


def package_rows(cap, by_n):
    return cap * ROWS + (2 * BH if by_n * (1 + LEV) > 4 * cap else BH)


def block_rows(flat, start, row):
    return flat[pl.ds(start + row * SUB, SUB, stride=SUB), :]


def block_start(i):
    return lax.div(i, SUB) * (ROWS * SUB) + lax.rem(i, SUB)


def plan(n, cap, bx_n, me, dest, source, count, todo, wanted):
    slots = todo.shape[0] - 1
    for k in range(n + 1):
        count[k] = 0
    for at in range(n * cap + 1):
        source[at] = 0

    def assign(i, found):
        d = dest[0, me * slots + i]
        used = d >= 0
        place = jnp.maximum(d, 0)
        owner = lax.div(place, slots)
        k = jnp.where(used, lax.bitwise_xor(owner, me), n)
        c = count[k]
        count[k] = c + 1
        source[jnp.where(used, k * cap + c, n * cap)] = block_start(i)
        bx = lax.rem(place, bx_n)
        partner = lax.bitwise_xor(
            lax.rem(owner + jnp.where(bx == 0, n - 1, 1), n), me
        )
        todo[found] = i
        holds = used & ((bx == 0) | (bx == bx_n - 1)) & wanted(partner)
        return found + holds.astype(jnp.int32)

    return lax.fori_loop(0, slots, assign, 0, unroll=4)


def fill_strips(n, bx_n, by_n, me, dest, flat, strips, todo, found):
    slots = bx_n * by_n
    spot_lane = lanes() & (HALF - 1)

    def strip(at, carry):
        i = todo[at]
        place = dest[0, me * slots + i]
        spot = lax.rem(place, slots)
        by = lax.div(spot, bx_n)
        side = (lax.rem(spot, bx_n) == 0).astype(jnp.int32)
        owner = lax.div(place, slots)
        k = lax.bitwise_xor(lax.rem(owner + jnp.where(side == 0, 1, n - 1), n), me)
        start = block_start(i)
        origin = jnp.where(side == 0, BW - HALO, 0)
        for level in range(LEV):
            target = strip_lane(side, by, level, 0, by_n)
            amount = lax.rem(target - origin + LANES, LANES)
            here = (spot_lane >= target) & (spot_lane < target + HALO)
            for row in range(0, BH, SUB):
                value = block_rows(flat, start, level * BH + row)
                pltpu.store(
                    strips.at[k, row : row + SUB, :],
                    pltpu.roll(value, amount, 1),
                    mask=here,
                )
        return carry

    lax.fori_loop(0, found, strip, 0)


def assemble(out, k, cap, source, flat, strips, edges=None, which=None, in_blocks=0):
    spare = (lanes() & (HALF - 1)) >= HALF - HALO
    for c in range(cap):
        start = source[k * cap + c]
        for row in range(0, ROWS, SUB):
            value = block_rows(flat, start, row)
            at = c * ROWS + row
            if at < in_blocks:
                value = jnp.where(spare, edges[which, at : at + SUB, :], value)
            out[at : at + SUB, :] = value
    for row in range(0, BH, SUB):
        at = cap * ROWS + row
        out[at : at + SUB, :] = strips[k, row : row + SUB, :]


def first_kernel(n, cap, bx_n, by_n, leader, *refs):
    me_ref, dest_hbm, blocks_hbm = refs[:3]
    out, flat, dest, source, todo, blocks, strips, count, sems = refs[3:]
    groups = blocks.shape[0]
    me = me_ref[0]
    lane = lanes()
    first = pltpu.make_async_copy(dest_hbm, dest, sems.at[groups])
    first.start()

    def loading(g):
        rows = pl.ds(pl.multiple_of(g * SUB, SUB), SUB)
        return pltpu.make_async_copy(
            blocks_hbm.at[0, rows, :], blocks.at[g], sems.at[g]
        )

    for g in range(groups):
        loading(g).start()
    first.wait()
    found = plan(
        n, cap, bx_n, me, dest, source, count, todo, lambda k: k == leader
    )

    def regroup(group, carry):
        loading(group).wait()

        def load(q):
            return blocks[group, :, q * LANES : (q + 1) * LANES]

        limit = blocks.shape[2] // LANES - 1
        for row in range(ROWS):
            q, o = divmod(row * BW, LANES)
            p = (ROWS + row) * BW // LANES
            if o == 0:
                value = jnp.where(lane >= HALF, load(p), load(q))
            elif o <= HALF:
                low = load(p if o == HALF else min(p + 1, limit))
                value = jnp.where(lane >= o, load(q), low)
                if o < HALF:
                    value = jnp.where(lane >= o + HALF, load(p), value)
            else:
                value = jnp.where(lane >= o - HALF, load(p), load(q + 1))
                value = jnp.where(lane >= o, load(q), value)
            at = pl.multiple_of(group * (ROWS * SUB) + row * SUB, SUB)
            flat[pl.ds(at, SUB), :] = turn(value, -o)
        return carry

    lax.fori_loop(0, groups, regroup, 0)
    fill_strips(n, bx_n, by_n, me, dest, flat, strips, todo, found)
    assemble(out, leader, cap, source, flat, strips)


def second_kernel(n, cap, bx_n, by_n, leader, *refs):
    me_ref, dest_hbm, flat, kmt_hbm, kappa_hbm = refs[:5]
    outs = refs[5 : n + 4]
    dest, source, todo, kmt, kappa, strips, edges, count, sems = refs[n + 4 :]
    me = me_ref[0]
    lane = lanes()
    length = outs[0].shape[0]
    cols = kmt.shape[1]
    first, *copies = [
        pltpu.make_async_copy(dest_hbm, dest, sems.at[0]),
        pltpu.make_async_copy(kmt_hbm, kmt, sems.at[1]),
        pltpu.make_async_copy(kappa_hbm, kappa, sems.at[2]),
    ]
    for copy in (first, *copies):
        copy.start()
    first.wait()
    found = plan(
        n, cap, bx_n, me, dest, source, count, todo, lambda k: k != leader
    )
    fill_strips(n, bx_n, by_n, me, dest, flat, strips, todo, found)
    for copy in copies:
        copy.wait()
    zero = jnp.zeros((SUB, LANES), F32)
    for at in range(0, edges.shape[1], SUB):
        for side in range(2):
            edges[side, at : at + SUB, :] = zero
    for side, start in ((0, cols - HALO), (1, 0)):
        tile = start // LANES * LANES
        width = min(LANES, cols - tile)
        for piece in range(by_n * (1 + LEV)):
            by, ch = divmod(piece, 1 + LEV)
            base, target = edge_spot(cap, piece)
            if piece >= 4 * cap:
                base -= cap * ROWS + BH - 2 * cap * BH
            here = (lane >= target) & (lane < target + HALO)
            for row in range(0, BH, SUB):
                at = slice(by * BH + row, by * BH + row + SUB)
                if ch == 0:
                    value = kmt[at, tile : tile + width].astype(F32)
                else:
                    value = kappa[ch - 1, at, tile : tile + width]
                if width < LANES:
                    value = jnp.concatenate([value, zero[:, width:]], axis=1)
                pltpu.store(
                    edges.at[side, base + row : base + row + SUB, :],
                    turn(value, target - (start - tile)),
                    mask=here,
                )
    eastern = lax.bitwise_xor(lax.rem(me + 1, n), me)
    in_blocks = min(edges.shape[1], 2 * cap * BH)
    for out, k in zip(outs, [k for k in range(n) if k != leader]):
        if k % 2 == 0:
            assemble(out, k, cap, source, flat, strips)
            continue
        which = jnp.where(eastern == k, 0, 1)
        assemble(out, k, cap, source, flat, strips, edges, which, in_blocks)
        if length > cap * ROWS + BH:
            for row in range(0, BH, SUB):
                at = cap * ROWS + BH + row
                out[at : at + SUB, :] = edges[
                    which, in_blocks + row : in_blocks + row + SUB, :
                ]


def base_kernel(n, cap, bx_n, by_n, me_ref, dest, kmt, kappa, table, grid, bringer):
    me = me_ref[0]
    slots = bx_n * by_n
    channels, tiles, deep, _ = grid.shape
    cols = kmt.shape[1]
    zero = jnp.zeros((SUB, LANES), F32)
    west = lax.rem(me + n - 1, n)
    east = lax.rem(me + 1, n)
    for at in range(n * (cap + 1)):
        table[at] = -1
    sides = [(west, by * bx_n + bx_n - 1) for by in range(by_n)]
    sides += [(east, by * bx_n) for by in range(by_n)]
    for owner, spot in sides:
        bringer[owner * slots + spot + 1] = -1

    def owner_loop(s, carry):
        k = lax.bitwise_xor(s, me)

        def slot_loop(i, c):
            d = dest[0, s * slots + i]
            bringer[d + 1] = k
            spot = d - me * slots
            mine = (spot >= 0) & (spot < slots)
            table[k * (cap + 1) + c] = jnp.where(mine, spot, -1)
            return c + mine.astype(jnp.int32)

        lax.fori_loop(0, slots, slot_loop, 0, unroll=8)
        return carry

    lax.fori_loop(0, n, owner_loop, 0)
    counts = n * (cap + 1)
    lists = counts + n + 1
    for k in range(n + 1):
        table[counts + k] = 0
    for at, (owner, spot) in enumerate(sides):
        k = bringer[owner * slots + spot + 1]
        k = jnp.where(k < 0, n, k)
        c = table[counts + k]
        table[counts + k] = c + 1
        table[lists + k * len(sides) + c] = at

    def clear(g, carry):
        at = pl.ds(pl.multiple_of(g * SUB, SUB), SUB)
        for ch in range(channels):
            for j in range(tiles):
                grid[ch, j, at, :] = zero
        return carry

    lax.fori_loop(0, deep // SUB, clear, 0)

    def lay(g, carry):
        at = pl.ds(pl.multiple_of(g * SUB, SUB), SUB)
        out = pl.ds(pl.multiple_of(g * SUB + PAD, SUB), SUB)
        for ch in range(1 + LEV):
            for j in range(tiles):
                width = min(LANES, cols - j * LANES)
                part = slice(j * LANES, j * LANES + width)
                if ch == 0:
                    value = kmt[at, part].astype(F32)
                else:
                    value = kappa[ch - 1, at, part]
                grid[ch, j, out, 0:width] = value
        return carry

    lax.fori_loop(0, kmt.shape[0] // SUB, lay, 0)


def place_kernel(n, cap, bx_n, by_n, cols, which, *refs):
    count = len(which)
    me_ref, table, _ = refs[:3]
    odd = me_ref[1]
    packs = refs[3 : 3 + count]
    grid, *rims = refs[3 + count :]
    me = me_ref[0]
    lane = lanes()
    channels, tiles, deep, _ = grid.shape
    last = tiles - 1
    own = cols - last * LANES
    halo_lane = (own, LANES - HALO)

    def mark(ch, at, value, start):
        here = (lane >= start) & (lane < start + HALO)
        pltpu.store(grid.at[ch, last, at, :], value, mask=here)

    for k, pack in zip(which, packs):

        for c in range(cap):
            spot = table[k * (cap + 1) + c]
            valid = spot >= 0
            spot = jnp.maximum(spot, 0)
            by = lax.div(spot, bx_n)
            offset = lax.rem(spot, bx_n) * BW
            tile = lax.div(offset, LANES)
            following = jnp.minimum(tile + 1, last)
            start = lax.rem(offset, LANES)
            begin = jnp.where(valid, start, LANES)
            here = (lane >= begin) & (lane < begin + BW)
            spill = lane < jnp.where(valid, start + BW - LANES, 0)
            for row in range(0, BH, SUB):
                at = pl.ds(pl.multiple_of(by * BH + row + PAD, SUB), SUB)
                depth = grid[0, tile, at, :], grid[0, following, at, :]
                for level in range(LEV):
                    place = c * ROWS + level * BH + row
                    value = pack[place : place + SUB, :]
                    masks = here & (depth[0] > level), spill & (depth[1] > level)
                    for tracer in range(2):
                        ch = 1 + LEV + tracer * LEV + level
                        turned = pltpu.roll(
                            value, lax.rem(start + tracer * HALF, LANES), 1
                        )
                        for target, mask in zip((tile, following), masks):
                            pltpu.store(grid.at[ch, target, at, :], turned, mask=mask)

        counts = n * (cap + 1)
        lists = counts + n + 1 + k * 2 * by_n

        def strip(at, carry, pack=pack, lists=lists):
            index = table[lists + at]
            by = lax.rem(index, by_n)
            start = jnp.where(index < by_n, halo_lane[1], halo_lane[0])
            for row in range(0, BH, SUB):
                rows = pl.ds(pl.multiple_of(by * BH + row + PAD, SUB), SUB)
                value = pack[cap * ROWS + row : cap * ROWS + row + SUB, :]
                for level in range(LEV):
                    for tracer in range(2):
                        origin = strip_lane(0, index, level, tracer, by_n)
                        amount = lax.rem(start - origin + LANES, LANES)
                        mark(
                            1 + LEV + tracer * LEV + level,
                            rows,
                            pltpu.roll(value, amount, 1),
                            start,
                        )
            return carry

        lax.fori_loop(0, table[counts + k], strip, 0)

        for neighbour, start in ((me + n - 1, halo_lane[1]), (me + 1, halo_lane[0])):
            if k % 2 == 0:
                continue

            @pl.when(lax.bitwise_xor(lax.rem(neighbour, n), me) == k)
            def _(start=start, pack=pack):
                for piece in range(by_n * (1 + LEV)):
                    by, ch = divmod(piece, 1 + LEV)
                    base, origin = edge_spot(cap, piece)
                    for row in range(0, BH, SUB):
                        at = by * BH + row + PAD
                        mark(
                            ch,
                            slice(at, at + SUB),
                            turn(pack[base + row : base + row + SUB, :], start - origin),
                            start,
                        )

    if not rims:
        return
    rim = (lane >= own) & (lane < own + HALO) | (lane >= LANES - HALO)

    def mask(g, carry):
        at = pl.ds(pl.multiple_of(g * SUB + PAD, SUB), SUB)
        wet = grid[0, last, at, :]
        for ch in range(1 + LEV, channels):
            level = (ch - 1 - LEV) % LEV
            grid[ch, last, at, :] = jnp.where(
                rim & (wet <= level), 0.0, grid[ch, last, at, :]
            )
        return carry

    lax.fori_loop(0, deep // SUB - 2, mask, 0, unroll=4)
    low = deep - PAD - HALO
    for rows, first in zip(rims, (1 - odd, odd)):
        at = jnp.where(first == 1, PAD, low)
        for ch in range(channels):
            for j in range(tiles):
                spot = (ch * tiles + j) * HALO
                rows[spot : spot + HALO, :] = grid[ch, j, pl.ds(at, HALO), :]


def sideways(values):
    lane = lanes()
    count = len(values)
    left = [turn(v, 1) for v in values]
    right = [turn(v, -1) for v in values]
    west = [
        jnp.where(lane == 0, left[(j - 1) % count], left[j]) for j in range(count)
    ]
    east = [
        jnp.where(lane == LANES - 1, right[(j + 1) % count], right[j])
        for j in range(count)
    ]
    return east, west


def three(load, start):
    return load(start), load(start - 1), load(start + 1)


def diffuse(load, start):
    tiles = len(load(0, start))
    span = range(tiles)
    level_c, level_a, level_b = three(functools.partial(load, 0), start)
    level_e, _ = sideways(level_c)
    both_e = [jnp.minimum(level_c[j], level_e[j]) for j in span]
    both_a = [jnp.minimum(level_c[j], level_a[j]) for j in span]
    both_b = [jnp.minimum(level_c[j], level_b[j]) for j in span]
    forcing = [None] * tiles
    fresh = [[None] * LEV for _ in range(2)]
    for level in range(LEV):
        kappa_c, kappa_a, kappa_b = three(functools.partial(load, 1 + level), start)
        kappa_e, _ = sideways(kappa_c)
        face_e, face_a, face_b = (
            [jnp.where(both[j] > level, kappa_c[j] + other[j], 0.0) for j in span]
            for both, other in (
                (both_e, kappa_e),
                (both_a, kappa_a),
                (both_b, kappa_b),
            )
        )
        for tracer in range(2):
            ch = 1 + LEV + tracer * LEV + level
            here, above, below = three(functools.partial(load, ch), start)
            to_east, _ = sideways(here)
            flux = [face_e[j] * (to_east[j] - here[j]) for j in span]
            _, flux_w = sideways(flux)
            fresh[tracer][level] = [
                jnp.where(
                    level_c[j] > level,
                    here[j]
                    + 0.5
                    * (
                        (flux[j] - flux_w[j])
                        + face_a[j] * (above[j] - here[j])
                        + face_b[j] * (below[j] - here[j])
                    ),
                    0.0,
                )
                for j in span
            ]
        thickness = 1.0 + 0.5 * level
        for j in span:
            temp, salt = fresh[0][level][j], fresh[1][level][j]
            density = haline * salt - temp * (thermal + cabbeling * temp)
            if level:
                density = forcing[j] + thickness * density
            forcing[j] = density
    return fresh, forcing


def apply(here, above, below, levels):
    span = range(len(here))
    pair = [above[j] + below[j] for j in span]
    mixed = [here[j] + 0.5 * pair[j] for j in span]
    east, west = sideways(mixed)
    result = []
    for j in span:
        diagonal = 6.0 - SHIFT + 1.0
        total = jnp.full((SUB, LANES), diagonal / SCALE, F32)
        for k in range(1, LEV):
            diagonal += 1.0 + 0.5 * k
            total = jnp.where(levels[j] > k, diagonal / SCALE, total)
        total = total * here[j] - (pair[j] + (east[j] + west[j])) * (1.0 / SCALE)
        result.append(jnp.where(levels[j] > 0, total, 0.0))
    return result


def gather_products(carry, powers, centre, keep):
    carry = list(carry)
    span = range(len(powers[0]))
    for j in span:
        q0, q1, q2, q3 = (keep(q[j], j) for q in powers)
        b1 = q1 - centre * q0
        c2 = q2 - centre * q1
        c3 = q3 - centre * q2
        b2 = c2 - centre * b1
        b3 = (c3 - centre * c2) - centre * b2
        terms = (q0, b1, b2, b3)
        for at, (x, y) in enumerate(PAIRS):
            carry[at] = carry[at] + terms[x] * terms[y]
    return tuple(carry)


def total_row(totals):
    lane = lanes()[:1]
    row = jnp.zeros((1, LANES), F32)
    for at, total in enumerate(totals):
        total = jnp.sum(total, axis=(0, 1), keepdims=True)
        row = jnp.where(lane == at + 1, total, row)
    return row


def put_tracer(target, fresh, cols, at):
    for tracer in range(2):
        for level in range(LEV):
            for j, value in enumerate(fresh[tracer][level]):
                width = min(LANES, cols - j * LANES)
                target[tracer, level, at, j * LANES : j * LANES + width] = value[
                    :, :width
                ]


def inner_kernel(cols, grid, tracer_out, powers, sums, edges, fresh_rows, sems):
    lane = lanes()
    line = lax.broadcasted_iota(jnp.int32, (SUB, LANES), 0)
    _, tiles, deep, _ = grid.shape
    own = cols - (tiles - 1) * LANES
    first, end = PAD // SUB, (deep - PAD) // SUB
    zero = jnp.zeros((SUB, LANES), F32)

    def rows(ref, lead, start):
        return [ref[lead, j, pl.ds(start, SUB), :] for j in range(tiles)]

    def top(g):
        return pl.multiple_of(g * SUB, SUB)

    def step(g, carry):
        fresh, forcing = diffuse(functools.partial(rows, grid), top(g))
        put_tracer(
            fresh_rows, fresh, cols, pl.ds(pl.multiple_of(g * SUB - PAD, SUB), SUB)
        )
        for j in range(tiles):
            powers[0, j, pl.ds(top(g), SUB), :] = forcing[j]
        return carry

    chunks = sems.shape[0]
    size = (end - first) // chunks
    copies = []
    for chunk in range(chunks):
        begin = first + chunk * size
        stop = end if chunk == chunks - 1 else begin + size
        lax.fori_loop(begin, stop, step, 0, unroll=2)
        at = pl.ds(begin * SUB - PAD, (stop - begin) * SUB)
        copies.append(
            pltpu.make_async_copy(
                fresh_rows.at[:, :, at, :], tracer_out.at[:, :, at, :], sems.at[chunk]
            )
        )
        copies[-1].start()
    height = fresh_rows.shape[2]
    for tracer in range(2):
        for level in range(LEV):
            for side, row in ((0, 0), (1, height - SUB)):
                edges[side, tracer, level] = fresh_rows[
                    tracer, level, row : row + SUB, :
                ]

    def inside(value, j):
        return value if j < tiles - 1 else jnp.where(lane < own, value, 0.0)

    def upper(value, j):
        return jnp.where(line >= HALO, inside(value, j), 0.0)

    def lower(value, j):
        return jnp.where(line < SUB - HALO, inside(value, j), 0.0)

    def power(g, source):
        here, above, below = three(functools.partial(rows, powers, source), top(g))
        return here, apply(here, above, below, rows(grid, 0, top(g)))

    def put(g, target):
        here, result = power(g, target - 1)
        for j in range(tiles):
            powers[target, j, pl.ds(top(g), SUB), :] = result[j]
        return here, result

    def first_power(g, carry, keep=inside):
        here, result = put(g, 1)
        a, b = carry
        for j in range(tiles):
            v = keep(here[j], j)
            a = a + v * v
            b = b + v * keep(result[j], j)
        return a, b

    def everywhere(body, carry):
        carry = body(first, carry, upper)
        carry = lax.fori_loop(first + 1, end - 1, body, carry, unroll=end - first - 2)
        return body(end - 1, carry, lower)

    a, b = everywhere(first_power, (zero, zero))
    a = jnp.sum(a, axis=(0, 1), keepdims=True)
    b = jnp.sum(b, axis=(0, 1), keepdims=True)
    centre = jnp.where(a > 0, b / jnp.where(a > 0, a, 1.0), 0.0)
    centre = jnp.broadcast_to(centre, (SUB, LANES))
    lax.fori_loop(
        first, end, lambda g, c: (put(g, 2), c)[1], 0, unroll=end - first
    )

    def products(g, carry, keep=inside):
        here, result = power(g, 2)
        lower_powers = [rows(powers, k, top(g)) for k in range(2)]
        return gather_products(carry, (*lower_powers, here, result), centre, keep)

    totals = everywhere(products, (zero,) * len(PAIRS))
    for at, total in enumerate((*totals, centre)):
        sums[at] = total
    for copy in copies:
        copy.wait()


def border_kernel(
    cols, me_ref, grid, other_rows, pair_rows, powers, part, edges, border, sums,
    fresh_rows, field, local,
):
    lane = lanes()
    line = lax.broadcasted_iota(jnp.int32, (SUB, LANES), 0)
    channels, tiles, deep, _ = grid.shape
    own = cols - (tiles - 1) * LANES
    half = EDGE // 2
    even = me_ref[1] == 0
    for ch in range(channels):
        for j in range(tiles):
            at = slice((ch * tiles + j) * HALO, (ch * tiles + j + 1) * HALO)
            field[0, ch, j, half : half + SUB, :] = grid[ch, j, PAD : PAD + SUB, :]
            field[1, ch, j, half - SUB : half, :] = grid[
                ch, j, deep - PAD - SUB : deep - PAD, :
            ]
            pair, other = pair_rows[at, :], other_rows[at, :]
            field[0, ch, j, half - HALO : half, :] = jnp.where(even, other, pair)
            field[1, ch, j, half : half + HALO, :] = jnp.where(even, pair, other)
    for k in range(3):
        for j in range(tiles):
            local[0, k, j, half : half + SUB, :] = powers[k, j, PAD : PAD + SUB, :]
            local[1, k, j, half - SUB : half, :] = powers[
                k, j, deep - PAD - SUB : deep - PAD, :
            ]
    centre = part[len(PAIRS)]

    def rows_of(side):
        def rows(ref, lead, start):
            return [ref[side, lead, j, pl.ds(start, SUB), :] for j in range(tiles)]

        return rows

    start = half - HALO
    for side in range(2):
        fresh, forcing = diffuse(functools.partial(rows_of(side), field), start)
        for j in range(tiles):
            local[side, 0, j, start : start + SUB, :] = forcing[j]
        mine = line == (0 if side == 0 else SUB - 1)
        for tracer in range(2):
            for level in range(LEV):
                for j in range(tiles):
                    width = min(LANES, cols - j * LANES)
                    part_lanes = slice(j * LANES, j * LANES + width)
                    moved = pltpu.roll(fresh[tracer][level][j], HALO, 0)
                    fresh_rows[side, tracer, level, :, part_lanes] = jnp.where(
                        mine[:, :width],
                        moved[:, :width],
                        edges[side, tracer, level, :, part_lanes],
                    )

    def power(side, source):
        rows = rows_of(side)
        here, above, below = three(functools.partial(rows, local, source), start)
        return here, apply(here, above, below, rows(field, 0, start))

    for target in range(1, 3):
        for side in range(2):
            result = power(side, target - 1)[1]
            for j in range(tiles):
                local[side, target, j, start : start + SUB, :] = result[j]
    totals = tuple(part[at] for at in range(len(PAIRS)))
    for side in range(2):
        here, result = power(side, 2)
        lower_powers = [rows_of(side)(local, k, start) for k in range(2)]
        own_rows = half - side * SUB
        for k in range(3):
            for j in range(tiles):
                border[side, k, j] = local[side, k, j, own_rows : own_rows + SUB, :]
        bound = (1 - side) * HALO
        rim = (line >= bound) & (line < bound + HALO)

        def keep(value, j, rim=rim):
            inside = rim if j < tiles - 1 else rim & (lane < own)
            return jnp.where(inside, value, 0.0)

        totals = gather_products(
            totals, (*lower_powers, here, result), centre, keep
        )
    row = jnp.where(lane[:1] == 0, centre[:1], total_row(totals))
    sums[...] = jnp.broadcast_to(row, sums.shape)


PAIRS = ((0, 0), (0, 1), (0, 2), (0, 3), (1, 1), (1, 2), (1, 3), (2, 2), (2, 3))


def combine_kernel(
    cols, sums, powers, border, fresh_rows, tracer_in, tracer_out, stream_out, stream, sems
):
    rows = tracer_out.shape[2]
    patches = [
        pltpu.make_async_copy(
            fresh_rows.at[side],
            tracer_out.at[:, :, pl.ds(side * (rows - SUB), SUB), :],
            sems.at[2 + side],
        )
        for side in range(2)
    ]
    for copy in patches:
        copy.start()
    values = sums[...]
    lane = lax.broadcasted_iota(jnp.int32, values.shape, 1)

    def column(k):
        return jnp.sum(jnp.where(lane == k, values, 0.0), axis=1, keepdims=True)

    centre = column(0)
    gram = {pair: column(at + 1) for at, pair in enumerate(PAIRS)}

    def local(c):
        c = list(c) + [None] * (4 - len(c))
        c0, c1, c2, c3 = c
        result = [c0 + jnp.zeros_like(centre)]
        if c1 is not None:
            inner = c1
            slope = c1 + jnp.zeros_like(centre)
            if c2 is not None:
                inner = c1 + centre * (c2 if c3 is None else c2 + centre * c3)
                slope = c1 + centre * (
                    2.0 * c2 if c3 is None else 2.0 * c2 + 3.0 * (centre * c3)
                )
            result = [c0 + centre * inner, slope]
        if c2 is not None:
            result.append(c2 + jnp.zeros_like(centre) if c3 is None else c2 + 3.0 * (centre * c3))
        if c3 is not None:
            result.append(c3 + jnp.zeros_like(centre))
        return result

    def inner(x, y):
        u, v = local(x), local(y)
        total = jnp.zeros_like(centre)
        for i in range(len(u)):
            for j in range(len(v)):
                total = total + (u[i] * v[j]) * gram[(min(i, j), max(i, j))]
        return jnp.sum(total, axis=0, keepdims=True)

    def operate(c):
        result = [SHIFT * x for x in c] + [None]
        for i, x in enumerate(c):
            term = SCALE * x
            result[i + 1] = term if result[i + 1] is None else result[i + 1] + term
        return result

    one = jnp.ones((1, 1), F32)
    stream_c = [None] * 3
    residual, direction = [one], [one]
    norm = inner(residual, residual)
    for step in range(3):
        image = operate(direction)
        alpha = norm / inner(direction, image)
        for i, x in enumerate(direction):
            stream_c[i] = alpha * x if stream_c[i] is None else stream_c[i] + alpha * x
        if step == 2:
            break
        residual = [
            (residual[i] - alpha * image[i]) if i < len(residual) else -alpha * image[i]
            for i in range(len(image))
        ]
        fresh = inner(residual, residual)
        ratio = fresh / norm
        direction = [
            (residual[i] + ratio * direction[i]) if i < len(direction) else residual[i]
            for i in range(len(residual))
        ]
        norm = fresh

    tiles = powers.shape[1]
    height = stream.shape[0]
    weights = [jnp.broadcast_to(c, (SUB, LANES)) for c in stream_c]

    def put(out, load):
        for j in range(tiles):
            width = min(LANES, cols - j * LANES)
            value = sum(weights[k] * load(k, j) for k in range(3))
            stream[out, j * LANES : j * LANES + width] = value[:, :width]

    def write(g, carry):
        at = pl.ds(pl.multiple_of(g * SUB + PAD, SUB), SUB)
        out = pl.ds(pl.multiple_of(g * SUB, SUB), SUB)
        put(out, lambda k, j: powers[k, j, at, :])
        return carry

    middle = height // SUB // 2 * SUB
    copies = [
        pltpu.make_async_copy(stream.at[part, :], stream_out.at[part, :], sems.at[at])
        for at, part in enumerate((pl.ds(0, middle), pl.ds(middle, height - middle)))
    ]
    put(slice(0, SUB), lambda k, j: border[0, k, j])
    lax.fori_loop(1, middle // SUB, write, 0, unroll=3)
    copies[0].start()
    lax.fori_loop(middle // SUB, height // SUB - 1, write, 0, unroll=3)
    put(slice(height - SUB, height), lambda k, j: border[1, k, j])
    copies[1].start()
    for copy in (*patches, *copies):
        copy.wait()


def body(checkpoint, slot_dest, kmt, kappa):
    n = lax.axis_size("lon")
    lats = lax.axis_size("lat")
    lat = lax.axis_index("lat")
    me = jnp.stack([lax.axis_index("lon"), lax.rem(lat, 2)]).astype(jnp.int32)
    _, slots, values = checkpoint.shape
    rows, cols = kmt.shape
    by_n, bx_n = rows // BH, cols // BW
    cap = slots // n
    length = package_rows(cap, by_n)
    tiles = -(-(cols + 2 * HALO) // LANES)
    groups = slots // SUB
    edge_rows = -(-by_n * (1 + LEV) // 2) * BH
    if by_n * (1 + LEV) > 4 * cap:
        edge_rows = 2 * cap * BH + BH

    def fixed(value):
        return pltpu.with_memory_space_constraint(value, pltpu.HBM)

    order = sorted(range(1, n), key=lambda k: (k & 1, k < 2, -bin(k >> 1).count("1"), k))
    leader = order[0]
    kernels = (n, cap, bx_n, by_n, leader)
    lists = [
        pltpu.SMEM((1, n * slots), jnp.int32),
        pltpu.SMEM((n * cap + 1,), jnp.int32),
        pltpu.SMEM((slots + 1,), jnp.int32),
    ]
    leading, flat = pl.pallas_call(
        functools.partial(first_kernel, *kernels),
        out_shape=[shaped(length, LANES), shaped(slots * ROWS, LANES)],
        in_specs=[SM, HB, HB],
        out_specs=[VM, VM],
        scratch_shapes=lists
        + [
            pltpu.VMEM((groups, SUB, values), F32),
            pltpu.VMEM((n, BH, LANES), F32),
            pltpu.SMEM((n + 1,), jnp.int32),
            pltpu.SemaphoreType.DMA((groups + 1,)),
        ],
        compiler_params=params(),
        cost_estimate=cost(2 << 20, 4 << 20),
        name="first",
    )(me, fixed(slot_dest), fixed(checkpoint))

    def send(value, k):
        return lax.ppermute(value, "lon", [(i, i ^ k) for i in range(n)])

    received = {leader: send(leading, leader)}
    second = pl.pallas_call(
        functools.partial(second_kernel, *kernels),
        out_shape=[shaped(length, LANES)] * (n - 1),
        in_specs=[SM, HB, VM, HB, HB],
        out_specs=[VM] * (n - 1),
        scratch_shapes=lists
        + [
            pltpu.VMEM((rows, cols), jnp.int32),
            pltpu.VMEM((LEV, rows, cols), F32),
            pltpu.VMEM((n, BH, LANES), F32),
            pltpu.VMEM((2, edge_rows, LANES), F32),
            pltpu.SMEM((n + 1,), jnp.int32),
            pltpu.SemaphoreType.DMA((3,)),
        ],
        compiler_params=params(),
        cost_estimate=cost(16 << 20, 16 << 20),
        name="second",
    )
    operands = [fixed(x) for x in (slot_dest, kmt, kappa)]
    own, *packs = second(me, operands[0], flat, *operands[1:])
    packs = dict(zip([k for k in range(1, n) if k != leader], packs))
    received |= {k: send(packs[k], k) for k in order[1:]}
    received[0] = own

    channels = 1 + 3 * LEV
    deep = rows + 2 * PAD
    table, grid = pl.pallas_call(
        functools.partial(base_kernel, n, cap, bx_n, by_n),
        out_shape=[
            shaped(n * (cap + 1) + (n + 1) * (1 + 2 * by_n), dtype=jnp.int32),
            shaped(channels, tiles, deep, LANES),
        ],
        in_specs=[SM, SM, VM, VM],
        out_specs=[SM, VM],
        scratch_shapes=[pltpu.SMEM((n * slots + 1,), jnp.int32)],
        compiler_params=params(),
        cost_estimate=cost(1 << 20, 2 << 20),
        name="base",
    )(me, slot_dest, kmt, kappa)

    def held(value):
        return pltpu.with_memory_space_constraint(value, pltpu.VMEM)

    rim = channels * tiles * HALO
    half, quarter = n // 2 - 1, n // 4
    odd = order[half:]
    parts = [
        [0] + order[:half],
        odd[-1:] + odd[: quarter - 1],
        odd[quarter - 1 : -2],
        odd[-2:-1],
    ]
    parts = [part for part in parts if part]
    for stage, which in enumerate(parts):
        shapes = [shaped(channels, tiles, deep, LANES)]
        if stage == len(parts) - 1:
            shapes += [shaped(rim, LANES)] * 2
        grid, *rims = pl.pallas_call(
            functools.partial(place_kernel, n, cap, bx_n, by_n, cols, which),
            out_shape=shapes,
            in_specs=[SM, SM] + [VM] * (1 + len(which)),
            out_specs=[VM] * len(shapes),
            input_output_aliases={2: 0},
            compiler_params=params(),
            cost_estimate=cost(2 << 20, 2 << 20),
        )(me, table, held(grid), *[received[k] for k in which])

    swaps = [
        [(i, i ^ 1) for i in range(lats) if i ^ 1 < lats],
        [(i, j) for i in range(lats) for j in [(i - 1 ^ 1) + 1] if 0 <= j < lats],
    ]
    other_rows, pair_rows = (
        lax.ppermute(value, "lat", swap) for value, swap in zip(rims, swaps[::-1])
    )

    devices = n * lats
    tracer_shape = shaped(2, LEV, rows, cols)
    tracer, powers, part, edges = pl.pallas_call(
        functools.partial(inner_kernel, cols),
        out_shape=[
            tracer_shape,
            shaped(3, tiles, deep, LANES),
            shaped(len(PAIRS) + 1, SUB, LANES),
            shaped(2, 2, LEV, SUB, cols),
        ],
        in_specs=[VM],
        out_specs=[HB, VM, VM, VM],
        scratch_shapes=[
            pltpu.VMEM((2, LEV, rows, cols), F32),
            pltpu.SemaphoreType.DMA((5,)),
        ],
        compiler_params=params(),
        cost_estimate=cost(16 << 20, 6 << 20),
        name="inner",
    )(grid)
    border, sums, fresh_rows = pl.pallas_call(
        functools.partial(border_kernel, cols),
        out_shape=[
            shaped(2, 3, tiles, SUB, LANES),
            shaped(devices, LANES),
            shaped(2, 2, LEV, SUB, cols),
        ],
        in_specs=[SM, VM, VM, VM, VM, VM, VM],
        out_specs=[VM, VM, VM],
        scratch_shapes=[
            pltpu.VMEM((2, channels, tiles, EDGE, LANES), F32),
            pltpu.VMEM((2, 3, tiles, EDGE, LANES), F32),
        ],
        compiler_params=params(),
        cost_estimate=cost(2 << 20, 1 << 20),
        name="border",
    )(me, grid, other_rows, pair_rows, powers, part, edges)

    everyone = lax.all_to_all(sums, ("lon", "lat"), 0, 0, tiled=True)
    tracer, stream = pl.pallas_call(
        functools.partial(combine_kernel, cols),
        out_shape=[tracer_shape, shaped(rows, cols)],
        in_specs=[VM, VM, VM, VM, HB],
        out_specs=[HB, HB],
        scratch_shapes=[
            pltpu.VMEM((rows, cols), F32),
            pltpu.SemaphoreType.DMA((4,)),
        ],
        input_output_aliases={4: 0},
        compiler_params=params(),
        cost_estimate=cost(1 << 20, 2 << 20),
        name="combine",
    )(everyone, powers, border, fresh_rows, fixed(tracer))
    return tracer, stream


def solution(mesh):
    placed = (P("lat", "lon", None), P("lat", None), P("lat", "lon"), P(None, "lat", "lon"))
    return jax.shard_map(
        body,
        mesh=mesh,
        in_specs=placed,
        out_specs=(P(None, None, "lat", "lon"), P("lat", "lon")),
        check_vma=False,
    )
```

```python
import functools

import jax
import jax.numpy as jnp
from jax import lax
from jax.experimental import pallas as pl
from jax.experimental.pallas import tpu as pltpu
from jax.sharding import PartitionSpec as P


BH = 40
BW = 60
LEV = 2
HALO = 4
LANES = 128
SUB = 8
PAD = SUB
EDGE = 4 * SUB
ROWS = LEV * BH
HALF = LANES // 2
SHIFT = 8.0
SCALE = 8.0

thermal = 0.25
haline = 0.75
cabbeling = 0.05

VM = pl.BlockSpec(memory_space=pltpu.VMEM)
SM = pl.BlockSpec(memory_space=pltpu.SMEM)
HB = pl.BlockSpec(memory_space=pltpu.HBM)
F32 = jnp.float32


def params():
    return pltpu.CompilerParams(vmem_limit_bytes=24 << 20)


def cost(flops, moved):
    return pl.CostEstimate(flops=flops, bytes_accessed=moved, transcendentals=0)


def shaped(*dims, dtype=F32):
    return jax.ShapeDtypeStruct(dims, dtype)


def lanes():
    return lax.broadcasted_iota(jnp.int32, (SUB, LANES), 1)


def turn(value, amount):
    if isinstance(amount, int):
        amount %= LANES
        if amount == 0:
            return value
    return pltpu.roll(value, amount, 1)


def strip_lane(side, by, level, tracer, block_rows):
    return HALO * ((side * block_rows + by) * LEV + level) + HALF * tracer


def edge_spot(cap, piece):
    if piece < 4 * cap:
        return piece // 2 * BH, HALF * (1 + piece % 2) - HALO
    return cap * ROWS + BH, HALO * (piece - 4 * cap)


def package_rows(cap, by_n):
    return cap * ROWS + (2 * BH if by_n * (1 + LEV) > 4 * cap else BH)


def block_rows(flat, start, row):
    return flat[pl.ds(start + row * SUB, SUB, stride=SUB), :]


def block_start(i):
    return lax.div(i, SUB) * (ROWS * SUB) + lax.rem(i, SUB)


def plan(n, cap, bx_n, me, dest, source, count, todo, wanted):
    slots = todo.shape[0] - 1
    for k in range(n + 1):
        count[k] = 0
    for at in range(n * cap + 1):
        source[at] = 0

    def assign(i, found):
        d = dest[0, me * slots + i]
        used = d >= 0
        place = jnp.maximum(d, 0)
        owner = lax.div(place, slots)
        k = jnp.where(used, lax.bitwise_xor(owner, me), n)
        c = count[k]
        count[k] = c + 1
        source[jnp.where(used, k * cap + c, n * cap)] = block_start(i)
        bx = lax.rem(place, bx_n)
        partner = lax.bitwise_xor(
            lax.rem(owner + jnp.where(bx == 0, n - 1, 1), n), me
        )
        todo[found] = i
        holds = used & ((bx == 0) | (bx == bx_n - 1)) & wanted(partner)
        return found + holds.astype(jnp.int32)

    return lax.fori_loop(0, slots, assign, 0, unroll=4)


def fill_strips(n, bx_n, by_n, me, dest, flat, strips, todo, found):
    slots = bx_n * by_n
    spot_lane = lanes() & (HALF - 1)

    def strip(at, carry):
        i = todo[at]
        place = dest[0, me * slots + i]
        spot = lax.rem(place, slots)
        by = lax.div(spot, bx_n)
        side = (lax.rem(spot, bx_n) == 0).astype(jnp.int32)
        owner = lax.div(place, slots)
        k = lax.bitwise_xor(lax.rem(owner + jnp.where(side == 0, 1, n - 1), n), me)
        start = block_start(i)
        origin = jnp.where(side == 0, BW - HALO, 0)
        for level in range(LEV):
            target = strip_lane(side, by, level, 0, by_n)
            amount = lax.rem(target - origin + LANES, LANES)
            here = (spot_lane >= target) & (spot_lane < target + HALO)
            for row in range(0, BH, SUB):
                value = block_rows(flat, start, level * BH + row)
                pltpu.store(
                    strips.at[k, row : row + SUB, :],
                    pltpu.roll(value, amount, 1),
                    mask=here,
                )
        return carry

    lax.fori_loop(0, found, strip, 0)


def assemble(out, k, cap, source, flat, strips, edges=None, which=None, in_blocks=0):
    spare = (lanes() & (HALF - 1)) >= HALF - HALO
    for c in range(cap):
        start = source[k * cap + c]
        for row in range(0, ROWS, SUB):
            value = block_rows(flat, start, row)
            at = c * ROWS + row
            if at < in_blocks:
                value = jnp.where(spare, edges[which, at : at + SUB, :], value)
            out[at : at + SUB, :] = value
    for row in range(0, BH, SUB):
        at = cap * ROWS + row
        out[at : at + SUB, :] = strips[k, row : row + SUB, :]


def first_kernel(n, cap, bx_n, by_n, *refs):
    me_ref, dest_hbm, blocks_hbm = refs[:3]
    outs = refs[3 : n // 2 + 2]
    flat, dest, source, todo, blocks, strips, count, sems = refs[n // 2 + 2 :]
    groups = blocks.shape[0]
    slots = groups * SUB
    me = me_ref[0]
    lane = lanes()
    first = pltpu.make_async_copy(dest_hbm, dest, sems.at[groups])
    first.start()

    def loading(g):
        rows = pl.ds(pl.multiple_of(g * SUB, SUB), SUB)
        return pltpu.make_async_copy(
            blocks_hbm.at[0, rows, :], blocks.at[g], sems.at[g]
        )

    for g in range(groups):
        loading(g).start()
    first.wait()
    found = plan(
        n, cap, bx_n, me, dest, source, count, todo, lambda k: (k > 0) & (k & 1 == 0)
    )

    def regroup(group, carry):
        loading(group).wait()

        def load(q):
            return blocks[group, :, q * LANES : (q + 1) * LANES]

        limit = blocks.shape[2] // LANES - 1
        for row in range(ROWS):
            q, o = divmod(row * BW, LANES)
            p = (ROWS + row) * BW // LANES
            if o == 0:
                value = jnp.where(lane >= HALF, load(p), load(q))
            elif o <= HALF:
                low = load(p if o == HALF else min(p + 1, limit))
                value = jnp.where(lane >= o, load(q), low)
                if o < HALF:
                    value = jnp.where(lane >= o + HALF, load(p), value)
            else:
                value = jnp.where(lane >= o - HALF, load(p), load(q + 1))
                value = jnp.where(lane >= o, load(q), value)
            at = pl.multiple_of(group * (ROWS * SUB) + row * SUB, SUB)
            flat[pl.ds(at, SUB), :] = turn(value, -o)
        return carry

    lax.fori_loop(0, groups, regroup, 0)
    fill_strips(n, bx_n, by_n, me, dest, flat, strips, todo, found)
    for k in range(2, n, 2):
        assemble(outs[k // 2 - 1], k, cap, source, flat, strips)


def second_kernel(n, cap, bx_n, by_n, *refs):
    me_ref, dest_hbm, flat, kmt_hbm, kappa_hbm = refs[:5]
    outs = refs[5 : n // 2 + 6]
    dest, source, todo, kmt, kappa, strips, edges, count, sems = refs[n // 2 + 6 :]
    me = me_ref[0]
    lane = lanes()
    length = outs[0].shape[0]
    cols = kmt.shape[1]
    first, *copies = [
        pltpu.make_async_copy(dest_hbm, dest, sems.at[0]),
        pltpu.make_async_copy(kmt_hbm, kmt, sems.at[1]),
        pltpu.make_async_copy(kappa_hbm, kappa, sems.at[2]),
    ]
    for copy in (first, *copies):
        copy.start()
    first.wait()
    found = plan(
        n, cap, bx_n, me, dest, source, count, todo, lambda k: (k == 0) | (k & 1 == 1)
    )
    fill_strips(n, bx_n, by_n, me, dest, flat, strips, todo, found)
    for copy in copies:
        copy.wait()
    zero = jnp.zeros((SUB, LANES), F32)
    for at in range(0, edges.shape[1], SUB):
        for side in range(2):
            edges[side, at : at + SUB, :] = zero
    for side, start in ((0, cols - HALO), (1, 0)):
        tile = start // LANES * LANES
        width = min(LANES, cols - tile)
        for piece in range(by_n * (1 + LEV)):
            by, ch = divmod(piece, 1 + LEV)
            base, target = edge_spot(cap, piece)
            if piece >= 4 * cap:
                base -= cap * ROWS + BH - 2 * cap * BH
            here = (lane >= target) & (lane < target + HALO)
            for row in range(0, BH, SUB):
                at = slice(by * BH + row, by * BH + row + SUB)
                if ch == 0:
                    value = kmt[at, tile : tile + width].astype(F32)
                else:
                    value = kappa[ch - 1, at, tile : tile + width]
                if width < LANES:
                    value = jnp.concatenate([value, zero[:, width:]], axis=1)
                pltpu.store(
                    edges.at[side, base + row : base + row + SUB, :],
                    turn(value, target - (start - tile)),
                    mask=here,
                )
    eastern = lax.bitwise_xor(lax.rem(me + 1, n), me)
    in_blocks = min(edges.shape[1], 2 * cap * BH)
    for out, k in zip(outs, [0, *range(1, n, 2)]):
        which = jnp.where(eastern == k, 0, 1)
        assemble(out, k, cap, source, flat, strips, edges, which, in_blocks)
        if length > cap * ROWS + BH:
            for row in range(0, BH, SUB):
                at = cap * ROWS + BH + row
                out[at : at + SUB, :] = edges[
                    which, in_blocks + row : in_blocks + row + SUB, :
                ]


def base_kernel(n, cap, bx_n, by_n, me_ref, dest, kmt, kappa, table, grid, bringer):
    me = me_ref[0]
    slots = bx_n * by_n
    channels, tiles, deep, _ = grid.shape
    cols = kmt.shape[1]
    zero = jnp.zeros((SUB, LANES), F32)
    west = lax.rem(me + n - 1, n)
    east = lax.rem(me + 1, n)
    for at in range(n * (cap + 1)):
        table[at] = -1
    sides = [(west, by * bx_n + bx_n - 1) for by in range(by_n)]
    sides += [(east, by * bx_n) for by in range(by_n)]
    for owner, spot in sides:
        bringer[owner * slots + spot + 1] = -1

    def owner_loop(s, carry):
        k = lax.bitwise_xor(s, me)

        def slot_loop(i, c):
            d = dest[0, s * slots + i]
            bringer[d + 1] = k
            spot = d - me * slots
            mine = (spot >= 0) & (spot < slots)
            table[k * (cap + 1) + c] = jnp.where(mine, spot, -1)
            return c + mine.astype(jnp.int32)

        lax.fori_loop(0, slots, slot_loop, 0, unroll=8)
        return carry

    lax.fori_loop(0, n, owner_loop, 0)
    counts = n * (cap + 1)
    lists = counts + n + 1
    for k in range(n + 1):
        table[counts + k] = 0
    for at, (owner, spot) in enumerate(sides):
        k = bringer[owner * slots + spot + 1]
        k = jnp.where(k < 0, n, k)
        c = table[counts + k]
        table[counts + k] = c + 1
        table[lists + k * len(sides) + c] = at

    def clear(g, carry):
        at = pl.ds(pl.multiple_of(g * SUB, SUB), SUB)
        for ch in range(channels):
            for j in range(tiles):
                grid[ch, j, at, :] = zero
        return carry

    lax.fori_loop(0, deep // SUB, clear, 0)

    def lay(g, carry):
        at = pl.ds(pl.multiple_of(g * SUB, SUB), SUB)
        out = pl.ds(pl.multiple_of(g * SUB + PAD, SUB), SUB)
        for ch in range(1 + LEV):
            for j in range(tiles):
                width = min(LANES, cols - j * LANES)
                part = slice(j * LANES, j * LANES + width)
                if ch == 0:
                    value = kmt[at, part].astype(F32)
                else:
                    value = kappa[ch - 1, at, part]
                grid[ch, j, out, 0:width] = value
        return carry

    lax.fori_loop(0, kmt.shape[0] // SUB, lay, 0)


def place_kernel(n, cap, bx_n, by_n, cols, which, left, *refs):
    count = len(which)
    me_ref, table, _ = refs[:3]
    odd = me_ref[1]
    packs = refs[3 : 3 + count]
    grid, *rims = refs[3 + count :]
    me = me_ref[0]
    lane = lanes()
    channels, tiles, deep, _ = grid.shape
    last = tiles - 1
    own = cols - last * LANES
    halo_lane = (own, LANES - HALO)

    def mark(ch, at, value, start, allowed=True):
        here = (lane >= start) & (lane < start + HALO) & allowed
        pltpu.store(grid.at[ch, last, at, :], value, mask=here)

    for k, pack in zip(which, packs):

        for c in range(cap):
            spot = table[k * (cap + 1) + c]
            valid = spot >= 0
            spot = jnp.maximum(spot, 0)
            by = lax.div(spot, bx_n)
            offset = lax.rem(spot, bx_n) * BW
            tile = lax.div(offset, LANES)
            following = jnp.minimum(tile + 1, last)
            start = lax.rem(offset, LANES)
            begin = jnp.where(valid, start, LANES)
            here = (lane >= begin) & (lane < begin + BW)
            spill = lane < jnp.where(valid, start + BW - LANES, 0)
            for row in range(0, BH, SUB):
                at = pl.ds(pl.multiple_of(by * BH + row + PAD, SUB), SUB)
                depth = grid[0, tile, at, :], grid[0, following, at, :]
                for level in range(LEV):
                    place = c * ROWS + level * BH + row
                    value = pack[place : place + SUB, :]
                    masks = here & (depth[0] > level), spill & (depth[1] > level)
                    for tracer in range(2):
                        ch = 1 + LEV + tracer * LEV + level
                        turned = pltpu.roll(
                            value, lax.rem(start + tracer * HALF, LANES), 1
                        )
                        for target, mask in zip((tile, following), masks):
                            pltpu.store(grid.at[ch, target, at, :], turned, mask=mask)

        counts = n * (cap + 1)
        lists = counts + n + 1 + k * 2 * by_n

        def strip(at, carry, pack=pack, lists=lists):
            index = table[lists + at]
            by = lax.rem(index, by_n)
            start = jnp.where(index < by_n, halo_lane[1], halo_lane[0])
            for row in range(0, BH, SUB):
                rows = pl.ds(pl.multiple_of(by * BH + row + PAD, SUB), SUB)
                value = pack[cap * ROWS + row : cap * ROWS + row + SUB, :]
                wet = grid[0, last, rows, :]
                for level in range(LEV):
                    for tracer in range(2):
                        origin = strip_lane(0, index, level, tracer, by_n)
                        amount = lax.rem(start - origin + LANES, LANES)
                        mark(
                            1 + LEV + tracer * LEV + level,
                            rows,
                            pltpu.roll(value, amount, 1),
                            start,
                            wet > level if left == 0 else True,
                        )
            return carry

        lax.fori_loop(0, table[counts + k], strip, 0)

        for neighbour, start in ((me + n - 1, halo_lane[1]), (me + 1, halo_lane[0])):
            if k % 2 == 0:
                continue

            @pl.when(lax.bitwise_xor(lax.rem(neighbour, n), me) == k)
            def _(start=start, pack=pack):
                for piece in range(by_n * (1 + LEV)):
                    by, ch = divmod(piece, 1 + LEV)
                    base, origin = edge_spot(cap, piece)
                    for row in range(0, BH, SUB):
                        at = by * BH + row + PAD
                        mark(
                            ch,
                            slice(at, at + SUB),
                            turn(pack[base + row : base + row + SUB, :], start - origin),
                            start,
                        )

    if left > 1:
        return
    rim = (lane >= own) & (lane < own + HALO) | (lane >= LANES - HALO)

    def mask(g, carry):
        at = pl.ds(pl.multiple_of(g * SUB + PAD, SUB), SUB)
        wet = grid[0, last, at, :]
        for ch in range(1 + LEV, channels):
            level = (ch - 1 - LEV) % LEV
            grid[ch, last, at, :] = jnp.where(
                rim & (wet <= level), 0.0, grid[ch, last, at, :]
            )
        return carry

    if left == 1:
        lax.fori_loop(0, deep // SUB - 2, mask, 0, unroll=4)
        return
    low = deep - PAD - HALO
    for rows, first in zip(rims, (1 - odd, odd)):
        at = jnp.where(first == 1, PAD, low)
        for ch in range(channels):
            for j in range(tiles):
                spot = (ch * tiles + j) * HALO
                rows[spot : spot + HALO, :] = grid[ch, j, pl.ds(at, HALO), :]


def sideways(values):
    lane = lanes()
    count = len(values)
    left = [turn(v, 1) for v in values]
    right = [turn(v, -1) for v in values]
    west = [
        jnp.where(lane == 0, left[(j - 1) % count], left[j]) for j in range(count)
    ]
    east = [
        jnp.where(lane == LANES - 1, right[(j + 1) % count], right[j])
        for j in range(count)
    ]
    return east, west


def three(load, start):
    return load(start), load(start - 1), load(start + 1)


def diffuse(load, start):
    tiles = len(load(0, start))
    span = range(tiles)
    level_c, level_a, level_b = three(functools.partial(load, 0), start)
    level_e, _ = sideways(level_c)
    both_e = [jnp.minimum(level_c[j], level_e[j]) for j in span]
    both_a = [jnp.minimum(level_c[j], level_a[j]) for j in span]
    both_b = [jnp.minimum(level_c[j], level_b[j]) for j in span]
    forcing = [None] * tiles
    fresh = [[None] * LEV for _ in range(2)]
    for level in range(LEV):
        kappa_c, kappa_a, kappa_b = three(functools.partial(load, 1 + level), start)
        kappa_e, _ = sideways(kappa_c)
        face_e, face_a, face_b = (
            [jnp.where(both[j] > level, kappa_c[j] + other[j], 0.0) for j in span]
            for both, other in (
                (both_e, kappa_e),
                (both_a, kappa_a),
                (both_b, kappa_b),
            )
        )
        for tracer in range(2):
            ch = 1 + LEV + tracer * LEV + level
            here, above, below = three(functools.partial(load, ch), start)
            to_east, _ = sideways(here)
            flux = [face_e[j] * (to_east[j] - here[j]) for j in span]
            _, flux_w = sideways(flux)
            fresh[tracer][level] = [
                jnp.where(
                    level_c[j] > level,
                    here[j]
                    + 0.5
                    * (
                        (flux[j] - flux_w[j])
                        + face_a[j] * (above[j] - here[j])
                        + face_b[j] * (below[j] - here[j])
                    ),
                    0.0,
                )
                for j in span
            ]
        thickness = 1.0 + 0.5 * level
        for j in span:
            temp, salt = fresh[0][level][j], fresh[1][level][j]
            density = haline * salt - temp * (thermal + cabbeling * temp)
            if level:
                density = forcing[j] + thickness * density
            forcing[j] = density
    return fresh, forcing


def apply(here, above, below, levels):
    span = range(len(here))
    pair = [above[j] + below[j] for j in span]
    mixed = [here[j] + 0.5 * pair[j] for j in span]
    east, west = sideways(mixed)
    result = []
    for j in span:
        diagonal = 6.0 - SHIFT + 1.0
        total = jnp.full((SUB, LANES), diagonal / SCALE, F32)
        for k in range(1, LEV):
            diagonal += 1.0 + 0.5 * k
            total = jnp.where(levels[j] > k, diagonal / SCALE, total)
        total = total * here[j] - (pair[j] + (east[j] + west[j])) * (1.0 / SCALE)
        result.append(jnp.where(levels[j] > 0, total, 0.0))
    return result


def gather_products(carry, powers, centre, keep):
    carry = list(carry)
    span = range(len(powers[0]))
    for j in span:
        q0, q1, q2, q3 = (keep(q[j], j) for q in powers)
        b1 = q1 - centre * q0
        c2 = q2 - centre * q1
        c3 = q3 - centre * q2
        b2 = c2 - centre * b1
        b3 = (c3 - centre * c2) - centre * b2
        terms = (q0, b1, b2, b3)
        for at, (x, y) in enumerate(PAIRS):
            carry[at] = carry[at] + terms[x] * terms[y]
    return tuple(carry)


def total_row(totals):
    lane = lanes()[:1]
    row = jnp.zeros((1, LANES), F32)
    for at, total in enumerate(totals):
        total = jnp.sum(total, axis=(0, 1), keepdims=True)
        row = jnp.where(lane == at + 1, total, row)
    return row


def put_tracer(target, fresh, cols, at):
    for tracer in range(2):
        for level in range(LEV):
            for j, value in enumerate(fresh[tracer][level]):
                width = min(LANES, cols - j * LANES)
                target[tracer, level, at, j * LANES : j * LANES + width] = value[
                    :, :width
                ]


def inner_kernel(cols, grid, tracer_out, powers, sums, edges, fresh_rows, sems):
    lane = lanes()
    line = lax.broadcasted_iota(jnp.int32, (SUB, LANES), 0)
    _, tiles, deep, _ = grid.shape
    own = cols - (tiles - 1) * LANES
    first, end = PAD // SUB, (deep - PAD) // SUB
    zero = jnp.zeros((SUB, LANES), F32)

    def rows(ref, lead, start):
        return [ref[lead, j, pl.ds(start, SUB), :] for j in range(tiles)]

    def top(g):
        return pl.multiple_of(g * SUB, SUB)

    def step(g, carry):
        fresh, forcing = diffuse(functools.partial(rows, grid), top(g))
        put_tracer(
            fresh_rows, fresh, cols, pl.ds(pl.multiple_of(g * SUB - PAD, SUB), SUB)
        )
        for j in range(tiles):
            powers[0, j, pl.ds(top(g), SUB), :] = forcing[j]
        return carry

    chunks = sems.shape[0]
    size = (end - first) // chunks
    copies = []
    for chunk in range(chunks):
        begin = first + chunk * size
        stop = end if chunk == chunks - 1 else begin + size
        lax.fori_loop(begin, stop, step, 0, unroll=2)
        at = pl.ds(begin * SUB - PAD, (stop - begin) * SUB)
        copies.append(
            pltpu.make_async_copy(
                fresh_rows.at[:, :, at, :], tracer_out.at[:, :, at, :], sems.at[chunk]
            )
        )
        copies[-1].start()
    height = fresh_rows.shape[2]
    for tracer in range(2):
        for level in range(LEV):
            for side, row in ((0, 0), (1, height - SUB)):
                edges[side, tracer, level] = fresh_rows[
                    tracer, level, row : row + SUB, :
                ]

    def inside(value, j):
        return value if j < tiles - 1 else jnp.where(lane < own, value, 0.0)

    def upper(value, j):
        return jnp.where(line >= HALO, inside(value, j), 0.0)

    def lower(value, j):
        return jnp.where(line < SUB - HALO, inside(value, j), 0.0)

    def power(g, source):
        here, above, below = three(functools.partial(rows, powers, source), top(g))
        return here, apply(here, above, below, rows(grid, 0, top(g)))

    def put(g, target):
        here, result = power(g, target - 1)
        for j in range(tiles):
            powers[target, j, pl.ds(top(g), SUB), :] = result[j]
        return here, result

    def first_power(g, carry, keep=inside):
        here, result = put(g, 1)
        a, b = carry
        for j in range(tiles):
            v = keep(here[j], j)
            a = a + v * v
            b = b + v * keep(result[j], j)
        return a, b

    def everywhere(body, carry):
        carry = body(first, carry, upper)
        carry = lax.fori_loop(first + 1, end - 1, body, carry, unroll=end - first - 2)
        return body(end - 1, carry, lower)

    a, b = everywhere(first_power, (zero, zero))
    a = jnp.sum(a, axis=(0, 1), keepdims=True)
    b = jnp.sum(b, axis=(0, 1), keepdims=True)
    centre = jnp.where(a > 0, b / jnp.where(a > 0, a, 1.0), 0.0)
    centre = jnp.broadcast_to(centre, (SUB, LANES))
    lax.fori_loop(
        first, end, lambda g, c: (put(g, 2), c)[1], 0, unroll=end - first
    )

    def products(g, carry, keep=inside):
        here, result = power(g, 2)
        lower_powers = [rows(powers, k, top(g)) for k in range(2)]
        return gather_products(carry, (*lower_powers, here, result), centre, keep)

    totals = everywhere(products, (zero,) * len(PAIRS))
    for at, total in enumerate((*totals, centre)):
        sums[at] = total
    for copy in copies:
        copy.wait()


def border_kernel(
    cols, me_ref, grid, other_rows, pair_rows, powers, part, edges, border, sums,
    fresh_rows, field, local,
):
    lane = lanes()
    line = lax.broadcasted_iota(jnp.int32, (SUB, LANES), 0)
    channels, tiles, deep, _ = grid.shape
    own = cols - (tiles - 1) * LANES
    half = EDGE // 2
    even = me_ref[1] == 0
    for ch in range(channels):
        for j in range(tiles):
            at = slice((ch * tiles + j) * HALO, (ch * tiles + j + 1) * HALO)
            field[0, ch, j, half : half + SUB, :] = grid[ch, j, PAD : PAD + SUB, :]
            field[1, ch, j, half - SUB : half, :] = grid[
                ch, j, deep - PAD - SUB : deep - PAD, :
            ]
            pair, other = pair_rows[at, :], other_rows[at, :]
            field[0, ch, j, half - HALO : half, :] = jnp.where(even, other, pair)
            field[1, ch, j, half : half + HALO, :] = jnp.where(even, pair, other)
    for k in range(3):
        for j in range(tiles):
            local[0, k, j, half : half + SUB, :] = powers[k, j, PAD : PAD + SUB, :]
            local[1, k, j, half - SUB : half, :] = powers[
                k, j, deep - PAD - SUB : deep - PAD, :
            ]
    centre = part[len(PAIRS)]

    def rows_of(side):
        def rows(ref, lead, start):
            return [ref[side, lead, j, pl.ds(start, SUB), :] for j in range(tiles)]

        return rows

    start = half - HALO
    for side in range(2):
        fresh, forcing = diffuse(functools.partial(rows_of(side), field), start)
        for j in range(tiles):
            local[side, 0, j, start : start + SUB, :] = forcing[j]
        mine = line == (0 if side == 0 else SUB - 1)
        for tracer in range(2):
            for level in range(LEV):
                for j in range(tiles):
                    width = min(LANES, cols - j * LANES)
                    part_lanes = slice(j * LANES, j * LANES + width)
                    moved = pltpu.roll(fresh[tracer][level][j], HALO, 0)
                    fresh_rows[side, tracer, level, :, part_lanes] = jnp.where(
                        mine[:, :width],
                        moved[:, :width],
                        edges[side, tracer, level, :, part_lanes],
                    )

    def power(side, source):
        rows = rows_of(side)
        here, above, below = three(functools.partial(rows, local, source), start)
        return here, apply(here, above, below, rows(field, 0, start))

    for target in range(1, 3):
        for side in range(2):
            result = power(side, target - 1)[1]
            for j in range(tiles):
                local[side, target, j, start : start + SUB, :] = result[j]
    totals = tuple(part[at] for at in range(len(PAIRS)))
    for side in range(2):
        here, result = power(side, 2)
        lower_powers = [rows_of(side)(local, k, start) for k in range(2)]
        own_rows = half - side * SUB
        for k in range(3):
            for j in range(tiles):
                border[side, k, j] = local[side, k, j, own_rows : own_rows + SUB, :]
        bound = (1 - side) * HALO
        rim = (line >= bound) & (line < bound + HALO)

        def keep(value, j, rim=rim):
            inside = rim if j < tiles - 1 else rim & (lane < own)
            return jnp.where(inside, value, 0.0)

        totals = gather_products(
            totals, (*lower_powers, here, result), centre, keep
        )
    row = jnp.where(lane[:1] == 0, centre[:1], total_row(totals))
    sums[...] = jnp.broadcast_to(row, sums.shape)


PAIRS = ((0, 0), (0, 1), (0, 2), (0, 3), (1, 1), (1, 2), (1, 3), (2, 2), (2, 3))


def combine_kernel(
    cols, sums, powers, border, fresh_rows, tracer_in, tracer_out, stream_out, stream, sems
):
    rows = tracer_out.shape[2]
    patches = [
        pltpu.make_async_copy(
            fresh_rows.at[side],
            tracer_out.at[:, :, pl.ds(side * (rows - SUB), SUB), :],
            sems.at[2 + side],
        )
        for side in range(2)
    ]
    for copy in patches:
        copy.start()
    values = sums[...]
    lane = lax.broadcasted_iota(jnp.int32, values.shape, 1)

    def column(k):
        return jnp.sum(jnp.where(lane == k, values, 0.0), axis=1, keepdims=True)

    centre = column(0)
    gram = {pair: column(at + 1) for at, pair in enumerate(PAIRS)}

    def local(c):
        c = list(c) + [None] * (4 - len(c))
        c0, c1, c2, c3 = c
        result = [c0 + jnp.zeros_like(centre)]
        if c1 is not None:
            inner = c1
            slope = c1 + jnp.zeros_like(centre)
            if c2 is not None:
                inner = c1 + centre * (c2 if c3 is None else c2 + centre * c3)
                slope = c1 + centre * (
                    2.0 * c2 if c3 is None else 2.0 * c2 + 3.0 * (centre * c3)
                )
            result = [c0 + centre * inner, slope]
        if c2 is not None:
            result.append(c2 + jnp.zeros_like(centre) if c3 is None else c2 + 3.0 * (centre * c3))
        if c3 is not None:
            result.append(c3 + jnp.zeros_like(centre))
        return result

    def inner(x, y):
        u, v = local(x), local(y)
        total = jnp.zeros_like(centre)
        for i in range(len(u)):
            for j in range(len(v)):
                total = total + (u[i] * v[j]) * gram[(min(i, j), max(i, j))]
        return jnp.sum(total, axis=0, keepdims=True)

    def operate(c):
        result = [SHIFT * x for x in c] + [None]
        for i, x in enumerate(c):
            term = SCALE * x
            result[i + 1] = term if result[i + 1] is None else result[i + 1] + term
        return result

    one = jnp.ones((1, 1), F32)
    stream_c = [None] * 3
    residual, direction = [one], [one]
    norm = inner(residual, residual)
    for step in range(3):
        image = operate(direction)
        alpha = norm / inner(direction, image)
        for i, x in enumerate(direction):
            stream_c[i] = alpha * x if stream_c[i] is None else stream_c[i] + alpha * x
        if step == 2:
            break
        residual = [
            (residual[i] - alpha * image[i]) if i < len(residual) else -alpha * image[i]
            for i in range(len(image))
        ]
        fresh = inner(residual, residual)
        ratio = fresh / norm
        direction = [
            (residual[i] + ratio * direction[i]) if i < len(direction) else residual[i]
            for i in range(len(residual))
        ]
        norm = fresh

    tiles = powers.shape[1]
    height = stream.shape[0]
    weights = [jnp.broadcast_to(c, (SUB, LANES)) for c in stream_c]

    def put(out, load):
        for j in range(tiles):
            width = min(LANES, cols - j * LANES)
            value = sum(weights[k] * load(k, j) for k in range(3))
            stream[out, j * LANES : j * LANES + width] = value[:, :width]

    def write(g, carry):
        at = pl.ds(pl.multiple_of(g * SUB + PAD, SUB), SUB)
        out = pl.ds(pl.multiple_of(g * SUB, SUB), SUB)
        put(out, lambda k, j: powers[k, j, at, :])
        return carry

    middle = height // SUB // 2 * SUB
    copies = [
        pltpu.make_async_copy(stream.at[part, :], stream_out.at[part, :], sems.at[at])
        for at, part in enumerate((pl.ds(0, middle), pl.ds(middle, height - middle)))
    ]
    put(slice(0, SUB), lambda k, j: border[0, k, j])
    lax.fori_loop(1, middle // SUB, write, 0, unroll=3)
    copies[0].start()
    lax.fori_loop(middle // SUB, height // SUB - 1, write, 0, unroll=3)
    put(slice(height - SUB, height), lambda k, j: border[1, k, j])
    copies[1].start()
    for copy in (*patches, *copies):
        copy.wait()


def body(checkpoint, slot_dest, kmt, kappa):
    n = lax.axis_size("lon")
    lats = lax.axis_size("lat")
    lat = lax.axis_index("lat")
    me = jnp.stack([lax.axis_index("lon"), lax.rem(lat, 2)]).astype(jnp.int32)
    _, slots, values = checkpoint.shape
    rows, cols = kmt.shape
    by_n, bx_n = rows // BH, cols // BW
    cap = slots // n
    length = package_rows(cap, by_n)
    tiles = -(-(cols + 2 * HALO) // LANES)
    groups = slots // SUB
    edge_rows = -(-by_n * (1 + LEV) // 2) * BH
    if by_n * (1 + LEV) > 4 * cap:
        edge_rows = 2 * cap * BH + BH

    def fixed(value):
        return pltpu.with_memory_space_constraint(value, pltpu.HBM)

    kernels = (n, cap, bx_n, by_n)
    lists = [
        pltpu.SMEM((1, n * slots), jnp.int32),
        pltpu.SMEM((n * cap + 1,), jnp.int32),
        pltpu.SMEM((slots + 1,), jnp.int32),
    ]
    *packs, flat = pl.pallas_call(
        functools.partial(first_kernel, *kernels),
        out_shape=[shaped(length, LANES)] * (n // 2 - 1)
        + [shaped(slots * ROWS, LANES)],
        in_specs=[SM, HB, HB],
        out_specs=[VM] * (n // 2),
        scratch_shapes=lists
        + [
            pltpu.VMEM((groups, SUB, values), F32),
            pltpu.VMEM((n, BH, LANES), F32),
            pltpu.SMEM((n + 1,), jnp.int32),
            pltpu.SemaphoreType.DMA((groups + 1,)),
        ],
        compiler_params=params(),
        cost_estimate=cost(2 << 20, 4 << 20),
        name="first",
    )(me, fixed(slot_dest), fixed(checkpoint))

    def send(value, k):
        return lax.ppermute(value, "lon", [(i, i ^ k) for i in range(n)])

    order = sorted(range(1, n), key=lambda k: (k & 1, k < 2, -bin(k >> 1).count("1"), k))
    received = {k: send(packs[k // 2 - 1], k) for k in order if k % 2 == 0}
    own, *packs = pl.pallas_call(
        functools.partial(second_kernel, *kernels),
        out_shape=[shaped(length, LANES)] * (n // 2 + 1),
        in_specs=[SM, HB, VM, HB, HB],
        out_specs=[VM] * (n // 2 + 1),
        scratch_shapes=lists
        + [
            pltpu.VMEM((rows, cols), jnp.int32),
            pltpu.VMEM((LEV, rows, cols), F32),
            pltpu.VMEM((n, BH, LANES), F32),
            pltpu.VMEM((2, edge_rows, LANES), F32),
            pltpu.SMEM((n + 1,), jnp.int32),
            pltpu.SemaphoreType.DMA((3,)),
        ],
        compiler_params=params(),
        cost_estimate=cost(2 << 20, 4 << 20),
        name="second",
    )(me, fixed(slot_dest), flat, fixed(kmt), fixed(kappa))
    received |= {k: send(packs[k // 2], k) for k in order if k % 2}
    received[0] = own

    channels = 1 + 3 * LEV
    deep = rows + 2 * PAD
    table, grid = pl.pallas_call(
        functools.partial(base_kernel, n, cap, bx_n, by_n),
        out_shape=[
            shaped(n * (cap + 1) + (n + 1) * (1 + 2 * by_n), dtype=jnp.int32),
            shaped(channels, tiles, deep, LANES),
        ],
        in_specs=[SM, SM, VM, VM],
        out_specs=[SM, VM],
        scratch_shapes=[pltpu.SMEM((n * slots + 1,), jnp.int32)],
        compiler_params=params(),
        cost_estimate=cost(1 << 20, 2 << 20),
        name="base",
    )(me, slot_dest, kmt, kappa)

    def held(value):
        return pltpu.with_memory_space_constraint(value, pltpu.VMEM)

    rim = channels * tiles * HALO
    half, quarter = n // 2 - 1, n // 4
    odd = order[half:]
    parts = [
        [0] + order[:half],
        odd[-1:] + odd[: quarter - 1],
        odd[quarter - 1 : -2],
        odd[-2:-1],
    ]
    parts = [part for part in parts if part]
    for stage, which in enumerate(parts):
        shapes = [shaped(channels, tiles, deep, LANES)]
        if stage == len(parts) - 1:
            shapes += [shaped(rim, LANES)] * 2
        grid, *rims = pl.pallas_call(
            functools.partial(
                place_kernel, n, cap, bx_n, by_n, cols, which, len(parts) - 1 - stage
            ),
            out_shape=shapes,
            in_specs=[SM, SM] + [VM] * (1 + len(which)),
            out_specs=[VM] * len(shapes),
            input_output_aliases={2: 0},
            compiler_params=params(),
            cost_estimate=cost(2 << 20, 2 << 20),
            name=f"place{stage}",
        )(me, table, held(grid), *[received[k] for k in which])

    swaps = [
        [(i, i ^ 1) for i in range(lats) if i ^ 1 < lats],
        [(i, j) for i in range(lats) for j in [(i - 1 ^ 1) + 1] if 0 <= j < lats],
    ]
    other_rows, pair_rows = (
        lax.ppermute(value, "lat", swap) for value, swap in zip(rims, swaps[::-1])
    )

    devices = n * lats
    tracer_shape = shaped(2, LEV, rows, cols)
    tracer, powers, part, edges = pl.pallas_call(
        functools.partial(inner_kernel, cols),
        out_shape=[
            tracer_shape,
            shaped(3, tiles, deep, LANES),
            shaped(len(PAIRS) + 1, SUB, LANES),
            shaped(2, 2, LEV, SUB, cols),
        ],
        in_specs=[VM],
        out_specs=[HB, VM, VM, VM],
        scratch_shapes=[
            pltpu.VMEM((2, LEV, rows, cols), F32),
            pltpu.SemaphoreType.DMA((5,)),
        ],
        compiler_params=params(),
        cost_estimate=cost(16 << 20, 6 << 20),
        name="inner",
    )(grid)
    border, sums, fresh_rows = pl.pallas_call(
        functools.partial(border_kernel, cols),
        out_shape=[
            shaped(2, 3, tiles, SUB, LANES),
            shaped(devices, LANES),
            shaped(2, 2, LEV, SUB, cols),
        ],
        in_specs=[SM, VM, VM, VM, VM, VM, VM],
        out_specs=[VM, VM, VM],
        scratch_shapes=[
            pltpu.VMEM((2, channels, tiles, EDGE, LANES), F32),
            pltpu.VMEM((2, 3, tiles, EDGE, LANES), F32),
        ],
        compiler_params=params(),
        cost_estimate=cost(2 << 20, 1 << 20),
        name="border",
    )(me, grid, other_rows, pair_rows, powers, part, edges)

    everyone = lax.all_to_all(sums, ("lon", "lat"), 0, 0, tiled=True)
    tracer, stream = pl.pallas_call(
        functools.partial(combine_kernel, cols),
        out_shape=[tracer_shape, shaped(rows, cols)],
        in_specs=[VM, VM, VM, VM, HB],
        out_specs=[HB, HB],
        scratch_shapes=[
            pltpu.VMEM((rows, cols), F32),
            pltpu.SemaphoreType.DMA((4,)),
        ],
        input_output_aliases={4: 0},
        compiler_params=params(),
        cost_estimate=cost(1 << 20, 2 << 20),
        name="combine",
    )(everyone, powers, border, fresh_rows, fixed(tracer))
    return tracer, stream


def solution(mesh):
    placed = (P("lat", "lon", None), P("lat", None), P("lat", "lon"), P(None, "lat", "lon"))
    return jax.shard_map(
        body,
        mesh=mesh,
        in_specs=placed,
        out_specs=(P(None, None, "lat", "lon"), P("lat", "lon")),
        check_vma=False,
    )
```

```python
import functools

import jax
import jax.numpy as jnp
from jax import lax
from jax.experimental import pallas as pl
from jax.experimental.pallas import tpu as pltpu
from jax.sharding import PartitionSpec as P


BH = 40
BW = 60
LEV = 2
HALO = 4
LANES = 128
SUB = 8
PAD = SUB
EDGE = 4 * SUB
ROWS = LEV * BH
HALF = LANES // 2
SHIFT = 8.0
SCALE = 8.0

thermal = 0.25
haline = 0.75
cabbeling = 0.05

VM = pl.BlockSpec(memory_space=pltpu.VMEM)
SM = pl.BlockSpec(memory_space=pltpu.SMEM)
HB = pl.BlockSpec(memory_space=pltpu.HBM)
F32 = jnp.float32


def params():
    return pltpu.CompilerParams(vmem_limit_bytes=24 << 20)


def cost(flops, moved):
    return pl.CostEstimate(flops=flops, bytes_accessed=moved, transcendentals=0)


def shaped(*dims, dtype=F32):
    return jax.ShapeDtypeStruct(dims, dtype)


def lanes():
    return lax.broadcasted_iota(jnp.int32, (SUB, LANES), 1)


def turn(value, amount):
    if isinstance(amount, int):
        amount %= LANES
        if amount == 0:
            return value
    return pltpu.roll(value, amount, 1)


def strip_lane(side, by, level, tracer, block_rows):
    return HALO * ((side * block_rows + by) * LEV + level) + HALF * tracer


def edge_spot(cap, piece):
    if piece < 4 * cap:
        return piece // 2 * BH, HALF * (1 + piece % 2) - HALO
    return cap * ROWS + BH, HALO * (piece - 4 * cap)


def package_rows(cap, by_n):
    return cap * ROWS + (2 * BH if by_n * (1 + LEV) > 4 * cap else BH)


def block_rows(flat, start, row):
    return flat[pl.ds(start + row * SUB, SUB, stride=SUB), :]


def block_start(i):
    return lax.div(i, SUB) * (ROWS * SUB) + lax.rem(i, SUB)


def plan(n, cap, bx_n, me, dest, source, count, todo, wanted):
    slots = todo.shape[0] - 1
    for k in range(n + 1):
        count[k] = 0
    for at in range(n * cap + 1):
        source[at] = 0

    def assign(i, found):
        d = dest[0, me * slots + i]
        used = d >= 0
        place = jnp.maximum(d, 0)
        owner = lax.div(place, slots)
        k = jnp.where(used, lax.bitwise_xor(owner, me), n)
        c = count[k]
        count[k] = c + 1
        source[jnp.where(used, k * cap + c, n * cap)] = block_start(i)
        bx = lax.rem(place, bx_n)
        partner = lax.bitwise_xor(
            lax.rem(owner + jnp.where(bx == 0, n - 1, 1), n), me
        )
        todo[found] = i
        holds = used & ((bx == 0) | (bx == bx_n - 1)) & wanted(partner)
        return found + holds.astype(jnp.int32)

    return lax.fori_loop(0, slots, assign, 0, unroll=4)


def fill_strips(n, bx_n, by_n, me, dest, flat, strips, todo, found):
    slots = bx_n * by_n
    spot_lane = lanes() & (HALF - 1)

    def strip(at, carry):
        i = todo[at]
        place = dest[0, me * slots + i]
        spot = lax.rem(place, slots)
        by = lax.div(spot, bx_n)
        side = (lax.rem(spot, bx_n) == 0).astype(jnp.int32)
        owner = lax.div(place, slots)
        k = lax.bitwise_xor(lax.rem(owner + jnp.where(side == 0, 1, n - 1), n), me)
        start = block_start(i)
        origin = jnp.where(side == 0, BW - HALO, 0)
        for level in range(LEV):
            target = strip_lane(side, by, level, 0, by_n)
            amount = lax.rem(target - origin + LANES, LANES)
            here = (spot_lane >= target) & (spot_lane < target + HALO)
            for row in range(0, BH, SUB):
                value = block_rows(flat, start, level * BH + row)
                pltpu.store(
                    strips.at[k, row : row + SUB, :],
                    pltpu.roll(value, amount, 1),
                    mask=here,
                )
        return carry

    lax.fori_loop(0, found, strip, 0)


def assemble(out, k, cap, source, flat, strips, edges=None, which=None, in_blocks=0):
    spare = (lanes() & (HALF - 1)) >= HALF - HALO
    for c in range(cap):
        start = source[k * cap + c]
        for row in range(0, ROWS, SUB):
            value = block_rows(flat, start, row)
            at = c * ROWS + row
            if at < in_blocks:
                value = jnp.where(spare, edges[which, at : at + SUB, :], value)
            out[at : at + SUB, :] = value
    for row in range(0, BH, SUB):
        at = cap * ROWS + row
        out[at : at + SUB, :] = strips[k, row : row + SUB, :]


def first_kernel(n, cap, bx_n, by_n, *refs):
    me_ref, dest_hbm, blocks_hbm = refs[:3]
    outs = refs[3 : n // 2 + 2]
    flat, dest, source, todo, blocks, strips, count, sems = refs[n // 2 + 2 :]
    groups = blocks.shape[0]
    slots = groups * SUB
    me = me_ref[0]
    lane = lanes()
    first = pltpu.make_async_copy(dest_hbm, dest, sems.at[groups])
    first.start()

    def loading(g):
        rows = pl.ds(pl.multiple_of(g * SUB, SUB), SUB)
        return pltpu.make_async_copy(
            blocks_hbm.at[0, rows, :], blocks.at[g], sems.at[g]
        )

    for g in range(groups):
        loading(g).start()
    first.wait()
    found = plan(
        n, cap, bx_n, me, dest, source, count, todo, lambda k: (k > 0) & (k & 1 == 0)
    )

    def regroup(group, carry):
        loading(group).wait()

        def load(q):
            return blocks[group, :, q * LANES : (q + 1) * LANES]

        limit = blocks.shape[2] // LANES - 1
        for row in range(ROWS):
            q, o = divmod(row * BW, LANES)
            p = (ROWS + row) * BW // LANES
            if o == 0:
                value = jnp.where(lane >= HALF, load(p), load(q))
            elif o <= HALF:
                low = load(p if o == HALF else min(p + 1, limit))
                value = jnp.where(lane >= o, load(q), low)
                if o < HALF:
                    value = jnp.where(lane >= o + HALF, load(p), value)
            else:
                value = jnp.where(lane >= o - HALF, load(p), load(q + 1))
                value = jnp.where(lane >= o, load(q), value)
            at = pl.multiple_of(group * (ROWS * SUB) + row * SUB, SUB)
            flat[pl.ds(at, SUB), :] = turn(value, -o)
        return carry

    lax.fori_loop(0, groups, regroup, 0)
    fill_strips(n, bx_n, by_n, me, dest, flat, strips, todo, found)
    for k in range(2, n, 2):
        assemble(outs[k // 2 - 1], k, cap, source, flat, strips)


def second_kernel(n, cap, bx_n, by_n, *refs):
    me_ref, dest_hbm, flat, kmt_hbm, kappa_hbm = refs[:5]
    outs = refs[5 : n // 2 + 6]
    dest, source, todo, kmt, kappa, strips, edges, count, sems = refs[n // 2 + 6 :]
    me = me_ref[0]
    lane = lanes()
    length = outs[0].shape[0]
    cols = kmt.shape[1]
    first, *copies = [
        pltpu.make_async_copy(dest_hbm, dest, sems.at[0]),
        pltpu.make_async_copy(kmt_hbm, kmt, sems.at[1]),
        pltpu.make_async_copy(kappa_hbm, kappa, sems.at[2]),
    ]
    for copy in (first, *copies):
        copy.start()
    first.wait()
    found = plan(
        n, cap, bx_n, me, dest, source, count, todo, lambda k: (k == 0) | (k & 1 == 1)
    )
    fill_strips(n, bx_n, by_n, me, dest, flat, strips, todo, found)
    for copy in copies:
        copy.wait()
    zero = jnp.zeros((SUB, LANES), F32)
    for at in range(0, edges.shape[1], SUB):
        for side in range(2):
            edges[side, at : at + SUB, :] = zero
    for side, start in ((0, cols - HALO), (1, 0)):
        tile = start // LANES * LANES
        width = min(LANES, cols - tile)
        for piece in range(by_n * (1 + LEV)):
            by, ch = divmod(piece, 1 + LEV)
            base, target = edge_spot(cap, piece)
            if piece >= 4 * cap:
                base -= cap * ROWS + BH - 2 * cap * BH
            here = (lane >= target) & (lane < target + HALO)
            for row in range(0, BH, SUB):
                at = slice(by * BH + row, by * BH + row + SUB)
                if ch == 0:
                    value = kmt[at, tile : tile + width].astype(F32)
                else:
                    value = kappa[ch - 1, at, tile : tile + width]
                if width < LANES:
                    value = jnp.concatenate([value, zero[:, width:]], axis=1)
                pltpu.store(
                    edges.at[side, base + row : base + row + SUB, :],
                    turn(value, target - (start - tile)),
                    mask=here,
                )
    eastern = lax.bitwise_xor(lax.rem(me + 1, n), me)
    in_blocks = min(edges.shape[1], 2 * cap * BH)
    for out, k in zip(outs, [0, *range(1, n, 2)]):
        which = jnp.where(eastern == k, 0, 1)
        assemble(out, k, cap, source, flat, strips, edges, which, in_blocks)
        if length > cap * ROWS + BH:
            for row in range(0, BH, SUB):
                at = cap * ROWS + BH + row
                out[at : at + SUB, :] = edges[
                    which, in_blocks + row : in_blocks + row + SUB, :
                ]


def base_kernel(n, cap, bx_n, by_n, me_ref, dest, kmt, kappa, table, grid, bringer):
    me = me_ref[0]
    slots = bx_n * by_n
    channels, tiles, deep, _ = grid.shape
    cols = kmt.shape[1]
    zero = jnp.zeros((SUB, LANES), F32)
    west = lax.rem(me + n - 1, n)
    east = lax.rem(me + 1, n)
    for at in range(n * (cap + 1)):
        table[at] = -1
    sides = [(west, by * bx_n + bx_n - 1) for by in range(by_n)]
    sides += [(east, by * bx_n) for by in range(by_n)]
    for owner, spot in sides:
        bringer[owner * slots + spot + 1] = -1

    def owner_loop(s, carry):
        k = lax.bitwise_xor(s, me)

        def slot_loop(i, c):
            d = dest[0, s * slots + i]
            bringer[d + 1] = k
            spot = d - me * slots
            mine = (spot >= 0) & (spot < slots)
            table[k * (cap + 1) + c] = jnp.where(mine, spot, -1)
            return c + mine.astype(jnp.int32)

        lax.fori_loop(0, slots, slot_loop, 0, unroll=8)
        return carry

    lax.fori_loop(0, n, owner_loop, 0)
    counts = n * (cap + 1)
    lists = counts + n + 1
    for k in range(n + 1):
        table[counts + k] = 0
    for at, (owner, spot) in enumerate(sides):
        k = bringer[owner * slots + spot + 1]
        k = jnp.where(k < 0, n, k)
        c = table[counts + k]
        table[counts + k] = c + 1
        table[lists + k * len(sides) + c] = at

    def clear(g, carry):
        at = pl.ds(pl.multiple_of(g * SUB, SUB), SUB)
        for ch in range(channels):
            for j in range(tiles):
                grid[ch, j, at, :] = zero
        return carry

    lax.fori_loop(0, deep // SUB, clear, 0)

    def lay(g, carry):
        at = pl.ds(pl.multiple_of(g * SUB, SUB), SUB)
        out = pl.ds(pl.multiple_of(g * SUB + PAD, SUB), SUB)
        for ch in range(1 + LEV):
            for j in range(tiles):
                width = min(LANES, cols - j * LANES)
                part = slice(j * LANES, j * LANES + width)
                if ch == 0:
                    value = kmt[at, part].astype(F32)
                else:
                    value = kappa[ch - 1, at, part]
                grid[ch, j, out, 0:width] = value
        return carry

    lax.fori_loop(0, kmt.shape[0] // SUB, lay, 0)


def place_kernel(n, cap, bx_n, by_n, cols, which, left, *refs):
    count = len(which)
    me_ref, table, _ = refs[:3]
    odd = me_ref[1]
    packs = refs[3 : 3 + count]
    grid, *rims = refs[3 + count :]
    me = me_ref[0]
    lane = lanes()
    channels, tiles, deep, _ = grid.shape
    last = tiles - 1
    own = cols - last * LANES
    halo_lane = (own, LANES - HALO)

    def mark(ch, at, value, start, allowed=True):
        here = (lane >= start) & (lane < start + HALO) & allowed
        pltpu.store(grid.at[ch, last, at, :], value, mask=here)

    for k, pack in zip(which, packs):

        for c in range(cap):
            spot = table[k * (cap + 1) + c]
            valid = spot >= 0
            spot = jnp.maximum(spot, 0)
            by = lax.div(spot, bx_n)
            offset = lax.rem(spot, bx_n) * BW
            tile = lax.div(offset, LANES)
            following = jnp.minimum(tile + 1, last)
            start = lax.rem(offset, LANES)
            begin = jnp.where(valid, start, LANES)
            here = (lane >= begin) & (lane < begin + BW)
            spill = lane < jnp.where(valid, start + BW - LANES, 0)
            for row in range(0, BH, SUB):
                at = pl.ds(pl.multiple_of(by * BH + row + PAD, SUB), SUB)
                depth = grid[0, tile, at, :], grid[0, following, at, :]
                for level in range(LEV):
                    place = c * ROWS + level * BH + row
                    value = pack[place : place + SUB, :]
                    masks = here & (depth[0] > level), spill & (depth[1] > level)
                    for tracer in range(2):
                        ch = 1 + LEV + tracer * LEV + level
                        turned = pltpu.roll(
                            value, lax.rem(start + tracer * HALF, LANES), 1
                        )
                        for target, mask in zip((tile, following), masks):
                            pltpu.store(grid.at[ch, target, at, :], turned, mask=mask)

        counts = n * (cap + 1)
        lists = counts + n + 1 + k * 2 * by_n

        def strip(at, carry, pack=pack, lists=lists):
            index = table[lists + at]
            by = lax.rem(index, by_n)
            start = jnp.where(index < by_n, halo_lane[1], halo_lane[0])
            for row in range(0, BH, SUB):
                rows = pl.ds(pl.multiple_of(by * BH + row + PAD, SUB), SUB)
                value = pack[cap * ROWS + row : cap * ROWS + row + SUB, :]
                wet = grid[0, last, rows, :]
                for level in range(LEV):
                    for tracer in range(2):
                        origin = strip_lane(0, index, level, tracer, by_n)
                        amount = lax.rem(start - origin + LANES, LANES)
                        mark(
                            1 + LEV + tracer * LEV + level,
                            rows,
                            pltpu.roll(value, amount, 1),
                            start,
                            wet > level if left == 0 else True,
                        )
            return carry

        lax.fori_loop(0, table[counts + k], strip, 0)

        for neighbour, start in ((me + n - 1, halo_lane[1]), (me + 1, halo_lane[0])):
            if k % 2 == 0:
                continue

            @pl.when(lax.bitwise_xor(lax.rem(neighbour, n), me) == k)
            def _(start=start, pack=pack):
                for piece in range(by_n * (1 + LEV)):
                    by, ch = divmod(piece, 1 + LEV)
                    base, origin = edge_spot(cap, piece)
                    for row in range(0, BH, SUB):
                        at = by * BH + row + PAD
                        mark(
                            ch,
                            slice(at, at + SUB),
                            turn(pack[base + row : base + row + SUB, :], start - origin),
                            start,
                        )

    if left > 1:
        return
    rim = (lane >= own) & (lane < own + HALO) | (lane >= LANES - HALO)

    def mask(g, carry):
        at = pl.ds(pl.multiple_of(g * SUB + PAD, SUB), SUB)
        wet = grid[0, last, at, :]
        for ch in range(1 + LEV, channels):
            level = (ch - 1 - LEV) % LEV
            grid[ch, last, at, :] = jnp.where(
                rim & (wet <= level), 0.0, grid[ch, last, at, :]
            )
        return carry

    if left == 1:
        lax.fori_loop(0, deep // SUB - 2, mask, 0, unroll=4)
        return
    low = deep - PAD - HALO
    for rows, first in zip(rims, (1 - odd, odd)):
        at = jnp.where(first == 1, PAD, low)
        for ch in range(channels):
            for j in range(tiles):
                spot = (ch * tiles + j) * HALO
                rows[spot : spot + HALO, :] = grid[ch, j, pl.ds(at, HALO), :]


def sideways(values):
    lane = lanes()
    count = len(values)
    left = [turn(v, 1) for v in values]
    right = [turn(v, -1) for v in values]
    west = [
        jnp.where(lane == 0, left[(j - 1) % count], left[j]) for j in range(count)
    ]
    east = [
        jnp.where(lane == LANES - 1, right[(j + 1) % count], right[j])
        for j in range(count)
    ]
    return east, west


def three(load, start):
    return load(start), load(start - 1), load(start + 1)


def diffuse(load, start):
    tiles = len(load(0, start))
    span = range(tiles)
    level_c, level_a, level_b = three(functools.partial(load, 0), start)
    level_e, _ = sideways(level_c)
    both_e = [jnp.minimum(level_c[j], level_e[j]) for j in span]
    both_a = [jnp.minimum(level_c[j], level_a[j]) for j in span]
    both_b = [jnp.minimum(level_c[j], level_b[j]) for j in span]
    forcing = [None] * tiles
    fresh = [[None] * LEV for _ in range(2)]
    for level in range(LEV):
        kappa_c, kappa_a, kappa_b = three(functools.partial(load, 1 + level), start)
        kappa_e, _ = sideways(kappa_c)
        face_e, face_a, face_b = (
            [jnp.where(both[j] > level, kappa_c[j] + other[j], 0.0) for j in span]
            for both, other in (
                (both_e, kappa_e),
                (both_a, kappa_a),
                (both_b, kappa_b),
            )
        )
        for tracer in range(2):
            ch = 1 + LEV + tracer * LEV + level
            here, above, below = three(functools.partial(load, ch), start)
            to_east, _ = sideways(here)
            flux = [face_e[j] * (to_east[j] - here[j]) for j in span]
            _, flux_w = sideways(flux)
            fresh[tracer][level] = [
                jnp.where(
                    level_c[j] > level,
                    here[j]
                    + 0.5
                    * (
                        (flux[j] - flux_w[j])
                        + face_a[j] * (above[j] - here[j])
                        + face_b[j] * (below[j] - here[j])
                    ),
                    0.0,
                )
                for j in span
            ]
        thickness = 1.0 + 0.5 * level
        for j in span:
            temp, salt = fresh[0][level][j], fresh[1][level][j]
            density = haline * salt - temp * (thermal + cabbeling * temp)
            if level:
                density = forcing[j] + thickness * density
            forcing[j] = density
    return fresh, forcing


def apply(here, above, below, levels):
    span = range(len(here))
    pair = [above[j] + below[j] for j in span]
    mixed = [here[j] + 0.5 * pair[j] for j in span]
    east, west = sideways(mixed)
    result = []
    for j in span:
        diagonal = 6.0 - SHIFT + 1.0
        total = jnp.full((SUB, LANES), diagonal / SCALE, F32)
        for k in range(1, LEV):
            diagonal += 1.0 + 0.5 * k
            total = jnp.where(levels[j] > k, diagonal / SCALE, total)
        total = total * here[j] - (pair[j] + (east[j] + west[j])) * (1.0 / SCALE)
        result.append(jnp.where(levels[j] > 0, total, 0.0))
    return result


def gather_products(carry, powers, centre, keep):
    carry = list(carry)
    span = range(len(powers[0]))
    for j in span:
        q0, q1, q2, q3 = (keep(q[j], j) for q in powers)
        b1 = q1 - centre * q0
        c2 = q2 - centre * q1
        c3 = q3 - centre * q2
        b2 = c2 - centre * b1
        b3 = (c3 - centre * c2) - centre * b2
        terms = (q0, b1, b2, b3)
        for at, (x, y) in enumerate(PAIRS):
            carry[at] = carry[at] + terms[x] * terms[y]
    return tuple(carry)


def total_row(totals):
    lane = lanes()[:1]
    row = jnp.zeros((1, LANES), F32)
    for at, total in enumerate(totals):
        total = jnp.sum(total, axis=(0, 1), keepdims=True)
        row = jnp.where(lane == at + 1, total, row)
    return row


def put_tracer(target, fresh, cols, at):
    for tracer in range(2):
        for level in range(LEV):
            for j, value in enumerate(fresh[tracer][level]):
                width = min(LANES, cols - j * LANES)
                target[tracer, level, at, j * LANES : j * LANES + width] = value[
                    :, :width
                ]


def inner_kernel(cols, grid, tracer_out, powers, sums, edges, fresh_rows, sems):
    lane = lanes()
    line = lax.broadcasted_iota(jnp.int32, (SUB, LANES), 0)
    _, tiles, deep, _ = grid.shape
    own = cols - (tiles - 1) * LANES
    first, end = PAD // SUB, (deep - PAD) // SUB
    zero = jnp.zeros((SUB, LANES), F32)

    def rows(ref, lead, start):
        return [ref[lead, j, pl.ds(start, SUB), :] for j in range(tiles)]

    def top(g):
        return pl.multiple_of(g * SUB, SUB)

    def step(g, carry):
        fresh, forcing = diffuse(functools.partial(rows, grid), top(g))
        put_tracer(
            fresh_rows, fresh, cols, pl.ds(pl.multiple_of(g * SUB - PAD, SUB), SUB)
        )
        for j in range(tiles):
            powers[0, j, pl.ds(top(g), SUB), :] = forcing[j]
        return carry

    chunks = sems.shape[0]
    size = (end - first) // chunks
    copies = []
    for chunk in range(chunks):
        begin = first + chunk * size
        stop = end if chunk == chunks - 1 else begin + size
        lax.fori_loop(begin, stop, step, 0, unroll=2)
        at = pl.ds(begin * SUB - PAD, (stop - begin) * SUB)
        copies.append(
            pltpu.make_async_copy(
                fresh_rows.at[:, :, at, :], tracer_out.at[:, :, at, :], sems.at[chunk]
            )
        )
        copies[-1].start()
    height = fresh_rows.shape[2]
    for tracer in range(2):
        for level in range(LEV):
            for side, row in ((0, 0), (1, height - SUB)):
                edges[side, tracer, level] = fresh_rows[
                    tracer, level, row : row + SUB, :
                ]

    def inside(value, j):
        return value if j < tiles - 1 else jnp.where(lane < own, value, 0.0)

    def upper(value, j):
        return jnp.where(line >= HALO, inside(value, j), 0.0)

    def lower(value, j):
        return jnp.where(line < SUB - HALO, inside(value, j), 0.0)

    def power(g, source):
        here, above, below = three(functools.partial(rows, powers, source), top(g))
        return here, apply(here, above, below, rows(grid, 0, top(g)))

    def put(g, target):
        here, result = power(g, target - 1)
        for j in range(tiles):
            powers[target, j, pl.ds(top(g), SUB), :] = result[j]
        return here, result

    def first_power(g, carry, keep=inside):
        here, result = put(g, 1)
        a, b = carry
        for j in range(tiles):
            v = keep(here[j], j)
            a = a + v * v
            b = b + v * keep(result[j], j)
        return a, b

    def everywhere(body, carry):
        carry = body(first, carry, upper)
        carry = lax.fori_loop(first + 1, end - 1, body, carry, unroll=end - first - 2)
        return body(end - 1, carry, lower)

    a, b = everywhere(first_power, (zero, zero))
    a = jnp.sum(a, axis=(0, 1), keepdims=True)
    b = jnp.sum(b, axis=(0, 1), keepdims=True)
    centre = jnp.where(a > 0, b / jnp.where(a > 0, a, 1.0), 0.0)
    centre = jnp.broadcast_to(centre, (SUB, LANES))
    lax.fori_loop(
        first, end, lambda g, c: (put(g, 2), c)[1], 0, unroll=end - first
    )

    def products(g, carry, keep=inside):
        here, result = power(g, 2)
        lower_powers = [rows(powers, k, top(g)) for k in range(2)]
        return gather_products(carry, (*lower_powers, here, result), centre, keep)

    totals = everywhere(products, (zero,) * len(PAIRS))
    for at, total in enumerate((*totals, centre)):
        sums[at] = total
    for copy in copies:
        copy.wait()


def border_kernel(
    cols, me_ref, grid, other_rows, pair_rows, powers, part, edges, border, sums,
    fresh_rows, field, local,
):
    lane = lanes()
    line = lax.broadcasted_iota(jnp.int32, (SUB, LANES), 0)
    channels, tiles, deep, _ = grid.shape
    own = cols - (tiles - 1) * LANES
    half = EDGE // 2
    even = me_ref[1] == 0
    for ch in range(channels):
        for j in range(tiles):
            at = slice((ch * tiles + j) * HALO, (ch * tiles + j + 1) * HALO)
            field[0, ch, j, half : half + SUB, :] = grid[ch, j, PAD : PAD + SUB, :]
            field[1, ch, j, half - SUB : half, :] = grid[
                ch, j, deep - PAD - SUB : deep - PAD, :
            ]
            pair, other = pair_rows[at, :], other_rows[at, :]
            field[0, ch, j, half - HALO : half, :] = jnp.where(even, other, pair)
            field[1, ch, j, half : half + HALO, :] = jnp.where(even, pair, other)
    for k in range(3):
        for j in range(tiles):
            local[0, k, j, half : half + SUB, :] = powers[k, j, PAD : PAD + SUB, :]
            local[1, k, j, half - SUB : half, :] = powers[
                k, j, deep - PAD - SUB : deep - PAD, :
            ]
    centre = part[len(PAIRS)]

    def rows_of(side):
        def rows(ref, lead, start):
            return [ref[side, lead, j, pl.ds(start, SUB), :] for j in range(tiles)]

        return rows

    start = half - HALO
    for side in range(2):
        fresh, forcing = diffuse(functools.partial(rows_of(side), field), start)
        for j in range(tiles):
            local[side, 0, j, start : start + SUB, :] = forcing[j]
        mine = line == (0 if side == 0 else SUB - 1)
        for tracer in range(2):
            for level in range(LEV):
                for j in range(tiles):
                    width = min(LANES, cols - j * LANES)
                    part_lanes = slice(j * LANES, j * LANES + width)
                    moved = pltpu.roll(fresh[tracer][level][j], HALO, 0)
                    fresh_rows[side, tracer, level, :, part_lanes] = jnp.where(
                        mine[:, :width],
                        moved[:, :width],
                        edges[side, tracer, level, :, part_lanes],
                    )

    def power(side, source):
        rows = rows_of(side)
        here, above, below = three(functools.partial(rows, local, source), start)
        return here, apply(here, above, below, rows(field, 0, start))

    for target in range(1, 3):
        for side in range(2):
            result = power(side, target - 1)[1]
            for j in range(tiles):
                local[side, target, j, start : start + SUB, :] = result[j]
    totals = tuple(part[at] for at in range(len(PAIRS)))
    for side in range(2):
        here, result = power(side, 2)
        lower_powers = [rows_of(side)(local, k, start) for k in range(2)]
        own_rows = half - side * SUB
        for k in range(3):
            for j in range(tiles):
                border[side, k, j] = local[side, k, j, own_rows : own_rows + SUB, :]
        bound = (1 - side) * HALO
        rim = (line >= bound) & (line < bound + HALO)

        def keep(value, j, rim=rim):
            inside = rim if j < tiles - 1 else rim & (lane < own)
            return jnp.where(inside, value, 0.0)

        totals = gather_products(
            totals, (*lower_powers, here, result), centre, keep
        )
    row = jnp.where(lane[:1] == 0, centre[:1], total_row(totals))
    sums[...] = jnp.broadcast_to(row, sums.shape)


PAIRS = ((0, 0), (0, 1), (0, 2), (0, 3), (1, 1), (1, 2), (1, 3), (2, 2), (2, 3))


def combine_kernel(
    cols, sums, powers, border, fresh_rows, tracer_in, tracer_out, stream_out, stream, sems
):
    rows = tracer_out.shape[2]
    patches = [
        pltpu.make_async_copy(
            fresh_rows.at[side],
            tracer_out.at[:, :, pl.ds(side * (rows - SUB), SUB), :],
            sems.at[2 + side],
        )
        for side in range(2)
    ]
    for copy in patches:
        copy.start()
    values = sums[...]
    lane = lax.broadcasted_iota(jnp.int32, values.shape, 1)

    def column(k):
        return jnp.sum(jnp.where(lane == k, values, 0.0), axis=1, keepdims=True)

    centre = column(0)
    gram = {pair: column(at + 1) for at, pair in enumerate(PAIRS)}

    def local(c):
        c = list(c) + [None] * (4 - len(c))
        c0, c1, c2, c3 = c
        result = [c0 + jnp.zeros_like(centre)]
        if c1 is not None:
            inner = c1
            slope = c1 + jnp.zeros_like(centre)
            if c2 is not None:
                inner = c1 + centre * (c2 if c3 is None else c2 + centre * c3)
                slope = c1 + centre * (
                    2.0 * c2 if c3 is None else 2.0 * c2 + 3.0 * (centre * c3)
                )
            result = [c0 + centre * inner, slope]
        if c2 is not None:
            result.append(c2 + jnp.zeros_like(centre) if c3 is None else c2 + 3.0 * (centre * c3))
        if c3 is not None:
            result.append(c3 + jnp.zeros_like(centre))
        return result

    def inner(x, y):
        u, v = local(x), local(y)
        total = jnp.zeros_like(centre)
        for i in range(len(u)):
            for j in range(len(v)):
                total = total + (u[i] * v[j]) * gram[(min(i, j), max(i, j))]
        return jnp.sum(total, axis=0, keepdims=True)

    def operate(c):
        result = [SHIFT * x for x in c] + [None]
        for i, x in enumerate(c):
            term = SCALE * x
            result[i + 1] = term if result[i + 1] is None else result[i + 1] + term
        return result

    one = jnp.ones((1, 1), F32)
    stream_c = [None] * 3
    residual, direction = [one], [one]
    norm = inner(residual, residual)
    for step in range(3):
        image = operate(direction)
        alpha = norm / inner(direction, image)
        for i, x in enumerate(direction):
            stream_c[i] = alpha * x if stream_c[i] is None else stream_c[i] + alpha * x
        if step == 2:
            break
        residual = [
            (residual[i] - alpha * image[i]) if i < len(residual) else -alpha * image[i]
            for i in range(len(image))
        ]
        fresh = inner(residual, residual)
        ratio = fresh / norm
        direction = [
            (residual[i] + ratio * direction[i]) if i < len(direction) else residual[i]
            for i in range(len(residual))
        ]
        norm = fresh

    tiles = powers.shape[1]
    height = stream.shape[0]
    weights = [jnp.broadcast_to(c, (SUB, LANES)) for c in stream_c]

    def put(out, load):
        for j in range(tiles):
            width = min(LANES, cols - j * LANES)
            value = sum(weights[k] * load(k, j) for k in range(3))
            stream[out, j * LANES : j * LANES + width] = value[:, :width]

    def write(g, carry):
        at = pl.ds(pl.multiple_of(g * SUB + PAD, SUB), SUB)
        out = pl.ds(pl.multiple_of(g * SUB, SUB), SUB)
        put(out, lambda k, j: powers[k, j, at, :])
        return carry

    middle = height // SUB // 2 * SUB
    copies = [
        pltpu.make_async_copy(stream.at[part, :], stream_out.at[part, :], sems.at[at])
        for at, part in enumerate((pl.ds(0, middle), pl.ds(middle, height - middle)))
    ]
    put(slice(0, SUB), lambda k, j: border[0, k, j])
    lax.fori_loop(1, middle // SUB, write, 0, unroll=9)
    copies[0].start()
    lax.fori_loop(middle // SUB, height // SUB - 1, write, 0, unroll=9)
    put(slice(height - SUB, height), lambda k, j: border[1, k, j])
    copies[1].start()
    for copy in (*patches, *copies):
        copy.wait()


def body(checkpoint, slot_dest, kmt, kappa):
    n = lax.axis_size("lon")
    lats = lax.axis_size("lat")
    lat = lax.axis_index("lat")
    me = jnp.stack([lax.axis_index("lon"), lax.rem(lat, 2)]).astype(jnp.int32)
    _, slots, values = checkpoint.shape
    rows, cols = kmt.shape
    by_n, bx_n = rows // BH, cols // BW
    cap = slots // n
    length = package_rows(cap, by_n)
    tiles = -(-(cols + 2 * HALO) // LANES)
    groups = slots // SUB
    edge_rows = -(-by_n * (1 + LEV) // 2) * BH
    if by_n * (1 + LEV) > 4 * cap:
        edge_rows = 2 * cap * BH + BH

    def fixed(value):
        return pltpu.with_memory_space_constraint(value, pltpu.HBM)

    kernels = (n, cap, bx_n, by_n)
    lists = [
        pltpu.SMEM((1, n * slots), jnp.int32),
        pltpu.SMEM((n * cap + 1,), jnp.int32),
        pltpu.SMEM((slots + 1,), jnp.int32),
    ]
    *packs, flat = pl.pallas_call(
        functools.partial(first_kernel, *kernels),
        out_shape=[shaped(length, LANES)] * (n // 2 - 1)
        + [shaped(slots * ROWS, LANES)],
        in_specs=[SM, HB, HB],
        out_specs=[VM] * (n // 2),
        scratch_shapes=lists
        + [
            pltpu.VMEM((groups, SUB, values), F32),
            pltpu.VMEM((n, BH, LANES), F32),
            pltpu.SMEM((n + 1,), jnp.int32),
            pltpu.SemaphoreType.DMA((groups + 1,)),
        ],
        compiler_params=params(),
        cost_estimate=cost(2 << 20, 4 << 20),
        name="first",
    )(me, fixed(slot_dest), fixed(checkpoint))

    def send(value, k):
        return lax.ppermute(value, "lon", [(i, i ^ k) for i in range(n)])

    order = sorted(range(1, n), key=lambda k: (k & 1, k < 2, -bin(k >> 1).count("1"), k))
    received = {k: send(packs[k // 2 - 1], k) for k in order if k % 2 == 0}
    own, *packs = pl.pallas_call(
        functools.partial(second_kernel, *kernels),
        out_shape=[shaped(length, LANES)] * (n // 2 + 1),
        in_specs=[SM, HB, VM, HB, HB],
        out_specs=[VM] * (n // 2 + 1),
        scratch_shapes=lists
        + [
            pltpu.VMEM((rows, cols), jnp.int32),
            pltpu.VMEM((LEV, rows, cols), F32),
            pltpu.VMEM((n, BH, LANES), F32),
            pltpu.VMEM((2, edge_rows, LANES), F32),
            pltpu.SMEM((n + 1,), jnp.int32),
            pltpu.SemaphoreType.DMA((3,)),
        ],
        compiler_params=params(),
        cost_estimate=cost(2 << 20, 4 << 20),
        name="second",
    )(me, fixed(slot_dest), flat, fixed(kmt), fixed(kappa))
    received |= {k: send(packs[k // 2], k) for k in order if k % 2}
    received[0] = own

    channels = 1 + 3 * LEV
    deep = rows + 2 * PAD
    table, grid = pl.pallas_call(
        functools.partial(base_kernel, n, cap, bx_n, by_n),
        out_shape=[
            shaped(n * (cap + 1) + (n + 1) * (1 + 2 * by_n), dtype=jnp.int32),
            shaped(channels, tiles, deep, LANES),
        ],
        in_specs=[SM, SM, VM, VM],
        out_specs=[SM, VM],
        scratch_shapes=[pltpu.SMEM((n * slots + 1,), jnp.int32)],
        compiler_params=params(),
        cost_estimate=cost(1 << 20, 2 << 20),
        name="base",
    )(me, slot_dest, kmt, kappa)

    def held(value):
        return pltpu.with_memory_space_constraint(value, pltpu.VMEM)

    rim = channels * tiles * HALO
    half, quarter = n // 2 - 1, n // 4
    odd = order[half:]
    parts = [
        [0] + order[:half],
        odd[-1:] + odd[: quarter - 1],
        odd[quarter - 1 : -2],
        odd[-2:-1],
    ]
    parts = [part for part in parts if part]
    for stage, which in enumerate(parts):
        shapes = [shaped(channels, tiles, deep, LANES)]
        if stage == len(parts) - 1:
            shapes += [shaped(rim, LANES)] * 2
        grid, *rims = pl.pallas_call(
            functools.partial(
                place_kernel, n, cap, bx_n, by_n, cols, which, len(parts) - 1 - stage
            ),
            out_shape=shapes,
            in_specs=[SM, SM] + [VM] * (1 + len(which)),
            out_specs=[VM] * len(shapes),
            input_output_aliases={2: 0},
            compiler_params=params(),
            cost_estimate=cost(2 << 20, 2 << 20),
            name=f"place{stage}",
        )(me, table, held(grid), *[received[k] for k in which])

    swaps = [
        [(i, i ^ 1) for i in range(lats) if i ^ 1 < lats],
        [(i, j) for i in range(lats) for j in [(i - 1 ^ 1) + 1] if 0 <= j < lats],
    ]
    other_rows, pair_rows = (
        lax.ppermute(value, "lat", swap) for value, swap in zip(rims, swaps[::-1])
    )

    devices = n * lats
    tracer_shape = shaped(2, LEV, rows, cols)
    tracer, powers, part, edges = pl.pallas_call(
        functools.partial(inner_kernel, cols),
        out_shape=[
            tracer_shape,
            shaped(3, tiles, deep, LANES),
            shaped(len(PAIRS) + 1, SUB, LANES),
            shaped(2, 2, LEV, SUB, cols),
        ],
        in_specs=[VM],
        out_specs=[HB, VM, VM, VM],
        scratch_shapes=[
            pltpu.VMEM((2, LEV, rows, cols), F32),
            pltpu.SemaphoreType.DMA((5,)),
        ],
        compiler_params=params(),
        cost_estimate=cost(16 << 20, 6 << 20),
        name="inner",
    )(grid)
    border, sums, fresh_rows = pl.pallas_call(
        functools.partial(border_kernel, cols),
        out_shape=[
            shaped(2, 3, tiles, SUB, LANES),
            shaped(devices, LANES),
            shaped(2, 2, LEV, SUB, cols),
        ],
        in_specs=[SM, VM, VM, VM, VM, VM, VM],
        out_specs=[VM, VM, VM],
        scratch_shapes=[
            pltpu.VMEM((2, channels, tiles, EDGE, LANES), F32),
            pltpu.VMEM((2, 3, tiles, EDGE, LANES), F32),
        ],
        compiler_params=params(),
        cost_estimate=cost(2 << 20, 1 << 20),
        name="border",
    )(me, grid, other_rows, pair_rows, powers, part, edges)

    everyone = lax.all_to_all(sums, ("lon", "lat"), 0, 0, tiled=True)
    tracer, stream = pl.pallas_call(
        functools.partial(combine_kernel, cols),
        out_shape=[tracer_shape, shaped(rows, cols)],
        in_specs=[VM, VM, VM, VM, HB],
        out_specs=[HB, HB],
        scratch_shapes=[
            pltpu.VMEM((rows, cols), F32),
            pltpu.SemaphoreType.DMA((4,)),
        ],
        input_output_aliases={4: 0},
        compiler_params=params(),
        cost_estimate=cost(1 << 20, 2 << 20),
        name="combine",
    )(everyone, powers, border, fresh_rows, fixed(tracer))
    return tracer, stream


def solution(mesh):
    placed = (P("lat", "lon", None), P("lat", None), P("lat", "lon"), P(None, "lat", "lon"))
    return jax.shard_map(
        body,
        mesh=mesh,
        in_specs=placed,
        out_specs=(P(None, None, "lat", "lon"), P("lat", "lon")),
        check_vma=False,
    )
```
